32 devices in a mesh: dp: 2 (over x), ctx: 4 (over z), tp: 4 (over y, core).
Axes of the slice: x: 2, y: 2, z: 4, core: 2. Of those that a mesh axis runs over, the one named last changes fastest.
Arguments:
- block_input: bfloat16 [4, 4096, 768], P('dp', ('ctx', 'tp')), may hold values from -6 to 6
- lengths: int32 [4], P('dp'), may hold values from 1024 to 4096, as said below
- cotangent: bfloat16 [4, 4096, 768], P('dp', ('ctx', 'tp')), may hold values from -6 to 6
- query_weight: float32 [768, 768], P(('dp', 'ctx'), 'tp'), may hold values from -0.3125 to 0.3125
- query_bias: float32 [768], P('tp'), may hold values from -3 to 3
- key_weight: float32 [768, 768], P(('dp', 'ctx'), 'tp'), may hold values from -0.21875 to 0.21875
- value_weight: float32 [768, 768], P(('dp', 'ctx'), 'tp'), may hold values from -0.21875 to 0.21875
- value_bias: float32 [768], P('tp'), may hold values from -3 to 3
- output_weight: float32 [768, 768], P('tp', ('dp', 'ctx')), may hold values from -0.875 to 0.875
- output_bias: float32 [768], replicated, may hold values from -3 to 3
- first_gain: float32 [768], replicated, may hold values from 0.25 to 1.75
- first_shift: float32 [768], replicated, may hold values from -3 to 3
- inner_weight: float32 [768, 3072], P(('dp', 'ctx'), 'tp'), may hold values from -0.21875 to 0.21875
- inner_bias: float32 [3072], P('tp'), may hold values from -3 to 3
- outer_weight: float32 [3072, 768], P('tp', ('dp', 'ctx')), may hold values from -0.21875 to 0.21875
- closing_offset_vector: float32 [768], replicated, may hold values from -3 to 3
- second_gain: float32 [768], replicated, may hold values from 0.25 to 1.75
- second_shift: float32 [768], replicated, may hold values from -3 to 3
Outputs:
- output: float32 [4, 4096, 768], P('dp', ('ctx', 'tp'))
- input_grad: float32 [4, 4096, 768], P('dp', ('ctx', 'tp'))
- query_weight_grad: float32 [768, 768], P(('dp', 'ctx'), 'tp')
- query_bias_grad: float32 [768], P('tp')
- key_weight_grad: float32 [768, 768], P(('dp', 'ctx'), 'tp')
- value_weight_grad: float32 [768, 768], P(('dp', 'ctx'), 'tp')
- value_bias_grad: float32 [768], P('tp')
- output_weight_grad: float32 [768, 768], P('tp', ('dp', 'ctx'))
- output_bias_grad: float32 [768], replicated
- first_gain_grad: float32 [768], replicated
- first_shift_grad: float32 [768], replicated
- inner_weight_grad: float32 [768, 3072], P(('dp', 'ctx'), 'tp')
- inner_bias_grad: float32 [3072], P('tp')
- outer_weight_grad: float32 [3072, 768], P('tp', ('dp', 'ctx'))
- outer_bias_grad: float32 [768], replicated
- second_gain_grad: float32 [768], replicated
- second_shift_grad: float32 [768], replicated
The draws below stay inside these ranges and needn't reach their ends.
Inputs may be any that keep to these rules, and one draw needn't show every extreme that they name: `lengths`: valid slots come first in each sequence; some sequence has exactly 4096 valid slots and another exactly 1024.
All inputs are finite; a program needn't handle non-finite values.
Results may differ from the reference program's by a relative error of at most 0.02.
The reference program's roundings to bfloat16 on the way count: a program that leaves them out, or rounds other values in their place, can miss the bound.
Values may be sent and summed in bfloat16 or wider, within the bound.
No kernel may reach another device: no remote copies, remote signals or barrier semaphores. Data moves between devices by JAX's collectives and lax.ppermute only.
A program may use at most 192 MiB of HBM per device.

```python
import math
import jax
import jax.numpy as jnp
from jax import lax

D = 768
HEADS = 12
HD = 64
FF = 3072
LEN = 4096
MIN_LEN = 1024
SEQS = 4


def draw_lengths(key, part):
    drawn = jax.random.randint(jax.random.fold_in(key, 11), (SEQS,), MIN_LEN, LEN + 1, dtype=jnp.int32)
    shuffle = jax.random.permutation(jax.random.fold_in(key, 12), SEQS)
    drawn = drawn.at[shuffle[0]].set(LEN)
    return drawn.at[shuffle[1]].set(MIN_LEN)


def block_scale(rng, shape, split, smallest, top_value):
    loudness = 1.0
    for axis_at, parts in split:
        steps = jax.random.uniform(jax.random.fold_in(jax.random.fold_in(rng, 6), axis_at), (parts,), jnp.float32, smallest / len(split), top_value / len(split))
        loudness = loudness * jnp.repeat(jnp.exp(steps), shape[axis_at] // parts).reshape((-1,) + (1,) * (len(shape) - 1 - axis_at))
    return loudness


def scatter_about(key, shape, deviation, reach, shards=(), kind=jnp.bfloat16):
    array = deviation * jax.random.normal(key, shape, jnp.float32)
    if shards:
        array = array * block_scale(key, shape, shards, -0.22, 0.18)
    return jnp.clip(array, -reach, reach).astype(kind)


def setup_inputs(seed: int = 0) -> dict:
    keys = jax.random.split(jax.random.key(seed), 19)
    block_input = scatter_about(keys[0], (SEQS, LEN, D), 1.0, 6.0, ((0, 2), (1, 16)))
    lengths = draw_lengths(jax.random.fold_in(keys[18], 71), 0)
    cotangent = scatter_about(keys[2], (SEQS, LEN, D), 1.0, 6.0, ((0, 2), (1, 16)))
    query_weight = scatter_about(keys[3], (D, D), (D // 2) ** -0.5, 0.3125, ((0, 8), (1, 4)), jnp.float32)
    query_bias = scatter_about(keys[4], (D,), 0.5, 3.0, ((0, 4),), jnp.float32)
    key_weight = scatter_about(keys[5], (D, D), D ** -0.5, 0.21875, ((0, 8), (1, 4)), jnp.float32)
    value_weight = scatter_about(keys[6], (D, D), D ** -0.5, 0.21875, ((0, 8), (1, 4)), jnp.float32)
    value_bias = scatter_about(keys[7], (D,), 0.5, 3.0, ((0, 4),), jnp.float32)
    output_weight = scatter_about(keys[8], (D, D), (D // 16) ** -0.5, 0.875, ((0, 4), (1, 8)), jnp.float32)
    output_bias = scatter_about(keys[9], (D,), 0.5, 3.0, (), jnp.float32)
    first_gain = jnp.clip(1.0 + 0.15 * jax.random.normal(keys[10], (D,), jnp.float32), 0.25, 1.75)
    first_shift = scatter_about(keys[11], (D,), 0.5, 3.0, (), jnp.float32)
    inner_weight = scatter_about(keys[12], (D, FF), D ** -0.5, 0.21875, ((0, 8), (1, 4)), jnp.float32)
    inner_bias = scatter_about(keys[13], (FF,), 0.5, 3.0, ((0, 4),), jnp.float32)
    outer_weight = scatter_about(keys[14], (FF, D), (FF // 4) ** -0.5, 0.21875, ((0, 4), (1, 8)), jnp.float32)
    closing_offset_vector = scatter_about(keys[15], (D,), 0.5, 3.0, (), jnp.float32)
    second_gain = jnp.clip(1.0 + 0.15 * jax.random.normal(keys[16], (D,), jnp.float32), 0.25, 1.75)
    second_shift = scatter_about(keys[17], (D,), 0.5, 3.0, (), jnp.float32)
    return {"block_input": block_input, "lengths": lengths, "cotangent": cotangent, "query_weight": query_weight, "query_bias": query_bias, "key_weight": key_weight, "value_weight": value_weight, "value_bias": value_bias, "output_weight": output_weight, "output_bias": output_bias, "first_gain": first_gain, "first_shift": first_shift, "inner_weight": inner_weight, "inner_bias": inner_bias, "outer_weight": outer_weight, "closing_offset_vector": closing_offset_vector, "second_gain": second_gain, "second_shift": second_shift}


@jax.custom_vjp
def low(v):
    return lax.optimization_barrier(v.astype(jnp.bfloat16)).astype(jnp.float32)

@jax.custom_vjp
def low_back(v):
    return v

def low_keep(v):
    return (low(v), None)

def low_pass(kept, grad):
    return (grad,)

def back_keep(v):
    return (v, None)

def back_low(kept, grad):
    return (low(grad),)
low.defvjp(low_keep, low_pass)
low_back.defvjp(back_keep, back_low)
EPSILON = 1e-12
NEGATIVE = -1e+30
HIGHEST = lax.Precision.HIGHEST

def both_ways(values):
    return low(low_back(values))

def matmul(floor_slot, ceiling_slot):
    return jnp.dot(floor_slot, ceiling_slot, precision=HIGHEST, preferred_element_type=jnp.float32)

def norm_rows(values, gain_vector, shift_vector):
    average = lax.optimization_barrier(jnp.mean(values, axis=-1, keepdims=True))
    centered = values - average
    variance = lax.optimization_barrier(jnp.mean(centered * centered, axis=-1, keepdims=True))
    return centered * lax.rsqrt(variance + EPSILON) * gain_vector + shift_vector

def attend(query, key, value, sentence_ceiling):
    factor = 1.0 / math.sqrt(HD)
    block_size = min(512, LEN)
    key_valid = jnp.arange(LEN, dtype=jnp.int32) < sentence_ceiling
    query_heads = query.reshape(LEN // block_size, block_size, HEADS, HD)
    key_heads = key.reshape(LEN, HEADS, HD)
    value_heads = value.reshape(LEN, HEADS, HD)

    @jax.checkpoint
    def one_block(query_block):
        scores = low_back(jnp.einsum('qhd,khd->hqk', query_block, key_heads, precision=HIGHEST) * factor)
        scores = jnp.where(key_valid[None, None, :], scores, NEGATIVE)
        highest = lax.optimization_barrier(jnp.max(scores, axis=-1, keepdims=True))
        exponent = jnp.where(key_valid[None, None, :], jnp.exp(scores - highest), 0.0)
        row_total = lax.optimization_barrier(jnp.sum(exponent, axis=-1))
        weighted = jnp.einsum('hqk,khd->qhd', low(exponent), value_heads, precision=HIGHEST)
        return weighted / row_total.T[:, :, None]
    return lax.map(one_block, query_heads).reshape(LEN, HEADS * HD)

def layer(seq_input, sentence_ceiling, params):
    query_weight, query_bias, key_weight, value_weight, value_bias, output_weight, output_bias, first_gain, first_shift, inner_weight, inner_bias, outer_weight, closing_offset_vector, second_gain, second_shift = params
    query = both_ways(matmul(seq_input, low(query_weight)) + query_bias)
    key = both_ways(matmul(seq_input, low(key_weight)))
    value = both_ways(matmul(seq_input, low(value_weight)) + value_bias)
    attended = both_ways(attend(query, key, value, sentence_ceiling))
    attention_part = low_back(matmul(attended, low(output_weight)))
    first_norm = norm_rows(seq_input + attention_part + output_bias, first_gain, first_shift)
    inner_values = low_back(matmul(low(first_norm), low(inner_weight)) + inner_bias)
    active_values = low(jax.nn.gelu(inner_values, approximate=False))
    outer_part = low_back(matmul(active_values, low(outer_weight)))
    second_norm = norm_rows(first_norm + outer_part + closing_offset_vector, second_gain, second_shift)
    row_valid = (jnp.arange(LEN, dtype=jnp.int32) < sentence_ceiling).astype(jnp.float32)
    return second_norm * row_valid[:, None]

def reference(block_input, lengths, cotangent, query_weight, query_bias, key_weight, value_weight, value_bias, output_weight, output_bias, first_gain, first_shift, inner_weight, inner_bias, outer_weight, closing_offset_vector, second_gain, second_shift):
    params = (query_weight.astype(jnp.float32), query_bias.astype(jnp.float32), key_weight.astype(jnp.float32), value_weight.astype(jnp.float32), value_bias.astype(jnp.float32), output_weight.astype(jnp.float32), output_bias.astype(jnp.float32), first_gain.astype(jnp.float32), first_shift.astype(jnp.float32), inner_weight.astype(jnp.float32), inner_bias.astype(jnp.float32), outer_weight.astype(jnp.float32), closing_offset_vector.astype(jnp.float32), second_gain.astype(jnp.float32), second_shift.astype(jnp.float32))
    inputs = block_input.astype(jnp.float32)
    seq_layer = jax.checkpoint(layer)

    def forward(inputs, params):

        def each_seq(folded, element):
            return (folded, seq_layer(element[0], element[1], params))
        _, result = lax.scan(each_seq, jnp.zeros((), jnp.float32), (inputs, lengths))
        return result
    output, pullback = jax.vjp(forward, inputs, params)
    input_grad, grads = pullback(cotangent.astype(jnp.float32))
    return (output, input_grad, grads[0], grads[1], grads[2], grads[3], grads[4], grads[5], grads[6], grads[7], grads[8], grads[9], grads[10], grads[11], grads[12], grads[13], grads[14])
```

```python
import functools
import math

import jax
import jax.numpy as jnp
from jax import lax
from jax.experimental import pallas as pl
from jax.experimental.pallas import tpu as pltpu
from jax.sharding import PartitionSpec as P

HD = 64
PAIR = 2 * HD
EPSILON = 1e-12
NEGATIVE = -1e30
LARGEST = 1e30
BF = jnp.bfloat16
F32 = jnp.float32
VMEM_LIMIT = 56 << 20

NN = (((1,), (0,)), ((), ()))
NT = (((1,), (1,)), ((), ()))
TN = (((0,), (0,)), ((), ()))


def dot(a, b, dims):
    return lax.dot_general(a, b, dims, preferred_element_type=F32)


def params():
    return pltpu.CompilerParams(vmem_limit_bytes=VMEM_LIMIT)


def cost(flops, moved, transcendentals=0):
    return pl.CostEstimate(flops=int(flops), bytes_accessed=int(moved), transcendentals=int(transcendentals))


def swap(value, axis, bit):
    count = lax.axis_size(axis)
    return lax.ppermute(value, axis, [(i, i ^ bit) for i in range(count)])


def ordered(mine, other, upper, dim):
    return jnp.concatenate([jnp.where(upper, other, mine), jnp.where(upper, mine, other)], axis=dim)


def bits_of(axis):
    count = lax.axis_size(axis)
    return [1 << k for k in range(count.bit_length() - 1)]


def gather_rows(value, axis):
    place = lax.axis_index(axis)
    for bit in bits_of(axis):
        value = ordered(value, swap(value, axis, bit), (place & bit) != 0, 0)
    return value


def scatter_rows(value, axis):
    place = lax.axis_index(axis)
    for bit in reversed(bits_of(axis)):
        upper = (place & bit) != 0
        half = value.shape[0] // 2
        low, high = value[:half], value[half:]
        sent = jnp.where(upper, low, high).astype(BF)
        kept = jnp.where(upper, high, low)
        value = kept.astype(F32) + swap(sent, axis, bit).astype(F32)
    return value


def half_lanes(value):
    lane = lax.broadcasted_iota(jnp.int32, value.shape, 1)
    zero = jnp.zeros_like(value)
    return [jnp.where(lane < HD, value, zero), jnp.where(lane >= HD, value, zero)]


def half_rows(value):
    row = lax.broadcasted_iota(jnp.int32, value.shape, 0)
    zero = jnp.zeros_like(value)
    return [jnp.where(row < HD, value, zero), jnp.where(row >= HD, value, zero)]


def below(shape, count):
    return lax.broadcasted_iota(jnp.int32, shape, 0) < count


def attend_kernel(slots, probe, counts, q_own, q_oth, *refs):
    kv = refs[:slots]
    o_own, o_oth, lse_ref, top, total, acc = refs[slots:]
    seq = pl.program_id(0)
    first_slot = counts[2 * slots]
    keys = kv[0].shape[1]
    rows = q_own.shape[1]
    query = jnp.concatenate([q_own[0], q_oth[0]], axis=0)
    heads = half_lanes(query)

    def split(k):
        both = kv[k][0]
        return both[:, :PAIR], both[:, PAIR:]

    def each_slot(run):
        for k in range(slots):
            valid = counts[seq * slots + k]
            pl.when(valid >= keys)(functools.partial(run, k, None))
            pl.when(jnp.logical_and(valid > 0, valid < keys))(functools.partial(run, k, valid))

    for k in range(slots):

        @pl.when(first_slot == k)
        def _(k=k):
            key = kv[k][0, :probe, :PAIR]
            for h in range(2):
                top[h : h + 1, :] = jnp.max(dot(key, heads[h], NT), axis=0, keepdims=True)

    total[...] = jnp.zeros_like(total)
    acc[...] = jnp.zeros_like(acc)

    def quick(k, valid):
        key, value = split(k)
        for h in range(2):
            at = slice(h * HD, h * HD + HD)
            expo = jnp.exp(dot(key, heads[h], NT) - top[h : h + 1, :])
            if valid is not None:
                expo = jnp.where(below(expo.shape, valid), expo, 0.0)
            total[h : h + 1, :] += jnp.sum(expo, axis=0, keepdims=True)
            acc[at, :] += dot(value, expo.astype(BF), TN)[at, :]

    each_slot(quick)
    largest = jnp.max(total[...])

    @pl.when(jnp.logical_not(largest < LARGEST))
    def _():
        total[...] = jnp.zeros_like(total)
        acc[...] = jnp.zeros_like(acc)

        def careful(k, valid):
            key, value = split(k)
            for h in range(2):
                at = slice(h * HD, h * HD + HD)
                one = slice(h, h + 1)
                scores = dot(key, heads[h], NT)
                if valid is not None:
                    scores = jnp.where(below(scores.shape, valid), scores, NEGATIVE)
                old = top[one, :]
                new = jnp.maximum(old, jnp.max(scores, axis=0, keepdims=True))
                expo = jnp.exp(scores - new)
                if valid is not None:
                    expo = jnp.where(below(expo.shape, valid), expo, 0.0)
                scale = jnp.exp(old - new)
                total[one, :] = total[one, :] * scale + jnp.sum(expo, axis=0, keepdims=True)
                acc[at, :] = acc[at, :] * scale + dot(value, expo.astype(BF), TN)[at, :]
                top[one, :] = new

        each_slot(careful)

    for h in range(2):
        at = slice(h * HD, h * HD + HD)
        sums = total[h : h + 1, :]
        part = acc[at, :] / sums
        o_own[0, at, :] = part[:, :rows]
        o_oth[0, at, :] = part[:, rows:].astype(BF)
        lse_ref[0, 0, h : h + 1, :] = top[h : h + 1, :] + jnp.log(sums)


def attend(counts, q_own, q_oth, kv):
    seqs, rows, width = q_own.shape
    slots, keys = len(kv), kv[0].shape[1]
    pairs = width // PAIR
    q_spec = pl.BlockSpec((1, rows, PAIR), lambda s, p, c: (s, 0, p))
    kv_spec = pl.BlockSpec((1, keys, 2 * PAIR), lambda s, p, c: (s, 0, p))
    o_spec = pl.BlockSpec((1, PAIR, rows), lambda s, p, c: (s, p, 0))
    total = seqs * width * 2 * rows * slots * keys
    return pl.pallas_call(
        functools.partial(attend_kernel, slots, min(128, keys)),
        grid_spec=pltpu.PrefetchScalarGridSpec(
            num_scalar_prefetch=1,
            grid=(seqs, pairs),
            in_specs=[q_spec, q_spec] + [kv_spec] * slots,
            out_specs=[o_spec, o_spec, pl.BlockSpec((1, 1, 2, 2 * rows), lambda s, p, c: (s, p, 0, 0))],
            scratch_shapes=[
                pltpu.VMEM((2, 2 * rows), F32),
                pltpu.VMEM((2, 2 * rows), F32),
                pltpu.VMEM((PAIR, 2 * rows), F32),
            ],
        ),
        out_shape=[
            jax.ShapeDtypeStruct((seqs, width, rows), F32),
            jax.ShapeDtypeStruct((seqs, width, rows), BF),
            jax.ShapeDtypeStruct((seqs, pairs, 2, 2 * rows), F32),
        ],
        compiler_params=params(),
        cost_estimate=cost(16 * total, 8 * q_own.size + 2 * slots * kv[0].size, total // HD),
        name="attend",
    )(counts, q_own, q_oth, *kv)


def attend_back_kernel(slots, counts, q_own, q_oth, g_own, g_oth, stats, *refs):
    kv, dq_own, dq_oth = refs[:slots], refs[slots], refs[slots + 1]
    dkv = refs[slots + 2 : 2 * slots + 2]
    acc = refs[2 * slots + 2]
    seq = pl.program_id(0)
    keys = kv[0].shape[1]
    rows = q_own.shape[1]
    acc[...] = jnp.zeros_like(acc)
    queries = [half_lanes(q_own[0]), half_lanes(q_oth[0])]
    grads = [half_rows(g_own[0]), half_rows(g_oth[0])]
    for k in range(slots):
        valid = counts[seq * slots + k]

        def run(masked, k=k, valid=valid):
            both = kv[k][0]
            key, value = both[:, :PAIR], both[:, PAIR:]
            d_key = d_value = None
            for block in range(2):
                lanes = slice(block * rows, block * rows + rows)
                for h in range(2):
                    at = slice(h * HD, h * HD + HD)
                    query, grad = queries[block][h], grads[block][h]
                    prob = jnp.exp(dot(key, query, NT) - stats[0, 0, h : h + 1, lanes])
                    if masked:
                        prob = jnp.where(below(prob.shape, valid), prob, 0.0)
                    change = dot(value, grad, NN) - stats[0, 0, 2 + h : 3 + h, lanes]
                    score = (prob * change).astype(BF)
                    to_value = dot(prob.astype(BF), grad, NT)
                    to_key = dot(score, query, NN)
                    d_value = to_value if d_value is None else d_value + to_value
                    d_key = to_key if d_key is None else d_key + to_key
                    acc[at, lanes] += dot(key, score, TN)[at, :]
            dkv[k][0, :, :PAIR] = d_key.astype(BF)
            dkv[k][0, :, PAIR:] = d_value.astype(BF)

        pl.when(valid >= keys)(functools.partial(run, False))
        pl.when(jnp.logical_and(valid > 0, valid < keys))(functools.partial(run, True))

        @pl.when(valid <= 0)
        def _(k=k):
            dkv[k][...] = jnp.zeros_like(dkv[k])

    scaled = acc[...] * (1.0 / math.sqrt(HD))
    dq_own[0] = scaled[:, :rows]
    dq_oth[0] = scaled[:, rows:].astype(BF)


def attend_back(counts, q_own, q_oth, g_own, g_oth, stats, kv):
    seqs, rows, width = q_own.shape
    slots, keys = len(kv), kv[0].shape[1]
    pairs = width // PAIR
    q_spec = pl.BlockSpec((1, rows, PAIR), lambda s, p, c: (s, 0, p))
    t_spec = pl.BlockSpec((1, PAIR, rows), lambda s, p, c: (s, p, 0))
    kv_spec = pl.BlockSpec((1, keys, 2 * PAIR), lambda s, p, c: (s, 0, p))
    total = seqs * width * 2 * rows * slots * keys
    out = pl.pallas_call(
        functools.partial(attend_back_kernel, slots),
        grid_spec=pltpu.PrefetchScalarGridSpec(
            num_scalar_prefetch=1,
            grid=(seqs, pairs),
            in_specs=[q_spec, q_spec, t_spec, t_spec]
            + [pl.BlockSpec((1, 1, 4, 2 * rows), lambda s, p, c: (s, p, 0, 0))]
            + [kv_spec] * slots,
            out_specs=[t_spec, t_spec] + [kv_spec] * slots,
            scratch_shapes=[pltpu.VMEM((PAIR, 2 * rows), F32)],
        ),
        out_shape=[
            jax.ShapeDtypeStruct((seqs, width, rows), F32),
            jax.ShapeDtypeStruct((seqs, width, rows), BF),
        ]
        + [jax.ShapeDtypeStruct(kv[0].shape, BF)] * slots,
        compiler_params=params(),
        cost_estimate=cost(40 * total, 14 * q_own.size + 4 * slots * kv[0].size, total // HD),
        name="attend_back",
    )(counts, q_own, q_oth, g_own, g_oth, stats, *kv)
    return out[0], out[1], out[2:]


def gelu_parts(u):
    density = jnp.exp(-0.5 * u * u)
    t = 1.0 / (1.0 + (0.3275911 / math.sqrt(2.0)) * jnp.abs(u))
    series = t * (
        0.254829592
        + t * (-0.284496736 + t * (1.421413741 + t * (-1.453152027 + t * 1.061405429)))
    )
    tail = 0.5 * series * density
    share = jnp.where(u < 0.0, tail, 1.0 - tail)
    return u * share, share + u * (density * (1.0 / math.sqrt(2.0 * math.pi)))


def feed_kernel(rows_ref, w_in, bias, w_out, active_ref, slope_ref, part_ref):
    inner = dot(rows_ref[...], w_in[...], NN) + bias[...]
    active, slope = gelu_parts(inner)
    active = active.astype(BF)
    active_ref[...] = active
    slope_ref[...] = slope.astype(BF)
    part_ref[...] = dot(active, w_out[...], NT)


def feed(rows, w_in, bias, w_out):
    count, width = rows.shape
    units = w_in.shape[1]
    block = min(256, count)
    whole = lambda i: (0, 0)
    by_row = lambda i: (i, 0)
    return pl.pallas_call(
        feed_kernel,
        grid=(count // block,),
        in_specs=[
            pl.BlockSpec((block, width), by_row),
            pl.BlockSpec((width, units), whole, pipeline_mode=pl.Buffered(1)),
            pl.BlockSpec((1, units), whole),
            pl.BlockSpec((width, units), whole, pipeline_mode=pl.Buffered(1)),
        ],
        out_specs=[
            pl.BlockSpec((block, units), by_row),
            pl.BlockSpec((block, units), by_row),
            pl.BlockSpec((block, width), by_row),
        ],
        out_shape=[
            jax.ShapeDtypeStruct((count, units), BF),
            jax.ShapeDtypeStruct((count, units), BF),
            jax.ShapeDtypeStruct((count, width), F32),
        ],
        compiler_params=params(),
        cost_estimate=cost(4 * count * width * units, 4 * width * units + 4 * count * units + 6 * count * width, count * units),
        name="feed",
    )(rows, w_in, bias, w_out)


def feed_back_kernel(steps, low_ref, rows_ref, active_ref, slope_ref, w_in, w_out, part_ref, d_in_ref, d_out_ref, d_bias_ref, d_in, d_out):
    step = pl.program_id(0)

    @pl.when(step == 0)
    def _():
        d_in[...] = jnp.zeros_like(d_in)
        d_out[...] = jnp.zeros_like(d_out)
        d_bias_ref[...] = jnp.zeros_like(d_bias_ref)

    low = low_ref[...]
    inner = (dot(low, w_out[...], NN) * slope_ref[...].astype(F32)).astype(BF)
    part_ref[...] = dot(inner, w_in[...], NT)
    d_out[...] += dot(low, active_ref[...], TN)
    d_in[...] += dot(rows_ref[...], inner, TN)
    d_bias_ref[...] += jnp.sum(inner.astype(F32), axis=0, keepdims=True)

    @pl.when(step == steps - 1)
    def _():
        d_in_ref[...] = d_in[...].astype(BF)
        d_out_ref[...] = d_out[...].astype(BF)


def feed_back(low, rows, active, slope, w_in, w_out):
    count, width = rows.shape
    units = w_in.shape[1]
    block = min(256, count)
    whole = lambda i: (0, 0)
    by_row = lambda i: (i, 0)
    once = pl.Buffered(1)
    return pl.pallas_call(
        functools.partial(feed_back_kernel, count // block),
        grid=(count // block,),
        in_specs=[
            pl.BlockSpec((block, width), by_row),
            pl.BlockSpec((block, width), by_row),
            pl.BlockSpec((block, units), by_row),
            pl.BlockSpec((block, units), by_row),
            pl.BlockSpec((width, units), whole, pipeline_mode=once),
            pl.BlockSpec((width, units), whole, pipeline_mode=once),
        ],
        out_specs=[
            pl.BlockSpec((block, width), by_row),
            pl.BlockSpec((width, units), whole),
            pl.BlockSpec((width, units), whole),
            pl.BlockSpec((1, units), whole),
        ],
        out_shape=[
            jax.ShapeDtypeStruct((count, width), F32),
            jax.ShapeDtypeStruct((width, units), BF),
            jax.ShapeDtypeStruct((width, units), BF),
            jax.ShapeDtypeStruct((1, units), F32),
        ],
        scratch_shapes=[pltpu.VMEM((width, units), F32), pltpu.VMEM((width, units), F32)],
        compiler_params=params(),
        cost_estimate=cost(8 * count * width * units, 8 * width * units + 4 * count * units + 8 * count * width),
        name="feed_back",
    )(low, rows, active, slope, w_in, w_out)


def centre(values):
    middle = values - jnp.mean(values, axis=-1, keepdims=True)
    scale = lax.rsqrt(jnp.mean(middle * middle, axis=-1, keepdims=True) + EPSILON)
    return middle * scale, scale


def back_through(weighted, normal, scale):
    first = jnp.mean(weighted, axis=-1, keepdims=True)
    second = jnp.mean(weighted * normal, axis=-1, keepdims=True)
    return (weighted - first - normal * second) * scale


def first_kernel(x_ref, mine_ref, came_ref, vec_ref, normal_ref, scale_ref, low_ref):
    sums = x_ref[...].astype(F32) + (mine_ref[...] + came_ref[...].astype(F32)) + vec_ref[0:1, :]
    normal, scale = centre(sums)
    normal_ref[...] = normal
    scale_ref[...] = scale
    low_ref[...] = (normal * vec_ref[1:2, :] + vec_ref[2:3, :]).astype(BF)


def second_kernel(per_seq, counts, normal_ref, mine_ref, came_ref, cot_ref, vec_ref, out_ref, grad_ref, low_ref, sums_ref):
    step = pl.program_id(0)
    block = normal_ref.shape[0]
    valid = counts[step // per_seq] - (step % per_seq) * block
    keep = lax.broadcasted_iota(jnp.int32, normal_ref.shape, 0) < valid

    @pl.when(step == 0)
    def _():
        sums_ref[...] = jnp.zeros_like(sums_ref)

    first = normal_ref[...] * vec_ref[1:2, :] + vec_ref[2:3, :]
    sums = first + (mine_ref[...] + came_ref[...].astype(F32)) + vec_ref[3:4, :]
    normal, scale = centre(sums)
    out_ref[...] = jnp.where(keep, normal * vec_ref[4:5, :] + vec_ref[5:6, :], 0.0)
    out_grad = jnp.where(keep, cot_ref[...].astype(F32), 0.0)
    grad = back_through(out_grad * vec_ref[4:5, :], normal, scale)
    grad_ref[...] = grad
    low_ref[...] = grad.astype(BF)
    sums_ref[0:1, :] += jnp.sum(out_grad * normal, axis=0, keepdims=True)
    sums_ref[1:2, :] += jnp.sum(out_grad, axis=0, keepdims=True)
    sums_ref[2:3, :] += jnp.sum(grad, axis=0, keepdims=True)


def first_back_kernel(grad_ref, mine_ref, came_ref, normal_ref, scale_ref, vec_ref, out_ref, low_ref, sums_ref):
    @pl.when(pl.program_id(0) == 0)
    def _():
        sums_ref[...] = jnp.zeros_like(sums_ref)

    given = grad_ref[...] + (mine_ref[...] + came_ref[...].astype(F32))
    normal = normal_ref[...]
    grad = back_through(given * vec_ref[1:2, :], normal, scale_ref[...])
    out_ref[...] = grad
    low_ref[...] = grad.astype(BF)
    sums_ref[0:1, :] += jnp.sum(given * normal, axis=0, keepdims=True)
    sums_ref[1:2, :] += jnp.sum(given, axis=0, keepdims=True)
    sums_ref[2:3, :] += jnp.sum(grad, axis=0, keepdims=True)


def row_call(kernel, name, block, count, width, inputs, whole_inputs, outs, sums, counts=None):
    by_row = lambda i, *c: (i, 0)
    whole = lambda i, *c: (0, 0)
    in_specs = [pl.BlockSpec((block, a.shape[1]), by_row) for a in inputs]
    in_specs += [pl.BlockSpec(a.shape, whole) for a in whole_inputs]
    out_specs = [pl.BlockSpec((block, w), by_row) for w, _ in outs]
    out_shape = [jax.ShapeDtypeStruct((count, w), t) for w, t in outs]
    if sums:
        out_specs.append(pl.BlockSpec((8, width), whole))
        out_shape.append(jax.ShapeDtypeStruct((8, width), F32))
    prefetch = 0 if counts is None else 1
    moved = sum(a.size * a.dtype.itemsize for a in inputs) + sum(count * w * 4 for w, _ in outs)
    return pl.pallas_call(
        kernel,
        grid_spec=pltpu.PrefetchScalarGridSpec(
            num_scalar_prefetch=prefetch, grid=(count // block,), in_specs=in_specs, out_specs=out_specs
        ),
        out_shape=out_shape,
        compiler_params=params(),
        cost_estimate=cost(20 * count * width, moved),
        name=name,
    )(*(() if counts is None else (counts,)), *inputs, *whole_inputs)


def interleaved(key, value):
    width = key.shape[1]
    pieces = []
    for start in range(0, width, PAIR):
        pieces += [key[:, start : start + PAIR], value[:, start : start + PAIR]]
    return jnp.concatenate(pieces, axis=1)


def apart(both):
    keys, values = [], []
    for start in range(0, both.shape[1], 2 * PAIR):
        keys.append(both[:, start : start + PAIR])
        values.append(both[:, start + PAIR : start + 2 * PAIR])
    return jnp.concatenate(keys, axis=1), jnp.concatenate(values, axis=1)


def on_device(
    block_input,
    lengths,
    cotangent,
    query_weight,
    query_bias,
    key_weight,
    value_weight,
    value_bias,
    output_weight,
    output_bias,
    first_gain,
    first_shift,
    inner_weight,
    inner_bias,
    outer_weight,
    closing_offset_vector,
    second_gain,
    second_shift,
):
    seqs, local, width = block_input.shape
    chip = 2 * local
    spots = lax.axis_size("ctx")
    spot = lax.axis_index("ctx")
    part = lax.axis_index("tp")
    core, side = part % 2, part // 2
    is_upper_core, is_upper_side = core == 1, side == 1
    span = local * lax.axis_size("tp")
    heads_width = query_weight.shape[1]
    unit_width = inner_weight.shape[1]
    count = seqs * local

    def other_core(value):
        return swap(value, "tp", 1)

    def other_side(value):
        return swap(value, "tp", 2)

    def chip_rows(value):
        return ordered(value, other_core(value), is_upper_core, 1)

    def core_sum_parts(partial):
        mine = jnp.where(is_upper_core, partial[:, local:], partial[:, :local])
        sent = jnp.where(is_upper_core, partial[:, :local], partial[:, local:]).astype(BF)
        return mine, other_core(sent)

    def flat(value):
        return value.reshape(-1, value.shape[-1])

    starts = jnp.stack([(spot ^ k) * span + side * chip for k in range(spots)])
    key_counts = jnp.clip(lengths[:, None] - starts[None, :], 0, chip).reshape(-1)
    counts = jnp.concatenate([key_counts, jnp.full((1,), spot, jnp.int32)]).astype(jnp.int32)
    row_counts = jnp.clip(lengths - (spot * span + part * local), 0, local).astype(jnp.int32)

    def all_rows(value):
        return gather_rows(value, "dp")

    attention_shard = jnp.concatenate([query_weight, key_weight, value_weight], axis=1).astype(BF)
    other_shard = jnp.concatenate([output_weight.T, inner_weight, outer_weight.T], axis=1).astype(BF)

    def both_sides(shard, widths):
        low = gather_rows(shard, "ctx")
        came = other_side(low)
        pieces, start = [], 0
        for w in widths:
            cut = slice(start, start + w)
            pieces.append(ordered(low[:, cut], came[:, cut], is_upper_side, 1))
            start += w
        return pieces

    query_c, key_c, value_c = both_sides(attention_shard, [heads_width] * 3)
    attention_full = all_rows(jnp.concatenate([query_c, interleaved(key_c, value_c)], axis=1))
    own_width = 2 * heads_width
    query_full, kv_full = attention_full[:, :own_width], attention_full[:, own_width:]
    output_c, inner_c, outer_c = both_sides(other_shard, [heads_width, unit_width, unit_width])
    output_full, inner_full, outer_full = all_rows(output_c), all_rows(inner_c), all_rows(outer_c)

    biases = jnp.concatenate([query_bias, value_bias, inner_bias])[None, :]
    biases_came = other_side(biases)
    query_b = ordered(biases[:, :heads_width], biases_came[:, :heads_width], is_upper_side, 1)
    cut = slice(heads_width, 2 * heads_width)
    value_b = ordered(biases[:, cut], biases_came[:, cut], is_upper_side, 1)
    cut = slice(2 * heads_width, None)
    inner_b = ordered(biases[:, cut], biases_came[:, cut], is_upper_side, 1)
    kv_bias = interleaved(jnp.zeros_like(value_b), value_b)

    if spots == 4:
        far = swap(block_input, "ctx", 2)
        near = swap(block_input, "ctx", 1)
        middle = lax.ppermute(block_input, "ctx", [(1, 2), (2, 1)])
        passed = lax.ppermute(far, "ctx", [(2, 3), (1, 0)])
        last = jnp.where(jnp.logical_or(spot == 1, spot == 2), middle, passed)
        arrived = [near, far, last]
    else:
        arrived = [swap(block_input, "ctx", k) for k in range(1, spots)]
    across = other_side(block_input)
    x_slots = [chip_rows(block_input)] + [chip_rows(a) for a in arrived]
    x_own, x_oth = x_slots[0], chip_rows(across)

    scale = 1.0 / math.sqrt(HD)

    def to_query(rows):
        made = jnp.einsum("srd,df->srf", rows, query_full, preferred_element_type=F32) + query_b
        return made.astype(BF) * jnp.asarray(scale, BF)

    def to_kv(rows):
        made = jnp.einsum("srd,df->srf", rows, kv_full, preferred_element_type=F32) + kv_bias
        return made.astype(BF)

    q_own, q_oth = to_query(x_own), to_query(x_oth)
    kv = [to_kv(rows) for rows in x_slots]

    o_own, o_oth, lse = attend(counts, q_own, q_oth, kv)
    o_came = other_side(o_oth)
    lse_own = lse[..., :chip]
    lse_came = other_side(lse[..., chip:])
    lse_top = jnp.maximum(lse_own, lse_came)
    share_own, share_came = jnp.exp(lse_own - lse_top), jnp.exp(lse_came - lse_top)
    share_sum = share_own + share_came
    lse_all = lse_top + jnp.log(share_sum)

    def by_head(value):
        return value.reshape(seqs, -1, 2, HD, chip)

    attended = by_head(o_own) * (share_own / share_sum)[:, :, :, None, :] + by_head(o_came).astype(F32) * (
        share_came / share_sum
    )[:, :, :, None, :]
    attended = attended.reshape(seqs, own_width, chip)
    attended_low = attended.astype(BF)

    vectors = jnp.stack([output_bias, first_gain, first_shift, closing_offset_vector, second_gain, second_shift])
    vectors = jnp.concatenate([vectors, jnp.zeros((2, width), F32)])
    block = local // 2

    attention_part = jnp.einsum("sfr,df->srd", attended_low, output_full, preferred_element_type=F32)
    mine, came = core_sum_parts(attention_part)
    normal, spread, first_low = row_call(
        first_kernel,
        "first_norm",
        block,
        count,
        width,
        [flat(block_input), flat(mine), flat(came)],
        [vectors],
        [(width, F32), (1, F32), (width, BF)],
        False,
    )
    first_rows = chip_rows(first_low.reshape(seqs, local, width))
    active, slope, feed_part = feed(flat(first_rows), inner_full, inner_b, outer_full)
    mine, came = core_sum_parts(feed_part.reshape(seqs, chip, width))
    output, second_grad, outer_low, second_sums = row_call(
        functools.partial(second_kernel, local // block),
        "second_norm",
        block,
        count,
        width,
        [normal, flat(mine), flat(came), flat(cotangent)],
        [vectors],
        [(width, F32), (width, F32), (width, BF)],
        True,
        row_counts,
    )
    outer_rows = chip_rows(outer_low.reshape(seqs, local, width))
    back_part, d_inner, d_outer, d_inner_bias = feed_back(
        flat(outer_rows), flat(first_rows), active, slope, inner_full, outer_full
    )
    mine, came = core_sum_parts(back_part.reshape(seqs, chip, width))
    first_grad, attn_low, first_sums = row_call(
        first_back_kernel,
        "first_norm_back",
        block,
        count,
        width,
        [second_grad, flat(mine), flat(came), normal, spread],
        [vectors],
        [(width, F32), (width, BF)],
        True,
    )
    attn_rows = chip_rows(attn_low.reshape(seqs, local, width))
    d_output = jnp.einsum("srd,sfr->df", attn_rows, attended_low, preferred_element_type=F32)
    g_own = jnp.einsum("srd,df->sfr", attn_rows, output_full, preferred_element_type=F32).astype(BF)
    delta = jnp.sum((g_own.astype(F32) * attended).reshape(seqs, -1, 2, HD, chip), axis=3)
    stats_own = jnp.concatenate([lse_all, delta], axis=2)
    g_oth, stats_oth = other_side(g_own), other_side(stats_own)
    stats = jnp.concatenate([stats_own, stats_oth], axis=3)

    dq_own, dq_oth, dkv = attend_back(counts, q_own, q_oth, g_own, g_oth, stats, kv)
    query_low = (dq_own + other_side(dq_oth).astype(F32)).astype(BF)
    d_query = jnp.einsum("srd,sfr->df", x_own, query_low, preferred_element_type=F32)
    d_kv = sum(
        jnp.einsum("srd,srf->df", rows, grads, preferred_element_type=F32) for rows, grads in zip(x_slots, dkv)
    )

    def to_input(grads):
        return jnp.einsum("srf,df->srd", grads, kv_full, preferred_element_type=F32)

    own_part = to_input(dkv[0]) + jnp.einsum("sfr,df->srd", query_low, query_full, preferred_element_type=F32)
    mine, came = core_sum_parts(own_part)
    input_grad = first_grad.reshape(seqs, local, width) + (mine + came.astype(F32))
    terms = []
    for grads in dkv[1:]:
        mine, came = core_sum_parts(to_input(grads))
        terms.append(mine + came.astype(F32))
    if spots == 4:
        near, far, last = terms
        last = last.astype(BF)
        far = far + lax.ppermute(last, "ctx", [(3, 2), (0, 1)]).astype(F32)
        middle = lax.ppermute(last, "ctx", [(1, 2), (2, 1)])
        arrived = [swap(near.astype(BF), "ctx", 1), swap(far.astype(BF), "ctx", 2), middle]
    else:
        arrived = [swap(t.astype(BF), "ctx", k + 1) for k, t in enumerate(terms)]
    for a in arrived:
        input_grad = input_grad + a.astype(F32)

    def to_owner(pieces):
        halves = [scatter_rows(p, "dp") for p in pieces]
        sent, kept = [], []
        for p in halves:
            w = p.shape[1] // 2
            sent.append(jnp.where(is_upper_side, p[:, :w], p[:, w:]).astype(BF))
            kept.append(jnp.where(is_upper_side, p[:, w:], p[:, :w]))
        sent, kept = jnp.concatenate(sent, axis=1), jnp.concatenate(kept, axis=1)
        return scatter_rows(kept + other_side(sent).astype(F32), "ctx")

    feed_owned = to_owner([d_inner, d_outer])
    output_owned = to_owner([d_output])
    d_key, d_value = apart(d_kv)
    attention_owned = to_owner([d_query, d_key, d_value])

    d_query_bias = jnp.sum(query_low.astype(F32), axis=(0, 2))
    d_value_bias = jnp.sum(apart(sum(jnp.sum(g.astype(F32), axis=(0, 1)) for g in dkv)[None, :])[1], axis=0)

    def everywhere(vector):
        for axis, bits in (("tp", [2]), ("ctx", bits_of("ctx")), ("dp", bits_of("dp"))):
            for bit in bits:
                vector = vector + swap(vector, axis, bit)
        return vector

    shared = jnp.concatenate([second_sums[:3], first_sums[:3]])
    shared = shared + other_core(shared)
    early = everywhere(jnp.concatenate([shared.reshape(-1), d_inner_bias.reshape(-1)])[None, :])[0]
    late = everywhere(jnp.concatenate([d_query_bias, d_value_bias])[None, :])[0]
    shared = early[: 6 * width].reshape(6, width)

    def own_side(vector):
        w = vector.shape[0] // 2
        return jnp.where(is_upper_side, vector[w:], vector[:w])

    return (
        output.reshape(seqs, local, width),
        input_grad,
        attention_owned[:, :heads_width],
        own_side(late[:own_width]),
        attention_owned[:, heads_width : 2 * heads_width],
        attention_owned[:, 2 * heads_width :],
        own_side(late[own_width:]),
        output_owned.T,
        shared[5],
        shared[3],
        shared[4],
        feed_owned[:, :unit_width],
        own_side(early[6 * width :]),
        feed_owned[:, unit_width:].T,
        shared[2],
        shared[0],
        shared[1],
    )


def solution(mesh):
    rows = P("dp", ("ctx", "tp"), None)
    into = P(("dp", "ctx"), "tp")
    out_of = P("tp", ("dp", "ctx"))
    split, whole = P("tp"), P()
    return jax.shard_map(
        on_device,
        mesh=mesh,
        in_specs=(
            rows, P("dp"), rows, into, split, into, into, split, out_of, whole, whole, whole,
            into, split, out_of, whole, whole, whole,
        ),
        out_specs=(
            rows, rows, into, split, into, into, split, out_of, whole, whole, whole,
            into, split, out_of, whole, whole, whole,
        ),
        check_vma=False,
    )
```

```python
import functools
import math

import jax
import jax.numpy as jnp
from jax import lax
from jax.experimental import pallas as pl
from jax.experimental.pallas import tpu as pltpu
from jax.sharding import PartitionSpec as P

HD = 64
PAIR = 2 * HD
EPSILON = 1e-12
NEGATIVE = -1e30
LARGEST = 1e30
BF = jnp.bfloat16
F32 = jnp.float32
VMEM_LIMIT = 56 << 20
FEED_ROWS = 512

NN = (((1,), (0,)), ((), ()))
NT = (((1,), (1,)), ((), ()))
TN = (((0,), (0,)), ((), ()))


def dot(a, b, dims):
    return lax.dot_general(a, b, dims, preferred_element_type=F32)


def params():
    return pltpu.CompilerParams(vmem_limit_bytes=VMEM_LIMIT)


def cost(flops, moved, transcendentals=0):
    return pl.CostEstimate(flops=int(flops), bytes_accessed=int(moved), transcendentals=int(transcendentals))


def after(value, *others):
    if not others:
        return value
    return lax.optimization_barrier((value, *others))[0]


def swap(value, axis, bit, start=(), done=()):
    count = lax.axis_size(axis)
    return after(lax.ppermute(after(value, *start), axis, [(i, i ^ bit) for i in range(count)]), *done)


def bits_of(axis):
    count = lax.axis_size(axis)
    return [1 << k for k in range(count.bit_length() - 1)]


def halves(value, upper, dim):
    size = value.shape[dim] // 2
    at = upper.astype(jnp.int32) * size
    mine = lax.dynamic_slice_in_dim(value, at, size, dim)
    return mine, lax.dynamic_slice_in_dim(value, size - at, size, dim)


def ordered(mine, other, upper, dim):
    return jnp.concatenate([jnp.where(upper, other, mine), jnp.where(upper, mine, other)], axis=dim)


def call(kernel, name, outs, *arrays, prefetch=None, scratch=(), flops=0):
    spec = lambda shape: pl.BlockSpec(shape, lambda i, *c: (0,) * len(shape))
    arrays_moved = sum(a.size * a.dtype.itemsize for a in arrays) + sum(4 * math.prod(shape) for shape, _ in outs)
    return pl.pallas_call(
        kernel,
        grid_spec=pltpu.PrefetchScalarGridSpec(
            num_scalar_prefetch=0 if prefetch is None else 1,
            grid=(1,),
            in_specs=[spec(a.shape) for a in arrays],
            out_specs=[spec(shape) for shape, _ in outs],
            scratch_shapes=list(scratch),
        ),
        out_shape=[jax.ShapeDtypeStruct(shape, kind) for shape, kind in outs],
        compiler_params=params(),
        cost_estimate=cost(flops, arrays_moved),
        name=name,
    )(*(() if prefetch is None else (prefetch,)), *arrays)


def fits(rows):
    return rows % 16 == 0


def pack(pieces, turned):
    widths = [p.shape[0] if t else p.shape[1] for p, t in zip(pieces, turned)]
    rows = pieces[0].shape[1] if turned[0] else pieces[0].shape[0]
    if not fits(rows):
        return jnp.concatenate([p.T if t else p for p, t in zip(pieces, turned)], axis=1).astype(BF)

    spare = -sum(widths) % 128

    def kernel(*refs):
        whole = [r[...].T if t else r[...] for r, t in zip(refs, turned)]
        if spare:
            whole.append(jnp.zeros((rows, spare), F32))
        refs[-1][...] = jnp.concatenate(whole, axis=1).astype(BF)

    return call(kernel, "pack", [((rows, sum(widths) + spare), BF)], *pieces)[0]


def stack(parts):
    rows, width = parts[0].shape
    if not fits(rows):
        return jnp.concatenate(parts, axis=0)

    def kernel(*refs):
        for k, ref in enumerate(refs[:-1]):
            refs[-1][k * rows : k * rows + rows, :] = ref[...]

    return call(kernel, "stack", [((rows * len(parts), width), BF)], *parts)[0]


def over_dp(arrays, done=()):
    found = [arrays]
    for bit in bits_of("dp"):
        found = found + [[swap(a, "dp", bit, (), done) for a in one] for one in found]
    return found


def place(found, widths, joined):
    spots, spot = lax.axis_size("ctx"), lax.axis_index("ctx")
    line, side = lax.axis_index("dp"), lax.axis_index("tp") // 2
    lines = len(found)
    starts = [sum(widths[:k]) for k in range(len(widths))]
    block = found[0][0].shape[0]
    rows = block // spots
    cuts = list(zip(starts, widths))
    shapes = [(block * lines, 2 * sum(widths[m] for m in members)) for members in joined]
    if not fits(rows):
        order = ((jnp.arange(lines)[:, None] ^ line) * spots + (jnp.arange(spots)[None, :] ^ spot)).reshape(-1)
        own, oth = (
            jnp.stack([f[h] for f in found]).reshape(lines * spots, rows, -1)[order].reshape(lines * block, -1)
            for h in range(2)
        )
        low, high = jnp.where(side == 1, oth, own), jnp.where(side == 1, own, oth)
        full = [jnp.concatenate([low[:, t : t + w], high[:, t : t + w]], axis=1) for t, w in cuts]
        return [full[m[0]] if len(m) == 1 else interleaved(full[m[0]], full[m[1]]) for m in joined]

    def kernel(where, *refs):
        outs = refs[2 * lines :]
        upper = where[2] == 1
        for k in range(lines):
            own_ref, oth_ref = refs[2 * k], refs[2 * k + 1]
            for c in range(spots):
                came = pl.ds(pl.multiple_of((where[0] ^ c) * rows, rows), rows)
                to = pl.ds(pl.multiple_of(((where[1] ^ k) * spots + c) * rows, rows), rows)
                own, oth = own_ref[came, :], oth_ref[came, :]
                low, high = jnp.where(upper, oth, own), jnp.where(upper, own, oth)
                full = [jnp.concatenate([low[:, t : t + w], high[:, t : t + w]], axis=1) for t, w in cuts]
                for out, members in zip(outs, joined):
                    if len(members) == 1:
                        out[to, :] = full[members[0]]
                    else:
                        both = []
                        for p in range(0, full[members[0]].shape[1], PAIR):
                            both += [full[m][:, p : p + PAIR] for m in members]
                        out[to, :] = jnp.concatenate(both, axis=1)

    where = jnp.stack([spot, line, side]).astype(jnp.int32)
    flat = [a for one in found for a in one]
    return call(kernel, "place", [(shape, BF) for shape in shapes], *flat, prefetch=where)


def fold_sides(pairs, cuts):
    rows = pairs[0][0].shape[0]
    width = sum(w for low, _ in cuts for _, _, w in low)
    spare = -width % 128
    width += spare
    side = lax.axis_index("tp") // 2

    def both(totals):
        end = [jnp.zeros((totals[0].shape[0], spare), F32)] if spare else []
        low = jnp.concatenate([totals[p][:, t : t + w] for cut, _ in cuts for p, t, w in cut] + end, axis=1)
        high = jnp.concatenate([totals[p][:, t : t + w] for _, cut in cuts for p, t, w in cut] + end, axis=1)
        return low, high

    if not fits(rows):
        low, high = both([a.astype(F32) + b.astype(F32) for a, b in pairs])
        return jnp.where(side == 1, high, low), jnp.where(side == 1, low, high).astype(BF)

    block = rows // 4 if fits(rows // 4) else rows
    steps = rows // block

    def kernel(where, *refs):
        kept, sent = refs[2 * len(pairs) :]
        totals = [refs[2 * k][...].astype(F32) + refs[2 * k + 1][...].astype(F32) for k in range(len(pairs))]
        low, high = both(totals)
        upper = where[0] == 1
        kept[...] = jnp.where(upper, high, low)
        sent[...] = jnp.where(upper, low, high).astype(BF)

    spec = lambda w: pl.BlockSpec((block, w), lambda i, c: (i, 0))
    flat = [a for pair in pairs for a in pair]
    return pl.pallas_call(
        kernel,
        grid_spec=pltpu.PrefetchScalarGridSpec(
            num_scalar_prefetch=1,
            grid=(steps,),
            in_specs=[spec(a.shape[1]) for a in flat],
            out_specs=[spec(width), spec(width)],
        ),
        out_shape=[jax.ShapeDtypeStruct((rows, width), F32), jax.ShapeDtypeStruct((rows, width), BF)],
        compiler_params=params(),
        cost_estimate=cost(0, sum(a.size * a.dtype.itemsize for a in flat) + 6 * rows * width),
        name="fold_sides",
    )(side.astype(jnp.int32).reshape(1), *flat)


def fold_spots(kept, came):
    spots, spot = lax.axis_size("ctx"), lax.axis_index("ctx")
    rows, width = kept.shape[0] // spots, kept.shape[1]
    if not fits(rows):
        total = kept + came.astype(F32)
        cut = lambda k: lax.dynamic_slice_in_dim(total, (spot ^ k) * rows, rows, 0)
        return [cut(0)] + [cut(k).astype(BF) for k in range(1, spots)]

    def kernel(where, kept_ref, came_ref, *outs):
        for k, out in enumerate(outs):
            at = pl.ds(pl.multiple_of((where[0] ^ k) * rows, rows), rows)
            out[...] = (kept_ref[at, :] + came_ref[at, :].astype(F32)).astype(out.dtype)

    outs = [((rows, width), F32)] + [((rows, width), BF)] * (spots - 1)
    return call(kernel, "fold_spots", outs, kept, came, prefetch=spot.astype(jnp.int32).reshape(1))


def own_rows(where, value, rows):
    mine = pl.ds(pl.multiple_of(where * rows, rows), rows)
    other = pl.ds(pl.multiple_of((1 - where) * rows, rows), rows)
    return value[mine, :], value[other, :]


def assemble(upper, pieces, held):
    local = pieces[0].shape[0]
    for k in range(len(pieces) // 2):
        mine, came = pieces[2 * k][...], pieces[2 * k + 1][...]
        held[2 * k * local : (2 * k + 1) * local, :] = jnp.where(upper, came, mine)
        held[(2 * k + 1) * local : (2 * k + 2) * local, :] = jnp.where(upper, mine, came)


def project_kernel(slots, where, *refs):
    pieces = refs[: 2 * slots + 2]
    w_query, w_kv, b_query, b_kv, query_ref, kv_ref, held = refs[2 * slots + 2 :]
    local = pieces[0].shape[0]

    @pl.when(pl.program_id(0) == 0)
    def _():
        assemble(where[0] == 1, pieces, held)

    rows = 2 * slots * local
    kv_ref[...] = (dot(held[:rows, :], w_kv[...], NN) + b_kv[...]).astype(BF)
    scale = jnp.asarray(1.0 / math.sqrt(HD), BF)
    for start, to in ((0, 0), (rows, 2 * local)):
        query = (dot(held[start : start + 2 * local, :], w_query[...], NN) + b_query[...]).astype(BF)
        query_ref[to : to + 2 * local, :] = query * scale


def project(where, pieces, w_query, w_kv, b_query, b_kv):
    slots = len(pieces) - 1
    local, width = pieces[0][0].shape
    whole = lambda p, c: (0, 0)
    across = lambda p, c: (0, p)
    flat = [p for pair in pieces for p in pair]
    q_width, kv_width = w_query.shape[1], w_kv.shape[1]
    return pl.pallas_call(
        functools.partial(project_kernel, slots),
        grid_spec=pltpu.PrefetchScalarGridSpec(
            num_scalar_prefetch=1,
            grid=(q_width // PAIR,),
            in_specs=[pl.BlockSpec(a.shape, whole, pipeline_mode=pl.Buffered(1)) for a in flat]
            + [
                pl.BlockSpec((width, PAIR), across),
                pl.BlockSpec((width, 2 * PAIR), across),
                pl.BlockSpec((1, PAIR), across),
                pl.BlockSpec((1, 2 * PAIR), across),
            ],
            out_specs=[
                pl.BlockSpec((4 * local, PAIR), across),
                pl.BlockSpec((2 * slots * local, 2 * PAIR), across),
            ],
            scratch_shapes=[pltpu.VMEM(((2 * slots + 2) * local, width), BF)],
        ),
        out_shape=[
            jax.ShapeDtypeStruct((4 * local, q_width), BF),
            jax.ShapeDtypeStruct((2 * slots * local, kv_width), BF),
        ],
        compiler_params=params(),
        cost_estimate=cost(4 * slots * local * width * (kv_width + q_width // 2), 2 * len(flat) * local * width + 4 * slots * local * kv_width),
        name="project",
    )(where, *flat, w_query, w_kv, b_query, b_kv)


def kv_back_kernel(slots, steps, split, first, where, *refs):
    pieces = refs[: 2 * slots]
    at = 2 * slots
    dkv, w_kv = refs[at : at + 2]
    at += 2
    if not first:
        before, bias_before = refs[at : at + 2]
        at += 2
    mine_ref, other_ref, bias_ref = refs[at : at + 3]
    weight_refs = refs[at + 3 : -2]
    turned, part = refs[-2:]
    local = pieces[0].shape[0]
    step = pl.program_id(0)
    upper = where[0] == 1

    @pl.when(step == 0)
    def _():
        for k in range(slots):
            mine, came = pieces[2 * k][...], pieces[2 * k + 1][...]
            turned[:, 2 * k * local : (2 * k + 1) * local] = jnp.where(upper, came, mine).T
            turned[:, (2 * k + 1) * local : (2 * k + 2) * local] = jnp.where(upper, mine, came).T

    grads = dkv[...]
    total = dot(turned[...], grads, NN)
    bias = jnp.sum(grads.astype(F32), axis=0, keepdims=True)
    if not first:
        total, bias = total + before[...], bias + bias_before[...]
    bias_ref[...] = bias
    half = total.shape[0] // 2
    if split:
        lower_line = where[1] == 0
        weight_refs[0][...] = jnp.where(lower_line, total[:half], total[half:])
        weight_refs[1][...] = jnp.where(lower_line, total[half:], total[:half]).astype(BF)
    else:
        weight_refs[0][...] = total
    term = dot(grads, w_kv[...], NT)

    @pl.when(step == 0)
    def _():
        part[...] = term

    @pl.when(jnp.logical_and(step > 0, step < steps - 1))
    def _():
        part[...] += term

    @pl.when(step == steps - 1)
    def _():
        for k in range(slots):
            low = slice(2 * k * local, (2 * k + 1) * local)
            high = slice((2 * k + 1) * local, (2 * k + 2) * local)
            to = slice(k * local, k * local + local)
            low_part, high_part = part[low, :] + term[low], part[high, :] + term[high]
            mine_ref[to, :] = jnp.where(upper, high_part, low_part)
            other_ref[to, :] = jnp.where(upper, low_part, high_part).astype(BF)


def kv_back(where, pieces, dkv, w_kv, before, last):
    slots = len(pieces)
    local, width = pieces[0][0].shape
    kv_width = w_kv.shape[1]
    split = last and lax.axis_size("dp") == 2
    whole = lambda p, c: (0, 0)
    across = lambda p, c: (0, p)
    once = pl.Buffered(1)
    flat = [p for pair in pieces for p in pair]
    extra = () if before is None else before
    if split:
        weight_outs = [((width // 2, kv_width), F32), ((width // 2, kv_width), BF)]
    else:
        weight_outs = [((width, kv_width), F32)]
    steps = kv_width // (2 * PAIR)
    return pl.pallas_call(
        functools.partial(kv_back_kernel, slots, steps, split, before is None),
        grid_spec=pltpu.PrefetchScalarGridSpec(
            num_scalar_prefetch=1,
            grid=(steps,),
            in_specs=[pl.BlockSpec((local, width), whole, pipeline_mode=once) for _ in flat]
            + [pl.BlockSpec((a.shape[0], 2 * PAIR), across) for a in (dkv, w_kv, *extra)],
            out_specs=[
                pl.BlockSpec((slots * local, width), whole, pipeline_mode=once),
                pl.BlockSpec((slots * local, width), whole, pipeline_mode=once),
                pl.BlockSpec((1, 2 * PAIR), across),
            ]
            + [pl.BlockSpec((shape[0], 2 * PAIR), across) for shape, _ in weight_outs],
            scratch_shapes=[pltpu.VMEM((width, 2 * slots * local), BF), pltpu.VMEM((2 * slots * local, width), F32)],
        ),
        out_shape=[
            jax.ShapeDtypeStruct((slots * local, width), F32),
            jax.ShapeDtypeStruct((slots * local, width), BF),
            jax.ShapeDtypeStruct((1, kv_width), F32),
        ]
        + [jax.ShapeDtypeStruct(shape, kind) for shape, kind in weight_outs],
        compiler_params=params(),
        cost_estimate=cost(8 * slots * local * width * kv_width, 12 * slots * local * width + 4 * width * kv_width),
        name="kv_back",
    )(where, *flat, dkv, w_kv, *extra)


def query_back_kernel(seqs, lines, where, *refs):
    dq_own, dq_came, own, came = (refs[k * seqs : k * seqs + seqs] for k in range(4))
    weight, mine_ref, other_ref, bias_ref = refs[4 * seqs : 4 * seqs + 4]
    weight_refs, total = refs[4 * seqs + 4 : -1], refs[-1]
    upper = where[0] == 1
    half = own[0].shape[0]
    bias = None
    for s in range(seqs):
        low = (dq_own[s][...] + dq_came[s][...].astype(F32)).astype(BF)
        rows = jnp.concatenate(
            [jnp.where(upper, came[s][...], own[s][...]), jnp.where(upper, own[s][...], came[s][...])], axis=0
        )
        part = dot(low, weight[...], (((0,), (1,)), ((), ())))
        to = slice(s * half, s * half + half)
        mine_ref[to, :] = jnp.where(upper, part[half:], part[:half])
        other_ref[to, :] = jnp.where(upper, part[:half], part[half:]).astype(BF)
        grad = dot(rows, low, (((0,), (1,)), ((), ())))
        total[...] = grad if s == 0 else total[...] + grad
        sums = jnp.sum(low.astype(F32), axis=1, keepdims=True)
        bias = sums if bias is None else bias + sums
    bias_ref[...] = bias
    if lines == 2:
        kept, sent = own_rows(where[1], total, total.shape[0] // 2)
        weight_refs[0][...] = kept
        weight_refs[1][...] = sent.astype(BF)
    else:
        weight_refs[0][...] = total[...]


def query_back(where, dq_own, dq_came, own, came, weight):
    seqs, lines = len(dq_own), lax.axis_size("dp")
    local, width = own[0].shape
    own_width = weight.shape[1]
    outs = [((seqs * local, width), F32), ((seqs * local, width), BF), ((own_width, 1), F32)]
    if lines == 2:
        outs += [((width // 2, own_width), F32), ((width // 2, own_width), BF)]
    else:
        outs += [((width, own_width), F32)]
    return call(
        functools.partial(query_back_kernel, seqs, lines),
        "query_back",
        outs,
        *dq_own,
        *dq_came,
        *own,
        *came,
        weight,
        prefetch=where,
        scratch=[pltpu.VMEM((width, own_width), F32)],
        flops=8 * seqs * local * width * own_width,
    )


def half_lanes(value):
    lane = lax.broadcasted_iota(jnp.int32, value.shape, 1)
    zero = jnp.zeros_like(value)
    return [jnp.where(lane < HD, value, zero), jnp.where(lane >= HD, value, zero)]


def half_rows(value):
    row = lax.broadcasted_iota(jnp.int32, value.shape, 0)
    zero = jnp.zeros_like(value)
    return [jnp.where(row < HD, value, zero), jnp.where(row >= HD, value, zero)]


def top_bits(value):
    spread = value * 65537.0
    return spread - (spread - value)


def in_three(value):
    first = top_bits(value)
    rest = value - first
    second = top_bits(rest)
    return first.astype(BF), second.astype(BF), (rest - second).astype(BF)


def packed_rows(values):
    terms = jnp.concatenate(in_three(values), axis=0)
    return jnp.concatenate([terms, jnp.zeros((16 - terms.shape[0], terms.shape[1]), BF)], axis=0)


def unpacked_rows(packed, count):
    packed = packed.astype(F32)
    return packed[:count] + packed[count : 2 * count] + packed[2 * count : 3 * count]


def below(shape, count):
    return lax.broadcasted_iota(jnp.int32, shape, 0) < count


def attend_kernel(slots, probe, counts, queries, kv, *refs):
    o_own, packed, lse_ref, top, total, acc, heads = refs[-7:]
    rows = queries.shape[0] // 2
    keys = kv.shape[0] // slots
    for h, query in enumerate(half_lanes(queries[...])):
        heads[h] = query

    def block(k):
        at = pl.ds(pl.multiple_of(k * keys, keys), keys)
        return kv[at, :PAIR], kv[at, PAIR:]

    first = pl.ds(pl.multiple_of(counts[slots] * keys, keys), probe)
    for h in range(2):
        top[h] = jnp.max(dot(kv[first, :PAIR], heads[h], NT), axis=0, keepdims=True)
    total[...] = jnp.zeros_like(total)
    acc[...] = jnp.zeros_like(acc)

    def quick(k, h, valid):
        key, value = block(k)
        expo = jnp.exp(dot(key, heads[h], NT) - top[h])
        if valid is not None:
            expo = jnp.where(below(expo.shape, valid), expo, 0.0)
        total[h] += jnp.sum(expo, axis=0, keepdims=True)
        acc[h] += dot(value, expo.astype(BF), TN)

    @pl.loop(0, slots)
    def _(k):
        valid = counts[k]

        @pl.when(valid >= keys)
        def _():
            quick(k, 0, None)
            quick(k, 1, None)

        @pl.when(jnp.logical_and(valid > 0, valid < keys))
        def _():
            pl.loop(0, 2)(lambda h: quick(k, h, valid))

    @pl.when(jnp.logical_not(jnp.max(total[...]) < LARGEST))
    def _():
        total[...] = jnp.zeros_like(total)
        acc[...] = jnp.zeros_like(acc)

        def careful(k, h, valid):
            key, value = block(k)
            scores = dot(key, heads[h], NT)
            scores = jnp.where(below(scores.shape, valid), scores, NEGATIVE)
            old = top[h]
            new = jnp.maximum(old, jnp.max(scores, axis=0, keepdims=True))
            expo = jnp.where(below(scores.shape, valid), jnp.exp(scores - new), 0.0)
            scale = jnp.exp(old - new)
            total[h] = total[h] * scale + jnp.sum(expo, axis=0, keepdims=True)
            acc[h] = acc[h] * scale + dot(value, expo.astype(BF), TN)
            top[h] = new

        @pl.loop(0, slots)
        def _(k):
            valid = counts[k]

            @pl.when(valid > 0)
            def _():
                pl.loop(0, 2)(lambda h: careful(k, h, valid))

    lse = []
    for h in range(2):
        at = slice(h * HD, h * HD + HD)
        part = acc[h, at, :] / total[h]
        o_own[0, at, :] = part[:, :rows]
        packed[at, :] = part[:, rows:].astype(BF)
        lse.append(top[h] + jnp.log(total[h]))
        lse_ref[0, 0, h : h + 1, :] = lse[h][:, :rows]
    packed[PAIR:, :] = packed_rows(jnp.concatenate([l[:, rows:] for l in lse], axis=0))


def attend(counts, slots, seqs, s, queries, kv, before):
    rows, width = queries.shape[0] // 2, queries.shape[1]
    pairs = width // PAIR
    keys = kv.shape[0] // slots
    total = width * 2 * rows * kv.shape[0]
    anywhere = pl.BlockSpec(memory_space=pl.ANY)
    return pl.pallas_call(
        functools.partial(attend_kernel, slots, min(128, keys)),
        grid_spec=pltpu.PrefetchScalarGridSpec(
            num_scalar_prefetch=1,
            grid=(pairs,),
            in_specs=[
                pl.BlockSpec((2 * rows, PAIR), lambda p, c: (0, p)),
                pl.BlockSpec((kv.shape[0], 2 * PAIR), lambda p, c: (0, p)),
            ]
            + [anywhere] * len(before),
            out_specs=[
                pl.BlockSpec((1, PAIR, rows), lambda p, c: (s, p, 0)),
                pl.BlockSpec((PAIR + 16, rows), lambda p, c: (p, 0)),
                pl.BlockSpec((1, 1, 2, rows), lambda p, c: (s, p, 0, 0)),
            ],
            scratch_shapes=[
                pltpu.VMEM((2, 1, 2 * rows), F32),
                pltpu.VMEM((2, 1, 2 * rows), F32),
                pltpu.VMEM((2, PAIR, 2 * rows), F32),
                pltpu.VMEM((2, 2 * rows, PAIR), BF),
            ],
        ),
        out_shape=[
            jax.ShapeDtypeStruct((seqs, width, rows), F32),
            jax.ShapeDtypeStruct((pairs * (PAIR + 16), rows), BF),
            jax.ShapeDtypeStruct((seqs, pairs, 2, rows), F32),
        ],
        input_output_aliases={3: 0, 4: 2} if before else {},
        compiler_params=params(),
        cost_estimate=cost(16 * total, 8 * queries.size + 2 * kv.size, total // HD),
        name="attend",
    )(counts, queries, kv, *before)


def attend_back_kernel(slots, counts, both, g_own, g_oth, kv, dq_own, dq_oth, dkv, acc, queries, grads, summed, facts):
    rows = both.shape[0] // 2
    keys = kv.shape[0] // slots
    acc[...] = jnp.zeros_like(acc)
    for block, g_ref in enumerate((g_own, g_oth)):
        stats = unpacked_rows(g_ref[PAIR:, :], 4)
        for h, (query, grad) in enumerate(
            zip(half_lanes(both[block * rows : block * rows + rows, :]), half_rows(g_ref[:PAIR, :]))
        ):
            queries[2 * block + h] = query
            grads[2 * block + h] = grad
            facts[2 * block + h, 0:1, :] = stats[h : h + 1]
            facts[2 * block + h, 1:2, :] = stats[2 + h : 3 + h]

    @pl.loop(0, slots)
    def _(k):
        valid = counts[k]
        rows_at = pl.ds(pl.multiple_of(k * keys, keys), keys)

        def one(at, valid):
            key, value = kv[rows_at, :PAIR], kv[rows_at, PAIR:]
            query, grad = queries[at], grads[at]
            prob = jnp.exp(dot(key, query, NT) - facts[at, 0:1, :])
            if valid is not None:
                prob = jnp.where(below(prob.shape, valid), prob, 0.0)
            change = dot(value, grad, NN) - facts[at, 1:2, :]
            score = (prob * change).astype(BF)
            summed[:, PAIR:] += dot(prob.astype(BF), grad, NT)
            summed[:, :PAIR] += dot(score, query, NN)
            acc[at] += dot(key, score, TN)

        summed[...] = jnp.zeros_like(summed)

        @pl.when(valid >= keys)
        def _():
            for at in range(4):
                one(at, None)

        @pl.when(jnp.logical_and(valid > 0, valid < keys))
        def _():
            pl.loop(0, 4)(lambda at: one(at, valid))

        dkv[rows_at, :] = summed[...].astype(BF)

    scale = 1.0 / math.sqrt(HD)
    for h in range(2):
        at = slice(h * HD, h * HD + HD)
        dq_own[at, :] = acc[h, at, :] * scale
        dq_oth[at, :] = (acc[2 + h, at, :] * scale).astype(BF)


def attend_back(counts, slots, both, g_own, g_oth, kv):
    rows, width = both.shape[0] // 2, both.shape[1]
    pairs = width // PAIR
    keys = kv.shape[0] // slots
    q_spec = pl.BlockSpec((2 * rows, PAIR), lambda p, c: (0, p))
    t_spec = pl.BlockSpec((PAIR, rows), lambda p, c: (p, 0))
    g_spec = pl.BlockSpec((PAIR + 16, rows), lambda p, c: (p, 0))
    kv_spec = pl.BlockSpec((kv.shape[0], 2 * PAIR), lambda p, c: (0, p))
    total = width * 2 * rows * kv.shape[0]
    return pl.pallas_call(
        functools.partial(attend_back_kernel, slots),
        grid_spec=pltpu.PrefetchScalarGridSpec(
            num_scalar_prefetch=1,
            grid=(pairs,),
            in_specs=[q_spec, g_spec, g_spec, kv_spec],
            out_specs=[t_spec, t_spec, kv_spec],
            scratch_shapes=[
                pltpu.VMEM((4, PAIR, rows), F32),
                pltpu.VMEM((4, rows, PAIR), BF),
                pltpu.VMEM((4, PAIR, rows), BF),
                pltpu.VMEM((keys, 2 * PAIR), F32),
                pltpu.VMEM((4, 2, rows), F32),
            ],
        ),
        out_shape=[
            jax.ShapeDtypeStruct((width, rows), F32),
            jax.ShapeDtypeStruct((width, rows), BF),
            jax.ShapeDtypeStruct(kv.shape, BF),
        ],
        compiler_params=params(),
        cost_estimate=cost(40 * total, 8 * both.size + 4 * kv.size, total // HD),
        name="attend_back",
    )(counts, both, g_own, g_oth, kv)


def merge_kernel(pairs, seqs, where, o_own, lse_own, *refs):
    packs = refs[:seqs]
    weight, full_ref, low_ref, mine_ref, other_ref, lse_ref, low_s, packed = refs[seqs:]
    rows = o_own.shape[2]
    for s in range(seqs):

        @pl.when(pl.program_id(0) == s)
        def _(s=s):
            packed[...] = packs[s][...]

    for p in range(pairs):
        base = p * (PAIR + 16)
        own = lse_own[0, p]
        came = unpacked_rows(packed[base + PAIR : base + PAIR + 16, :], 2)
        highest = jnp.maximum(own, came)
        share_own, share_came = jnp.exp(own - highest), jnp.exp(came - highest)
        both = share_own + share_came
        lse_ref[0, p] = highest + jnp.log(both)
        share_own, share_came = share_own / both, share_came / both
        for h in range(2):
            at = slice(p * PAIR + h * HD, p * PAIR + h * HD + HD)
            term = packed[base + h * HD : base + h * HD + HD, :].astype(F32)
            merged = o_own[0, at, :] * share_own[h : h + 1] + term * share_came[h : h + 1]
            full_ref[0, at, :] = merged
            low_s[at, :] = merged.astype(BF)
    low_ref[0] = low_s[...]
    half = rows // 2
    mine = pl.ds(pl.multiple_of(where[0] * half, half), half)
    other = pl.ds(pl.multiple_of((1 - where[0]) * half, half), half)
    dims = (((0,), (1,)), ((), ()))
    mine_ref[0] = dot(low_s[:, mine], weight[...], dims)
    other_ref[0] = dot(low_s[:, other], weight[...], dims).astype(BF)


def merge(where, o_own, lse_own, packs, weight):
    seqs, width, rows = o_own.shape
    pairs = width // PAIR
    model = weight.shape[0]
    one = lambda *shape: pl.BlockSpec((1, *shape), lambda s, w: (s,) + (0,) * len(shape))
    return pl.pallas_call(
        functools.partial(merge_kernel, pairs, seqs),
        grid_spec=pltpu.PrefetchScalarGridSpec(
            num_scalar_prefetch=1,
            grid=(seqs,),
            in_specs=[
                one(width, rows),
                one(pairs, 2, rows),
            ]
            + [pl.BlockSpec(p.shape, lambda s, w: (0, 0)) for p in packs]
            + [
                pl.BlockSpec(weight.shape, lambda s, w: (0, 0)),
            ],
            out_specs=[one(width, rows), one(width, rows), one(rows // 2, model), one(rows // 2, model), one(pairs, 2, rows)],
            scratch_shapes=[pltpu.VMEM((width, rows), BF), pltpu.VMEM(packs[0].shape, BF)],
        ),
        out_shape=[
            jax.ShapeDtypeStruct((seqs, width, rows), F32),
            jax.ShapeDtypeStruct((seqs, width, rows), BF),
            jax.ShapeDtypeStruct((seqs, rows // 2, model), F32),
            jax.ShapeDtypeStruct((seqs, rows // 2, model), BF),
            jax.ShapeDtypeStruct((seqs, pairs, 2, rows), F32),
        ],
        compiler_params=params(),
        cost_estimate=cost(2 * seqs * width * rows * model, 12 * o_own.size + 4 * seqs * rows * model),
        name="merge",
    )(where, o_own, lse_own, *packs, weight)


def turn_kernel(pairs, seqs, lines, where, own_ref, came_ref, weight, full_ref, low_ref, lse_ref, *refs):
    packs, weight_refs = refs[:seqs], refs[seqs:-2]
    d_weight, packed = refs[-2:]
    step = pl.program_id(0)
    upper = where[0] == 1
    own, came = own_ref[0], came_ref[0]
    rows = jnp.concatenate([jnp.where(upper, came, own), jnp.where(upper, own, came)], axis=0)
    grad = dot(weight[...], rows, (((0,), (1,)), ((), ()))).astype(BF)
    product = grad.astype(F32) * full_ref[0]
    for p in range(pairs):
        base = p * (PAIR + 16)
        packed[base : base + PAIR, :] = grad[p * PAIR : p * PAIR + PAIR]
        stats = [lse_ref[0, p]]
        for h in range(2):
            at = slice(p * PAIR + h * HD, p * PAIR + h * HD + HD)
            stats.append(jnp.sum(product[at], axis=0, keepdims=True))
        packed[base + PAIR : base + PAIR + 16, :] = packed_rows(jnp.concatenate(stats, axis=0))
    for s in range(seqs):

        @pl.when(step == s)
        def _(s=s):
            packs[s][...] = packed[...]

    @pl.when(step == 0)
    def _():
        d_weight[...] = jnp.zeros_like(d_weight)

    d_weight[...] += dot(rows, low_ref[0], (((0,), (1,)), ((), ())))

    @pl.when(step == seqs - 1)
    def _():
        if lines == 2:
            kept, sent = own_rows(where[1], d_weight, d_weight.shape[0] // 2)
            weight_refs[0][...] = kept
            weight_refs[1][...] = sent.astype(BF)
        else:
            weight_refs[0][...] = d_weight[...]


def turn(where, own, came, weight, full, low, lse):
    seqs, width, rows = full.shape
    pairs = width // PAIR
    one = lambda *shape: pl.BlockSpec((1, *shape), lambda s, w: (s,) + (0,) * len(shape))
    whole = lambda *shape: pl.BlockSpec(shape, lambda s, w: (0, 0))
    lines = lax.axis_size("dp")
    pack_shape = (pairs * (PAIR + 16), rows)
    half = (weight.shape[0] // 2, weight.shape[1])
    weight_outs = [(half, F32), (half, BF)] if lines == 2 else [(weight.shape, F32)]
    return pl.pallas_call(
        functools.partial(turn_kernel, pairs, seqs, lines),
        grid_spec=pltpu.PrefetchScalarGridSpec(
            num_scalar_prefetch=1,
            grid=(seqs,),
            in_specs=[
                one(*own.shape[1:]),
                one(*own.shape[1:]),
                whole(*weight.shape),
                one(width, rows),
                one(width, rows),
                one(pairs, 2, rows),
            ],
            out_specs=[whole(*pack_shape)] * seqs + [whole(*shape) for shape, _ in weight_outs],
            scratch_shapes=[pltpu.VMEM(weight.shape, F32), pltpu.VMEM(pack_shape, BF)],
        ),
        out_shape=[jax.ShapeDtypeStruct(pack_shape, BF)] * seqs
        + [jax.ShapeDtypeStruct(shape, kind) for shape, kind in weight_outs],
        compiler_params=params(),
        cost_estimate=cost(4 * seqs * rows * weight.size, 8 * full.size + 4 * own.size),
        name="turn",
    )(where, own, came, weight, full, low, lse)


def gelu_parts(u):
    density = jnp.exp(-0.5 * u * u)
    t = 1.0 / (1.0 + (0.3275911 / math.sqrt(2.0)) * jnp.abs(u))
    series = t * (
        0.254829592
        + t * (-0.284496736 + t * (1.421413741 + t * (-1.453152027 + t * 1.061405429)))
    )
    tail = 0.5 * series * density
    share = jnp.where(u < 0.0, tail, 1.0 - tail)
    return u * share, share + u * (density * (1.0 / math.sqrt(2.0 * math.pi)))


def feed_kernel(chunk, half, own_ref, came_ref, w_in, bias, w_out, active_ref, slope_ref, mine_ref, other_ref):
    step = pl.program_id(0)
    rows = jnp.where(step < half, own_ref[...], came_ref[...])
    part = None
    for start in range(0, w_in.shape[1], chunk):
        at = slice(start, start + chunk)
        inner = dot(rows, w_in[:, at], NN) + bias[:, at]
        active, slope = gelu_parts(inner)
        active = active.astype(BF)
        active_ref[:, at] = active
        slope_ref[:, at] = slope.astype(BF)
        term = dot(active, w_out[:, at], NT)
        part = term if part is None else part + term

    @pl.when(step < half)
    def _():
        mine_ref[...] = part

    @pl.when(step >= half)
    def _():
        other_ref[...] = part.astype(BF)


def row_specs(block, half, width):
    own = pl.BlockSpec((block, width), lambda i, *c: (jnp.minimum(i, half - 1), 0))
    came = pl.BlockSpec((block, width), lambda i, *c: (jnp.maximum(i - half, 0), 0))
    return own, came


def feed(own, came, w_in, bias, w_out):
    count, width = own.shape
    units = w_in.shape[1]
    block = min(FEED_ROWS, count)
    half = count // block
    whole = lambda i: (0, 0)
    by_row = lambda i: (i, 0)
    own_spec, came_spec = row_specs(block, half, width)
    return pl.pallas_call(
        functools.partial(feed_kernel, units // 3 if units % 384 == 0 else units, half),
        grid=(2 * half,),
        in_specs=[
            own_spec,
            came_spec,
            pl.BlockSpec((width, units), whole, pipeline_mode=pl.Buffered(1)),
            pl.BlockSpec((1, units), whole),
            pl.BlockSpec((width, units), whole, pipeline_mode=pl.Buffered(1)),
        ],
        out_specs=[pl.BlockSpec((block, units), by_row), pl.BlockSpec((block, units), by_row), own_spec, came_spec],
        out_shape=[
            jax.ShapeDtypeStruct((2 * count, units), BF),
            jax.ShapeDtypeStruct((2 * count, units), BF),
            jax.ShapeDtypeStruct((count, width), F32),
            jax.ShapeDtypeStruct((count, width), BF),
        ],
        compiler_params=params(),
        cost_estimate=cost(8 * count * width * units, 4 * width * units + 8 * count * units + 12 * count * width, 2 * count * units),
        name="feed",
    )(own, came, w_in, bias, w_out)


def feed_back_kernel(half, lines, where, low_own, low_came, own_ref, came_ref, active_ref, slope_ref, w_in, w_out, *refs):
    mine_ref, other_ref, d_bias_ref = refs[:3]
    weight_refs, (d_in, d_out) = refs[3:-2], refs[-2:]
    step = pl.program_id(0)
    units = w_in.shape[1]

    @pl.when(step == 0)
    def _():
        d_in[...] = jnp.zeros_like(d_in)
        d_out[...] = jnp.zeros_like(d_out)
        d_bias_ref[...] = jnp.zeros_like(d_bias_ref)

    low = jnp.where(step < half, low_own[...], low_came[...])
    rows = jnp.where(step < half, own_ref[...], came_ref[...])
    inner = (dot(low, w_out[...], NN) * slope_ref[...].astype(F32)).astype(BF)
    part = dot(inner, w_in[...], NT)
    d_out[...] += dot(low, active_ref[...], TN)
    d_in[...] += dot(rows, inner, TN)
    d_bias_ref[...] += jnp.sum(inner.astype(F32), axis=0, keepdims=True)

    @pl.when(step < half)
    def _():
        mine_ref[...] = part

    @pl.when(step >= half)
    def _():
        other_ref[...] = part.astype(BF)

    @pl.when(step == 2 * half - 1)
    def _():
        for total, cut in ((d_in, slice(0, units)), (d_out, slice(units, 2 * units))):
            if lines == 2:
                kept, sent = own_rows(where[1], total, total.shape[0] // 2)
                weight_refs[0][:, cut] = kept.astype(BF)
                weight_refs[1][:, cut] = sent.astype(BF)
            else:
                weight_refs[0][:, cut] = total[...].astype(BF)


def feed_back(where, low_own, low_came, own, came, active, slope, w_in, w_out):
    count, width = own.shape
    units = w_in.shape[1]
    block = min(FEED_ROWS, count)
    half = count // block
    whole = lambda i, *c: (0, 0)
    by_row = lambda i, *c: (i, 0)
    once = pl.Buffered(1)
    lines = lax.axis_size("dp")
    own_spec, came_spec = row_specs(block, half, width)
    d_shape = (width // 2 if lines == 2 else width, 2 * units)
    d_count = 2 if lines == 2 else 1
    return pl.pallas_call(
        functools.partial(feed_back_kernel, half, lines),
        grid_spec=pltpu.PrefetchScalarGridSpec(
            num_scalar_prefetch=1,
            grid=(2 * half,),
            in_specs=[
                own_spec,
                came_spec,
                own_spec,
                came_spec,
                pl.BlockSpec((block, units), by_row),
                pl.BlockSpec((block, units), by_row),
                pl.BlockSpec((width, units), whole, pipeline_mode=once),
                pl.BlockSpec((width, units), whole, pipeline_mode=once),
            ],
            out_specs=[own_spec, came_spec, pl.BlockSpec((1, units), whole)]
            + [pl.BlockSpec(d_shape, whole, pipeline_mode=once)] * d_count,
            scratch_shapes=[pltpu.VMEM((width, units), F32), pltpu.VMEM((width, units), F32)],
        ),
        out_shape=[
            jax.ShapeDtypeStruct((count, width), F32),
            jax.ShapeDtypeStruct((count, width), BF),
            jax.ShapeDtypeStruct((1, units), F32),
        ]
        + [jax.ShapeDtypeStruct(d_shape, BF)] * d_count,
        compiler_params=params(),
        cost_estimate=cost(16 * count * width * units, 8 * width * units + 8 * count * units + 16 * count * width),
        name="feed_back",
    )(where, low_own, low_came, own, came, active, slope, w_in, w_out)


def centre(values):
    middle = values - jnp.mean(values, axis=-1, keepdims=True)
    scale = lax.rsqrt(jnp.mean(middle * middle, axis=-1, keepdims=True) + EPSILON)
    return middle * scale, scale


def back_through(weighted, normal, scale):
    first = jnp.mean(weighted, axis=-1, keepdims=True)
    second = jnp.mean(weighted * normal, axis=-1, keepdims=True)
    return (weighted - first - normal * second) * scale


def first_kernel(x_ref, mine_ref, came_ref, vec_ref, normal_ref, scale_ref, low_ref):
    sums = x_ref[...].astype(F32) + (mine_ref[...] + came_ref[...].astype(F32)) + vec_ref[0:1, :]
    normal, scale = centre(sums)
    normal_ref[...] = normal
    scale_ref[...] = scale
    low_ref[...] = (normal * vec_ref[1:2, :] + vec_ref[2:3, :]).astype(BF)


def second_kernel(per_seq, counts, normal_ref, mine_ref, came_ref, cot_ref, vec_ref, out_ref, grad_ref, low_ref, sums_ref):
    step = pl.program_id(0)
    block = normal_ref.shape[0]
    valid = counts[step // per_seq] - (step % per_seq) * block
    keep = lax.broadcasted_iota(jnp.int32, normal_ref.shape, 0) < valid

    @pl.when(step == 0)
    def _():
        sums_ref[...] = jnp.zeros_like(sums_ref)

    first = normal_ref[...] * vec_ref[1:2, :] + vec_ref[2:3, :]
    sums = first + (mine_ref[...] + came_ref[...].astype(F32)) + vec_ref[3:4, :]
    normal, scale = centre(sums)
    out_ref[...] = jnp.where(keep, normal * vec_ref[4:5, :] + vec_ref[5:6, :], 0.0)
    out_grad = jnp.where(keep, cot_ref[...].astype(F32), 0.0)
    grad = back_through(out_grad * vec_ref[4:5, :], normal, scale)
    grad_ref[...] = grad
    low_ref[...] = grad.astype(BF)
    sums_ref[0:1, :] += jnp.sum(out_grad * normal, axis=0, keepdims=True)
    sums_ref[1:2, :] += jnp.sum(out_grad, axis=0, keepdims=True)
    sums_ref[2:3, :] += jnp.sum(grad, axis=0, keepdims=True)


def first_back_kernel(grad_ref, mine_ref, came_ref, normal_ref, scale_ref, vec_ref, out_ref, low_ref, sums_ref):
    @pl.when(pl.program_id(0) == 0)
    def _():
        sums_ref[...] = jnp.zeros_like(sums_ref)

    given = grad_ref[...] + (mine_ref[...] + came_ref[...].astype(F32))
    normal = normal_ref[...]
    grad = back_through(given * vec_ref[1:2, :], normal, scale_ref[...])
    out_ref[...] = grad
    low_ref[...] = grad.astype(BF)
    sums_ref[0:1, :] += jnp.sum(given * normal, axis=0, keepdims=True)
    sums_ref[1:2, :] += jnp.sum(given, axis=0, keepdims=True)
    sums_ref[2:3, :] += jnp.sum(grad, axis=0, keepdims=True)


def row_call(kernel, name, block, count, width, inputs, whole_inputs, outs, sums, counts=None):
    by_row = lambda i, *c: (i, 0)
    whole = lambda i, *c: (0, 0)
    in_specs = [pl.BlockSpec((block, a.shape[1]), by_row) for a in inputs]
    in_specs += [pl.BlockSpec(a.shape, whole) for a in whole_inputs]
    out_specs = [pl.BlockSpec((block, w), by_row) for w, _ in outs]
    out_shape = [jax.ShapeDtypeStruct((count, w), t) for w, t in outs]
    if sums:
        out_specs.append(pl.BlockSpec((8, width), whole))
        out_shape.append(jax.ShapeDtypeStruct((8, width), F32))
    prefetch = 0 if counts is None else 1
    moved = sum(a.size * a.dtype.itemsize for a in inputs) + sum(count * w * 4 for w, _ in outs)
    return pl.pallas_call(
        kernel,
        grid_spec=pltpu.PrefetchScalarGridSpec(
            num_scalar_prefetch=prefetch, grid=(count // block,), in_specs=in_specs, out_specs=out_specs
        ),
        out_shape=out_shape,
        compiler_params=params(),
        cost_estimate=cost(20 * count * width, moved),
        name=name,
    )(*(() if counts is None else (counts,)), *inputs, *whole_inputs)


def interleaved(key, value):
    width = key.shape[1]
    pieces = []
    for start in range(0, width, PAIR):
        pieces += [key[:, start : start + PAIR], value[:, start : start + PAIR]]
    return jnp.concatenate(pieces, axis=1)


def apart(both):
    keys, values = [], []
    for start in range(0, both.shape[1], 2 * PAIR):
        keys.append(both[:, start : start + PAIR])
        values.append(both[:, start + PAIR : start + 2 * PAIR])
    return jnp.concatenate(keys, axis=1), jnp.concatenate(values, axis=1)


def on_device(
    block_input,
    lengths,
    cotangent,
    query_weight,
    query_bias,
    key_weight,
    value_weight,
    value_bias,
    output_weight,
    output_bias,
    first_gain,
    first_shift,
    inner_weight,
    inner_bias,
    outer_weight,
    closing_offset_vector,
    second_gain,
    second_shift,
):
    seqs, local, width = block_input.shape
    chip = 2 * local
    spots = lax.axis_size("ctx")
    spot = lax.axis_index("ctx")
    part = lax.axis_index("tp")
    core, side = part % 2, part // 2
    is_upper_core, is_upper_side = core == 1, side == 1
    span = local * lax.axis_size("tp")
    heads_width = query_weight.shape[1]
    unit_width = inner_weight.shape[1]
    count = seqs * local

    def other_core(value, **ties):
        return swap(value, "tp", 1, **ties)

    def other_side(value, **ties):
        return swap(value, "tp", 2, **ties)

    def flat(value):
        return value.reshape(-1, value.shape[-1])

    starts = jnp.stack([(spot ^ k) * span + side * chip for k in range(spots)])
    key_counts = jnp.clip(lengths[:, None] - starts[None, :], 0, chip)
    counts = jnp.concatenate([key_counts, jnp.full((seqs, 1), spot, jnp.int32)], axis=1).astype(jnp.int32)
    row_counts = jnp.clip(lengths - (spot * span + part * local), 0, local).astype(jnp.int32)
    where = jnp.stack([core, lax.axis_index("dp")]).astype(jnp.int32)

    def together(*values):
        return lax.optimization_barrier(values)

    def over_spots(value, done=()):
        return [swap(value, "ctx", k, (), done) for k in range(1, spots)]

    lines = lax.axis_size("dp")
    own_width = 2 * heads_width
    attention_shard = pack([query_weight, key_weight, value_weight], [False] * 3)
    feed_shard = pack([output_weight, inner_weight, outer_weight], [True, False, True])
    biases = jnp.concatenate([query_bias, value_bias, inner_bias])[None, :]
    x_rows = [block_input[s] for s in range(seqs)]

    came, biases_came, *near = together(other_core(block_input), other_side(biases), *over_spots(attention_shard))
    attention_near = stack([attention_shard] + near)

    def send_near(own):
        return [swap(own, "ctx", 2), swap(own, "ctx", 1)] if spots == 4 else over_spots(own)

    def send_last(own, far):
        return [
            lax.ppermute(own, "ctx", [(1, 2), (2, 1)]),
            lax.ppermute(far, "ctx", [(2, 3), (1, 0)]),
        ]

    def finish(nears, lasts):
        if spots != 4:
            return nears
        in_middle = jnp.logical_or(spot == 1, spot == 2)
        return [nears[1], nears[0], jnp.where(in_middle, lasts[0], lasts[1])]

    begin = together(attention_near, *x_rows)
    attention_near, first_rows_out = begin[0], begin[1]
    attention_other, attention_line, across_0, *nears = together(
        other_side(attention_near),
        swap(attention_near, "dp", 1),
        other_side(first_rows_out),
        *send_near(first_rows_out),
    )
    other_line = swap(attention_other, "dp", 1)
    across = [across_0, other_side(after(x_rows[1], attention_other))]
    cores = [other_core(n) for n in nears]
    lasts = send_last(after(x_rows[0], *nears), nears[0]) if spots == 4 else []
    other_line, across[1], *rest = together(other_line, across[1], *lasts, *cores)
    lasts, cores = rest[: len(lasts)], rest[len(lasts) :]
    arrived = [finish(nears, lasts)]
    if spots == 4:
        cores = [cores[1], cores[0], other_core(arrived[0][2])]
    if lines == 2:
        attention_all = [[attention_near, attention_other], [attention_line, other_line]]
    else:
        attention_all = over_dp([attention_near, attention_other])
    query_full, kv_full = place(attention_all, [heads_width] * 3, [(0,), (1, 2)])

    query_b = ordered(biases[:, :heads_width], biases_came[:, :heads_width], is_upper_side, 1)
    cut = slice(heads_width, own_width)
    value_b = ordered(biases[:, cut], biases_came[:, cut], is_upper_side, 1)
    cut = slice(own_width, None)
    inner_b = ordered(biases[:, cut], biases_came[:, cut], is_upper_side, 1)
    kv_bias = interleaved(jnp.zeros_like(value_b), value_b)

    pieces = [[(x_rows[0], came[0])] + list(zip(arrived[0], cores))]
    across_core = other_core(across[0])
    feed_shard = after(feed_shard, arrived[0][-1])
    feed_near = over_spots(feed_shard)
    second_nears = send_near(after(x_rows[1], arrived[0][-1]))
    q, made = project(where, pieces[0] + [(across[0], across_core)], query_full, kv_full, query_b, kv_bias)
    queries, kv = [q], [made]
    own, packed, lse = attend(counts[0], spots, seqs, 0, q, made, ())
    packs = [packed]

    own, *rest = together(own, *feed_near, *second_nears)
    feed_near, nears = rest[: len(feed_near)], rest[len(feed_near) :]
    across_core = other_core(across[1])
    feed_near = stack([feed_shard] + feed_near)
    second = after(x_rows[1], own)
    cores = [other_core(n) for n in nears]
    lasts = send_last(after(second, *nears), nears[0]) if spots == 4 else []
    feed_other, near_line, *rest = together(other_side(feed_near), swap(feed_near, "dp", 1), *lasts, *cores)
    lasts, cores = rest[: len(lasts)], rest[len(lasts) :]
    arrived.append(finish(nears, lasts))
    if spots == 4:
        cores = [cores[1], cores[0], other_core(arrived[1][2])]
    pieces.append([(x_rows[1], came[1])] + list(zip(arrived[1], cores)))
    packs[0] = other_side(after(packs[0], feed_other))
    q, made = project(where, pieces[1] + [(across[1], across_core)], query_full, kv_full, query_b, kv_bias)
    queries.append(q)
    kv.append(made)
    own, packed, lse = attend(counts[1], spots, seqs, 1, q, made, (own, lse))
    packs.append(other_side(packed))
    buffers = (own, lse)
    if lines == 2:
        feed_all = [[feed_near, feed_other], [near_line, swap(feed_other, "dp", 1, (), (own,))]]
    else:
        feed_all = over_dp([feed_near, feed_other])
    output_full, inner_full, outer_full = place(feed_all, [heads_width, unit_width, unit_width], [(0,), (1,), (2,)])

    vectors = jnp.stack([output_bias, first_gain, first_shift, closing_offset_vector, second_gain, second_shift])
    vectors = jnp.concatenate([vectors, jnp.zeros((2, width), F32)])
    block = local // 2

    attended, attended_low, mine, other, lse_all = merge(where, *buffers, packs, output_full)
    normal, spread, first_low = row_call(
        first_kernel,
        "first_norm",
        block,
        count,
        width,
        [flat(block_input), flat(mine), flat(other_core(other))],
        [vectors],
        [(width, F32), (1, F32), (width, BF)],
        False,
    )
    first_came = other_core(first_low)
    active, slope, mine, other = feed(first_low, first_came, inner_full, inner_b, outer_full)
    output, second_grad, outer_low, second_sums = row_call(
        functools.partial(second_kernel, local // block),
        "second_norm",
        block,
        count,
        width,
        [normal, mine, other_core(other), flat(cotangent)],
        [vectors],
        [(width, F32), (width, F32), (width, BF)],
        True,
        row_counts,
    )
    mine, other, d_inner_bias, *d_feed = feed_back(
        where, outer_low, other_core(outer_low), first_low, first_came, active, slope, inner_full, outer_full
    )
    first_grad, attn_low, first_sums = row_call(
        first_back_kernel,
        "first_norm_back",
        block,
        count,
        width,
        [second_grad, mine, other_core(other), normal, spread],
        [vectors],
        [(width, F32), (width, BF)],
        True,
    )
    attn_low = attn_low.reshape(seqs, local, width)
    turned = turn(
        where, attn_low, other_core(attn_low), output_full, attended, attended_low, lse_all
    )
    g_own, d_output = turned[:seqs], turned[seqs:]
    g_oth = [other_side(g) for g in g_own]

    lines = lax.axis_size("dp")

    def over_lines(made, done=()):
        if lines == 2:
            return made[0], swap(made[1], "dp", 1, (), done)
        value, place_at = made[0].astype(F32), lax.axis_index("dp")
        for bit in reversed(bits_of("dp")):
            mine, sent = halves(value, (place_at & bit) != 0, 0)
            term = swap(sent.astype(BF), "dp", bit, (), done)
            value = mine + term.astype(F32)
        return mine, term

    def sides_of(pair, width_of_side):
        return [(pair, 0, width_of_side)], [(pair, width_of_side, width_of_side)]

    def kv_step(s, dkv, before):
        mine, other, bias, *grads = kv_back(where, pieces[s], dkv, kv_full, before, s == seqs - 1)
        total = (mine + other_core(other).astype(F32)).reshape(spots, local, width)
        return total[0], [total[k].astype(BF) for k in range(1, spots)], bias, grads

    own, oth, dkv = attend_back(counts[0], spots, queries[0], g_own[0], g_oth[0], kv[0])
    dq_own, dq_came = [own], [other_side(oth)]
    feed_pairs = [over_lines(d_feed, (dkv,))]
    output_pair = over_lines(d_output, (dkv,))
    kept_0, sent_0, kv_bias_sum, kv_grads = kv_step(0, dkv, None)
    feed_kept, feed_sent = fold_sides(
        feed_pairs,
        [
            sides_of(0, unit_width),
            ([(0, 2 * unit_width, unit_width)], [(0, 3 * unit_width, unit_width)]),
        ],
    )
    feed_term = other_side(feed_sent)
    came_0 = [swap(t, "ctx", k + 1) for k, t in enumerate(sent_0)]
    g_in = after(g_oth[1], feed_sent, *sent_0)
    own, oth, dkv = attend_back(counts[1], spots, queries[1], g_own[1], g_in, kv[1])
    dq_own.append(own)
    dq_came.append(other_side(oth))

    dkv, feed_term, *came_0 = together(dkv, feed_term, *came_0)
    feed_rows = fold_spots(feed_kept, feed_term)
    feed_terms = [swap(t, "ctx", k + 1) for k, t in enumerate(feed_rows[1:])]
    dkv = after(dkv, *feed_rows)
    kept_1, sent_1, kv_bias_sum, kv_grads = kv_step(1, dkv, (kv_grads[0], kv_bias_sum))
    kv_pair = over_lines(kv_grads)
    mine, other, query_bias_sum, *query_grads = query_back(
        where, dq_own, [dq_came[0], after(dq_came[1], *kv_grads)], x_rows, [came[s] for s in range(seqs)], query_full
    )
    query_term = (mine + other_core(other).astype(F32)).reshape(seqs, local, width)
    query_pair = over_lines(query_grads)
    value_bias_sum = apart(kv_bias_sum)[1]
    shared = jnp.concatenate([second_sums[:3], first_sums[:3]])
    shared = shared + other_core(shared)
    vector = jnp.concatenate(
        [shared.reshape(1, -1), d_inner_bias, query_bias_sum.reshape(1, -1), value_bias_sum], axis=1
    )
    for bit in bits_of("dp"):
        vector = vector + swap(vector, "dp", bit)
    if lines == 2:
        query_last, kv_last, vector, *feed_terms = together(query_pair[1], kv_pair[1], vector, *feed_terms)
        query_pair, kv_pair = (query_pair[0], query_last), (kv_pair[0], kv_last)
    came_1 = [swap(after(t, vector), "ctx", k + 1) for k, t in enumerate(sent_1)]

    def side_cuts(pair, offset):
        cuts = []
        for start in (0, heads_width):
            pieces_of, at = [], start
            while at < start + heads_width:
                w = min(PAIR - at % PAIR, start + heads_width - at)
                pieces_of.append((pair, 2 * (at - at % PAIR) + offset + at % PAIR, w))
                at += w
            cuts.append(pieces_of)
        return tuple(cuts)

    kept, sent = fold_sides(
        [query_pair, kv_pair, output_pair],
        [sides_of(0, heads_width), side_cuts(1, 0), side_cuts(1, PAIR), sides_of(2, heads_width)],
    )
    term, *came_1 = together(other_side(sent), *came_1)
    rows = fold_spots(kept, term)
    vector = vector + sum(swap(vector, "ctx", k) for k in range(1, spots))
    terms = [swap(t, "ctx", k + 1) for k, t in enumerate(rows[1:])]
    vector = (vector + other_side(vector))[0]
    feed_owned = feed_rows[0] + sum(t.astype(F32) for t in feed_terms)
    owned = rows[0] + sum(t.astype(F32) for t in terms)
    first_grad = first_grad.reshape(seqs, local, width)
    input_grad = jnp.stack(
        [
            first_grad[s] + query_term[s] + kept + sum(t.astype(F32) for t in came)
            for s, (kept, came) in enumerate(((kept_0, came_0), (kept_1, came_1)))
        ]
    )

    shared = vector[: 6 * width].reshape(6, width)

    def own_side(start, size):
        return jnp.where(is_upper_side, vector[start + size : start + 2 * size], vector[start : start + size])

    base = 6 * width
    after_inner = base + 2 * unit_width
    return (
        output.reshape(seqs, local, width),
        input_grad,
        owned[:, :heads_width],
        own_side(after_inner, heads_width),
        owned[:, heads_width:own_width],
        owned[:, own_width : own_width + heads_width],
        own_side(after_inner + own_width, heads_width),
        owned[:, 3 * heads_width : 4 * heads_width].T,
        shared[5],
        shared[3],
        shared[4],
        feed_owned[:, :unit_width],
        own_side(base, unit_width),
        feed_owned[:, unit_width : 2 * unit_width].T,
        shared[2],
        shared[0],
        shared[1],
    )


def solution(mesh):
    rows = P("dp", ("ctx", "tp"), None)
    into = P(("dp", "ctx"), "tp")
    out_of = P("tp", ("dp", "ctx"))
    split, whole = P("tp"), P()
    return jax.shard_map(
        on_device,
        mesh=mesh,
        in_specs=(
            rows, P("dp"), rows, into, split, into, into, split, out_of, whole, whole, whole,
            into, split, out_of, whole, whole, whole,
        ),
        out_specs=(
            rows, rows, into, split, into, into, split, out_of, whole, whole, whole,
            into, split, out_of, whole, whole, whole,
        ),
        check_vma=False,
    )
```

```python
import functools
import math

import jax
import jax.numpy as jnp
from jax import lax
from jax.experimental import pallas as pl
from jax.experimental.pallas import tpu as pltpu
from jax.sharding import PartitionSpec as P

HD = 64
PAIR = 2 * HD
EPSILON = 1e-12
NEGATIVE = -1e30
LARGEST = 1e30
BF = jnp.bfloat16
F32 = jnp.float32
VMEM_LIMIT = 56 << 20
FEED_ROWS = 512

NN = (((1,), (0,)), ((), ()))
NT = (((1,), (1,)), ((), ()))
TN = (((0,), (0,)), ((), ()))


def dot(a, b, dims):
    return lax.dot_general(a, b, dims, preferred_element_type=F32)


def params():
    return pltpu.CompilerParams(vmem_limit_bytes=VMEM_LIMIT)


def cost(flops, moved, transcendentals=0):
    return pl.CostEstimate(flops=int(flops), bytes_accessed=int(moved), transcendentals=int(transcendentals))


def after(value, *others):
    if not others:
        return value
    return lax.optimization_barrier((value, *others))[0]


def swap(value, axis, bit, start=(), done=()):
    count = lax.axis_size(axis)
    return after(lax.ppermute(after(value, *start), axis, [(i, i ^ bit) for i in range(count)]), *done)


def bits_of(axis):
    count = lax.axis_size(axis)
    return [1 << k for k in range(count.bit_length() - 1)]


def halves(value, upper, dim):
    size = value.shape[dim] // 2
    at = upper.astype(jnp.int32) * size
    mine = lax.dynamic_slice_in_dim(value, at, size, dim)
    return mine, lax.dynamic_slice_in_dim(value, size - at, size, dim)


def ordered(mine, other, upper, dim):
    return jnp.concatenate([jnp.where(upper, other, mine), jnp.where(upper, mine, other)], axis=dim)


def call(kernel, name, outs, *arrays, prefetch=None, scratch=(), flops=0):
    spec = lambda shape: pl.BlockSpec(shape, lambda i, *c: (0,) * len(shape))
    arrays_moved = sum(a.size * a.dtype.itemsize for a in arrays) + sum(4 * math.prod(shape) for shape, _ in outs)
    return pl.pallas_call(
        kernel,
        grid_spec=pltpu.PrefetchScalarGridSpec(
            num_scalar_prefetch=0 if prefetch is None else 1,
            grid=(1,),
            in_specs=[spec(a.shape) for a in arrays],
            out_specs=[spec(shape) for shape, _ in outs],
            scratch_shapes=list(scratch),
        ),
        out_shape=[jax.ShapeDtypeStruct(shape, kind) for shape, kind in outs],
        compiler_params=params(),
        cost_estimate=cost(flops, arrays_moved),
        name=name,
    )(*(() if prefetch is None else (prefetch,)), *arrays)


def fits(rows):
    return rows % 16 == 0


def pack(groups):
    flat = [piece for group in groups for piece in group]
    widths = [sum(w.shape[0] if t else w.shape[1] for w, t in group) for group in groups]
    first, turned = flat[0]
    rows = first.shape[1] if turned else first.shape[0]

    def joined(values):
        values, out = list(values), []
        for group, width in zip(groups, widths):
            out += [values.pop(0) for _ in group]
            if -width % 128:
                out.append(jnp.zeros((rows, -width % 128), F32))
        return jnp.concatenate(out, axis=1).astype(BF)

    if not fits(rows):
        return joined(w.T if t else w for w, t in flat)

    def kernel(*refs):
        refs[-1][...] = joined(r[...].T if t else r[...] for r, (_, t) in zip(refs, flat))

    total = sum(w + -w % 128 for w in widths)
    return call(kernel, "pack", [((rows, total), BF)], *[w for w, _ in flat])[0]


def stack(parts, cuts=None):
    rows, width = parts[0].shape
    ranges = [(0, width)] if cuts is None else [(0, cuts), (cuts, width)]
    if not fits(rows):
        whole = jnp.concatenate(parts, axis=0)
        return [whole[:, start:stop] for start, stop in ranges]

    def kernel(*refs):
        for k, ref in enumerate(refs[: len(parts)]):
            for out, (start, stop) in zip(refs[len(parts) :], ranges):
                out[k * rows : k * rows + rows, :] = ref[:, start:stop]

    return call(kernel, "stack", [((rows * len(parts), stop - start), BF) for start, stop in ranges], *parts)


def over_dp(arrays, done=()):
    found = [arrays]
    for bit in bits_of("dp"):
        found = found + [[swap(a, "dp", bit, (), done) for a in one] for one in found]
    return found


def place(found, widths, joined):
    spots, spot = lax.axis_size("ctx"), lax.axis_index("ctx")
    line, side = lax.axis_index("dp"), lax.axis_index("tp") // 2
    lines = len(found)
    starts = [sum(widths[:k]) for k in range(len(widths))]
    block = found[0][0].shape[0]
    rows = block // spots
    cuts = list(zip(starts, widths))
    shapes = [(block * lines, 2 * sum(widths[m] for m in members)) for members in joined]
    if not fits(rows):
        order = ((jnp.arange(lines)[:, None] ^ line) * spots + (jnp.arange(spots)[None, :] ^ spot)).reshape(-1)
        own, oth = (
            jnp.stack([f[h] for f in found]).reshape(lines * spots, rows, -1)[order].reshape(lines * block, -1)
            for h in range(2)
        )
        low, high = jnp.where(side == 1, oth, own), jnp.where(side == 1, own, oth)
        full = [jnp.concatenate([low[:, t : t + w], high[:, t : t + w]], axis=1) for t, w in cuts]
        return [full[m[0]] if len(m) == 1 else interleaved(full[m[0]], full[m[1]]) for m in joined]

    def kernel(where, *refs):
        outs = refs[2 * lines :]
        upper = where[2] == 1
        for k in range(lines):
            own_ref, oth_ref = refs[2 * k], refs[2 * k + 1]
            for c in range(spots):
                came = pl.ds(pl.multiple_of((where[0] ^ c) * rows, rows), rows)
                to = pl.ds(pl.multiple_of(((where[1] ^ k) * spots + c) * rows, rows), rows)
                own, oth = own_ref[came, :], oth_ref[came, :]
                low, high = jnp.where(upper, oth, own), jnp.where(upper, own, oth)
                full = [jnp.concatenate([low[:, t : t + w], high[:, t : t + w]], axis=1) for t, w in cuts]
                for out, members in zip(outs, joined):
                    if len(members) == 1:
                        out[to, :] = full[members[0]]
                    else:
                        both = []
                        for p in range(0, full[members[0]].shape[1], PAIR):
                            both += [full[m][:, p : p + PAIR] for m in members]
                        out[to, :] = jnp.concatenate(both, axis=1)

    where = jnp.stack([spot, line, side]).astype(jnp.int32)
    flat = [a for one in found for a in one]
    return call(kernel, "place", [(shape, BF) for shape in shapes], *flat, prefetch=where)


def fold_sides(pairs, cuts):
    rows = pairs[0][0].shape[0]
    width = sum(w for low, _ in cuts for _, _, w in low)
    spare = -width % 128
    width += spare
    side = lax.axis_index("tp") // 2

    def both(totals):
        end = [jnp.zeros((totals[0].shape[0], spare), F32)] if spare else []
        low = jnp.concatenate([totals[p][:, t : t + w] for cut, _ in cuts for p, t, w in cut] + end, axis=1)
        high = jnp.concatenate([totals[p][:, t : t + w] for _, cut in cuts for p, t, w in cut] + end, axis=1)
        return low, high

    if not fits(rows):
        low, high = both([a.astype(F32) + b.astype(F32) for a, b in pairs])
        return jnp.where(side == 1, high, low), jnp.where(side == 1, low, high).astype(BF)

    block = rows // 4 if fits(rows // 4) else rows
    steps = rows // block

    def kernel(where, *refs):
        kept, sent = refs[2 * len(pairs) :]
        totals = [refs[2 * k][...].astype(F32) + refs[2 * k + 1][...].astype(F32) for k in range(len(pairs))]
        low, high = both(totals)
        upper = where[0] == 1
        kept[...] = jnp.where(upper, high, low)
        sent[...] = jnp.where(upper, low, high).astype(BF)

    spec = lambda w: pl.BlockSpec((block, w), lambda i, c: (i, 0))
    flat = [a for pair in pairs for a in pair]
    return pl.pallas_call(
        kernel,
        grid_spec=pltpu.PrefetchScalarGridSpec(
            num_scalar_prefetch=1,
            grid=(steps,),
            in_specs=[spec(a.shape[1]) for a in flat],
            out_specs=[spec(width), spec(width)],
        ),
        out_shape=[jax.ShapeDtypeStruct((rows, width), F32), jax.ShapeDtypeStruct((rows, width), BF)],
        compiler_params=params(),
        cost_estimate=cost(0, sum(a.size * a.dtype.itemsize for a in flat) + 6 * rows * width),
        name="fold_sides",
    )(side.astype(jnp.int32).reshape(1), *flat)


def fold_spots(kept, came):
    spots, spot = lax.axis_size("ctx"), lax.axis_index("ctx")
    rows, width = kept.shape[0] // spots, kept.shape[1]
    if not fits(rows):
        total = kept + came.astype(F32)
        cut = lambda k: lax.dynamic_slice_in_dim(total, (spot ^ k) * rows, rows, 0)
        return [cut(0)] + [cut(k).astype(BF) for k in range(1, spots)]

    def kernel(where, kept_ref, came_ref, *outs):
        for k, out in enumerate(outs):
            at = pl.ds(pl.multiple_of((where[0] ^ k) * rows, rows), rows)
            out[...] = (kept_ref[at, :] + came_ref[at, :].astype(F32)).astype(out.dtype)

    outs = [((rows, width), F32)] + [((rows, width), BF)] * (spots - 1)
    return call(kernel, "fold_spots", outs, kept, came, prefetch=spot.astype(jnp.int32).reshape(1))


def add_low(kept, came):
    if not fits(kept.shape[0] // 4):
        return (kept + came.astype(F32)).astype(BF)

    def kernel(kept_ref, came_ref, out):
        out[...] = (kept_ref[...] + came_ref[...].astype(F32)).astype(BF)

    rows, width = kept.shape
    spec = pl.BlockSpec((rows // 4, width), lambda i: (i, 0))
    return pl.pallas_call(
        kernel,
        grid=(4,),
        in_specs=[spec, spec],
        out_specs=spec,
        out_shape=jax.ShapeDtypeStruct(kept.shape, BF),
        compiler_params=params(),
        cost_estimate=cost(kept.size, 8 * kept.size),
        name="add_low",
    )(kept, came)


def own_rows(where, value, rows):
    mine = pl.ds(pl.multiple_of(where * rows, rows), rows)
    other = pl.ds(pl.multiple_of((1 - where) * rows, rows), rows)
    return value[mine, :], value[other, :]


def assemble(upper, pieces, held):
    local = pieces[0].shape[0]
    for k in range(len(pieces) // 2):
        mine, came = pieces[2 * k][...], pieces[2 * k + 1][...]
        held[2 * k * local : (2 * k + 1) * local, :] = jnp.where(upper, came, mine)
        held[(2 * k + 1) * local : (2 * k + 2) * local, :] = jnp.where(upper, mine, came)


def query_back_kernel(seqs, lines, where, *refs):
    dq_own, dq_came, own, came = (refs[k * seqs : k * seqs + seqs] for k in range(4))
    weight, mine_ref, other_ref, bias_ref = refs[4 * seqs : 4 * seqs + 4]
    weight_refs, total = refs[4 * seqs + 4 : -1], refs[-1]
    upper = where[0] == 1
    half = own[0].shape[0]
    bias = None
    for s in range(seqs):
        low = (dq_own[s][...] + dq_came[s][...].astype(F32)).astype(BF)
        rows = jnp.concatenate(
            [jnp.where(upper, came[s][...], own[s][...]), jnp.where(upper, own[s][...], came[s][...])], axis=0
        )
        part = dot(low, weight[...], (((0,), (1,)), ((), ())))
        to = slice(s * half, s * half + half)
        mine_ref[to, :] = jnp.where(upper, part[half:], part[:half])
        other_ref[to, :] = jnp.where(upper, part[:half], part[half:]).astype(BF)
        grad = dot(rows, low, (((0,), (1,)), ((), ())))
        total[...] = grad if s == 0 else total[...] + grad
        sums = jnp.sum(low.astype(F32), axis=1, keepdims=True)
        bias = sums if bias is None else bias + sums
    bias_ref[...] = bias
    if lines == 2:
        kept, sent = own_rows(where[1], total, total.shape[0] // 2)
        weight_refs[0][...] = kept
        weight_refs[1][...] = sent.astype(BF)
    else:
        weight_refs[0][...] = total[...]


def query_back(where, dq_own, dq_came, own, came, weight):
    seqs, lines = len(dq_own), lax.axis_size("dp")
    local, width = own[0].shape
    own_width = weight.shape[1]
    outs = [((seqs * local, width), F32), ((seqs * local, width), BF), ((own_width, 1), F32)]
    if lines == 2:
        outs += [((width // 2, own_width), F32), ((width // 2, own_width), BF)]
    else:
        outs += [((width, own_width), F32)]
    return call(
        functools.partial(query_back_kernel, seqs, lines),
        "query_back",
        outs,
        *dq_own,
        *dq_came,
        *own,
        *came,
        weight,
        prefetch=where,
        scratch=[pltpu.VMEM((width, own_width), F32)],
        flops=8 * seqs * local * width * own_width,
    )


def half_lanes(value):
    lane = lax.broadcasted_iota(jnp.int32, value.shape, 1)
    zero = jnp.zeros_like(value)
    return [jnp.where(lane < HD, value, zero), jnp.where(lane >= HD, value, zero)]


def half_rows(value):
    row = lax.broadcasted_iota(jnp.int32, value.shape, 0)
    zero = jnp.zeros_like(value)
    return [jnp.where(row < HD, value, zero), jnp.where(row >= HD, value, zero)]


def top_bits(value):
    spread = value * 65537.0
    return spread - (spread - value)


def in_three(value):
    first = top_bits(value)
    rest = value - first
    second = top_bits(rest)
    return first.astype(BF), second.astype(BF), (rest - second).astype(BF)


def packed_rows(values):
    terms = jnp.concatenate(in_three(values), axis=0)
    return jnp.concatenate([terms, jnp.zeros((16 - terms.shape[0], terms.shape[1]), BF)], axis=0)


def unpacked_rows(packed, count):
    packed = packed.astype(F32)
    return packed[:count] + packed[count : 2 * count] + packed[2 * count : 3 * count]


def below(shape, count):
    return lax.broadcasted_iota(jnp.int32, shape, 0) < count


def attend_kernel(slots, probe, old, counts, *refs):
    pieces = refs[: 2 * slots + 2]
    w_query, w_kv, b_query, b_kv = refs[2 * slots + 2 : 2 * slots + 6]
    queries, kv, o_own, packed, lse_ref, held, top, total, acc, heads = refs[2 * slots + 6 + old :]
    local = pieces[0].shape[0]
    rows = keys = 2 * local

    @pl.when(pl.program_id(0) == 0)
    def _():
        assemble(counts[slots + 1] == 1, pieces, held)

    scale = jnp.asarray(1.0 / math.sqrt(HD), BF)
    for start, to in ((0, 0), (slots * keys, rows)):
        query = (dot(held[start : start + rows, :], w_query[...], NN) + b_query[...]).astype(BF)
        queries[to : to + rows, :] = query * scale
    for h, query in enumerate(half_lanes(queries[...])):
        heads[h] = query

    @pl.loop(0, slots)
    def _(k):
        at = pl.ds(pl.multiple_of(k * keys, keys), keys)

        @pl.when(counts[k] > 0)
        def _():
            kv[at, :] = (dot(held[at, :], w_kv[...], NN) + b_kv[...]).astype(BF)

        @pl.when(counts[k] <= 0)
        def _():
            kv[at, :] = jnp.zeros((keys, 2 * PAIR), BF)

    def block(k):
        at = pl.ds(pl.multiple_of(k * keys, keys), keys)
        return kv[at, :PAIR], kv[at, PAIR:]

    first = pl.ds(pl.multiple_of(counts[slots] * keys, keys), probe)
    for h in range(2):
        top[h] = jnp.max(dot(kv[first, :PAIR], heads[h], NT), axis=0, keepdims=True)
    total[...] = jnp.zeros_like(total)
    acc[...] = jnp.zeros_like(acc)

    def quick(k, h, valid):
        key, value = block(k)
        expo = jnp.exp(dot(key, heads[h], NT) - top[h])
        if valid is not None:
            expo = jnp.where(below(expo.shape, valid), expo, 0.0)
        total[h] += jnp.sum(expo, axis=0, keepdims=True)
        acc[h] += dot(value, expo.astype(BF), TN)

    @pl.loop(0, slots)
    def _(k):
        valid = counts[k]

        @pl.when(valid >= keys)
        def _():
            quick(k, 0, None)
            quick(k, 1, None)

        @pl.when(jnp.logical_and(valid > 0, valid < keys))
        def _():
            pl.loop(0, 2)(lambda h: quick(k, h, valid))

    @pl.when(jnp.logical_not(jnp.max(total[...]) < LARGEST))
    def _():
        total[...] = jnp.zeros_like(total)
        acc[...] = jnp.zeros_like(acc)

        def careful(k, h, valid):
            key, value = block(k)
            scores = dot(key, heads[h], NT)
            scores = jnp.where(below(scores.shape, valid), scores, NEGATIVE)
            before = top[h]
            new = jnp.maximum(before, jnp.max(scores, axis=0, keepdims=True))
            expo = jnp.where(below(scores.shape, valid), jnp.exp(scores - new), 0.0)
            ratio = jnp.exp(before - new)
            total[h] = total[h] * ratio + jnp.sum(expo, axis=0, keepdims=True)
            acc[h] = acc[h] * ratio + dot(value, expo.astype(BF), TN)
            top[h] = new

        @pl.loop(0, slots)
        def _(k):
            valid = counts[k]

            @pl.when(valid > 0)
            def _():
                pl.loop(0, 2)(lambda h: careful(k, h, valid))

    lse = []
    for h in range(2):
        at = slice(h * HD, h * HD + HD)
        part = acc[h, at, :] / total[h]
        o_own[0, at, :] = part[:, :rows]
        packed[at, :] = part[:, rows:].astype(BF)
        lse.append(top[h] + jnp.log(total[h]))
        lse_ref[0, 0, h : h + 1, :] = lse[h][:, :rows]
    packed[PAIR:, :] = packed_rows(jnp.concatenate([l[:, rows:] for l in lse], axis=0))


def attend(counts, seqs, s, pieces, weights, before):
    w_query, w_kv, b_query, b_kv = weights
    slots = len(pieces) - 1
    local, model = pieces[0][0].shape
    rows, width = 2 * local, w_query.shape[1]
    pairs = width // PAIR
    keys = 2 * local
    total = width * 2 * rows * slots * keys
    anywhere = pl.BlockSpec(memory_space=pl.ANY)
    across = lambda p, c: (0, p)
    flat = [p for pair in pieces for p in pair]
    held = ((slots + 1) * keys, model)
    return pl.pallas_call(
        functools.partial(attend_kernel, slots, min(128, keys), len(before)),
        grid_spec=pltpu.PrefetchScalarGridSpec(
            num_scalar_prefetch=1,
            grid=(pairs,),
            in_specs=[pl.BlockSpec((local, model), lambda p, c: (0, 0), pipeline_mode=pl.Buffered(1)) for _ in flat]
            + [
                pl.BlockSpec((model, PAIR), across),
                pl.BlockSpec((model, 2 * PAIR), across),
                pl.BlockSpec((1, PAIR), across),
                pl.BlockSpec((1, 2 * PAIR), across),
            ]
            + [anywhere] * len(before),
            out_specs=[
                pl.BlockSpec((2 * rows, PAIR), across),
                pl.BlockSpec((slots * keys, 2 * PAIR), across),
                pl.BlockSpec((1, PAIR, rows), lambda p, c: (s, p, 0)),
                pl.BlockSpec((PAIR + 16, rows), lambda p, c: (p, 0)),
                pl.BlockSpec((1, 1, 2, rows), lambda p, c: (s, p, 0, 0)),
            ],
            scratch_shapes=[
                pltpu.VMEM(held, BF),
                pltpu.VMEM((2, 1, 2 * rows), F32),
                pltpu.VMEM((2, 1, 2 * rows), F32),
                pltpu.VMEM((2, PAIR, 2 * rows), F32),
                pltpu.VMEM((2, 2 * rows, PAIR), BF),
            ],
        ),
        out_shape=[
            jax.ShapeDtypeStruct((2 * rows, width), BF),
            jax.ShapeDtypeStruct((slots * keys, 2 * width), BF),
            jax.ShapeDtypeStruct((seqs, width, rows), F32),
            jax.ShapeDtypeStruct((pairs * (PAIR + 16), rows), BF),
            jax.ShapeDtypeStruct((seqs, pairs, 2, rows), F32),
        ],
        input_output_aliases={2 * slots + 7: 2, 2 * slots + 8: 4} if before else {},
        compiler_params=params(),
        cost_estimate=cost(16 * total, 2 * len(flat) * local * model + 8 * slots * keys * width, total // HD),
        name="attend",
    )(counts, *flat, *weights, *before)


def attend_back_kernel(slots, steps, split, first, counts, both, g_own, g_oth, kv, w_kv, *refs):
    pieces = refs[: 2 * slots]
    refs = refs[2 * slots :]
    if not first:
        before, bias_before = refs[:2]
        refs = refs[2:]
    dq_own, dq_oth, mine_ref, other_ref, bias_ref = refs[:5]
    weight_refs = refs[5:-8]
    acc, queries, grads, summed, facts, turned, part, d_weight = refs[-8:]
    rows = both.shape[0] // 2
    local = pieces[0].shape[0]
    keys = 2 * local
    step = pl.program_id(0)
    upper = counts[slots + 1] == 1

    @pl.when(step == 0)
    def _():
        part[...] = jnp.zeros_like(part)
        for k in range(slots):
            mine, came = pieces[2 * k][...], pieces[2 * k + 1][...]
            turned[:, 2 * k * local : (2 * k + 1) * local] = jnp.where(upper, came, mine).T
            turned[:, (2 * k + 1) * local : (2 * k + 2) * local] = jnp.where(upper, mine, came).T

    acc[...] = jnp.zeros_like(acc)
    d_weight[...] = jnp.zeros_like(d_weight) if first else before[...]
    bias_ref[...] = jnp.zeros_like(bias_ref) if first else bias_before[...]
    for block, g_ref in enumerate((g_own, g_oth)):
        stats = unpacked_rows(g_ref[PAIR:, :], 4)
        for h, (query, grad) in enumerate(
            zip(half_lanes(both[block * rows : block * rows + rows, :]), half_rows(g_ref[:PAIR, :]))
        ):
            queries[2 * block + h] = query
            grads[2 * block + h] = grad
            facts[2 * block + h, 0:1, :] = stats[h : h + 1]
            facts[2 * block + h, 1:2, :] = stats[2 + h : 3 + h]

    @pl.loop(0, slots)
    def _(k):
        valid = counts[k]
        rows_at = pl.ds(pl.multiple_of(k * keys, keys), keys)

        def one(at, valid):
            key, value = kv[rows_at, :PAIR], kv[rows_at, PAIR:]
            query, grad = queries[at], grads[at]
            prob = jnp.exp(dot(key, query, NT) - facts[at, 0:1, :])
            if valid is not None:
                prob = jnp.where(below(prob.shape, valid), prob, 0.0)
            change = dot(value, grad, NN) - facts[at, 1:2, :]
            score = (prob * change).astype(BF)
            summed[:, PAIR:] += dot(prob.astype(BF), grad, NT)
            summed[:, :PAIR] += dot(score, query, NN)
            acc[at] += dot(key, score, TN)

        summed[...] = jnp.zeros_like(summed)

        @pl.when(valid >= keys)
        def _():
            for at in range(4):
                one(at, None)

        @pl.when(jnp.logical_and(valid > 0, valid < keys))
        def _():
            pl.loop(0, 4)(lambda at: one(at, valid))

        @pl.when(valid > 0)
        def _():
            low = summed[...].astype(BF)
            part[rows_at, :] += dot(low, w_kv[...], NT)
            d_weight[...] += dot(turned[:, rows_at], low, NN)
            bias_ref[...] += jnp.sum(low.astype(F32), axis=0, keepdims=True)

    scale = 1.0 / math.sqrt(HD)
    for h in range(2):
        at = slice(h * HD, h * HD + HD)
        dq_own[at, :] = acc[h, at, :] * scale
        dq_oth[at, :] = (acc[2 + h, at, :] * scale).astype(BF)
    half = d_weight.shape[0] // 2
    if split:
        lower_line = counts[slots + 2] == 0
        low_half, high_half = d_weight[:half, :], d_weight[half:, :]
        weight_refs[0][...] = jnp.where(lower_line, low_half, high_half)
        weight_refs[1][...] = jnp.where(lower_line, high_half, low_half).astype(BF)
    else:
        weight_refs[0][...] = d_weight[...]

    @pl.when(step == steps - 1)
    def _():
        for k in range(slots):
            low = part[2 * k * local : (2 * k + 1) * local, :]
            high = part[(2 * k + 1) * local : (2 * k + 2) * local, :]
            to = slice(k * local, k * local + local)
            mine_ref[to, :] = jnp.where(upper, high, low)
            other_ref[to, :] = jnp.where(upper, low, high).astype(BF)


def attend_back(counts, both, g_own, g_oth, kv, w_kv, pieces, before, last):
    rows, width = both.shape[0] // 2, both.shape[1]
    pairs = width // PAIR
    slots = len(pieces)
    local, model = pieces[0][0].shape
    keys = 2 * local
    split = last and lax.axis_size("dp") == 2
    across = lambda p, c: (0, p)
    whole = lambda p, c: (0, 0)
    once = pl.Buffered(1)
    t_spec = pl.BlockSpec((PAIR, rows), lambda p, c: (p, 0))
    g_spec = pl.BlockSpec((PAIR + 16, rows), lambda p, c: (p, 0))
    flat = [p for pair in pieces for p in pair]
    extra = () if before is None else before
    if split:
        weight_outs = [((model // 2, 2 * width), F32), ((model // 2, 2 * width), BF)]
    else:
        weight_outs = [((model, 2 * width), F32)]
    total = width * 2 * rows * kv.shape[0]
    return pl.pallas_call(
        functools.partial(attend_back_kernel, slots, pairs, split, before is None),
        grid_spec=pltpu.PrefetchScalarGridSpec(
            num_scalar_prefetch=1,
            grid=(pairs,),
            in_specs=[
                pl.BlockSpec((2 * rows, PAIR), across),
                g_spec,
                g_spec,
                pl.BlockSpec((kv.shape[0], 2 * PAIR), across),
                pl.BlockSpec((model, 2 * PAIR), across),
            ]
            + [pl.BlockSpec((local, model), whole, pipeline_mode=once) for _ in flat]
            + [pl.BlockSpec((a.shape[0], 2 * PAIR), across) for a in extra],
            out_specs=[
                t_spec,
                t_spec,
                pl.BlockSpec((slots * local, model), whole, pipeline_mode=once),
                pl.BlockSpec((slots * local, model), whole, pipeline_mode=once),
                pl.BlockSpec((1, 2 * PAIR), across),
            ]
            + [pl.BlockSpec((shape[0], 2 * PAIR), across) for shape, _ in weight_outs],
            scratch_shapes=[
                pltpu.VMEM((4, PAIR, rows), F32),
                pltpu.VMEM((4, rows, PAIR), BF),
                pltpu.VMEM((4, PAIR, rows), BF),
                pltpu.VMEM((keys, 2 * PAIR), F32),
                pltpu.VMEM((4, 2, rows), F32),
                pltpu.VMEM((model, slots * keys), BF),
                pltpu.VMEM((slots * keys, model), F32),
                pltpu.VMEM((model, 2 * PAIR), F32),
            ],
        ),
        out_shape=[
            jax.ShapeDtypeStruct((width, rows), F32),
            jax.ShapeDtypeStruct((width, rows), BF),
            jax.ShapeDtypeStruct((slots * local, model), F32),
            jax.ShapeDtypeStruct((slots * local, model), BF),
            jax.ShapeDtypeStruct((1, 2 * width), F32),
        ]
        + [jax.ShapeDtypeStruct(shape, kind) for shape, kind in weight_outs],
        compiler_params=params(),
        cost_estimate=cost(40 * total, 8 * both.size + 4 * kv.size + 8 * len(flat) * local * model, total // HD),
        name="attend_back",
    )(counts, both, g_own, g_oth, kv, w_kv, *flat, *extra)


def merge_kernel(pairs, seqs, where, o_own, lse_own, *refs):
    packs = refs[:seqs]
    weight, full_ref, low_ref, mine_ref, other_ref, lse_ref, low_s, packed = refs[seqs:]
    rows = o_own.shape[2]
    for s in range(seqs):

        @pl.when(pl.program_id(0) == s)
        def _(s=s):
            packed[...] = packs[s][...]

    for p in range(pairs):
        base = p * (PAIR + 16)
        own = lse_own[0, p]
        came = unpacked_rows(packed[base + PAIR : base + PAIR + 16, :], 2)
        highest = jnp.maximum(own, came)
        share_own, share_came = jnp.exp(own - highest), jnp.exp(came - highest)
        both = share_own + share_came
        lse_ref[0, p] = highest + jnp.log(both)
        share_own, share_came = share_own / both, share_came / both
        for h in range(2):
            at = slice(p * PAIR + h * HD, p * PAIR + h * HD + HD)
            term = packed[base + h * HD : base + h * HD + HD, :].astype(F32)
            merged = o_own[0, at, :] * share_own[h : h + 1] + term * share_came[h : h + 1]
            full_ref[0, at, :] = merged
            low_s[at, :] = merged.astype(BF)
    low_ref[0] = low_s[...]
    half = rows // 2
    mine = pl.ds(pl.multiple_of(where[0] * half, half), half)
    other = pl.ds(pl.multiple_of((1 - where[0]) * half, half), half)
    dims = (((0,), (1,)), ((), ()))
    mine_ref[0] = dot(low_s[:, mine], weight[...], dims)
    other_ref[0] = dot(low_s[:, other], weight[...], dims).astype(BF)


def merge(where, o_own, lse_own, packs, weight):
    seqs, width, rows = o_own.shape
    pairs = width // PAIR
    model = weight.shape[0]
    one = lambda *shape: pl.BlockSpec((1, *shape), lambda s, w: (s,) + (0,) * len(shape))
    return pl.pallas_call(
        functools.partial(merge_kernel, pairs, seqs),
        grid_spec=pltpu.PrefetchScalarGridSpec(
            num_scalar_prefetch=1,
            grid=(seqs,),
            in_specs=[
                one(width, rows),
                one(pairs, 2, rows),
            ]
            + [pl.BlockSpec(p.shape, lambda s, w: (0, 0)) for p in packs]
            + [
                pl.BlockSpec(weight.shape, lambda s, w: (0, 0)),
            ],
            out_specs=[one(width, rows), one(width, rows), one(rows // 2, model), one(rows // 2, model), one(pairs, 2, rows)],
            scratch_shapes=[pltpu.VMEM((width, rows), BF), pltpu.VMEM(packs[0].shape, BF)],
        ),
        out_shape=[
            jax.ShapeDtypeStruct((seqs, width, rows), F32),
            jax.ShapeDtypeStruct((seqs, width, rows), BF),
            jax.ShapeDtypeStruct((seqs, rows // 2, model), F32),
            jax.ShapeDtypeStruct((seqs, rows // 2, model), BF),
            jax.ShapeDtypeStruct((seqs, pairs, 2, rows), F32),
        ],
        compiler_params=params(),
        cost_estimate=cost(2 * seqs * width * rows * model, 12 * o_own.size + 4 * seqs * rows * model),
        name="merge",
    )(where, o_own, lse_own, *packs, weight)


def turn_kernel(pairs, seqs, lines, where, own_ref, came_ref, weight, full_ref, low_ref, lse_ref, *refs):
    packs, weight_refs = refs[:seqs], refs[seqs:-2]
    d_weight, packed = refs[-2:]
    step = pl.program_id(0)
    upper = where[0] == 1
    own, came = own_ref[0], came_ref[0]
    rows = jnp.concatenate([jnp.where(upper, came, own), jnp.where(upper, own, came)], axis=0)
    grad = dot(weight[...], rows, (((0,), (1,)), ((), ()))).astype(BF)
    product = grad.astype(F32) * full_ref[0]
    for p in range(pairs):
        base = p * (PAIR + 16)
        packed[base : base + PAIR, :] = grad[p * PAIR : p * PAIR + PAIR]
        stats = [lse_ref[0, p]]
        for h in range(2):
            at = slice(p * PAIR + h * HD, p * PAIR + h * HD + HD)
            stats.append(jnp.sum(product[at], axis=0, keepdims=True))
        packed[base + PAIR : base + PAIR + 16, :] = packed_rows(jnp.concatenate(stats, axis=0))
    for s in range(seqs):

        @pl.when(step == s)
        def _(s=s):
            packs[s][...] = packed[...]

    @pl.when(step == 0)
    def _():
        d_weight[...] = jnp.zeros_like(d_weight)

    d_weight[...] += dot(rows, low_ref[0], (((0,), (1,)), ((), ())))

    @pl.when(step == seqs - 1)
    def _():
        if lines == 2:
            kept, sent = own_rows(where[1], d_weight, d_weight.shape[0] // 2)
            weight_refs[0][...] = kept
            weight_refs[1][...] = sent.astype(BF)
        else:
            weight_refs[0][...] = d_weight[...]


def turn(where, own, came, weight, full, low, lse):
    seqs, width, rows = full.shape
    pairs = width // PAIR
    one = lambda *shape: pl.BlockSpec((1, *shape), lambda s, w: (s,) + (0,) * len(shape))
    whole = lambda *shape: pl.BlockSpec(shape, lambda s, w: (0, 0))
    lines = lax.axis_size("dp")
    pack_shape = (pairs * (PAIR + 16), rows)
    half = (weight.shape[0] // 2, weight.shape[1])
    weight_outs = [(half, F32), (half, BF)] if lines == 2 else [(weight.shape, F32)]
    return pl.pallas_call(
        functools.partial(turn_kernel, pairs, seqs, lines),
        grid_spec=pltpu.PrefetchScalarGridSpec(
            num_scalar_prefetch=1,
            grid=(seqs,),
            in_specs=[
                one(*own.shape[1:]),
                one(*own.shape[1:]),
                whole(*weight.shape),
                one(width, rows),
                one(width, rows),
                one(pairs, 2, rows),
            ],
            out_specs=[whole(*pack_shape)] * seqs + [whole(*shape) for shape, _ in weight_outs],
            scratch_shapes=[pltpu.VMEM(weight.shape, F32), pltpu.VMEM(pack_shape, BF)],
        ),
        out_shape=[jax.ShapeDtypeStruct(pack_shape, BF)] * seqs
        + [jax.ShapeDtypeStruct(shape, kind) for shape, kind in weight_outs],
        compiler_params=params(),
        cost_estimate=cost(4 * seqs * rows * weight.size, 8 * full.size + 4 * own.size),
        name="turn",
    )(where, own, came, weight, full, low, lse)


def gelu_parts(u):
    density = jnp.exp(-0.5 * u * u)
    t = 1.0 / (1.0 + (0.3275911 / math.sqrt(2.0)) * jnp.abs(u))
    series = t * (
        0.254829592
        + t * (-0.284496736 + t * (1.421413741 + t * (-1.453152027 + t * 1.061405429)))
    )
    tail = 0.5 * series * density
    share = jnp.where(u < 0.0, tail, 1.0 - tail)
    return u * share, share + u * (density * (1.0 / math.sqrt(2.0 * math.pi)))


def feed_kernel(chunk, half, own_ref, came_ref, w_in, bias, w_out, active_ref, slope_ref, mine_ref, other_ref):
    step = pl.program_id(0)
    rows = jnp.where(step < half, own_ref[...], came_ref[...])
    part = None
    for start in range(0, w_in.shape[1], chunk):
        at = slice(start, start + chunk)
        inner = dot(rows, w_in[:, at], NN) + bias[:, at]
        active, slope = gelu_parts(inner)
        active = active.astype(BF)
        active_ref[:, at] = active
        slope_ref[:, at] = slope.astype(BF)
        term = dot(active, w_out[:, at], NT)
        part = term if part is None else part + term

    @pl.when(step < half)
    def _():
        mine_ref[...] = part

    @pl.when(step >= half)
    def _():
        other_ref[...] = part.astype(BF)


def row_specs(block, half, width):
    own = pl.BlockSpec((block, width), lambda i, *c: (jnp.minimum(i, half - 1), 0))
    came = pl.BlockSpec((block, width), lambda i, *c: (jnp.maximum(i - half, 0), 0))
    return own, came


def feed(own, came, w_in, bias, w_out):
    count, width = own.shape
    units = w_in.shape[1]
    block = min(FEED_ROWS, count)
    half = count // block
    whole = lambda i: (0, 0)
    by_row = lambda i: (i, 0)
    own_spec, came_spec = row_specs(block, half, width)
    return pl.pallas_call(
        functools.partial(feed_kernel, units // 3 if units % 384 == 0 else units, half),
        grid=(2 * half,),
        in_specs=[
            own_spec,
            came_spec,
            pl.BlockSpec((width, units), whole, pipeline_mode=pl.Buffered(1)),
            pl.BlockSpec((1, units), whole),
            pl.BlockSpec((width, units), whole, pipeline_mode=pl.Buffered(1)),
        ],
        out_specs=[pl.BlockSpec((block, units), by_row), pl.BlockSpec((block, units), by_row), own_spec, came_spec],
        out_shape=[
            jax.ShapeDtypeStruct((2 * count, units), BF),
            jax.ShapeDtypeStruct((2 * count, units), BF),
            jax.ShapeDtypeStruct((count, width), F32),
            jax.ShapeDtypeStruct((count, width), BF),
        ],
        compiler_params=params(),
        cost_estimate=cost(8 * count * width * units, 4 * width * units + 8 * count * units + 12 * count * width, 2 * count * units),
        name="feed",
    )(own, came, w_in, bias, w_out)


def feed_back_kernel(half, lines, where, low_own, low_came, own_ref, came_ref, active_ref, slope_ref, w_in, w_out, *refs):
    mine_ref, other_ref, d_bias_ref = refs[:3]
    weight_refs, (d_in, d_out) = refs[3:-2], refs[-2:]
    step = pl.program_id(0)
    units = w_in.shape[1]

    @pl.when(step == 0)
    def _():
        d_in[...] = jnp.zeros_like(d_in)
        d_out[...] = jnp.zeros_like(d_out)
        d_bias_ref[...] = jnp.zeros_like(d_bias_ref)

    low = jnp.where(step < half, low_own[...], low_came[...])
    rows = jnp.where(step < half, own_ref[...], came_ref[...])
    inner = (dot(low, w_out[...], NN) * slope_ref[...].astype(F32)).astype(BF)
    part = dot(inner, w_in[...], NT)
    d_out[...] += dot(low, active_ref[...], TN)
    d_in[...] += dot(rows, inner, TN)
    d_bias_ref[...] += jnp.sum(inner.astype(F32), axis=0, keepdims=True)

    @pl.when(step < half)
    def _():
        mine_ref[...] = part

    @pl.when(step >= half)
    def _():
        other_ref[...] = part.astype(BF)

    @pl.when(step == 2 * half - 1)
    def _():
        for total, cut in ((d_in, slice(0, units)), (d_out, slice(units, 2 * units))):
            if lines == 2:
                kept, sent = own_rows(where[1], total, total.shape[0] // 2)
                weight_refs[0][:, cut] = kept.astype(BF)
                weight_refs[1][:, cut] = sent.astype(BF)
            else:
                weight_refs[0][:, cut] = total[...].astype(BF)


def feed_back(where, low_own, low_came, own, came, active, slope, w_in, w_out):
    count, width = own.shape
    units = w_in.shape[1]
    block = min(FEED_ROWS, count)
    half = count // block
    whole = lambda i, *c: (0, 0)
    by_row = lambda i, *c: (i, 0)
    once = pl.Buffered(1)
    lines = lax.axis_size("dp")
    own_spec, came_spec = row_specs(block, half, width)
    d_shape = (width // 2 if lines == 2 else width, 2 * units)
    d_count = 2 if lines == 2 else 1
    return pl.pallas_call(
        functools.partial(feed_back_kernel, half, lines),
        grid_spec=pltpu.PrefetchScalarGridSpec(
            num_scalar_prefetch=1,
            grid=(2 * half,),
            in_specs=[
                own_spec,
                came_spec,
                own_spec,
                came_spec,
                pl.BlockSpec((block, units), by_row),
                pl.BlockSpec((block, units), by_row),
                pl.BlockSpec((width, units), whole, pipeline_mode=once),
                pl.BlockSpec((width, units), whole, pipeline_mode=once),
            ],
            out_specs=[own_spec, came_spec, pl.BlockSpec((1, units), whole)]
            + [pl.BlockSpec(d_shape, whole, pipeline_mode=once)] * d_count,
            scratch_shapes=[pltpu.VMEM((width, units), F32), pltpu.VMEM((width, units), F32)],
        ),
        out_shape=[
            jax.ShapeDtypeStruct((count, width), F32),
            jax.ShapeDtypeStruct((count, width), BF),
            jax.ShapeDtypeStruct((1, units), F32),
        ]
        + [jax.ShapeDtypeStruct(d_shape, BF)] * d_count,
        compiler_params=params(),
        cost_estimate=cost(16 * count * width * units, 8 * width * units + 8 * count * units + 16 * count * width),
        name="feed_back",
    )(where, low_own, low_came, own, came, active, slope, w_in, w_out)


def centre(values):
    middle = values - jnp.mean(values, axis=-1, keepdims=True)
    scale = lax.rsqrt(jnp.mean(middle * middle, axis=-1, keepdims=True) + EPSILON)
    return middle * scale, scale


def back_through(weighted, normal, scale):
    first = jnp.mean(weighted, axis=-1, keepdims=True)
    second = jnp.mean(weighted * normal, axis=-1, keepdims=True)
    return (weighted - first - normal * second) * scale


def first_kernel(x_ref, mine_ref, came_ref, vec_ref, normal_ref, scale_ref, low_ref):
    sums = x_ref[...].astype(F32) + (mine_ref[...] + came_ref[...].astype(F32)) + vec_ref[0:1, :]
    normal, scale = centre(sums)
    normal_ref[...] = normal
    scale_ref[...] = scale
    low_ref[...] = (normal * vec_ref[1:2, :] + vec_ref[2:3, :]).astype(BF)


def second_kernel(per_seq, counts, normal_ref, mine_ref, came_ref, cot_ref, vec_ref, out_ref, grad_ref, low_ref, sums_ref):
    step = pl.program_id(0)
    block = normal_ref.shape[0]
    valid = counts[step // per_seq] - (step % per_seq) * block
    keep = lax.broadcasted_iota(jnp.int32, normal_ref.shape, 0) < valid

    @pl.when(step == 0)
    def _():
        sums_ref[...] = jnp.zeros_like(sums_ref)

    first = normal_ref[...] * vec_ref[1:2, :] + vec_ref[2:3, :]
    sums = first + (mine_ref[...] + came_ref[...].astype(F32)) + vec_ref[3:4, :]
    normal, scale = centre(sums)
    out_ref[...] = jnp.where(keep, normal * vec_ref[4:5, :] + vec_ref[5:6, :], 0.0)
    out_grad = jnp.where(keep, cot_ref[...].astype(F32), 0.0)
    grad = back_through(out_grad * vec_ref[4:5, :], normal, scale)
    grad_ref[...] = grad
    low_ref[...] = grad.astype(BF)
    sums_ref[0:1, :] += jnp.sum(out_grad * normal, axis=0, keepdims=True)
    sums_ref[1:2, :] += jnp.sum(out_grad, axis=0, keepdims=True)
    sums_ref[2:3, :] += jnp.sum(grad, axis=0, keepdims=True)


def first_back_kernel(grad_ref, mine_ref, came_ref, normal_ref, scale_ref, vec_ref, out_ref, low_ref, sums_ref):
    @pl.when(pl.program_id(0) == 0)
    def _():
        sums_ref[...] = jnp.zeros_like(sums_ref)

    given = grad_ref[...] + (mine_ref[...] + came_ref[...].astype(F32))
    normal = normal_ref[...]
    grad = back_through(given * vec_ref[1:2, :], normal, scale_ref[...])
    out_ref[...] = grad
    low_ref[...] = grad.astype(BF)
    sums_ref[0:1, :] += jnp.sum(given * normal, axis=0, keepdims=True)
    sums_ref[1:2, :] += jnp.sum(given, axis=0, keepdims=True)
    sums_ref[2:3, :] += jnp.sum(grad, axis=0, keepdims=True)


def row_call(kernel, name, block, count, width, inputs, whole_inputs, outs, sums, counts=None):
    by_row = lambda i, *c: (i, 0)
    whole = lambda i, *c: (0, 0)
    in_specs = [pl.BlockSpec((block, a.shape[1]), by_row) for a in inputs]
    in_specs += [pl.BlockSpec(a.shape, whole) for a in whole_inputs]
    out_specs = [pl.BlockSpec((block, w), by_row) for w, _ in outs]
    out_shape = [jax.ShapeDtypeStruct((count, w), t) for w, t in outs]
    if sums:
        out_specs.append(pl.BlockSpec((8, width), whole))
        out_shape.append(jax.ShapeDtypeStruct((8, width), F32))
    prefetch = 0 if counts is None else 1
    moved = sum(a.size * a.dtype.itemsize for a in inputs) + sum(count * w * 4 for w, _ in outs)
    return pl.pallas_call(
        kernel,
        grid_spec=pltpu.PrefetchScalarGridSpec(
            num_scalar_prefetch=prefetch, grid=(count // block,), in_specs=in_specs, out_specs=out_specs
        ),
        out_shape=out_shape,
        compiler_params=params(),
        cost_estimate=cost(20 * count * width, moved),
        name=name,
    )(*(() if counts is None else (counts,)), *inputs, *whole_inputs)


def interleaved(key, value):
    width = key.shape[1]
    pieces = []
    for start in range(0, width, PAIR):
        pieces += [key[:, start : start + PAIR], value[:, start : start + PAIR]]
    return jnp.concatenate(pieces, axis=1)


def apart(both):
    keys, values = [], []
    for start in range(0, both.shape[1], 2 * PAIR):
        keys.append(both[:, start : start + PAIR])
        values.append(both[:, start + PAIR : start + 2 * PAIR])
    return jnp.concatenate(keys, axis=1), jnp.concatenate(values, axis=1)


def on_device(
    block_input,
    lengths,
    cotangent,
    query_weight,
    query_bias,
    key_weight,
    value_weight,
    value_bias,
    output_weight,
    output_bias,
    first_gain,
    first_shift,
    inner_weight,
    inner_bias,
    outer_weight,
    closing_offset_vector,
    second_gain,
    second_shift,
):
    seqs, local, width = block_input.shape
    chip = 2 * local
    spots = lax.axis_size("ctx")
    spot = lax.axis_index("ctx")
    part = lax.axis_index("tp")
    core, side = part % 2, part // 2
    is_upper_core, is_upper_side = core == 1, side == 1
    span = local * lax.axis_size("tp")
    heads_width = query_weight.shape[1]
    unit_width = inner_weight.shape[1]
    count = seqs * local

    def other_core(value, **ties):
        return swap(value, "tp", 1, **ties)

    def other_side(value, **ties):
        return swap(value, "tp", 2, **ties)

    def flat(value):
        return value.reshape(-1, value.shape[-1])

    starts = jnp.stack([(spot ^ k) * span + side * chip for k in range(spots)])
    key_counts = jnp.clip(lengths[:, None] - starts[None, :], 0, chip)
    facts = jnp.stack([spot, core, lax.axis_index("dp")]).astype(jnp.int32)
    counts = jnp.concatenate([key_counts.astype(jnp.int32), jnp.broadcast_to(facts, (seqs, 3))], axis=1)
    row_counts = jnp.clip(lengths - (spot * span + part * local), 0, local).astype(jnp.int32)
    where = jnp.stack([core, lax.axis_index("dp")]).astype(jnp.int32)

    def together(*values):
        return lax.optimization_barrier(values)

    def over_spots(value, done=()):
        return [swap(value, "ctx", k, (), done) for k in range(1, spots)]

    lines = lax.axis_size("dp")
    own_width = 2 * heads_width
    attention_shard = pack([[(query_weight, False), (key_weight, False), (value_weight, False)]])
    feed_shard = pack([[(output_weight, True), (inner_weight, False)], [(outer_weight, True)]])
    biases = jnp.concatenate([query_bias, value_bias, inner_bias])[None, :]
    x_rows = [block_input[s] for s in range(seqs)]

    def send_near(own):
        return [swap(own, "ctx", 2), swap(own, "ctx", 1)] if spots == 4 else over_spots(own)

    def send_last(own, far):
        return [
            lax.ppermute(own, "ctx", [(1, 2), (2, 1)]),
            lax.ppermute(far, "ctx", [(2, 3), (1, 0)]),
        ]

    def finish(nears, lasts):
        if spots != 4:
            return nears
        in_middle = jnp.logical_or(spot == 1, spot == 2)
        return [nears[1], nears[0], jnp.where(in_middle, lasts[0], lasts[1])]

    came, across, *near = together(other_core(block_input), other_side(block_input), *over_spots(attention_shard))
    first_out = after(x_rows[0], *near)
    (attention_near,) = stack([attention_shard, *near])
    diagonal = [(d * 4 + t, (1 - d) * 4 + (t ^ 2)) for d in range(2) for t in range(4)]
    over_both = [lax.ppermute(attention_near, ("dp", "tp"), diagonal)] if lines == 2 else []
    attention_other, attention_line, *nears = together(
        other_side(attention_near), swap(attention_near, "dp", 1), *over_both, *send_near(first_out)
    )
    if lines == 2:
        other_line, *nears = nears
    cores = [other_core(n) for n in nears]
    lasts = send_last(after(x_rows[0], *nears), nears[0]) if spots == 4 else []
    biases_came = other_side(after(biases, *nears))
    biases_came, *rest = together(biases_came, *lasts, *cores)
    lasts, cores = rest[: len(lasts)], rest[len(lasts) :]
    arrived = [finish(nears, lasts)]
    if spots == 4:
        cores = [cores[1], cores[0], other_core(arrived[0][2])]
    if lines == 2:
        attention_all = [[attention_near, attention_other], [attention_line, other_line]]
    else:
        attention_all = over_dp([attention_near, attention_other])
    query_full, kv_full = place(attention_all, [heads_width] * 3, [(0,), (1, 2)])

    query_b = ordered(biases[:, :heads_width], biases_came[:, :heads_width], is_upper_side, 1)
    cut = slice(heads_width, own_width)
    value_b = ordered(biases[:, cut], biases_came[:, cut], is_upper_side, 1)
    cut = slice(own_width, None)
    inner_b = ordered(biases[:, cut], biases_came[:, cut], is_upper_side, 1)
    kv_bias = interleaved(jnp.zeros_like(value_b), value_b)

    pieces = [[(x_rows[0], came[0])] + list(zip(arrived[0], cores))]
    across_core = other_core(across[0])
    feed_shard = after(feed_shard, arrived[0][-1])
    feed_near = over_spots(feed_shard)
    second_nears = send_near(after(x_rows[1], arrived[0][-1]))
    weights = (query_full, kv_full, query_b, kv_bias)
    q, made, own, packed, lse = attend(counts[0], seqs, 0, pieces[0] + [(across[0], across_core)], weights, ())
    queries, kv = [q], [made]
    packs = [packed]

    own, *rest = together(own, *feed_near, *second_nears)
    feed_near, nears = rest[: len(feed_near)], rest[len(feed_near) :]
    across_core = other_core(across[1])
    cores = [other_core(n) for n in nears]
    lasts = send_last(after(x_rows[1], own), nears[0]) if spots == 4 else []
    near_a, near_b = stack([after(feed_shard, *cores)] + feed_near, feed_shard.shape[1] - unit_width - -unit_width % 128)
    other_a, line_b, *rest = together(other_side(near_a), swap(near_b, "dp", 1), *lasts, *cores)
    packs[0] = other_side(after(packs[0], other_a))
    lasts, cores = rest[: len(lasts)], rest[len(lasts) :]
    arrived.append(finish(nears, lasts))
    if spots == 4:
        cores = [cores[1], cores[0], other_core(arrived[1][2])]
    pieces.append([(x_rows[1], came[1])] + list(zip(arrived[1], cores)))
    if lines == 2:
        last_b = [near_b, line_b]
        sent_a = [swap(after(a, line_b), "dp", 1) for a in (near_a, other_a)]
        sent_b = [other_side(after(b, other_a)) for b in last_b]
    q, made, own, packed, lse = attend(counts[1], seqs, 1, pieces[1] + [(across[1], across_core)], weights, (own, lse))
    queries.append(q)
    kv.append(made)
    buffers = (own, lse)
    packs.append(other_side(packed))
    if lines == 2:
        sent = together(*sent_a, *sent_b, own)
        sent_a, sent_b = list(sent[:2]), list(sent[2:4])
        all_a = [[near_a, other_a], sent_a]
        all_b = [[near_b, sent_b[0]], [line_b, sent_b[1]]]
    else:
        all_a, all_b = over_dp([near_a, other_a]), over_dp([near_b, other_side(near_b)])
    output_full, inner_full = place(all_a, [heads_width, unit_width], [(0,), (1,)])
    (outer_full,) = place(all_b, [unit_width], [(0,)])

    vectors = jnp.stack([output_bias, first_gain, first_shift, closing_offset_vector, second_gain, second_shift])
    vectors = jnp.concatenate([vectors, jnp.zeros((2, width), F32)])
    block = local // 2

    attended, attended_low, mine, other, lse_all = merge(where, *buffers, packs, output_full)
    normal, spread, first_low = row_call(
        first_kernel,
        "first_norm",
        block,
        count,
        width,
        [flat(block_input), flat(mine), flat(other_core(other))],
        [vectors],
        [(width, F32), (1, F32), (width, BF)],
        False,
    )
    first_came = other_core(first_low)
    active, slope, mine, other = feed(first_low, first_came, inner_full, inner_b, outer_full)
    output, second_grad, outer_low, second_sums = row_call(
        functools.partial(second_kernel, local // block),
        "second_norm",
        block,
        count,
        width,
        [normal, mine, other_core(other), flat(cotangent)],
        [vectors],
        [(width, F32), (width, F32), (width, BF)],
        True,
        row_counts,
    )
    mine, other, d_inner_bias, *d_feed = feed_back(
        where, outer_low, other_core(outer_low), first_low, first_came, active, slope, inner_full, outer_full
    )
    first_grad, attn_low, first_sums = row_call(
        first_back_kernel,
        "first_norm_back",
        block,
        count,
        width,
        [second_grad, mine, other_core(other), normal, spread],
        [vectors],
        [(width, F32), (width, BF)],
        True,
    )
    attn_low = attn_low.reshape(seqs, local, width)
    turned = turn(
        where, attn_low, other_core(attn_low), output_full, attended, attended_low, lse_all
    )
    g_own, d_output = turned[:seqs], turned[seqs:]
    g_oth = [other_side(g) for g in g_own]

    lines = lax.axis_size("dp")

    def over_lines(made, done=()):
        if lines == 2:
            return made[0], swap(made[1], "dp", 1, (), done)
        value, place_at = made[0].astype(F32), lax.axis_index("dp")
        for bit in reversed(bits_of("dp")):
            mine, sent = halves(value, (place_at & bit) != 0, 0)
            term = swap(sent.astype(BF), "dp", bit, (), done)
            value = mine + term.astype(F32)
        return mine, term

    def sides_of(pair, width_of_side):
        return [(pair, 0, width_of_side)], [(pair, width_of_side, width_of_side)]

    def back(s, g_in, before):
        return attend_back(
            counts[s], queries[s], g_own[s], g_in, kv[s], kv_full, pieces[s], before, s == seqs - 1
        )

    def by_spot(mine, came):
        total = (mine + came.astype(F32)).reshape(spots, local, width)
        return total[0], [total[k].astype(BF) for k in range(1, spots)]

    shared = jnp.concatenate([second_sums[:3], first_sums[:3]])
    shared_came = other_core(shared)
    output_mine, output_came = over_lines(d_output)
    g_in, output_came, shared_came = together(g_oth[0], output_came, shared_came)
    output_pair, shared = (output_mine, output_came), shared + shared_came
    own, oth, mine, other, kv_bias_sum, *kv_grads = back(0, g_in, None)
    dq_own = [own]
    dq_came_0 = other_side(oth)
    kept_0, sent_0 = by_spot(mine, other_core(other))
    feed_pairs = [over_lines(d_feed, (kv_bias_sum,))]
    feed_kept, feed_sent = fold_sides(
        feed_pairs,
        [
            sides_of(0, unit_width),
            ([(0, 2 * unit_width, unit_width)], [(0, 3 * unit_width, unit_width)]),
        ],
    )
    feed_term = other_side(feed_sent)
    came_0 = [swap(t, "ctx", k + 1) for k, t in enumerate(sent_0)]
    g_in, dq_came_0, *_ = together(g_oth[1], dq_came_0, feed_sent, *sent_0)
    own, oth, mine, other, kv_bias_sum, *kv_grads = back(1, g_in, (kv_grads[0], kv_bias_sum))
    dq_own.append(own)

    oth, other, feed_term, *rest = together(oth, other, feed_term, *came_0, *kv_grads)
    came_0, kv_grads = rest[: spots - 1], rest[spots - 1 :]
    dq_came_1 = other_side(oth)
    kept_1, sent_1 = by_spot(mine, other_core(other))
    feed_all_rows = add_low(feed_kept, feed_term)
    feed_spread = lax.all_to_all(feed_all_rows, "ctx", split_axis=0, concat_axis=0, tiled=True)
    dq_came = [dq_came_0, after(dq_came_1, feed_all_rows, *sent_1)]
    kv_pair = over_lines(kv_grads)
    mine, other, query_bias_sum, *query_grads = query_back(
        where, dq_own, dq_came, x_rows, [came[s] for s in range(seqs)], query_full
    )
    query_term = (mine + other_core(other).astype(F32)).reshape(seqs, local, width)
    query_pair = over_lines(query_grads)
    value_bias_sum = apart(kv_bias_sum)[1]
    vector = jnp.concatenate(
        [shared.reshape(1, -1), d_inner_bias, query_bias_sum.reshape(1, -1), value_bias_sum], axis=1
    )
    for bit in bits_of("dp"):
        vector = vector + swap(vector, "dp", bit)
    if lines == 2:
        query_last, kv_last, vector = together(query_pair[1], kv_pair[1], vector)
        query_pair, kv_pair = (query_pair[0], query_last), (kv_pair[0], kv_last)
    came_1 = [swap(t, "ctx", k + 1) for k, t in enumerate(sent_1)]

    def side_cuts(pair, offset):
        cuts = []
        for start in (0, heads_width):
            pieces_of, at = [], start
            while at < start + heads_width:
                w = min(PAIR - at % PAIR, start + heads_width - at)
                pieces_of.append((pair, 2 * (at - at % PAIR) + offset + at % PAIR, w))
                at += w
            cuts.append(pieces_of)
        return tuple(cuts)

    kept, sent = fold_sides(
        [query_pair, kv_pair, output_pair],
        [sides_of(0, heads_width), side_cuts(1, 0), side_cuts(1, PAIR), sides_of(2, heads_width)],
    )
    term, feed_spread, *came_1 = together(other_side(sent), feed_spread, *came_1)
    rows = fold_spots(kept, term)
    for bit in bits_of("ctx"):
        vector = vector + swap(vector, "ctx", bit)
    terms = [swap(t, "ctx", k + 1) for k, t in enumerate(rows[1:])]
    vector = (vector + other_side(vector))[0]
    feed_owned = jnp.sum(feed_spread.reshape(spots, -1, feed_spread.shape[1]).astype(F32), axis=0)
    owned = rows[0] + sum(t.astype(F32) for t in terms)
    first_grad = first_grad.reshape(seqs, local, width)
    input_grad = jnp.stack(
        [
            first_grad[s] + query_term[s] + kept + sum(t.astype(F32) for t in came)
            for s, (kept, came) in enumerate(((kept_0, came_0), (kept_1, came_1)))
        ]
    )

    shared = vector[: 6 * width].reshape(6, width)

    def own_side(start, size):
        return jnp.where(is_upper_side, vector[start + size : start + 2 * size], vector[start : start + size])

    base = 6 * width
    after_inner = base + 2 * unit_width
    return (
        output.reshape(seqs, local, width),
        input_grad,
        owned[:, :heads_width],
        own_side(after_inner, heads_width),
        owned[:, heads_width:own_width],
        owned[:, own_width : own_width + heads_width],
        own_side(after_inner + own_width, heads_width),
        owned[:, 3 * heads_width : 4 * heads_width].T,
        shared[5],
        shared[3],
        shared[4],
        feed_owned[:, :unit_width],
        own_side(base, unit_width),
        feed_owned[:, unit_width : 2 * unit_width].T,
        shared[2],
        shared[0],
        shared[1],
    )


def solution(mesh):
    rows = P("dp", ("ctx", "tp"), None)
    into = P(("dp", "ctx"), "tp")
    out_of = P("tp", ("dp", "ctx"))
    split, whole = P("tp"), P()
    return jax.shard_map(
        on_device,
        mesh=mesh,
        in_specs=(
            rows, P("dp"), rows, into, split, into, into, split, out_of, whole, whole, whole,
            into, split, out_of, whole, whole, whole,
        ),
        out_specs=(
            rows, rows, into, split, into, into, split, out_of, whole, whole, whole,
            into, split, out_of, whole, whole, whole,
        ),
        check_vma=False,
    )
```

```python
import functools
import math

import jax
import jax.numpy as jnp
from jax import lax
from jax.experimental import pallas as pl
from jax.experimental.pallas import tpu as pltpu
from jax.sharding import PartitionSpec as P

HD = 64
PAIR = 2 * HD
EPSILON = 1e-12
NEGATIVE = -1e30
LARGEST = 1e30
BF = jnp.bfloat16
F32 = jnp.float32
VMEM_LIMIT = 56 << 20
FEED_ROWS = 256

NN = (((1,), (0,)), ((), ()))
NT = (((1,), (1,)), ((), ()))
TN = (((0,), (0,)), ((), ()))


def dot(a, b, dims):
    return lax.dot_general(a, b, dims, preferred_element_type=F32)


def params():
    return pltpu.CompilerParams(vmem_limit_bytes=VMEM_LIMIT)


def cost(flops, moved, transcendentals=0):
    return pl.CostEstimate(flops=int(flops), bytes_accessed=int(moved), transcendentals=int(transcendentals))


def after(value, *others):
    if not others:
        return value
    return lax.optimization_barrier((value, *others))[0]


def swap(value, axis, bit, start=(), done=()):
    count = lax.axis_size(axis)
    return after(lax.ppermute(after(value, *start), axis, [(i, i ^ bit) for i in range(count)]), *done)


def bits_of(axis):
    count = lax.axis_size(axis)
    return [1 << k for k in range(count.bit_length() - 1)]


def halves(value, upper, dim):
    size = value.shape[dim] // 2
    at = upper.astype(jnp.int32) * size
    mine = lax.dynamic_slice_in_dim(value, at, size, dim)
    return mine, lax.dynamic_slice_in_dim(value, size - at, size, dim)


def ordered(mine, other, upper, dim):
    return jnp.concatenate([jnp.where(upper, other, mine), jnp.where(upper, mine, other)], axis=dim)


def call(kernel, name, outs, *arrays, prefetch=None, scratch=(), flops=0):
    spec = lambda shape: pl.BlockSpec(shape, lambda i, *c: (0,) * len(shape))
    arrays_moved = sum(a.size * a.dtype.itemsize for a in arrays) + sum(4 * math.prod(shape) for shape, _ in outs)
    return pl.pallas_call(
        kernel,
        grid_spec=pltpu.PrefetchScalarGridSpec(
            num_scalar_prefetch=0 if prefetch is None else 1,
            grid=(1,),
            in_specs=[spec(a.shape) for a in arrays],
            out_specs=[spec(shape) for shape, _ in outs],
            scratch_shapes=list(scratch),
        ),
        out_shape=[jax.ShapeDtypeStruct(shape, kind) for shape, kind in outs],
        compiler_params=params(),
        cost_estimate=cost(flops, arrays_moved),
        name=name,
    )(*(() if prefetch is None else (prefetch,)), *arrays)


def fits(rows):
    return rows % 16 == 0


def pack(groups):
    flat = [piece for group in groups for piece in group]
    widths = [sum(w.shape[0] if t else w.shape[1] for w, t in group) for group in groups]
    first, turned = flat[0]
    rows = first.shape[1] if turned else first.shape[0]

    def joined(values):
        values, out = list(values), []
        for group, width in zip(groups, widths):
            out += [values.pop(0) for _ in group]
            if -width % 128:
                out.append(jnp.zeros((rows, -width % 128), F32))
        return jnp.concatenate(out, axis=1).astype(BF)

    if not fits(rows):
        return joined(w.T if t else w for w, t in flat)

    def kernel(*refs):
        refs[-1][...] = joined(r[...].T if t else r[...] for r, (_, t) in zip(refs, flat))

    total = sum(w + -w % 128 for w in widths)
    return call(kernel, "pack", [((rows, total), BF)], *[w for w, _ in flat])[0]


def stack(parts, cuts=None):
    rows, width = parts[0].shape
    ranges = [(0, width)] if cuts is None else [(0, cuts), (cuts, width)]
    if not fits(rows):
        whole = jnp.concatenate(parts, axis=0)
        return [whole[:, start:stop] for start, stop in ranges]

    def kernel(*refs):
        for k, ref in enumerate(refs[: len(parts)]):
            for out, (start, stop) in zip(refs[len(parts) :], ranges):
                out[k * rows : k * rows + rows, :] = ref[:, start:stop]

    return call(kernel, "stack", [((rows * len(parts), stop - start), BF) for start, stop in ranges], *parts)


def over_dp(arrays, done=()):
    found = [arrays]
    for bit in bits_of("dp"):
        found = found + [[swap(a, "dp", bit, (), done) for a in one] for one in found]
    return found


def place(found, widths, joined):
    spots, spot = lax.axis_size("ctx"), lax.axis_index("ctx")
    line, side = lax.axis_index("dp"), lax.axis_index("tp") // 2
    lines = len(found)
    starts = [sum(widths[:k]) for k in range(len(widths))]
    block = found[0][0].shape[0]
    rows = block // spots
    cuts = list(zip(starts, widths))
    shapes = [(block * lines, 2 * sum(widths[m] for m in members)) for members in joined]
    if not fits(rows):
        order = ((jnp.arange(lines)[:, None] ^ line) * spots + (jnp.arange(spots)[None, :] ^ spot)).reshape(-1)
        own, oth = (
            jnp.stack([f[h] for f in found]).reshape(lines * spots, rows, -1)[order].reshape(lines * block, -1)
            for h in range(2)
        )
        low, high = jnp.where(side == 1, oth, own), jnp.where(side == 1, own, oth)
        full = [jnp.concatenate([low[:, t : t + w], high[:, t : t + w]], axis=1) for t, w in cuts]
        return [full[m[0]] if len(m) == 1 else interleaved(full[m[0]], full[m[1]]) for m in joined]

    def kernel(where, *refs):
        outs = refs[2 * lines :]
        upper = where[2] == 1
        for k in range(lines):
            own_ref, oth_ref = refs[2 * k], refs[2 * k + 1]
            for c in range(spots):
                came = pl.ds(pl.multiple_of((where[0] ^ c) * rows, rows), rows)
                to = pl.ds(pl.multiple_of(((where[1] ^ k) * spots + c) * rows, rows), rows)
                own, oth = own_ref[came, :], oth_ref[came, :]
                low, high = jnp.where(upper, oth, own), jnp.where(upper, own, oth)
                full = [jnp.concatenate([low[:, t : t + w], high[:, t : t + w]], axis=1) for t, w in cuts]
                for out, members in zip(outs, joined):
                    if len(members) == 1:
                        out[to, :] = full[members[0]]
                    else:
                        both = []
                        for p in range(0, full[members[0]].shape[1], PAIR):
                            both += [full[m][:, p : p + PAIR] for m in members]
                        out[to, :] = jnp.concatenate(both, axis=1)

    where = jnp.stack([spot, line, side]).astype(jnp.int32)
    flat = [a for one in found for a in one]
    return call(kernel, "place", [(shape, BF) for shape in shapes], *flat, prefetch=where)


def fold_sides(pairs, cuts):
    rows = pairs[0][0].shape[0]
    width = sum(w for low, _ in cuts for _, _, w in low)
    spare = -width % 128
    width += spare
    side = lax.axis_index("tp") // 2

    def both(totals):
        end = [jnp.zeros((totals[0].shape[0], spare), F32)] if spare else []
        low = jnp.concatenate([totals[p][:, t : t + w] for cut, _ in cuts for p, t, w in cut] + end, axis=1)
        high = jnp.concatenate([totals[p][:, t : t + w] for _, cut in cuts for p, t, w in cut] + end, axis=1)
        return low, high

    if not fits(rows):
        low, high = both([a.astype(F32) + b.astype(F32) for a, b in pairs])
        return jnp.where(side == 1, high, low), jnp.where(side == 1, low, high).astype(BF)

    block = rows // 4 if fits(rows // 4) else rows
    steps = rows // block

    def kernel(where, *refs):
        kept, sent = refs[2 * len(pairs) :]
        totals = [refs[2 * k][...].astype(F32) + refs[2 * k + 1][...].astype(F32) for k in range(len(pairs))]
        low, high = both(totals)
        upper = where[0] == 1
        kept[...] = jnp.where(upper, high, low)
        sent[...] = jnp.where(upper, low, high).astype(BF)

    spec = lambda w: pl.BlockSpec((block, w), lambda i, c: (i, 0))
    flat = [a for pair in pairs for a in pair]
    return pl.pallas_call(
        kernel,
        grid_spec=pltpu.PrefetchScalarGridSpec(
            num_scalar_prefetch=1,
            grid=(steps,),
            in_specs=[spec(a.shape[1]) for a in flat],
            out_specs=[spec(width), spec(width)],
        ),
        out_shape=[jax.ShapeDtypeStruct((rows, width), F32), jax.ShapeDtypeStruct((rows, width), BF)],
        compiler_params=params(),
        cost_estimate=cost(0, sum(a.size * a.dtype.itemsize for a in flat) + 6 * rows * width),
        name="fold_sides",
    )(side.astype(jnp.int32).reshape(1), *flat)


def fold_spots(kept, came, vector):
    spots, spot = lax.axis_size("ctx"), lax.axis_index("ctx")
    rows, width = kept.shape[0] // spots, kept.shape[1]
    count = vector.shape[0]
    below_rows = 3 * count + -3 * count % 16
    if not fits(rows):
        total = kept + came.astype(F32)
        cut = lambda k: lax.dynamic_slice_in_dim(total, (spot ^ k) * rows, rows, 0)
        terms = jnp.concatenate([*in_three(vector), jnp.zeros((below_rows - 3 * count, width), BF)], axis=0)
        return [cut(0)] + [jnp.concatenate([cut(k).astype(BF), terms], axis=0) for k in range(1, spots)]

    def kernel(where, kept_ref, came_ref, vector_ref, own, *outs):
        at = pl.ds(pl.multiple_of(where[0] * rows, rows), rows)
        own[...] = kept_ref[at, :] + came_ref[at, :].astype(F32)
        terms = jnp.concatenate(in_three(vector_ref[...]), axis=0)
        terms = jnp.concatenate([terms, jnp.zeros((below_rows - 3 * count, width), BF)], axis=0)
        for k, out in enumerate(outs):
            at = pl.ds(pl.multiple_of((where[0] ^ (k + 1)) * rows, rows), rows)
            out[:rows, :] = (kept_ref[at, :] + came_ref[at, :].astype(F32)).astype(BF)
            out[rows:, :] = terms

    outs = [((rows, width), F32)] + [((rows + below_rows, width), BF)] * (spots - 1)
    return call(kernel, "fold_spots", outs, kept, came, vector, prefetch=spot.astype(jnp.int32).reshape(1))


def add_low(kept, came):
    if not fits(kept.shape[0] // 4):
        return (kept + came.astype(F32)).astype(BF)

    def kernel(kept_ref, came_ref, out):
        out[...] = (kept_ref[...] + came_ref[...].astype(F32)).astype(BF)

    rows, width = kept.shape
    spec = pl.BlockSpec((rows // 4, width), lambda i: (i, 0))
    return pl.pallas_call(
        kernel,
        grid=(4,),
        in_specs=[spec, spec],
        out_specs=spec,
        out_shape=jax.ShapeDtypeStruct(kept.shape, BF),
        compiler_params=params(),
        cost_estimate=cost(kept.size, 8 * kept.size),
        name="add_low",
    )(kept, came)


def own_rows(where, value, rows):
    mine = pl.ds(pl.multiple_of(where * rows, rows), rows)
    other = pl.ds(pl.multiple_of((1 - where) * rows, rows), rows)
    return value[mine, :], value[other, :]


def assemble(upper, pieces, held):
    local = pieces[0].shape[0]
    for k in range(len(pieces) // 2):
        mine, came = pieces[2 * k][...], pieces[2 * k + 1][...]
        held[2 * k * local : (2 * k + 1) * local, :] = jnp.where(upper, came, mine)
        held[(2 * k + 1) * local : (2 * k + 2) * local, :] = jnp.where(upper, mine, came)


def query_back_kernel(seqs, lines, where, *refs):
    dq_own, dq_came, own, came = (refs[k * seqs : k * seqs + seqs] for k in range(4))
    weight, mine_ref, other_ref, bias_ref = refs[4 * seqs : 4 * seqs + 4]
    weight_refs, total = refs[4 * seqs + 4 : -1], refs[-1]
    upper = where[0] == 1
    half = own[0].shape[0]
    bias = None
    for s in range(seqs):
        low = (dq_own[s][...] + dq_came[s][...].astype(F32)).astype(BF)
        rows = jnp.concatenate(
            [jnp.where(upper, came[s][...], own[s][...]), jnp.where(upper, own[s][...], came[s][...])], axis=0
        )
        part = dot(low, weight[...], (((0,), (1,)), ((), ())))
        to = slice(s * half, s * half + half)
        mine_ref[to, :] = jnp.where(upper, part[half:], part[:half])
        other_ref[to, :] = jnp.where(upper, part[:half], part[half:]).astype(BF)
        grad = dot(rows, low, (((0,), (1,)), ((), ())))
        total[...] = grad if s == 0 else total[...] + grad
        sums = jnp.sum(low.astype(F32), axis=1, keepdims=True)
        bias = sums if bias is None else bias + sums
    bias_ref[...] = bias
    if lines == 2:
        kept, sent = own_rows(where[1], total, total.shape[0] // 2)
        weight_refs[0][...] = kept
        weight_refs[1][...] = sent.astype(BF)
    else:
        weight_refs[0][...] = total[...]


def query_back(where, dq_own, dq_came, own, came, weight):
    seqs, lines = len(dq_own), lax.axis_size("dp")
    local, width = own[0].shape
    own_width = weight.shape[1]
    outs = [((seqs * local, width), F32), ((seqs * local, width), BF), ((own_width, 1), F32)]
    if lines == 2:
        outs += [((width // 2, own_width), F32), ((width // 2, own_width), BF)]
    else:
        outs += [((width, own_width), F32)]
    return call(
        functools.partial(query_back_kernel, seqs, lines),
        "query_back",
        outs,
        *dq_own,
        *dq_came,
        *own,
        *came,
        weight,
        prefetch=where,
        scratch=[pltpu.VMEM((width, own_width), F32)],
        flops=8 * seqs * local * width * own_width,
    )


def half_lanes(value):
    lane = lax.broadcasted_iota(jnp.int32, value.shape, 1)
    zero = jnp.zeros_like(value)
    return [jnp.where(lane < HD, value, zero), jnp.where(lane >= HD, value, zero)]


def half_rows(value):
    row = lax.broadcasted_iota(jnp.int32, value.shape, 0)
    zero = jnp.zeros_like(value)
    return [jnp.where(row < HD, value, zero), jnp.where(row >= HD, value, zero)]


def top_bits(value):
    spread = value * 65537.0
    return spread - (spread - value)


def in_three(value):
    first = top_bits(value)
    rest = value - first
    second = top_bits(rest)
    return first.astype(BF), second.astype(BF), (rest - second).astype(BF)


def packed_rows(values):
    terms = jnp.concatenate(in_three(values), axis=0)
    return jnp.concatenate([terms, jnp.zeros((16 - terms.shape[0], terms.shape[1]), BF)], axis=0)


def unpacked_rows(packed, count):
    packed = packed.astype(F32)
    return packed[:count] + packed[count : 2 * count] + packed[2 * count : 3 * count]


def below(shape, count):
    return lax.broadcasted_iota(jnp.int32, shape, 0) < count


def attend_kernel(slots, probe, old, counts, *refs):
    pieces = refs[: 2 * slots + 2]
    w_query, w_kv, b_query, b_kv = refs[2 * slots + 2 : 2 * slots + 6]
    queries, kv, o_own, packed, lse_ref, held, top, total, acc, heads = refs[2 * slots + 6 + old :]
    local = pieces[0].shape[0]
    rows = keys = 2 * local

    @pl.when(pl.program_id(0) == 0)
    def _():
        assemble(counts[slots + 1] == 1, pieces, held)

    scale = jnp.asarray(1.0 / math.sqrt(HD), BF)
    for start, to in ((0, 0), (slots * keys, rows)):
        query = (dot(held[start : start + rows, :], w_query[...], NN) + b_query[...]).astype(BF)
        queries[to : to + rows, :] = query * scale
    for h, query in enumerate(half_lanes(queries[...])):
        heads[h] = query

    @pl.loop(0, slots)
    def _(k):
        at = pl.ds(pl.multiple_of(k * keys, keys), keys)

        @pl.when(counts[k] > 0)
        def _():
            kv[at, :] = (dot(held[at, :], w_kv[...], NN) + b_kv[...]).astype(BF)

        @pl.when(counts[k] <= 0)
        def _():
            kv[at, :] = jnp.zeros((keys, 2 * PAIR), BF)

    def block(k):
        at = pl.ds(pl.multiple_of(k * keys, keys), keys)
        return kv[at, :PAIR], kv[at, PAIR:]

    first = pl.ds(pl.multiple_of(counts[slots] * keys, keys), probe)
    for h in range(2):
        top[h] = jnp.max(dot(kv[first, :PAIR], heads[h], NT), axis=0, keepdims=True)
    total[...] = jnp.zeros_like(total)
    acc[...] = jnp.zeros_like(acc)

    def quick(k, h, valid):
        key, value = block(k)
        expo = jnp.exp(dot(key, heads[h], NT) - top[h])
        if valid is not None:
            expo = jnp.where(below(expo.shape, valid), expo, 0.0)
        total[h] += jnp.sum(expo, axis=0, keepdims=True)
        acc[h] += dot(value, expo.astype(BF), TN)

    @pl.loop(0, slots)
    def _(k):
        valid = counts[k]

        @pl.when(valid >= keys)
        def _():
            quick(k, 0, None)
            quick(k, 1, None)

        @pl.when(jnp.logical_and(valid > 0, valid < keys))
        def _():
            pl.loop(0, 2)(lambda h: quick(k, h, valid))

    @pl.when(jnp.logical_not(jnp.max(total[...]) < LARGEST))
    def _():
        total[...] = jnp.zeros_like(total)
        acc[...] = jnp.zeros_like(acc)

        def careful(k, h, valid):
            key, value = block(k)
            scores = dot(key, heads[h], NT)
            scores = jnp.where(below(scores.shape, valid), scores, NEGATIVE)
            before = top[h]
            new = jnp.maximum(before, jnp.max(scores, axis=0, keepdims=True))
            expo = jnp.where(below(scores.shape, valid), jnp.exp(scores - new), 0.0)
            ratio = jnp.exp(before - new)
            total[h] = total[h] * ratio + jnp.sum(expo, axis=0, keepdims=True)
            acc[h] = acc[h] * ratio + dot(value, expo.astype(BF), TN)
            top[h] = new

        @pl.loop(0, slots)
        def _(k):
            valid = counts[k]

            @pl.when(valid > 0)
            def _():
                pl.loop(0, 2)(lambda h: careful(k, h, valid))

    lse = []
    for h in range(2):
        at = slice(h * HD, h * HD + HD)
        part = acc[h, at, :] / total[h]
        o_own[0, at, :] = part[:, :rows]
        packed[at, :] = part[:, rows:].astype(BF)
        lse.append(top[h] + jnp.log(total[h]))
        lse_ref[0, 0, h : h + 1, :] = lse[h][:, :rows]
    packed[PAIR:, :] = packed_rows(jnp.concatenate([l[:, rows:] for l in lse], axis=0))


def attend(counts, seqs, s, pieces, weights, before):
    w_query, w_kv, b_query, b_kv = weights
    slots = len(pieces) - 1
    local, model = pieces[0][0].shape
    rows, width = 2 * local, w_query.shape[1]
    pairs = width // PAIR
    keys = 2 * local
    total = width * 2 * rows * slots * keys
    anywhere = pl.BlockSpec(memory_space=pl.ANY)
    across = lambda p, c: (0, p)
    flat = [p for pair in pieces for p in pair]
    held = ((slots + 1) * keys, model)
    return pl.pallas_call(
        functools.partial(attend_kernel, slots, min(128, keys), len(before)),
        grid_spec=pltpu.PrefetchScalarGridSpec(
            num_scalar_prefetch=1,
            grid=(pairs,),
            in_specs=[pl.BlockSpec((local, model), lambda p, c: (0, 0), pipeline_mode=pl.Buffered(1)) for _ in flat]
            + [
                pl.BlockSpec((model, PAIR), across),
                pl.BlockSpec((model, 2 * PAIR), across),
                pl.BlockSpec((1, PAIR), across),
                pl.BlockSpec((1, 2 * PAIR), across),
            ]
            + [anywhere] * len(before),
            out_specs=[
                pl.BlockSpec((2 * rows, PAIR), across),
                pl.BlockSpec((slots * keys, 2 * PAIR), across),
                pl.BlockSpec((1, PAIR, rows), lambda p, c: (s, p, 0)),
                pl.BlockSpec((PAIR + 16, rows), lambda p, c: (p, 0)),
                pl.BlockSpec((1, 1, 2, rows), lambda p, c: (s, p, 0, 0)),
            ],
            scratch_shapes=[
                pltpu.VMEM(held, BF),
                pltpu.VMEM((2, 1, 2 * rows), F32),
                pltpu.VMEM((2, 1, 2 * rows), F32),
                pltpu.VMEM((2, PAIR, 2 * rows), F32),
                pltpu.VMEM((2, 2 * rows, PAIR), BF),
            ],
        ),
        out_shape=[
            jax.ShapeDtypeStruct((2 * rows, width), BF),
            jax.ShapeDtypeStruct((slots * keys, 2 * width), BF),
            jax.ShapeDtypeStruct((seqs, width, rows), F32),
            jax.ShapeDtypeStruct((pairs * (PAIR + 16), rows), BF),
            jax.ShapeDtypeStruct((seqs, pairs, 2, rows), F32),
        ],
        input_output_aliases={2 * slots + 7: 2, 2 * slots + 8: 4} if before else {},
        compiler_params=params(),
        cost_estimate=cost(16 * total, 2 * len(flat) * local * model + 8 * slots * keys * width, total // HD),
        name="attend",
    )(counts, *flat, *weights, *before)


def attend_back_kernel(slots, steps, split, first, counts, both, g_own, g_oth, kv, w_kv, *refs):
    pieces = refs[: 2 * slots]
    refs = refs[2 * slots :]
    if not first:
        before, bias_before = refs[:2]
        refs = refs[2:]
    dq_own, dq_oth, mine_ref, other_ref, bias_ref = refs[:5]
    weight_refs = refs[5:-8]
    acc, queries, grads, summed, facts, turned, part, d_weight = refs[-8:]
    rows = both.shape[0] // 2
    local = pieces[0].shape[0]
    keys = 2 * local
    step = pl.program_id(0)
    upper = counts[slots + 1] == 1

    @pl.when(step == 0)
    def _():
        part[...] = jnp.zeros_like(part)
        for k in range(slots):
            mine, came = pieces[2 * k][...], pieces[2 * k + 1][...]
            turned[:, 2 * k * local : (2 * k + 1) * local] = jnp.where(upper, came, mine).T
            turned[:, (2 * k + 1) * local : (2 * k + 2) * local] = jnp.where(upper, mine, came).T

    acc[...] = jnp.zeros_like(acc)
    d_weight[...] = jnp.zeros_like(d_weight) if first else before[...]
    bias_ref[...] = jnp.zeros_like(bias_ref) if first else bias_before[...]
    for block, g_ref in enumerate((g_own, g_oth)):
        stats = unpacked_rows(g_ref[PAIR:, :], 4)
        for h, (query, grad) in enumerate(
            zip(half_lanes(both[block * rows : block * rows + rows, :]), half_rows(g_ref[:PAIR, :]))
        ):
            queries[2 * block + h] = query
            grads[2 * block + h] = grad
            facts[2 * block + h, 0:1, :] = stats[h : h + 1]
            facts[2 * block + h, 1:2, :] = stats[2 + h : 3 + h]

    @pl.loop(0, slots)
    def _(k):
        valid = counts[k]
        rows_at = pl.ds(pl.multiple_of(k * keys, keys), keys)

        def one(at, valid):
            key, value = kv[rows_at, :PAIR], kv[rows_at, PAIR:]
            query, grad = queries[at], grads[at]
            prob = jnp.exp(dot(key, query, NT) - facts[at, 0:1, :])
            if valid is not None:
                prob = jnp.where(below(prob.shape, valid), prob, 0.0)
            change = dot(value, grad, NN) - facts[at, 1:2, :]
            score = (prob * change).astype(BF)
            summed[:, PAIR:] += dot(prob.astype(BF), grad, NT)
            summed[:, :PAIR] += dot(score, query, NN)
            acc[at] += dot(key, score, TN)

        summed[...] = jnp.zeros_like(summed)

        @pl.when(valid >= keys)
        def _():
            for at in range(4):
                one(at, None)

        @pl.when(jnp.logical_and(valid > 0, valid < keys))
        def _():
            pl.loop(0, 4)(lambda at: one(at, valid))

        @pl.when(valid > 0)
        def _():
            low = summed[...].astype(BF)
            part[rows_at, :] += dot(low, w_kv[...], NT)
            d_weight[...] += dot(turned[:, rows_at], low, NN)
            bias_ref[...] += jnp.sum(low.astype(F32), axis=0, keepdims=True)

    scale = 1.0 / math.sqrt(HD)
    for h in range(2):
        at = slice(h * HD, h * HD + HD)
        dq_own[at, :] = acc[h, at, :] * scale
        dq_oth[at, :] = (acc[2 + h, at, :] * scale).astype(BF)
    half = d_weight.shape[0] // 2
    if split:
        lower_line = counts[slots + 2] == 0
        low_half, high_half = d_weight[:half, :], d_weight[half:, :]
        weight_refs[0][...] = jnp.where(lower_line, low_half, high_half)
        weight_refs[1][...] = jnp.where(lower_line, high_half, low_half).astype(BF)
    else:
        weight_refs[0][...] = d_weight[...]

    @pl.when(step == steps - 1)
    def _():
        for k in range(slots):
            low = part[2 * k * local : (2 * k + 1) * local, :]
            high = part[(2 * k + 1) * local : (2 * k + 2) * local, :]
            to = slice(k * local, k * local + local)
            mine_ref[to, :] = jnp.where(upper, high, low)
            other_ref[to, :] = jnp.where(upper, low, high).astype(BF)


def attend_back(counts, both, g_own, g_oth, kv, w_kv, pieces, before, last):
    rows, width = both.shape[0] // 2, both.shape[1]
    pairs = width // PAIR
    slots = len(pieces)
    local, model = pieces[0][0].shape
    keys = 2 * local
    split = last and lax.axis_size("dp") == 2
    across = lambda p, c: (0, p)
    whole = lambda p, c: (0, 0)
    once = pl.Buffered(1)
    t_spec = pl.BlockSpec((PAIR, rows), lambda p, c: (p, 0))
    g_spec = pl.BlockSpec((PAIR + 16, rows), lambda p, c: (p, 0))
    flat = [p for pair in pieces for p in pair]
    extra = () if before is None else before
    if split:
        weight_outs = [((model // 2, 2 * width), F32), ((model // 2, 2 * width), BF)]
    else:
        weight_outs = [((model, 2 * width), F32)]
    total = width * 2 * rows * kv.shape[0]
    return pl.pallas_call(
        functools.partial(attend_back_kernel, slots, pairs, split, before is None),
        grid_spec=pltpu.PrefetchScalarGridSpec(
            num_scalar_prefetch=1,
            grid=(pairs,),
            in_specs=[
                pl.BlockSpec((2 * rows, PAIR), across),
                g_spec,
                g_spec,
                pl.BlockSpec((kv.shape[0], 2 * PAIR), across),
                pl.BlockSpec((model, 2 * PAIR), across),
            ]
            + [pl.BlockSpec((local, model), whole, pipeline_mode=once) for _ in flat]
            + [pl.BlockSpec((a.shape[0], 2 * PAIR), across) for a in extra],
            out_specs=[
                t_spec,
                t_spec,
                pl.BlockSpec((slots * local, model), whole, pipeline_mode=once),
                pl.BlockSpec((slots * local, model), whole, pipeline_mode=once),
                pl.BlockSpec((1, 2 * PAIR), across),
            ]
            + [pl.BlockSpec((shape[0], 2 * PAIR), across) for shape, _ in weight_outs],
            scratch_shapes=[
                pltpu.VMEM((4, PAIR, rows), F32),
                pltpu.VMEM((4, rows, PAIR), BF),
                pltpu.VMEM((4, PAIR, rows), BF),
                pltpu.VMEM((keys, 2 * PAIR), F32),
                pltpu.VMEM((4, 2, rows), F32),
                pltpu.VMEM((model, slots * keys), BF),
                pltpu.VMEM((slots * keys, model), F32),
                pltpu.VMEM((model, 2 * PAIR), F32),
            ],
        ),
        out_shape=[
            jax.ShapeDtypeStruct((width, rows), F32),
            jax.ShapeDtypeStruct((width, rows), BF),
            jax.ShapeDtypeStruct((slots * local, model), F32),
            jax.ShapeDtypeStruct((slots * local, model), BF),
            jax.ShapeDtypeStruct((1, 2 * width), F32),
        ]
        + [jax.ShapeDtypeStruct(shape, kind) for shape, kind in weight_outs],
        compiler_params=params(),
        cost_estimate=cost(40 * total, 8 * both.size + 4 * kv.size + 8 * len(flat) * local * model, total // HD),
        name="attend_back",
    )(counts, both, g_own, g_oth, kv, w_kv, *flat, *extra)


def merge_kernel(pairs, seqs, where, o_own, lse_own, *refs):
    packs = refs[:seqs]
    weight, full_ref, low_ref, mine_ref, other_ref, lse_ref, low_s, packed = refs[seqs:]
    rows = o_own.shape[2]
    for s in range(seqs):

        @pl.when(pl.program_id(0) == s)
        def _(s=s):
            packed[...] = packs[s][...]

    for p in range(pairs):
        base = p * (PAIR + 16)
        own = lse_own[0, p]
        came = unpacked_rows(packed[base + PAIR : base + PAIR + 16, :], 2)
        highest = jnp.maximum(own, came)
        share_own, share_came = jnp.exp(own - highest), jnp.exp(came - highest)
        both = share_own + share_came
        lse_ref[0, p] = highest + jnp.log(both)
        share_own, share_came = share_own / both, share_came / both
        for h in range(2):
            at = slice(p * PAIR + h * HD, p * PAIR + h * HD + HD)
            term = packed[base + h * HD : base + h * HD + HD, :].astype(F32)
            merged = o_own[0, at, :] * share_own[h : h + 1] + term * share_came[h : h + 1]
            full_ref[0, at, :] = merged
            low_s[at, :] = merged.astype(BF)
    low_ref[0] = low_s[...]
    half = rows // 2
    mine = pl.ds(pl.multiple_of(where[0] * half, half), half)
    other = pl.ds(pl.multiple_of((1 - where[0]) * half, half), half)
    dims = (((0,), (1,)), ((), ()))
    mine_ref[0] = dot(low_s[:, mine], weight[...], dims)
    other_ref[0] = dot(low_s[:, other], weight[...], dims).astype(BF)


def merge(where, o_own, lse_own, packs, weight):
    seqs, width, rows = o_own.shape
    pairs = width // PAIR
    model = weight.shape[0]
    one = lambda *shape: pl.BlockSpec((1, *shape), lambda s, w: (s,) + (0,) * len(shape))
    return pl.pallas_call(
        functools.partial(merge_kernel, pairs, seqs),
        grid_spec=pltpu.PrefetchScalarGridSpec(
            num_scalar_prefetch=1,
            grid=(seqs,),
            in_specs=[
                one(width, rows),
                one(pairs, 2, rows),
            ]
            + [pl.BlockSpec(p.shape, lambda s, w: (0, 0)) for p in packs]
            + [
                pl.BlockSpec(weight.shape, lambda s, w: (0, 0)),
            ],
            out_specs=[one(width, rows), one(width, rows), one(rows // 2, model), one(rows // 2, model), one(pairs, 2, rows)],
            scratch_shapes=[pltpu.VMEM((width, rows), BF), pltpu.VMEM(packs[0].shape, BF)],
        ),
        out_shape=[
            jax.ShapeDtypeStruct((seqs, width, rows), F32),
            jax.ShapeDtypeStruct((seqs, width, rows), BF),
            jax.ShapeDtypeStruct((seqs, rows // 2, model), F32),
            jax.ShapeDtypeStruct((seqs, rows // 2, model), BF),
            jax.ShapeDtypeStruct((seqs, pairs, 2, rows), F32),
        ],
        compiler_params=params(),
        cost_estimate=cost(2 * seqs * width * rows * model, 12 * o_own.size + 4 * seqs * rows * model),
        name="merge",
    )(where, o_own, lse_own, *packs, weight)


def turn_kernel(pairs, seqs, where, own_ref, came_ref, weight, full_ref, lse_ref, *refs):
    packs, packed = refs[:seqs], refs[-1]
    step = pl.program_id(0)
    upper = where[0] == 1
    own, came = own_ref[0], came_ref[0]
    rows = jnp.concatenate([jnp.where(upper, came, own), jnp.where(upper, own, came)], axis=0)
    grad = dot(weight[...], rows, (((0,), (1,)), ((), ()))).astype(BF)
    product = grad.astype(F32) * full_ref[0]
    for p in range(pairs):
        base = p * (PAIR + 16)
        packed[base : base + PAIR, :] = grad[p * PAIR : p * PAIR + PAIR]
        stats = [lse_ref[0, p]]
        for h in range(2):
            at = slice(p * PAIR + h * HD, p * PAIR + h * HD + HD)
            stats.append(jnp.sum(product[at], axis=0, keepdims=True))
        packed[base + PAIR : base + PAIR + 16, :] = packed_rows(jnp.concatenate(stats, axis=0))
    for s in range(seqs):

        @pl.when(step == s)
        def _(s=s):
            packs[s][...] = packed[...]


def output_kernel(seqs, lines, where, own_ref, came_ref, low_ref, *refs):
    weight_refs, d_weight = refs[:-1], refs[-1]
    step = pl.program_id(0)
    upper = where[0] == 1
    own, came = own_ref[0], came_ref[0]
    rows = jnp.concatenate([jnp.where(upper, came, own), jnp.where(upper, own, came)], axis=0)

    @pl.when(step == 0)
    def _():
        d_weight[...] = jnp.zeros_like(d_weight)

    d_weight[...] += dot(rows, low_ref[0], (((0,), (1,)), ((), ())))

    @pl.when(step == seqs - 1)
    def _():
        if lines == 2:
            kept, sent = own_rows(where[1], d_weight, d_weight.shape[0] // 2)
            weight_refs[0][...] = kept
            weight_refs[1][...] = sent.astype(BF)
        else:
            weight_refs[0][...] = d_weight[...]


def output_grad(where, own, came, low):
    seqs, width, rows = low.shape
    model = own.shape[2]
    lines = lax.axis_size("dp")
    one = lambda *shape: pl.BlockSpec((1, *shape), lambda s, w: (s,) + (0,) * len(shape))
    outs = [((model // 2, width), F32), ((model // 2, width), BF)] if lines == 2 else [((model, width), F32)]
    return pl.pallas_call(
        functools.partial(output_kernel, seqs, lines),
        grid_spec=pltpu.PrefetchScalarGridSpec(
            num_scalar_prefetch=1,
            grid=(seqs,),
            in_specs=[one(*own.shape[1:]), one(*own.shape[1:]), one(width, rows)],
            out_specs=[pl.BlockSpec(shape, lambda s, w: (0, 0)) for shape, _ in outs],
            scratch_shapes=[pltpu.VMEM((model, width), F32)],
        ),
        out_shape=[jax.ShapeDtypeStruct(shape, kind) for shape, kind in outs],
        compiler_params=params(),
        cost_estimate=cost(2 * seqs * rows * model * width, 4 * low.size + 4 * own.size),
        name="output_grad",
    )(where, own, came, low)


def turn(where, own, came, weight, full, lse):
    seqs, width, rows = full.shape
    pairs = width // PAIR
    one = lambda *shape: pl.BlockSpec((1, *shape), lambda s, w: (s,) + (0,) * len(shape))
    whole = lambda *shape: pl.BlockSpec(shape, lambda s, w: (0, 0))
    pack_shape = (pairs * (PAIR + 16), rows)
    return pl.pallas_call(
        functools.partial(turn_kernel, pairs, seqs),
        grid_spec=pltpu.PrefetchScalarGridSpec(
            num_scalar_prefetch=1,
            grid=(seqs,),
            in_specs=[
                one(*own.shape[1:]),
                one(*own.shape[1:]),
                whole(*weight.shape),
                one(width, rows),
                one(pairs, 2, rows),
            ],
            out_specs=[whole(*pack_shape)] * seqs,
            scratch_shapes=[pltpu.VMEM(pack_shape, BF)],
        ),
        out_shape=[jax.ShapeDtypeStruct(pack_shape, BF)] * seqs,
        compiler_params=params(),
        cost_estimate=cost(2 * seqs * rows * weight.size, 6 * full.size + 4 * own.size),
        name="turn",
    )(where, own, came, weight, full, lse)


def gelu_parts(u):
    density = jnp.exp(-0.5 * u * u)
    t = 1.0 / (1.0 + (0.3275911 / math.sqrt(2.0)) * jnp.abs(u))
    series = t * (
        0.254829592
        + t * (-0.284496736 + t * (1.421413741 + t * (-1.453152027 + t * 1.061405429)))
    )
    tail = 0.5 * series * density
    share = jnp.where(u < 0.0, tail, 1.0 - tail)
    return u * share, share + u * (density * (1.0 / math.sqrt(2.0 * math.pi)))


def feed_kernel(chunk, half, own_ref, came_ref, w_in, bias, w_out, active_ref, slope_ref, mine_ref, other_ref):
    step = pl.program_id(0)
    rows = jnp.where(step < half, own_ref[...], came_ref[...])
    part = None
    for start in range(0, w_in.shape[1], chunk):
        at = slice(start, start + chunk)
        inner = dot(rows, w_in[:, at], NN) + bias[:, at]
        active, slope = gelu_parts(inner)
        active = active.astype(BF)
        active_ref[:, at] = active
        slope_ref[:, at] = slope.astype(BF)
        term = dot(active, w_out[:, at], NT)
        part = term if part is None else part + term

    @pl.when(step < half)
    def _():
        mine_ref[...] = part

    @pl.when(step >= half)
    def _():
        other_ref[...] = part.astype(BF)


def row_specs(block, half, width):
    own = pl.BlockSpec((block, width), lambda i, *c: (jnp.minimum(i, half - 1), 0))
    came = pl.BlockSpec((block, width), lambda i, *c: (jnp.maximum(i - half, 0), 0))
    return own, came


def feed(own, came, w_in, bias, w_out):
    count, width = own.shape
    units = w_in.shape[1]
    block = min(FEED_ROWS, count)
    half = count // block
    whole = lambda i: (0, 0)
    by_row = lambda i: (i, 0)
    own_spec, came_spec = row_specs(block, half, width)
    return pl.pallas_call(
        functools.partial(feed_kernel, units // 3 if units % 384 == 0 else units, half),
        grid=(2 * half,),
        in_specs=[
            own_spec,
            came_spec,
            pl.BlockSpec((width, units), whole, pipeline_mode=pl.Buffered(1)),
            pl.BlockSpec((1, units), whole),
            pl.BlockSpec((width, units), whole, pipeline_mode=pl.Buffered(1)),
        ],
        out_specs=[pl.BlockSpec((block, units), by_row), pl.BlockSpec((block, units), by_row), own_spec, came_spec],
        out_shape=[
            jax.ShapeDtypeStruct((2 * count, units), BF),
            jax.ShapeDtypeStruct((2 * count, units), BF),
            jax.ShapeDtypeStruct((count, width), F32),
            jax.ShapeDtypeStruct((count, width), BF),
        ],
        compiler_params=params(),
        cost_estimate=cost(8 * count * width * units, 4 * width * units + 8 * count * units + 12 * count * width, 2 * count * units),
        name="feed",
    )(own, came, w_in, bias, w_out)


def feed_back_kernel(half, lines, where, low_own, low_came, own_ref, came_ref, active_ref, slope_ref, w_in, w_out, *refs):
    mine_ref, other_ref, d_bias_ref = refs[:3]
    weight_refs, (d_in, d_out) = refs[3:-2], refs[-2:]
    step = pl.program_id(0)
    units = w_in.shape[1]

    @pl.when(step == 0)
    def _():
        d_in[...] = jnp.zeros_like(d_in)
        d_out[...] = jnp.zeros_like(d_out)
        d_bias_ref[...] = jnp.zeros_like(d_bias_ref)

    low = jnp.where(step < half, low_own[...], low_came[...])
    rows = jnp.where(step < half, own_ref[...], came_ref[...])
    inner = (dot(low, w_out[...], NN) * slope_ref[...].astype(F32)).astype(BF)
    part = dot(inner, w_in[...], NT)
    d_out[...] += dot(low, active_ref[...], TN)
    d_in[...] += dot(rows, inner, TN)
    d_bias_ref[...] += jnp.sum(inner.astype(F32), axis=0, keepdims=True)

    @pl.when(step < half)
    def _():
        mine_ref[...] = part

    @pl.when(step >= half)
    def _():
        other_ref[...] = part.astype(BF)

    @pl.when(step == 2 * half - 1)
    def _():
        for total, cut in ((d_in, slice(0, units)), (d_out, slice(units, 2 * units))):
            if lines == 2:
                kept, sent = own_rows(where[1], total, total.shape[0] // 2)
                weight_refs[0][:, cut] = kept.astype(BF)
                weight_refs[1][:, cut] = sent.astype(BF)
            else:
                weight_refs[0][:, cut] = total[...].astype(BF)


def feed_back(where, low_own, low_came, own, came, active, slope, w_in, w_out):
    count, width = own.shape
    units = w_in.shape[1]
    block = min(FEED_ROWS, count)
    half = count // block
    whole = lambda i, *c: (0, 0)
    by_row = lambda i, *c: (i, 0)
    once = pl.Buffered(1)
    lines = lax.axis_size("dp")
    own_spec, came_spec = row_specs(block, half, width)
    d_shape = (width // 2 if lines == 2 else width, 2 * units)
    d_count = 2 if lines == 2 else 1
    return pl.pallas_call(
        functools.partial(feed_back_kernel, half, lines),
        grid_spec=pltpu.PrefetchScalarGridSpec(
            num_scalar_prefetch=1,
            grid=(2 * half,),
            in_specs=[
                own_spec,
                came_spec,
                own_spec,
                came_spec,
                pl.BlockSpec((block, units), by_row),
                pl.BlockSpec((block, units), by_row),
                pl.BlockSpec((width, units), whole, pipeline_mode=once),
                pl.BlockSpec((width, units), whole, pipeline_mode=once),
            ],
            out_specs=[own_spec, came_spec, pl.BlockSpec((1, units), whole)]
            + [pl.BlockSpec(d_shape, whole, pipeline_mode=once)] * d_count,
            scratch_shapes=[pltpu.VMEM((width, units), F32), pltpu.VMEM((width, units), F32)],
        ),
        out_shape=[
            jax.ShapeDtypeStruct((count, width), F32),
            jax.ShapeDtypeStruct((count, width), BF),
            jax.ShapeDtypeStruct((1, units), F32),
        ]
        + [jax.ShapeDtypeStruct(d_shape, BF)] * d_count,
        compiler_params=params(),
        cost_estimate=cost(16 * count * width * units, 8 * width * units + 8 * count * units + 16 * count * width),
        name="feed_back",
    )(where, low_own, low_came, own, came, active, slope, w_in, w_out)


def centre(values):
    middle = values - jnp.mean(values, axis=-1, keepdims=True)
    scale = lax.rsqrt(jnp.mean(middle * middle, axis=-1, keepdims=True) + EPSILON)
    return middle * scale, scale


def back_through(weighted, normal, scale):
    first = jnp.mean(weighted, axis=-1, keepdims=True)
    second = jnp.mean(weighted * normal, axis=-1, keepdims=True)
    return (weighted - first - normal * second) * scale


def first_kernel(x_ref, mine_ref, came_ref, vec_ref, normal_ref, scale_ref, low_ref):
    sums = x_ref[...].astype(F32) + (mine_ref[...] + came_ref[...].astype(F32)) + vec_ref[0:1, :]
    normal, scale = centre(sums)
    normal_ref[...] = normal
    scale_ref[...] = scale
    low_ref[...] = (normal * vec_ref[1:2, :] + vec_ref[2:3, :]).astype(BF)


def second_kernel(per_seq, counts, normal_ref, mine_ref, came_ref, cot_ref, vec_ref, out_ref, grad_ref, low_ref, sums_ref):
    step = pl.program_id(0)
    block = normal_ref.shape[0]
    valid = counts[step // per_seq] - (step % per_seq) * block
    keep = lax.broadcasted_iota(jnp.int32, normal_ref.shape, 0) < valid

    @pl.when(step == 0)
    def _():
        sums_ref[...] = jnp.zeros_like(sums_ref)

    first = normal_ref[...] * vec_ref[1:2, :] + vec_ref[2:3, :]
    sums = first + (mine_ref[...] + came_ref[...].astype(F32)) + vec_ref[3:4, :]
    normal, scale = centre(sums)
    out_ref[...] = jnp.where(keep, normal * vec_ref[4:5, :] + vec_ref[5:6, :], 0.0)
    out_grad = jnp.where(keep, cot_ref[...].astype(F32), 0.0)
    grad = back_through(out_grad * vec_ref[4:5, :], normal, scale)
    grad_ref[...] = grad
    low_ref[...] = grad.astype(BF)
    sums_ref[0:1, :] += jnp.sum(out_grad * normal, axis=0, keepdims=True)
    sums_ref[1:2, :] += jnp.sum(out_grad, axis=0, keepdims=True)
    sums_ref[2:3, :] += jnp.sum(grad, axis=0, keepdims=True)


def first_back_kernel(grad_ref, mine_ref, came_ref, normal_ref, scale_ref, vec_ref, out_ref, low_ref, sums_ref):
    @pl.when(pl.program_id(0) == 0)
    def _():
        sums_ref[...] = jnp.zeros_like(sums_ref)

    given = grad_ref[...] + (mine_ref[...] + came_ref[...].astype(F32))
    normal = normal_ref[...]
    grad = back_through(given * vec_ref[1:2, :], normal, scale_ref[...])
    out_ref[...] = grad
    low_ref[...] = grad.astype(BF)
    sums_ref[0:1, :] += jnp.sum(given * normal, axis=0, keepdims=True)
    sums_ref[1:2, :] += jnp.sum(given, axis=0, keepdims=True)
    sums_ref[2:3, :] += jnp.sum(grad, axis=0, keepdims=True)


def row_call(kernel, name, block, count, width, inputs, whole_inputs, outs, sums, counts=None):
    by_row = lambda i, *c: (i, 0)
    whole = lambda i, *c: (0, 0)
    in_specs = [pl.BlockSpec((block, a.shape[1]), by_row) for a in inputs]
    in_specs += [pl.BlockSpec(a.shape, whole) for a in whole_inputs]
    out_specs = [pl.BlockSpec((block, w), by_row) for w, _ in outs]
    out_shape = [jax.ShapeDtypeStruct((count, w), t) for w, t in outs]
    if sums:
        out_specs.append(pl.BlockSpec((8, width), whole))
        out_shape.append(jax.ShapeDtypeStruct((8, width), F32))
    prefetch = 0 if counts is None else 1
    moved = sum(a.size * a.dtype.itemsize for a in inputs) + sum(count * w * 4 for w, _ in outs)
    return pl.pallas_call(
        kernel,
        grid_spec=pltpu.PrefetchScalarGridSpec(
            num_scalar_prefetch=prefetch, grid=(count // block,), in_specs=in_specs, out_specs=out_specs
        ),
        out_shape=out_shape,
        compiler_params=params(),
        cost_estimate=cost(20 * count * width, moved),
        name=name,
    )(*(() if counts is None else (counts,)), *inputs, *whole_inputs)


def interleaved(key, value):
    width = key.shape[1]
    pieces = []
    for start in range(0, width, PAIR):
        pieces += [key[:, start : start + PAIR], value[:, start : start + PAIR]]
    return jnp.concatenate(pieces, axis=1)


def apart(both):
    keys, values = [], []
    for start in range(0, both.shape[1], 2 * PAIR):
        keys.append(both[:, start : start + PAIR])
        values.append(both[:, start + PAIR : start + 2 * PAIR])
    return jnp.concatenate(keys, axis=1), jnp.concatenate(values, axis=1)


def on_device(
    block_input,
    lengths,
    cotangent,
    query_weight,
    query_bias,
    key_weight,
    value_weight,
    value_bias,
    output_weight,
    output_bias,
    first_gain,
    first_shift,
    inner_weight,
    inner_bias,
    outer_weight,
    closing_offset_vector,
    second_gain,
    second_shift,
):
    seqs, local, width = block_input.shape
    chip = 2 * local
    spots = lax.axis_size("ctx")
    spot = lax.axis_index("ctx")
    part = lax.axis_index("tp")
    core, side = part % 2, part // 2
    is_upper_core, is_upper_side = core == 1, side == 1
    span = local * lax.axis_size("tp")
    heads_width = query_weight.shape[1]
    unit_width = inner_weight.shape[1]
    count = seqs * local

    def other_core(value, **ties):
        return swap(value, "tp", 1, **ties)

    def other_side(value, **ties):
        return swap(value, "tp", 2, **ties)

    def flat(value):
        return value.reshape(-1, value.shape[-1])

    starts = jnp.stack([(spot ^ k) * span + side * chip for k in range(spots)])
    key_counts = jnp.clip(lengths[:, None] - starts[None, :], 0, chip)
    facts = jnp.stack([spot, core, lax.axis_index("dp")]).astype(jnp.int32)
    counts = jnp.concatenate([key_counts.astype(jnp.int32), jnp.broadcast_to(facts, (seqs, 3))], axis=1)
    row_counts = jnp.clip(lengths - (spot * span + part * local), 0, local).astype(jnp.int32)
    where = jnp.stack([core, lax.axis_index("dp")]).astype(jnp.int32)

    def together(*values):
        return lax.optimization_barrier(values)

    def over_spots(value, done=()):
        return [swap(value, "ctx", k, (), done) for k in range(1, spots)]

    lines = lax.axis_size("dp")
    own_width = 2 * heads_width
    attention_shard = pack([[(query_weight, False), (key_weight, False), (value_weight, False)]])
    biases = jnp.concatenate([query_bias, value_bias, inner_bias])[None, :]
    x_rows = [block_input[s] for s in range(seqs)]

    def send_near(own):
        return [swap(own, "ctx", 2), swap(own, "ctx", 1)] if spots == 4 else over_spots(own)

    def send_last(own, far):
        return [
            lax.ppermute(own, "ctx", [(1, 2), (2, 1)]),
            lax.ppermute(far, "ctx", [(2, 3), (1, 0)]),
        ]

    def finish(nears, lasts):
        if spots != 4:
            return nears
        in_middle = jnp.logical_or(spot == 1, spot == 2)
        return [nears[1], nears[0], jnp.where(in_middle, lasts[0], lasts[1])]

    came, across, *near = together(other_core(block_input), other_side(block_input), *over_spots(attention_shard))
    first_out = after(x_rows[0], *near)
    (attention_near,) = stack([attention_shard, *near])
    diagonal = [(d * 4 + t, (1 - d) * 4 + (t ^ 2)) for d in range(2) for t in range(4)]
    over_both = [lax.ppermute(attention_near, ("dp", "tp"), diagonal)] if lines == 2 else []
    attention_other, attention_line, *nears = together(
        other_side(attention_near), swap(attention_near, "dp", 1), *over_both, *send_near(first_out)
    )
    if lines == 2:
        other_line, *nears = nears
    cores = [other_core(n) for n in nears]
    lasts = send_last(after(x_rows[0], *nears), nears[0]) if spots == 4 else []
    biases_came = other_side(after(biases, *nears))
    biases_came, *rest = together(biases_came, *lasts, *cores)
    lasts, cores = rest[: len(lasts)], rest[len(lasts) :]
    arrived = [finish(nears, lasts)]
    if spots == 4:
        cores = [cores[1], cores[0], other_core(arrived[0][2])]
    if lines == 2:
        attention_all = [[attention_near, attention_other], [attention_line, other_line]]
    else:
        attention_all = over_dp([attention_near, attention_other])
    query_full, kv_full = place(attention_all, [heads_width] * 3, [(0,), (1, 2)])

    query_b = ordered(biases[:, :heads_width], biases_came[:, :heads_width], is_upper_side, 1)
    cut = slice(heads_width, own_width)
    value_b = ordered(biases[:, cut], biases_came[:, cut], is_upper_side, 1)
    cut = slice(own_width, None)
    inner_b = ordered(biases[:, cut], biases_came[:, cut], is_upper_side, 1)
    kv_bias = interleaved(jnp.zeros_like(value_b), value_b)

    pieces = [[(x_rows[0], came[0])] + list(zip(arrived[0], cores))]
    across_core = other_core(across[0])
    late_weights = together(output_weight, inner_weight, outer_weight, *nears)
    feed_shard = pack([[(late_weights[0], True), (late_weights[1], False)], [(late_weights[2], True)]])
    feed_shard = after(feed_shard, arrived[0][-1])
    feed_near = over_spots(feed_shard)
    second_nears = send_near(after(x_rows[1], arrived[0][-1]))
    weights = (query_full, kv_full, query_b, kv_bias)
    q, made, own, packed, lse = attend(counts[0], seqs, 0, pieces[0] + [(across[0], across_core)], weights, ())
    queries, kv = [q], [made]
    packs = [packed]

    own, *rest = together(own, *feed_near, *second_nears)
    feed_near, nears = rest[: len(feed_near)], rest[len(feed_near) :]
    across_core = other_core(across[1])
    cores = [other_core(n) for n in nears]
    lasts = send_last(after(x_rows[1], own), nears[0]) if spots == 4 else []
    near_a, near_b = stack([after(feed_shard, *cores)] + feed_near, feed_shard.shape[1] - unit_width - -unit_width % 128)
    other_a, line_b, *rest = together(other_side(near_a), swap(near_b, "dp", 1), *lasts, *cores)
    packs[0] = other_side(after(packs[0], other_a))
    lasts, cores = rest[: len(lasts)], rest[len(lasts) :]
    arrived.append(finish(nears, lasts))
    if spots == 4:
        cores = [cores[1], cores[0], other_core(arrived[1][2])]
    pieces.append([(x_rows[1], came[1])] + list(zip(arrived[1], cores)))
    if lines == 2:
        last_b = [near_b, line_b]
        sent_a = [swap(after(a, line_b), "dp", 1) for a in (near_a, other_a)]
        sent_b = [other_side(after(b, other_a)) for b in last_b]
    q, made, own, packed, lse = attend(counts[1], seqs, 1, pieces[1] + [(across[1], across_core)], weights, (own, lse))
    queries.append(q)
    kv.append(made)
    buffers = (own, lse)
    packs.append(other_side(packed))
    if lines == 2:
        sent = together(*sent_a, *sent_b, own)
        sent_a, sent_b = list(sent[:2]), list(sent[2:4])
        all_a = [[near_a, other_a], sent_a]
        all_b = [[near_b, sent_b[0]], [line_b, sent_b[1]]]
    else:
        all_a, all_b = over_dp([near_a, other_a]), over_dp([near_b, other_side(near_b)])
    output_full, inner_full = place(all_a, [heads_width, unit_width], [(0,), (1,)])
    (outer_full,) = place(all_b, [unit_width], [(0,)])

    vectors = jnp.stack([output_bias, first_gain, first_shift, closing_offset_vector, second_gain, second_shift])
    vectors = jnp.concatenate([vectors, jnp.zeros((2, width), F32)])
    block = local

    attended, attended_low, mine, other, lse_all = merge(where, *buffers, packs, output_full)
    normal, spread, first_low = row_call(
        first_kernel,
        "first_norm",
        block,
        count,
        width,
        [flat(block_input), flat(mine), flat(other_core(other))],
        [vectors],
        [(width, F32), (1, F32), (width, BF)],
        False,
    )
    first_came = other_core(first_low)
    active, slope, mine, other = feed(first_low, first_came, inner_full, inner_b, outer_full)
    output, second_grad, outer_low, second_sums = row_call(
        functools.partial(second_kernel, local // block),
        "second_norm",
        block,
        count,
        width,
        [normal, mine, other_core(other), flat(cotangent)],
        [vectors],
        [(width, F32), (width, F32), (width, BF)],
        True,
        row_counts,
    )
    mine, other, d_inner_bias, *d_feed = feed_back(
        where, outer_low, other_core(outer_low), first_low, first_came, active, slope, inner_full, outer_full
    )
    first_grad, attn_low, first_sums = row_call(
        first_back_kernel,
        "first_norm_back",
        block,
        count,
        width,
        [second_grad, mine, other_core(other), normal, spread],
        [vectors],
        [(width, F32), (width, BF)],
        True,
    )
    attn_low = attn_low.reshape(seqs, local, width)
    attn_came = other_core(attn_low)
    g_own = turn(where, attn_low, attn_came, output_full, attended, lse_all)
    d_output = output_grad(where, after(attn_low, *g_own), attn_came, attended_low)
    g_oth = [other_side(g) for g in g_own]

    lines = lax.axis_size("dp")

    def over_lines(made, done=()):
        if lines == 2:
            return made[0], swap(made[1], "dp", 1, (), done)
        value, place_at = made[0].astype(F32), lax.axis_index("dp")
        for bit in reversed(bits_of("dp")):
            mine, sent = halves(value, (place_at & bit) != 0, 0)
            term = swap(sent.astype(BF), "dp", bit, (), done)
            value = mine + term.astype(F32)
        return mine, term

    def sides_of(pair, width_of_side):
        return [(pair, 0, width_of_side)], [(pair, width_of_side, width_of_side)]

    def back(s, g_in, before):
        return attend_back(
            counts[s], queries[s], g_own[s], g_in, kv[s], kv_full, pieces[s], before, s == seqs - 1
        )

    def by_spot(mine, came):
        total = (mine + came.astype(F32)).reshape(spots, local, width)
        return total[0], [total[k].astype(BF) for k in range(1, spots)]

    shared = jnp.concatenate([second_sums[:3], first_sums[:3]])
    shared_came = other_core(shared)
    output_mine, output_came = over_lines(d_output)
    g_in, shared_came = together(g_oth[0], shared_came)
    early = jnp.concatenate([(shared + shared_came).reshape(1, -1), d_inner_bias], axis=1)
    early_near = swap(early, "ctx", 1)
    own, oth, mine, other, kv_bias_sum, *kv_grads = back(0, g_in, None)
    dq_own = [own]
    oth, other, g_oth[1], output_came, early_near = together(oth, other, g_oth[1], output_came, early_near)
    output_pair = (output_mine, output_came)
    dq_came_0 = other_side(oth)
    kept_0, sent_0 = by_spot(mine, other_core(other))
    early = early + early_near
    early_far = [swap(early, "ctx", bit) for bit in bits_of("ctx")[1:]]
    feed_pairs = [over_lines(d_feed, (kv_bias_sum,))]
    feed_kept, feed_sent = fold_sides(
        feed_pairs,
        [
            sides_of(0, unit_width),
            ([(0, 2 * unit_width, unit_width)], [(0, 3 * unit_width, unit_width)]),
        ],
    )
    feed_term = other_side(feed_sent)
    came_0 = [swap(t, "ctx", k + 1) for k, t in enumerate(sent_0)]
    g_in, dq_came_0, early, *rest = together(g_oth[1], dq_came_0, early, *early_far, feed_sent, *sent_0)
    early = sum(rest[: len(early_far)], early)
    own, oth, mine, other, kv_bias_sum, *kv_grads = back(1, g_in, (kv_grads[0], kv_bias_sum))
    dq_own.append(own)

    oth, other, feed_term, *rest = together(oth, other, feed_term, *came_0, *kv_grads)
    came_0, kv_grads = rest[: spots - 1], rest[spots - 1 :]
    dq_came_1 = other_side(oth)
    kept_1, sent_1 = by_spot(mine, other_core(other))
    feed_all_rows = add_low(feed_kept, feed_term)
    feed_spread = lax.all_to_all(feed_all_rows, "ctx", split_axis=0, concat_axis=0, tiled=True)
    dq_came = [dq_came_0, after(dq_came_1, feed_all_rows, *sent_1)]
    kv_pair = over_lines(kv_grads)
    mine, other, query_bias_sum, *query_grads = query_back(
        where, dq_own, dq_came, x_rows, [came[s] for s in range(seqs)], query_full
    )
    query_term = (mine + other_core(other).astype(F32)).reshape(seqs, local, width)
    query_pair = over_lines(query_grads)
    value_bias_sum = apart(kv_bias_sum)[1]
    vector = jnp.concatenate([early, query_bias_sum.reshape(1, -1), value_bias_sum], axis=1)
    for bit in bits_of("dp"):
        vector = vector + swap(vector, "dp", bit)
    if spots == 4:
        near_1, far_1, last_1 = sent_1
        first_1 = [
            lax.ppermute(last_1, "ctx", [(3, 2), (0, 1)]),
            lax.ppermute(last_1, "ctx", [(1, 2), (2, 1)]),
        ]
    else:
        first_1 = [swap(sent_1[0], "ctx", 1)]
    if lines == 2:
        query_last, kv_last, vector, *first_1 = together(query_pair[1], kv_pair[1], vector, *first_1)
        query_pair, kv_pair = (query_pair[0], query_last), (kv_pair[0], kv_last)
    if spots == 4:
        passed, middle = first_1
        far_1 = (far_1.astype(F32) + passed.astype(F32)).astype(BF)
        came_1 = [middle, swap(far_1, "ctx", 2), swap(near_1, "ctx", 1)]
        query_pair = (query_pair[0], after(query_pair[1], far_1))
    else:
        came_1 = first_1 + [swap(t, "ctx", k + 2) for k, t in enumerate(sent_1[1:])]

    def side_cuts(pair, offset):
        cuts = []
        for start in (0, heads_width):
            pieces_of, at = [], start
            while at < start + heads_width:
                w = min(PAIR - at % PAIR, start + heads_width - at)
                pieces_of.append((pair, 2 * (at - at % PAIR) + offset + at % PAIR, w))
                at += w
            cuts.append(pieces_of)
        return tuple(cuts)

    kept, sent = fold_sides(
        [query_pair, kv_pair, output_pair],
        [sides_of(0, heads_width), side_cuts(1, 0), side_cuts(1, PAIR), sides_of(2, heads_width)],
    )
    vector_came = other_side(vector)
    term, feed_spread, vector_came, *rest = together(other_side(sent), feed_spread, vector_came, *came_1[1:])
    came_1[1:] = rest
    vector = vector + vector_came
    early, vector = vector[:, : early.shape[1]], vector[:, early.shape[1] :]
    spare = -vector.shape[1] % kept.shape[1]
    vector = jnp.pad(vector, ((0, 0), (0, spare))).reshape(-1, kept.shape[1])
    rows = fold_spots(kept, term, vector)
    terms = [swap(t, "ctx", k + 1) for k, t in enumerate(rows[1:])]
    feed_owned = jnp.sum(feed_spread.reshape(spots, -1, feed_spread.shape[1]).astype(F32), axis=0)
    size = rows[0].shape[0]
    owned = rows[0] + sum(t[:size].astype(F32) for t in terms)
    vector = (vector + sum(unpacked_rows(t[size:], vector.shape[0]) for t in terms)).reshape(-1)
    first_grad = first_grad.reshape(seqs, local, width)
    input_grad = jnp.stack(
        [
            first_grad[s] + query_term[s] + kept + sum(t.astype(F32) for t in came)
            for s, (kept, came) in enumerate(((kept_0, came_0), (kept_1, came_1)))
        ]
    )

    early = early[0]
    shared = early[: 6 * width].reshape(6, width)

    def own_side(value, start, size):
        return jnp.where(is_upper_side, value[start + size : start + 2 * size], value[start : start + size])

    return (
        output.reshape(seqs, local, width),
        input_grad,
        owned[:, :heads_width],
        own_side(vector, 0, heads_width),
        owned[:, heads_width:own_width],
        owned[:, own_width : own_width + heads_width],
        own_side(vector, own_width, heads_width),
        owned[:, 3 * heads_width : 4 * heads_width].T,
        shared[5],
        shared[3],
        shared[4],
        feed_owned[:, :unit_width],
        own_side(early, 6 * width, unit_width),
        feed_owned[:, unit_width : 2 * unit_width].T,
        shared[2],
        shared[0],
        shared[1],
    )


def solution(mesh):
    rows = P("dp", ("ctx", "tp"), None)
    into = P(("dp", "ctx"), "tp")
    out_of = P("tp", ("dp", "ctx"))
    split, whole = P("tp"), P()
    return jax.shard_map(
        on_device,
        mesh=mesh,
        in_specs=(
            rows, P("dp"), rows, into, split, into, into, split, out_of, whole, whole, whole,
            into, split, out_of, whole, whole, whole,
        ),
        out_specs=(
            rows, rows, into, split, into, into, split, out_of, whole, whole, whole,
            into, split, out_of, whole, whole, whole,
        ),
        check_vma=False,
    )
```

```python
import functools
import math

import jax
import jax.numpy as jnp
from jax import lax
from jax.experimental import pallas as pl
from jax.experimental.pallas import tpu as pltpu
from jax.sharding import PartitionSpec as P

HD = 64
PAIR = 2 * HD
EPSILON = 1e-12
NEGATIVE = -1e30
LARGEST = 1e30
BF = jnp.bfloat16
F32 = jnp.float32
VMEM_LIMIT = 56 << 20
FEED_ROWS = 256

NN = (((1,), (0,)), ((), ()))
NT = (((1,), (1,)), ((), ()))
TN = (((0,), (0,)), ((), ()))


def dot(a, b, dims):
    return lax.dot_general(a, b, dims, preferred_element_type=F32)


def params():
    return pltpu.CompilerParams(vmem_limit_bytes=VMEM_LIMIT)


def cost(flops, moved, transcendentals=0):
    return pl.CostEstimate(flops=int(flops), bytes_accessed=int(moved), transcendentals=int(transcendentals))


def after(value, *others):
    if not others:
        return value
    return lax.optimization_barrier((value, *others))[0]


def swap(value, axis, bit, start=(), done=()):
    count = lax.axis_size(axis)
    return after(lax.ppermute(after(value, *start), axis, [(i, i ^ bit) for i in range(count)]), *done)


def bits_of(axis):
    count = lax.axis_size(axis)
    return [1 << k for k in range(count.bit_length() - 1)]


def halves(value, upper, dim):
    size = value.shape[dim] // 2
    at = upper.astype(jnp.int32) * size
    mine = lax.dynamic_slice_in_dim(value, at, size, dim)
    return mine, lax.dynamic_slice_in_dim(value, size - at, size, dim)


def ordered(mine, other, upper, dim):
    return jnp.concatenate([jnp.where(upper, other, mine), jnp.where(upper, mine, other)], axis=dim)


def call(kernel, name, outs, *arrays, prefetch=None, scratch=(), flops=0):
    spec = lambda shape: pl.BlockSpec(shape, lambda i, *c: (0,) * len(shape))
    arrays_moved = sum(a.size * a.dtype.itemsize for a in arrays) + sum(4 * math.prod(shape) for shape, _ in outs)
    return pl.pallas_call(
        kernel,
        grid_spec=pltpu.PrefetchScalarGridSpec(
            num_scalar_prefetch=0 if prefetch is None else 1,
            grid=(1,),
            in_specs=[spec(a.shape) for a in arrays],
            out_specs=[spec(shape) for shape, _ in outs],
            scratch_shapes=list(scratch),
        ),
        out_shape=[jax.ShapeDtypeStruct(shape, kind) for shape, kind in outs],
        compiler_params=params(),
        cost_estimate=cost(flops, arrays_moved),
        name=name,
    )(*(() if prefetch is None else (prefetch,)), *arrays)


def fits(rows):
    return rows % 16 == 0


def pack(groups):
    flat = [piece for group in groups for piece in group]
    widths = [sum(w.shape[0] if t else w.shape[1] for w, t in group) for group in groups]
    first, turned = flat[0]
    rows = first.shape[1] if turned else first.shape[0]

    def joined(values):
        values, out = list(values), []
        for group, width in zip(groups, widths):
            out += [values.pop(0) for _ in group]
            if -width % 128:
                out.append(jnp.zeros((rows, -width % 128), F32))
        return jnp.concatenate(out, axis=1).astype(BF)

    if not fits(rows):
        return joined(w.T if t else w for w, t in flat)

    def kernel(*refs):
        refs[-1][...] = joined(r[...].T if t else r[...] for r, (_, t) in zip(refs, flat))

    total = sum(w + -w % 128 for w in widths)
    return call(kernel, "pack", [((rows, total), BF)], *[w for w, _ in flat])[0]


def stack(parts, cuts=None):
    rows, width = parts[0].shape
    ranges = [(0, width)] if cuts is None else [(0, cuts), (cuts, width)]
    if not fits(rows):
        whole = jnp.concatenate(parts, axis=0)
        return [whole[:, start:stop] for start, stop in ranges]

    def kernel(*refs):
        for k, ref in enumerate(refs[: len(parts)]):
            for out, (start, stop) in zip(refs[len(parts) :], ranges):
                out[k * rows : k * rows + rows, :] = ref[:, start:stop]

    return call(kernel, "stack", [((rows * len(parts), stop - start), BF) for start, stop in ranges], *parts)


def over_dp(arrays, done=()):
    found = [arrays]
    for bit in bits_of("dp"):
        found = found + [[swap(a, "dp", bit, (), done) for a in one] for one in found]
    return found


def place(found, widths, joined):
    spots, spot = lax.axis_size("ctx"), lax.axis_index("ctx")
    line, side = lax.axis_index("dp"), lax.axis_index("tp") // 2
    lines = len(found)
    starts = [sum(widths[:k]) for k in range(len(widths))]
    block = found[0][0].shape[0]
    rows = block // spots
    cuts = list(zip(starts, widths))
    shapes = [(block * lines, 2 * sum(widths[m] for m in members)) for members in joined]
    if not fits(rows):
        order = ((jnp.arange(lines)[:, None] ^ line) * spots + (jnp.arange(spots)[None, :] ^ spot)).reshape(-1)
        own, oth = (
            jnp.stack([f[h] for f in found]).reshape(lines * spots, rows, -1)[order].reshape(lines * block, -1)
            for h in range(2)
        )
        low, high = jnp.where(side == 1, oth, own), jnp.where(side == 1, own, oth)
        full = [jnp.concatenate([low[:, t : t + w], high[:, t : t + w]], axis=1) for t, w in cuts]
        return [full[m[0]] if len(m) == 1 else interleaved(full[m[0]], full[m[1]]) for m in joined]

    def kernel(where, *refs):
        outs = refs[2 * lines :]
        upper = where[2] == 1
        for k in range(lines):
            own_ref, oth_ref = refs[2 * k], refs[2 * k + 1]
            for c in range(spots):
                came = pl.ds(pl.multiple_of((where[0] ^ c) * rows, rows), rows)
                to = pl.ds(pl.multiple_of(((where[1] ^ k) * spots + c) * rows, rows), rows)
                own, oth = own_ref[came, :], oth_ref[came, :]
                low, high = jnp.where(upper, oth, own), jnp.where(upper, own, oth)
                full = [jnp.concatenate([low[:, t : t + w], high[:, t : t + w]], axis=1) for t, w in cuts]
                for out, members in zip(outs, joined):
                    if len(members) == 1:
                        out[to, :] = full[members[0]]
                    else:
                        both = []
                        for p in range(0, full[members[0]].shape[1], PAIR):
                            both += [full[m][:, p : p + PAIR] for m in members]
                        out[to, :] = jnp.concatenate(both, axis=1)

    where = jnp.stack([spot, line, side]).astype(jnp.int32)
    flat = [a for one in found for a in one]
    return call(kernel, "place", [(shape, BF) for shape in shapes], *flat, prefetch=where)


def fold_sides(pairs, cuts):
    rows = pairs[0][0].shape[0]
    width = sum(w for low, _ in cuts for _, _, w in low)
    spare = -width % 128
    width += spare
    side = lax.axis_index("tp") // 2

    def both(totals):
        end = [jnp.zeros((totals[0].shape[0], spare), F32)] if spare else []
        low = jnp.concatenate([totals[p][:, t : t + w] for cut, _ in cuts for p, t, w in cut] + end, axis=1)
        high = jnp.concatenate([totals[p][:, t : t + w] for _, cut in cuts for p, t, w in cut] + end, axis=1)
        return low, high

    if not fits(rows):
        low, high = both([a.astype(F32) + b.astype(F32) for a, b in pairs])
        return jnp.where(side == 1, high, low), jnp.where(side == 1, low, high).astype(BF)

    block = rows // 4 if fits(rows // 4) else rows
    steps = rows // block

    def kernel(where, *refs):
        kept, sent = refs[2 * len(pairs) :]
        totals = [refs[2 * k][...].astype(F32) + refs[2 * k + 1][...].astype(F32) for k in range(len(pairs))]
        low, high = both(totals)
        upper = where[0] == 1
        kept[...] = jnp.where(upper, high, low)
        sent[...] = jnp.where(upper, low, high).astype(BF)

    spec = lambda w: pl.BlockSpec((block, w), lambda i, c: (i, 0))
    flat = [a for pair in pairs for a in pair]
    return pl.pallas_call(
        kernel,
        grid_spec=pltpu.PrefetchScalarGridSpec(
            num_scalar_prefetch=1,
            grid=(steps,),
            in_specs=[spec(a.shape[1]) for a in flat],
            out_specs=[spec(width), spec(width)],
        ),
        out_shape=[jax.ShapeDtypeStruct((rows, width), F32), jax.ShapeDtypeStruct((rows, width), BF)],
        compiler_params=params(),
        cost_estimate=cost(0, sum(a.size * a.dtype.itemsize for a in flat) + 6 * rows * width),
        name="fold_sides",
    )(side.astype(jnp.int32).reshape(1), *flat)


def fold_spots(kept, came, vector):
    spots, spot = lax.axis_size("ctx"), lax.axis_index("ctx")
    rows, width = kept.shape[0] // spots, kept.shape[1]
    count = vector.shape[0]
    below_rows = 3 * count + -3 * count % 16
    if not fits(rows):
        total = kept + came.astype(F32)
        cut = lambda k: lax.dynamic_slice_in_dim(total, (spot ^ k) * rows, rows, 0)
        terms = jnp.concatenate([*in_three(vector), jnp.zeros((below_rows - 3 * count, width), BF)], axis=0)
        return [cut(0)] + [jnp.concatenate([cut(k).astype(BF), terms], axis=0) for k in range(1, spots)]

    def kernel(where, kept_ref, came_ref, vector_ref, own, *outs):
        at = pl.ds(pl.multiple_of(where[0] * rows, rows), rows)
        own[...] = kept_ref[at, :] + came_ref[at, :].astype(F32)
        terms = jnp.concatenate(in_three(vector_ref[...]), axis=0)
        terms = jnp.concatenate([terms, jnp.zeros((below_rows - 3 * count, width), BF)], axis=0)
        for k, out in enumerate(outs):
            at = pl.ds(pl.multiple_of((where[0] ^ (k + 1)) * rows, rows), rows)
            out[:rows, :] = (kept_ref[at, :] + came_ref[at, :].astype(F32)).astype(BF)
            out[rows:, :] = terms

    outs = [((rows, width), F32)] + [((rows + below_rows, width), BF)] * (spots - 1)
    return call(kernel, "fold_spots", outs, kept, came, vector, prefetch=spot.astype(jnp.int32).reshape(1))


def add_low(kept, came):
    if not fits(kept.shape[0] // 4):
        return (kept + came.astype(F32)).astype(BF)

    def kernel(kept_ref, came_ref, out):
        out[...] = (kept_ref[...] + came_ref[...].astype(F32)).astype(BF)

    rows, width = kept.shape
    spec = pl.BlockSpec((rows // 4, width), lambda i: (i, 0))
    return pl.pallas_call(
        kernel,
        grid=(4,),
        in_specs=[spec, spec],
        out_specs=spec,
        out_shape=jax.ShapeDtypeStruct(kept.shape, BF),
        compiler_params=params(),
        cost_estimate=cost(kept.size, 8 * kept.size),
        name="add_low",
    )(kept, came)


def own_rows(where, value, rows):
    mine = pl.ds(pl.multiple_of(where * rows, rows), rows)
    other = pl.ds(pl.multiple_of((1 - where) * rows, rows), rows)
    return value[mine, :], value[other, :]


def assemble(upper, pieces, held):
    local = pieces[0].shape[0]
    for k in range(len(pieces) // 2):
        mine, came = pieces[2 * k][...], pieces[2 * k + 1][...]
        held[2 * k * local : (2 * k + 1) * local, :] = jnp.where(upper, came, mine)
        held[(2 * k + 1) * local : (2 * k + 2) * local, :] = jnp.where(upper, mine, came)


def query_back_kernel(seqs, lines, where, *refs):
    dq_own, dq_came, own, came = (refs[k * seqs : k * seqs + seqs] for k in range(4))
    weight, mine_ref, other_ref, bias_ref = refs[4 * seqs : 4 * seqs + 4]
    weight_refs, total = refs[4 * seqs + 4 : -1], refs[-1]
    upper = where[0] == 1
    half = own[0].shape[0]
    bias = None
    for s in range(seqs):
        low = (dq_own[s][...] + dq_came[s][...].astype(F32)).astype(BF)
        rows = jnp.concatenate(
            [jnp.where(upper, came[s][...], own[s][...]), jnp.where(upper, own[s][...], came[s][...])], axis=0
        )
        part = dot(low, weight[...], (((0,), (1,)), ((), ())))
        to = slice(s * half, s * half + half)
        mine_ref[to, :] = jnp.where(upper, part[half:], part[:half])
        other_ref[to, :] = jnp.where(upper, part[:half], part[half:]).astype(BF)
        grad = dot(rows, low, (((0,), (1,)), ((), ())))
        total[...] = grad if s == 0 else total[...] + grad
        sums = jnp.sum(low.astype(F32), axis=1, keepdims=True)
        bias = sums if bias is None else bias + sums
    bias_ref[...] = bias
    if lines == 2:
        kept, sent = own_rows(where[1], total, total.shape[0] // 2)
        weight_refs[0][...] = kept
        weight_refs[1][...] = sent.astype(BF)
    else:
        weight_refs[0][...] = total[...]


def query_back(where, dq_own, dq_came, own, came, weight):
    seqs, lines = len(dq_own), lax.axis_size("dp")
    local, width = own[0].shape
    own_width = weight.shape[1]
    outs = [((seqs * local, width), F32), ((seqs * local, width), BF), ((own_width, 1), F32)]
    if lines == 2:
        outs += [((width // 2, own_width), F32), ((width // 2, own_width), BF)]
    else:
        outs += [((width, own_width), F32)]
    return call(
        functools.partial(query_back_kernel, seqs, lines),
        "query_back",
        outs,
        *dq_own,
        *dq_came,
        *own,
        *came,
        weight,
        prefetch=where,
        scratch=[pltpu.VMEM((width, own_width), F32)],
        flops=8 * seqs * local * width * own_width,
    )


def half_lanes(value):
    lane = lax.broadcasted_iota(jnp.int32, value.shape, 1)
    zero = jnp.zeros_like(value)
    return [jnp.where(lane < HD, value, zero), jnp.where(lane >= HD, value, zero)]


def half_rows(value):
    row = lax.broadcasted_iota(jnp.int32, value.shape, 0)
    zero = jnp.zeros_like(value)
    return [jnp.where(row < HD, value, zero), jnp.where(row >= HD, value, zero)]


def top_bits(value):
    spread = value * 65537.0
    return spread - (spread - value)


def in_three(value):
    first = top_bits(value)
    rest = value - first
    second = top_bits(rest)
    return first.astype(BF), second.astype(BF), (rest - second).astype(BF)


def packed_rows(values):
    terms = jnp.concatenate(in_three(values), axis=0)
    return jnp.concatenate([terms, jnp.zeros((16 - terms.shape[0], terms.shape[1]), BF)], axis=0)


def unpacked_rows(packed, count):
    packed = packed.astype(F32)
    return packed[:count] + packed[count : 2 * count] + packed[2 * count : 3 * count]


def below(shape, count):
    return lax.broadcasted_iota(jnp.int32, shape, 0) < count


def attend_kernel(slots, probe, old, counts, *refs):
    pieces = refs[: 2 * slots + 2]
    w_query, w_kv, b_query, b_kv = refs[2 * slots + 2 : 2 * slots + 6]
    queries, kv, o_own, packed, lse_ref, held, top, total, acc, heads = refs[2 * slots + 6 + old :]
    local = pieces[0].shape[0]
    rows = keys = 2 * local

    @pl.when(pl.program_id(0) == 0)
    def _():
        assemble(counts[slots + 1] == 1, pieces, held)

    scale = jnp.asarray(1.0 / math.sqrt(HD), BF)
    for start, to in ((0, 0), (slots * keys, rows)):
        query = (dot(held[start : start + rows, :], w_query[...], NN) + b_query[...]).astype(BF)
        queries[to : to + rows, :] = query * scale
    for h, query in enumerate(half_lanes(queries[...])):
        heads[h] = query

    @pl.loop(0, slots)
    def _(k):
        at = pl.ds(pl.multiple_of(k * keys, keys), keys)

        @pl.when(counts[k] > 0)
        def _():
            kv[at, :] = (dot(held[at, :], w_kv[...], NN) + b_kv[...]).astype(BF)

        @pl.when(counts[k] <= 0)
        def _():
            kv[at, :] = jnp.zeros((keys, 2 * PAIR), BF)

    def block(k):
        at = pl.ds(pl.multiple_of(k * keys, keys), keys)
        return kv[at, :PAIR], kv[at, PAIR:]

    first = pl.ds(pl.multiple_of(counts[slots] * keys, keys), probe)
    for h in range(2):
        top[h] = jnp.max(dot(kv[first, :PAIR], heads[h], NT), axis=0, keepdims=True)
    total[...] = jnp.zeros_like(total)
    acc[...] = jnp.zeros_like(acc)

    def quick(k, h, valid):
        key, value = block(k)
        expo = jnp.exp(dot(key, heads[h], NT) - top[h])
        if valid is not None:
            expo = jnp.where(below(expo.shape, valid), expo, 0.0)
        total[h] += jnp.sum(expo, axis=0, keepdims=True)
        acc[h] += dot(value, expo.astype(BF), TN)

    @pl.loop(0, slots)
    def _(k):
        valid = counts[k]

        @pl.when(valid >= keys)
        def _():
            quick(k, 0, None)
            quick(k, 1, None)

        @pl.when(jnp.logical_and(valid > 0, valid < keys))
        def _():
            pl.loop(0, 2)(lambda h: quick(k, h, valid))

    @pl.when(jnp.logical_not(jnp.max(total[...]) < LARGEST))
    def _():
        total[...] = jnp.zeros_like(total)
        acc[...] = jnp.zeros_like(acc)

        def careful(k, h, valid):
            key, value = block(k)
            scores = dot(key, heads[h], NT)
            scores = jnp.where(below(scores.shape, valid), scores, NEGATIVE)
            before = top[h]
            new = jnp.maximum(before, jnp.max(scores, axis=0, keepdims=True))
            expo = jnp.where(below(scores.shape, valid), jnp.exp(scores - new), 0.0)
            ratio = jnp.exp(before - new)
            total[h] = total[h] * ratio + jnp.sum(expo, axis=0, keepdims=True)
            acc[h] = acc[h] * ratio + dot(value, expo.astype(BF), TN)
            top[h] = new

        @pl.loop(0, slots)
        def _(k):
            valid = counts[k]

            @pl.when(valid > 0)
            def _():
                pl.loop(0, 2)(lambda h: careful(k, h, valid))

    lse = []
    for h in range(2):
        at = slice(h * HD, h * HD + HD)
        part = acc[h, at, :] / total[h]
        o_own[0, at, :] = part[:, :rows]
        packed[at, :] = part[:, rows:].astype(BF)
        lse.append(top[h] + jnp.log(total[h]))
        lse_ref[0, 0, h : h + 1, :] = lse[h][:, :rows]
    packed[PAIR:, :] = packed_rows(jnp.concatenate([l[:, rows:] for l in lse], axis=0))


def attend(counts, seqs, s, pieces, weights, before):
    w_query, w_kv, b_query, b_kv = weights
    slots = len(pieces) - 1
    local, model = pieces[0][0].shape
    rows, width = 2 * local, w_query.shape[1]
    pairs = width // PAIR
    keys = 2 * local
    total = width * 2 * rows * slots * keys
    anywhere = pl.BlockSpec(memory_space=pl.ANY)
    across = lambda p, c: (0, p)
    flat = [p for pair in pieces for p in pair]
    held = ((slots + 1) * keys, model)
    return pl.pallas_call(
        functools.partial(attend_kernel, slots, min(128, keys), len(before)),
        grid_spec=pltpu.PrefetchScalarGridSpec(
            num_scalar_prefetch=1,
            grid=(pairs,),
            in_specs=[pl.BlockSpec((local, model), lambda p, c: (0, 0), pipeline_mode=pl.Buffered(1)) for _ in flat]
            + [
                pl.BlockSpec((model, PAIR), across),
                pl.BlockSpec((model, 2 * PAIR), across),
                pl.BlockSpec((1, PAIR), across),
                pl.BlockSpec((1, 2 * PAIR), across),
            ]
            + [anywhere] * len(before),
            out_specs=[
                pl.BlockSpec((2 * rows, PAIR), across),
                pl.BlockSpec((slots * keys, 2 * PAIR), across),
                pl.BlockSpec((1, PAIR, rows), lambda p, c: (s, p, 0)),
                pl.BlockSpec((PAIR + 16, rows), lambda p, c: (p, 0)),
                pl.BlockSpec((1, 1, 2, rows), lambda p, c: (s, p, 0, 0)),
            ],
            scratch_shapes=[
                pltpu.VMEM(held, BF),
                pltpu.VMEM((2, 1, 2 * rows), F32),
                pltpu.VMEM((2, 1, 2 * rows), F32),
                pltpu.VMEM((2, PAIR, 2 * rows), F32),
                pltpu.VMEM((2, 2 * rows, PAIR), BF),
            ],
        ),
        out_shape=[
            jax.ShapeDtypeStruct((2 * rows, width), BF),
            jax.ShapeDtypeStruct((slots * keys, 2 * width), BF),
            jax.ShapeDtypeStruct((seqs, width, rows), F32),
            jax.ShapeDtypeStruct((pairs * (PAIR + 16), rows), BF),
            jax.ShapeDtypeStruct((seqs, pairs, 2, rows), F32),
        ],
        input_output_aliases={2 * slots + 7: 2, 2 * slots + 8: 4} if before else {},
        compiler_params=params(),
        cost_estimate=cost(16 * total, 2 * len(flat) * local * model + 8 * slots * keys * width, total // HD),
        name="attend",
    )(counts, *flat, *weights, *before)


def attend_back_kernel(slots, steps, split, first, counts, both, g_own, g_oth, kv, w_kv, *refs):
    pieces = refs[: 2 * slots]
    refs = refs[2 * slots :]
    if not first:
        before, bias_before = refs[:2]
        refs = refs[2:]
    dq_own, dq_oth, mine_ref, other_ref, bias_ref = refs[:5]
    weight_refs = refs[5:-8]
    acc, queries, grads, summed, facts, turned, part, d_weight = refs[-8:]
    rows = both.shape[0] // 2
    local = pieces[0].shape[0]
    keys = 2 * local
    step = pl.program_id(0)
    upper = counts[slots + 1] == 1

    @pl.when(step == 0)
    def _():
        part[...] = jnp.zeros_like(part)
        for k in range(slots):
            mine, came = pieces[2 * k][...], pieces[2 * k + 1][...]
            turned[:, 2 * k * local : (2 * k + 1) * local] = jnp.where(upper, came, mine).T
            turned[:, (2 * k + 1) * local : (2 * k + 2) * local] = jnp.where(upper, mine, came).T

    acc[...] = jnp.zeros_like(acc)
    d_weight[...] = jnp.zeros_like(d_weight) if first else before[...]
    bias_ref[...] = jnp.zeros_like(bias_ref) if first else bias_before[...]
    for block, g_ref in enumerate((g_own, g_oth)):
        stats = unpacked_rows(g_ref[PAIR:, :], 4)
        for h, (query, grad) in enumerate(
            zip(half_lanes(both[block * rows : block * rows + rows, :]), half_rows(g_ref[:PAIR, :]))
        ):
            queries[2 * block + h] = query
            grads[2 * block + h] = grad
            facts[2 * block + h, 0:1, :] = stats[h : h + 1]
            facts[2 * block + h, 1:2, :] = stats[2 + h : 3 + h]

    @pl.loop(0, slots)
    def _(k):
        valid = counts[k]
        rows_at = pl.ds(pl.multiple_of(k * keys, keys), keys)

        def one(at, valid):
            key, value = kv[rows_at, :PAIR], kv[rows_at, PAIR:]
            query, grad = queries[at], grads[at]
            prob = jnp.exp(dot(key, query, NT) - facts[at, 0:1, :])
            if valid is not None:
                prob = jnp.where(below(prob.shape, valid), prob, 0.0)
            change = dot(value, grad, NN) - facts[at, 1:2, :]
            score = (prob * change).astype(BF)
            summed[:, PAIR:] += dot(prob.astype(BF), grad, NT)
            summed[:, :PAIR] += dot(score, query, NN)
            acc[at] += dot(key, score, TN)

        summed[...] = jnp.zeros_like(summed)

        @pl.when(valid >= keys)
        def _():
            for at in range(4):
                one(at, None)

        @pl.when(jnp.logical_and(valid > 0, valid < keys))
        def _():
            pl.loop(0, 4)(lambda at: one(at, valid))

        @pl.when(valid > 0)
        def _():
            low = summed[...].astype(BF)
            part[rows_at, :] += dot(low, w_kv[...], NT)
            d_weight[...] += dot(turned[:, rows_at], low, NN)
            bias_ref[...] += jnp.sum(low.astype(F32), axis=0, keepdims=True)

    scale = 1.0 / math.sqrt(HD)
    for h in range(2):
        at = slice(h * HD, h * HD + HD)
        dq_own[at, :] = acc[h, at, :] * scale
        dq_oth[at, :] = (acc[2 + h, at, :] * scale).astype(BF)
    half = d_weight.shape[0] // 2
    if split:
        lower_line = counts[slots + 2] == 0
        low_half, high_half = d_weight[:half, :], d_weight[half:, :]
        weight_refs[0][...] = jnp.where(lower_line, low_half, high_half)
        weight_refs[1][...] = jnp.where(lower_line, high_half, low_half).astype(BF)
    else:
        weight_refs[0][...] = d_weight[...]

    @pl.when(step == steps - 1)
    def _():
        for k in range(slots):
            low = part[2 * k * local : (2 * k + 1) * local, :]
            high = part[(2 * k + 1) * local : (2 * k + 2) * local, :]
            to = slice(k * local, k * local + local)
            mine_ref[to, :] = jnp.where(upper, high, low)
            other_ref[to, :] = jnp.where(upper, low, high).astype(BF)


def attend_back(counts, both, g_own, g_oth, kv, w_kv, pieces, before, last):
    rows, width = both.shape[0] // 2, both.shape[1]
    pairs = width // PAIR
    slots = len(pieces)
    local, model = pieces[0][0].shape
    keys = 2 * local
    split = last and lax.axis_size("dp") == 2
    across = lambda p, c: (0, p)
    whole = lambda p, c: (0, 0)
    once = pl.Buffered(1)
    t_spec = pl.BlockSpec((PAIR, rows), lambda p, c: (p, 0))
    g_spec = pl.BlockSpec((PAIR + 16, rows), lambda p, c: (p, 0))
    flat = [p for pair in pieces for p in pair]
    extra = () if before is None else before
    if split:
        weight_outs = [((model // 2, 2 * width), F32), ((model // 2, 2 * width), BF)]
    else:
        weight_outs = [((model, 2 * width), F32)]
    total = width * 2 * rows * kv.shape[0]
    return pl.pallas_call(
        functools.partial(attend_back_kernel, slots, pairs, split, before is None),
        grid_spec=pltpu.PrefetchScalarGridSpec(
            num_scalar_prefetch=1,
            grid=(pairs,),
            in_specs=[
                pl.BlockSpec((2 * rows, PAIR), across),
                g_spec,
                g_spec,
                pl.BlockSpec((kv.shape[0], 2 * PAIR), across),
                pl.BlockSpec((model, 2 * PAIR), across),
            ]
            + [pl.BlockSpec((local, model), whole, pipeline_mode=once) for _ in flat]
            + [pl.BlockSpec((a.shape[0], 2 * PAIR), across) for a in extra],
            out_specs=[
                t_spec,
                t_spec,
                pl.BlockSpec((slots * local, model), whole, pipeline_mode=once),
                pl.BlockSpec((slots * local, model), whole, pipeline_mode=once),
                pl.BlockSpec((1, 2 * PAIR), across),
            ]
            + [pl.BlockSpec((shape[0], 2 * PAIR), across) for shape, _ in weight_outs],
            scratch_shapes=[
                pltpu.VMEM((4, PAIR, rows), F32),
                pltpu.VMEM((4, rows, PAIR), BF),
                pltpu.VMEM((4, PAIR, rows), BF),
                pltpu.VMEM((keys, 2 * PAIR), F32),
                pltpu.VMEM((4, 2, rows), F32),
                pltpu.VMEM((model, slots * keys), BF),
                pltpu.VMEM((slots * keys, model), F32),
                pltpu.VMEM((model, 2 * PAIR), F32),
            ],
        ),
        out_shape=[
            jax.ShapeDtypeStruct((width, rows), F32),
            jax.ShapeDtypeStruct((width, rows), BF),
            jax.ShapeDtypeStruct((slots * local, model), F32),
            jax.ShapeDtypeStruct((slots * local, model), BF),
            jax.ShapeDtypeStruct((1, 2 * width), F32),
        ]
        + [jax.ShapeDtypeStruct(shape, kind) for shape, kind in weight_outs],
        compiler_params=params(),
        cost_estimate=cost(40 * total, 8 * both.size + 4 * kv.size + 8 * len(flat) * local * model, total // HD),
        name="attend_back",
    )(counts, both, g_own, g_oth, kv, w_kv, *flat, *extra)


def merge_kernel(pairs, seqs, where, o_own, lse_own, *refs):
    packs = refs[:seqs]
    weight, full_ref, low_ref, mine_ref, other_ref, lse_ref, low_s, packed = refs[seqs:]
    rows = o_own.shape[2]
    for s in range(seqs):

        @pl.when(pl.program_id(0) == s)
        def _(s=s):
            packed[...] = packs[s][...]

    for p in range(pairs):
        base = p * (PAIR + 16)
        own = lse_own[0, p]
        came = unpacked_rows(packed[base + PAIR : base + PAIR + 16, :], 2)
        highest = jnp.maximum(own, came)
        share_own, share_came = jnp.exp(own - highest), jnp.exp(came - highest)
        both = share_own + share_came
        lse_ref[0, p] = highest + jnp.log(both)
        share_own, share_came = share_own / both, share_came / both
        for h in range(2):
            at = slice(p * PAIR + h * HD, p * PAIR + h * HD + HD)
            term = packed[base + h * HD : base + h * HD + HD, :].astype(F32)
            merged = o_own[0, at, :] * share_own[h : h + 1] + term * share_came[h : h + 1]
            full_ref[0, at, :] = merged
            low_s[at, :] = merged.astype(BF)
    low_ref[0] = low_s[...]
    half = rows // 2
    mine = pl.ds(pl.multiple_of(where[0] * half, half), half)
    other = pl.ds(pl.multiple_of((1 - where[0]) * half, half), half)
    dims = (((0,), (1,)), ((), ()))
    mine_ref[0] = dot(low_s[:, mine], weight[...], dims)
    other_ref[0] = dot(low_s[:, other], weight[...], dims).astype(BF)


def merge(where, o_own, lse_own, packs, weight):
    seqs, width, rows = o_own.shape
    pairs = width // PAIR
    model = weight.shape[0]
    one = lambda *shape: pl.BlockSpec((1, *shape), lambda s, w: (s,) + (0,) * len(shape))
    return pl.pallas_call(
        functools.partial(merge_kernel, pairs, seqs),
        grid_spec=pltpu.PrefetchScalarGridSpec(
            num_scalar_prefetch=1,
            grid=(seqs,),
            in_specs=[
                one(width, rows),
                one(pairs, 2, rows),
            ]
            + [pl.BlockSpec(p.shape, lambda s, w: (0, 0)) for p in packs]
            + [
                pl.BlockSpec(weight.shape, lambda s, w: (0, 0)),
            ],
            out_specs=[one(width, rows), one(width, rows), one(rows // 2, model), one(rows // 2, model), one(pairs, 2, rows)],
            scratch_shapes=[pltpu.VMEM((width, rows), BF), pltpu.VMEM(packs[0].shape, BF)],
        ),
        out_shape=[
            jax.ShapeDtypeStruct((seqs, width, rows), F32),
            jax.ShapeDtypeStruct((seqs, width, rows), BF),
            jax.ShapeDtypeStruct((seqs, rows // 2, model), F32),
            jax.ShapeDtypeStruct((seqs, rows // 2, model), BF),
            jax.ShapeDtypeStruct((seqs, pairs, 2, rows), F32),
        ],
        compiler_params=params(),
        cost_estimate=cost(2 * seqs * width * rows * model, 12 * o_own.size + 4 * seqs * rows * model),
        name="merge",
    )(where, o_own, lse_own, *packs, weight)


def turn_kernel(pairs, seqs, where, own_ref, came_ref, weight, full_ref, lse_ref, *refs):
    packs, packed = refs[:seqs], refs[-1]
    step = pl.program_id(0)
    upper = where[0] == 1
    own, came = own_ref[0], came_ref[0]
    rows = jnp.concatenate([jnp.where(upper, came, own), jnp.where(upper, own, came)], axis=0)
    grad = dot(weight[...], rows, (((0,), (1,)), ((), ()))).astype(BF)
    product = grad.astype(F32) * full_ref[0]
    for p in range(pairs):
        base = p * (PAIR + 16)
        packed[base : base + PAIR, :] = grad[p * PAIR : p * PAIR + PAIR]
        stats = [lse_ref[0, p]]
        for h in range(2):
            at = slice(p * PAIR + h * HD, p * PAIR + h * HD + HD)
            stats.append(jnp.sum(product[at], axis=0, keepdims=True))
        packed[base + PAIR : base + PAIR + 16, :] = packed_rows(jnp.concatenate(stats, axis=0))
    for s in range(seqs):

        @pl.when(step == s)
        def _(s=s):
            packs[s][...] = packed[...]


def output_kernel(seqs, lines, where, own_ref, came_ref, low_ref, *refs):
    weight_refs, d_weight = refs[:-1], refs[-1]
    step = pl.program_id(0)
    upper = where[0] == 1
    own, came = own_ref[0], came_ref[0]
    rows = jnp.concatenate([jnp.where(upper, came, own), jnp.where(upper, own, came)], axis=0)

    @pl.when(step == 0)
    def _():
        d_weight[...] = jnp.zeros_like(d_weight)

    d_weight[...] += dot(rows, low_ref[0], (((0,), (1,)), ((), ())))

    @pl.when(step == seqs - 1)
    def _():
        if lines == 2:
            kept, sent = own_rows(where[1], d_weight, d_weight.shape[0] // 2)
            weight_refs[0][...] = kept
            weight_refs[1][...] = sent.astype(BF)
        else:
            weight_refs[0][...] = d_weight[...]


def output_grad(where, own, came, low):
    seqs, width, rows = low.shape
    model = own.shape[2]
    lines = lax.axis_size("dp")
    one = lambda *shape: pl.BlockSpec((1, *shape), lambda s, w: (s,) + (0,) * len(shape))
    outs = [((model // 2, width), F32), ((model // 2, width), BF)] if lines == 2 else [((model, width), F32)]
    return pl.pallas_call(
        functools.partial(output_kernel, seqs, lines),
        grid_spec=pltpu.PrefetchScalarGridSpec(
            num_scalar_prefetch=1,
            grid=(seqs,),
            in_specs=[one(*own.shape[1:]), one(*own.shape[1:]), one(width, rows)],
            out_specs=[pl.BlockSpec(shape, lambda s, w: (0, 0)) for shape, _ in outs],
            scratch_shapes=[pltpu.VMEM((model, width), F32)],
        ),
        out_shape=[jax.ShapeDtypeStruct(shape, kind) for shape, kind in outs],
        compiler_params=params(),
        cost_estimate=cost(2 * seqs * rows * model * width, 4 * low.size + 4 * own.size),
        name="output_grad",
    )(where, own, came, low)


def turn(where, own, came, weight, full, lse):
    seqs, width, rows = full.shape
    pairs = width // PAIR
    one = lambda *shape: pl.BlockSpec((1, *shape), lambda s, w: (s,) + (0,) * len(shape))
    whole = lambda *shape: pl.BlockSpec(shape, lambda s, w: (0, 0))
    pack_shape = (pairs * (PAIR + 16), rows)
    return pl.pallas_call(
        functools.partial(turn_kernel, pairs, seqs),
        grid_spec=pltpu.PrefetchScalarGridSpec(
            num_scalar_prefetch=1,
            grid=(seqs,),
            in_specs=[
                one(*own.shape[1:]),
                one(*own.shape[1:]),
                whole(*weight.shape),
                one(width, rows),
                one(pairs, 2, rows),
            ],
            out_specs=[whole(*pack_shape)] * seqs,
            scratch_shapes=[pltpu.VMEM(pack_shape, BF)],
        ),
        out_shape=[jax.ShapeDtypeStruct(pack_shape, BF)] * seqs,
        compiler_params=params(),
        cost_estimate=cost(2 * seqs * rows * weight.size, 6 * full.size + 4 * own.size),
        name="turn",
    )(where, own, came, weight, full, lse)


def gelu_parts(u):
    density = jnp.exp(-0.5 * u * u)
    t = 1.0 / (1.0 + (0.3275911 / math.sqrt(2.0)) * jnp.abs(u))
    series = t * (
        0.254829592
        + t * (-0.284496736 + t * (1.421413741 + t * (-1.453152027 + t * 1.061405429)))
    )
    tail = 0.5 * series * density
    share = jnp.where(u < 0.0, tail, 1.0 - tail)
    return u * share, share + u * (density * (1.0 / math.sqrt(2.0 * math.pi)))


def feed_kernel(chunk, half, own_ref, came_ref, w_in, bias, w_out, active_ref, slope_ref, mine_ref, other_ref):
    step = pl.program_id(0)
    rows = jnp.where(step < half, own_ref[...], came_ref[...])
    part = None
    for start in range(0, w_in.shape[1], chunk):
        at = slice(start, start + chunk)
        inner = dot(rows, w_in[:, at], NN) + bias[:, at]
        active, slope = gelu_parts(inner)
        active = active.astype(BF)
        active_ref[:, at] = active
        slope_ref[:, at] = slope.astype(BF)
        term = dot(active, w_out[:, at], NT)
        part = term if part is None else part + term

    @pl.when(step < half)
    def _():
        mine_ref[...] = part

    @pl.when(step >= half)
    def _():
        other_ref[...] = part.astype(BF)


def row_specs(block, half, width):
    own = pl.BlockSpec((block, width), lambda i, *c: (jnp.minimum(i, half - 1), 0))
    came = pl.BlockSpec((block, width), lambda i, *c: (jnp.maximum(i - half, 0), 0))
    return own, came


def feed(own, came, w_in, bias, w_out):
    count, width = own.shape
    units = w_in.shape[1]
    block = min(FEED_ROWS, count)
    half = count // block
    whole = lambda i: (0, 0)
    by_row = lambda i: (i, 0)
    own_spec, came_spec = row_specs(block, half, width)
    return pl.pallas_call(
        functools.partial(feed_kernel, units // 3 if units % 384 == 0 else units, half),
        grid=(2 * half,),
        in_specs=[
            own_spec,
            came_spec,
            pl.BlockSpec((width, units), whole, pipeline_mode=pl.Buffered(1)),
            pl.BlockSpec((1, units), whole),
            pl.BlockSpec((width, units), whole, pipeline_mode=pl.Buffered(1)),
        ],
        out_specs=[pl.BlockSpec((block, units), by_row), pl.BlockSpec((block, units), by_row), own_spec, came_spec],
        out_shape=[
            jax.ShapeDtypeStruct((2 * count, units), BF),
            jax.ShapeDtypeStruct((2 * count, units), BF),
            jax.ShapeDtypeStruct((count, width), F32),
            jax.ShapeDtypeStruct((count, width), BF),
        ],
        compiler_params=params(),
        cost_estimate=cost(8 * count * width * units, 4 * width * units + 8 * count * units + 12 * count * width, 2 * count * units),
        name="feed",
    )(own, came, w_in, bias, w_out)


def feed_back_kernel(half, lines, where, low_own, low_came, own_ref, came_ref, active_ref, slope_ref, w_in, w_out, *refs):
    mine_ref, other_ref, d_bias_ref = refs[:3]
    weight_refs, (d_in, d_out) = refs[3:-2], refs[-2:]
    step = pl.program_id(0)
    units = w_in.shape[1]

    @pl.when(step == 0)
    def _():
        d_in[...] = jnp.zeros_like(d_in)
        d_out[...] = jnp.zeros_like(d_out)
        d_bias_ref[...] = jnp.zeros_like(d_bias_ref)

    low = jnp.where(step < half, low_own[...], low_came[...])
    rows = jnp.where(step < half, own_ref[...], came_ref[...])
    inner = (dot(low, w_out[...], NN) * slope_ref[...].astype(F32)).astype(BF)
    part = dot(inner, w_in[...], NT)
    d_out[...] += dot(low, active_ref[...], TN)
    d_in[...] += dot(rows, inner, TN)
    d_bias_ref[...] += jnp.sum(inner.astype(F32), axis=0, keepdims=True)

    @pl.when(step < half)
    def _():
        mine_ref[...] = part

    @pl.when(step >= half)
    def _():
        other_ref[...] = part.astype(BF)

    @pl.when(step == 2 * half - 1)
    def _():
        for total, cut in ((d_in, slice(0, units)), (d_out, slice(units, 2 * units))):
            if lines == 2:
                kept, sent = own_rows(where[1], total, total.shape[0] // 2)
                weight_refs[0][:, cut] = kept.astype(BF)
                weight_refs[1][:, cut] = sent.astype(BF)
            else:
                weight_refs[0][:, cut] = total[...].astype(BF)


def feed_back(where, low_own, low_came, own, came, active, slope, w_in, w_out):
    count, width = own.shape
    units = w_in.shape[1]
    block = min(FEED_ROWS, count)
    half = count // block
    whole = lambda i, *c: (0, 0)
    by_row = lambda i, *c: (i, 0)
    once = pl.Buffered(1)
    lines = lax.axis_size("dp")
    own_spec, came_spec = row_specs(block, half, width)
    d_shape = (width // 2 if lines == 2 else width, 2 * units)
    d_count = 2 if lines == 2 else 1
    return pl.pallas_call(
        functools.partial(feed_back_kernel, half, lines),
        grid_spec=pltpu.PrefetchScalarGridSpec(
            num_scalar_prefetch=1,
            grid=(2 * half,),
            in_specs=[
                own_spec,
                came_spec,
                own_spec,
                came_spec,
                pl.BlockSpec((block, units), by_row),
                pl.BlockSpec((block, units), by_row),
                pl.BlockSpec((width, units), whole, pipeline_mode=once),
                pl.BlockSpec((width, units), whole, pipeline_mode=once),
            ],
            out_specs=[own_spec, came_spec, pl.BlockSpec((1, units), whole)]
            + [pl.BlockSpec(d_shape, whole, pipeline_mode=once)] * d_count,
            scratch_shapes=[pltpu.VMEM((width, units), F32), pltpu.VMEM((width, units), F32)],
        ),
        out_shape=[
            jax.ShapeDtypeStruct((count, width), F32),
            jax.ShapeDtypeStruct((count, width), BF),
            jax.ShapeDtypeStruct((1, units), F32),
        ]
        + [jax.ShapeDtypeStruct(d_shape, BF)] * d_count,
        compiler_params=params(),
        cost_estimate=cost(16 * count * width * units, 8 * width * units + 8 * count * units + 16 * count * width),
        name="feed_back",
    )(where, low_own, low_came, own, came, active, slope, w_in, w_out)


def centre(values):
    middle = values - jnp.mean(values, axis=-1, keepdims=True)
    scale = lax.rsqrt(jnp.mean(middle * middle, axis=-1, keepdims=True) + EPSILON)
    return middle * scale, scale


def back_through(weighted, normal, scale):
    first = jnp.mean(weighted, axis=-1, keepdims=True)
    second = jnp.mean(weighted * normal, axis=-1, keepdims=True)
    return (weighted - first - normal * second) * scale


def first_kernel(x_ref, mine_ref, came_ref, vec_ref, normal_ref, scale_ref, low_ref):
    sums = x_ref[...].astype(F32) + (mine_ref[...] + came_ref[...].astype(F32)) + vec_ref[0:1, :]
    normal, scale = centre(sums)
    normal_ref[...] = normal
    scale_ref[...] = scale
    low_ref[...] = (normal * vec_ref[1:2, :] + vec_ref[2:3, :]).astype(BF)


def second_kernel(per_seq, counts, normal_ref, mine_ref, came_ref, cot_ref, vec_ref, out_ref, grad_ref, low_ref, sums_ref):
    step = pl.program_id(0)
    block = normal_ref.shape[0]
    valid = counts[step // per_seq] - (step % per_seq) * block
    keep = lax.broadcasted_iota(jnp.int32, normal_ref.shape, 0) < valid

    @pl.when(step == 0)
    def _():
        sums_ref[...] = jnp.zeros_like(sums_ref)

    first = normal_ref[...] * vec_ref[1:2, :] + vec_ref[2:3, :]
    sums = first + (mine_ref[...] + came_ref[...].astype(F32)) + vec_ref[3:4, :]
    normal, scale = centre(sums)
    out_ref[...] = jnp.where(keep, normal * vec_ref[4:5, :] + vec_ref[5:6, :], 0.0)
    out_grad = jnp.where(keep, cot_ref[...].astype(F32), 0.0)
    grad = back_through(out_grad * vec_ref[4:5, :], normal, scale)
    grad_ref[...] = grad
    low_ref[...] = grad.astype(BF)
    sums_ref[0:1, :] += jnp.sum(out_grad * normal, axis=0, keepdims=True)
    sums_ref[1:2, :] += jnp.sum(out_grad, axis=0, keepdims=True)
    sums_ref[2:3, :] += jnp.sum(grad, axis=0, keepdims=True)


def first_back_kernel(grad_ref, mine_ref, came_ref, normal_ref, scale_ref, vec_ref, out_ref, low_ref, sums_ref):
    @pl.when(pl.program_id(0) == 0)
    def _():
        sums_ref[...] = jnp.zeros_like(sums_ref)

    given = grad_ref[...] + (mine_ref[...] + came_ref[...].astype(F32))
    normal = normal_ref[...]
    grad = back_through(given * vec_ref[1:2, :], normal, scale_ref[...])
    out_ref[...] = grad
    low_ref[...] = grad.astype(BF)
    sums_ref[0:1, :] += jnp.sum(given * normal, axis=0, keepdims=True)
    sums_ref[1:2, :] += jnp.sum(given, axis=0, keepdims=True)
    sums_ref[2:3, :] += jnp.sum(grad, axis=0, keepdims=True)


def row_call(kernel, name, block, count, width, inputs, whole_inputs, outs, sums, counts=None):
    by_row = lambda i, *c: (i, 0)
    whole = lambda i, *c: (0, 0)
    in_specs = [pl.BlockSpec((block, a.shape[1]), by_row) for a in inputs]
    in_specs += [pl.BlockSpec(a.shape, whole) for a in whole_inputs]
    out_specs = [pl.BlockSpec((block, w), by_row) for w, _ in outs]
    out_shape = [jax.ShapeDtypeStruct((count, w), t) for w, t in outs]
    if sums:
        out_specs.append(pl.BlockSpec((8, width), whole))
        out_shape.append(jax.ShapeDtypeStruct((8, width), F32))
    prefetch = 0 if counts is None else 1
    moved = sum(a.size * a.dtype.itemsize for a in inputs) + sum(count * w * 4 for w, _ in outs)
    return pl.pallas_call(
        kernel,
        grid_spec=pltpu.PrefetchScalarGridSpec(
            num_scalar_prefetch=prefetch, grid=(count // block,), in_specs=in_specs, out_specs=out_specs
        ),
        out_shape=out_shape,
        compiler_params=params(),
        cost_estimate=cost(20 * count * width, moved),
        name=name,
    )(*(() if counts is None else (counts,)), *inputs, *whole_inputs)


def interleaved(key, value):
    width = key.shape[1]
    pieces = []
    for start in range(0, width, PAIR):
        pieces += [key[:, start : start + PAIR], value[:, start : start + PAIR]]
    return jnp.concatenate(pieces, axis=1)


def apart(both):
    keys, values = [], []
    for start in range(0, both.shape[1], 2 * PAIR):
        keys.append(both[:, start : start + PAIR])
        values.append(both[:, start + PAIR : start + 2 * PAIR])
    return jnp.concatenate(keys, axis=1), jnp.concatenate(values, axis=1)


def on_device(
    block_input,
    lengths,
    cotangent,
    query_weight,
    query_bias,
    key_weight,
    value_weight,
    value_bias,
    output_weight,
    output_bias,
    first_gain,
    first_shift,
    inner_weight,
    inner_bias,
    outer_weight,
    closing_offset_vector,
    second_gain,
    second_shift,
):
    seqs, local, width = block_input.shape
    chip = 2 * local
    spots = lax.axis_size("ctx")
    spot = lax.axis_index("ctx")
    part = lax.axis_index("tp")
    core, side = part % 2, part // 2
    is_upper_core, is_upper_side = core == 1, side == 1
    span = local * lax.axis_size("tp")
    heads_width = query_weight.shape[1]
    unit_width = inner_weight.shape[1]
    count = seqs * local

    def other_core(value, **ties):
        return swap(value, "tp", 1, **ties)

    def other_side(value, **ties):
        return swap(value, "tp", 2, **ties)

    def flat(value):
        return value.reshape(-1, value.shape[-1])

    starts = jnp.stack([(spot ^ k) * span + side * chip for k in range(spots)])
    key_counts = jnp.clip(lengths[:, None] - starts[None, :], 0, chip)
    facts = jnp.stack([spot, core, lax.axis_index("dp")]).astype(jnp.int32)
    counts = jnp.concatenate([key_counts.astype(jnp.int32), jnp.broadcast_to(facts, (seqs, 3))], axis=1)
    row_counts = jnp.clip(lengths - (spot * span + part * local), 0, local).astype(jnp.int32)
    where = jnp.stack([core, lax.axis_index("dp")]).astype(jnp.int32)

    def together(*values):
        return lax.optimization_barrier(values)

    def over_spots(value, done=()):
        return [swap(value, "ctx", k, (), done) for k in range(1, spots)]

    lines = lax.axis_size("dp")
    own_width = 2 * heads_width
    attention_shard = pack([[(query_weight, False), (key_weight, False), (value_weight, False)]])
    biases = jnp.concatenate([query_bias, value_bias, inner_bias])[None, :]
    x_rows = [block_input[s] for s in range(seqs)]

    def send_near(own):
        return [swap(own, "ctx", 2), swap(own, "ctx", 1)] if spots == 4 else over_spots(own)

    def send_last(own, far):
        return [
            lax.ppermute(own, "ctx", [(1, 2), (2, 1)]),
            lax.ppermute(far, "ctx", [(2, 3), (1, 0)]),
        ]

    def finish(nears, lasts):
        if spots != 4:
            return nears
        in_middle = jnp.logical_or(spot == 1, spot == 2)
        return [nears[1], nears[0], jnp.where(in_middle, lasts[0], lasts[1])]

    came, across, *near = together(other_core(block_input), other_side(block_input), *over_spots(attention_shard))
    first_out = after(x_rows[0], *near)
    (attention_near,) = stack([attention_shard, *near])
    diagonal = [(d * 4 + t, (1 - d) * 4 + (t ^ 2)) for d in range(2) for t in range(4)]
    over_both = [lax.ppermute(attention_near, ("dp", "tp"), diagonal)] if lines == 2 else []
    attention_other, attention_line, *nears = together(
        other_side(attention_near), swap(attention_near, "dp", 1), *over_both, *send_near(first_out)
    )
    if lines == 2:
        other_line, *nears = nears
    cores = [other_core(n) for n in nears]
    lasts = send_last(after(x_rows[0], *nears), nears[0]) if spots == 4 else []
    biases_came = other_side(after(biases, *nears))
    biases_came, *rest = together(biases_came, *lasts, *cores)
    lasts, cores = rest[: len(lasts)], rest[len(lasts) :]
    arrived = [finish(nears, lasts)]
    if spots == 4:
        cores = [cores[1], cores[0], other_core(arrived[0][2])]
    if lines == 2:
        attention_all = [[attention_near, attention_other], [attention_line, other_line]]
    else:
        attention_all = over_dp([attention_near, attention_other])
    query_full, kv_full = place(attention_all, [heads_width] * 3, [(0,), (1, 2)])

    query_b = ordered(biases[:, :heads_width], biases_came[:, :heads_width], is_upper_side, 1)
    cut = slice(heads_width, own_width)
    value_b = ordered(biases[:, cut], biases_came[:, cut], is_upper_side, 1)
    cut = slice(own_width, None)
    inner_b = ordered(biases[:, cut], biases_came[:, cut], is_upper_side, 1)
    kv_bias = interleaved(jnp.zeros_like(value_b), value_b)

    pieces = [[(x_rows[0], came[0])] + list(zip(arrived[0], cores))]
    across_core = other_core(across[0])
    late_weights = together(output_weight, inner_weight, outer_weight, *nears)
    feed_shard = pack([[(late_weights[0], True), (late_weights[1], False)], [(late_weights[2], True)]])
    feed_shard = after(feed_shard, arrived[0][-1])
    feed_near = over_spots(feed_shard)
    second_nears = send_near(after(x_rows[1], arrived[0][-1]))
    weights = (query_full, kv_full, query_b, kv_bias)
    q, made, own, packed, lse = attend(counts[0], seqs, 0, pieces[0] + [(across[0], across_core)], weights, ())
    queries, kv = [q], [made]
    packs = [packed]

    own, *feed_near = together(own, *feed_near)
    near_a, near_b = stack([feed_shard] + feed_near, feed_shard.shape[1] - unit_width - -unit_width % 128)
    sending_a, sending_b = other_side(near_a), swap(near_b, "dp", 1)
    nears = together(near_a, *second_nears)[1:]
    across_core = other_core(across[1])
    cores = [other_core(n) for n in nears]
    lasts = send_last(after(x_rows[1], own), nears[0]) if spots == 4 else []
    other_a, line_b, *rest = together(sending_a, sending_b, *lasts, *cores)
    packs[0] = other_side(after(packs[0], other_a))
    lasts, cores = rest[: len(lasts)], rest[len(lasts) :]
    arrived.append(finish(nears, lasts))
    if spots == 4:
        cores = [cores[1], cores[0], other_core(arrived[1][2])]
    pieces.append([(x_rows[1], came[1])] + list(zip(arrived[1], cores)))
    if lines == 2:
        last_b = [near_b, line_b]
        sent_a = [swap(after(a, line_b), "dp", 1) for a in (near_a, other_a)]
        sent_b = [other_side(after(b, other_a)) for b in last_b]
    q, made, own, packed, lse = attend(counts[1], seqs, 1, pieces[1] + [(across[1], across_core)], weights, (own, lse))
    queries.append(q)
    kv.append(made)
    buffers = (own, lse)
    packs.append(other_side(packed))
    if lines == 2:
        sent = together(*sent_a, *sent_b, own)
        sent_a, sent_b = list(sent[:2]), list(sent[2:4])
        all_a = [[near_a, other_a], sent_a]
        all_b = [[near_b, sent_b[0]], [line_b, sent_b[1]]]
    else:
        all_a, all_b = over_dp([near_a, other_a]), over_dp([near_b, other_side(near_b)])
    output_full, inner_full = place(all_a, [heads_width, unit_width], [(0,), (1,)])
    (outer_full,) = place(all_b, [unit_width], [(0,)])

    vectors = jnp.stack([output_bias, first_gain, first_shift, closing_offset_vector, second_gain, second_shift])
    vectors = jnp.concatenate([vectors, jnp.zeros((2, width), F32)])
    block = local

    attended, attended_low, mine, other, lse_all = merge(where, *buffers, packs, output_full)
    normal, spread, first_low = row_call(
        first_kernel,
        "first_norm",
        block,
        count,
        width,
        [flat(block_input), flat(mine), flat(other_core(other))],
        [vectors],
        [(width, F32), (1, F32), (width, BF)],
        False,
    )
    first_came = other_core(first_low)
    active, slope, mine, other = feed(first_low, first_came, inner_full, inner_b, outer_full)
    output, second_grad, outer_low, second_sums = row_call(
        functools.partial(second_kernel, local // block),
        "second_norm",
        block,
        count,
        width,
        [normal, mine, other_core(other), flat(cotangent)],
        [vectors],
        [(width, F32), (width, F32), (width, BF)],
        True,
        row_counts,
    )
    mine, other, d_inner_bias, *d_feed = feed_back(
        where, outer_low, other_core(outer_low), first_low, first_came, active, slope, inner_full, outer_full
    )
    first_grad, attn_low, first_sums = row_call(
        first_back_kernel,
        "first_norm_back",
        block,
        count,
        width,
        [second_grad, mine, other_core(other), normal, spread],
        [vectors],
        [(width, F32), (width, BF)],
        True,
    )
    attn_low = attn_low.reshape(seqs, local, width)
    attn_came = other_core(attn_low)
    g_own = turn(where, attn_low, attn_came, output_full, attended, lse_all)
    d_output = output_grad(where, after(attn_low, *g_own), attn_came, attended_low)
    g_oth = [other_side(g) for g in g_own]

    lines = lax.axis_size("dp")

    def over_lines(made, done=()):
        if lines == 2:
            return made[0], swap(made[1], "dp", 1, (), done)
        value, place_at = made[0].astype(F32), lax.axis_index("dp")
        for bit in reversed(bits_of("dp")):
            mine, sent = halves(value, (place_at & bit) != 0, 0)
            term = swap(sent.astype(BF), "dp", bit, (), done)
            value = mine + term.astype(F32)
        return mine, term

    def sides_of(pair, width_of_side):
        return [(pair, 0, width_of_side)], [(pair, width_of_side, width_of_side)]

    def back(s, g_in, before):
        return attend_back(
            counts[s], queries[s], g_own[s], g_in, kv[s], kv_full, pieces[s], before, s == seqs - 1
        )

    def by_spot(mine, came):
        total = (mine + came.astype(F32)).reshape(spots, local, width)
        return total[0], [total[k].astype(BF) for k in range(1, spots)]

    shared = jnp.concatenate([second_sums[:3], first_sums[:3]])
    shared_came = other_core(shared)
    output_mine, output_came = over_lines(d_output)
    g_in, shared_came = together(g_oth[0], shared_came)
    early = jnp.concatenate([(shared + shared_came).reshape(1, -1), d_inner_bias], axis=1)
    early_near = swap(early, "ctx", 1)
    own, oth, mine, other, kv_bias_sum, *kv_grads = back(0, g_in, None)
    dq_own = [own]
    oth, other, g_oth[1], output_came, early_near = together(oth, other, g_oth[1], output_came, early_near)
    output_pair = (output_mine, output_came)
    dq_came_0 = other_side(oth)
    kept_0, sent_0 = by_spot(mine, other_core(other))
    early = early + early_near
    early_far = [swap(early, "ctx", bit) for bit in bits_of("ctx")[1:]]
    feed_pairs = [over_lines(d_feed, (kv_bias_sum,))]
    feed_kept, feed_sent = fold_sides(
        feed_pairs,
        [
            sides_of(0, unit_width),
            ([(0, 2 * unit_width, unit_width)], [(0, 3 * unit_width, unit_width)]),
        ],
    )
    feed_term = other_side(feed_sent)
    came_0 = [swap(t, "ctx", k + 1) for k, t in enumerate(sent_0)]
    g_in, dq_came_0, early, *rest = together(g_oth[1], dq_came_0, early, *early_far, feed_sent, *sent_0)
    early = sum(rest[: len(early_far)], early)
    own, oth, mine, other, kv_bias_sum, *kv_grads = back(1, g_in, (kv_grads[0], kv_bias_sum))
    dq_own.append(own)

    oth, other, feed_term, *rest = together(oth, other, feed_term, *came_0, *kv_grads)
    came_0, kv_grads = rest[: spots - 1], rest[spots - 1 :]
    dq_came_1 = other_side(oth)
    kept_1, sent_1 = by_spot(mine, other_core(other))
    feed_all_rows = add_low(feed_kept, feed_term)
    feed_spread = lax.all_to_all(feed_all_rows, "ctx", split_axis=0, concat_axis=0, tiled=True)
    dq_came = [dq_came_0, after(dq_came_1, feed_all_rows, *sent_1)]
    kv_pair = over_lines(kv_grads)
    mine, other, query_bias_sum, *query_grads = query_back(
        where, dq_own, dq_came, x_rows, [came[s] for s in range(seqs)], query_full
    )
    query_term = (mine + other_core(other).astype(F32)).reshape(seqs, local, width)
    query_pair = over_lines(query_grads)
    value_bias_sum = apart(kv_bias_sum)[1]
    vector = jnp.concatenate([early, query_bias_sum.reshape(1, -1), value_bias_sum], axis=1)
    for bit in bits_of("dp"):
        vector = vector + swap(vector, "dp", bit)
    if spots == 4:
        near_1, far_1, last_1 = sent_1
        first_1 = [
            lax.ppermute(last_1, "ctx", [(3, 2), (0, 1)]),
            lax.ppermute(last_1, "ctx", [(1, 2), (2, 1)]),
        ]
    else:
        first_1 = [swap(sent_1[0], "ctx", 1)]
    if lines == 2:
        query_last, kv_last, vector, *first_1 = together(query_pair[1], kv_pair[1], vector, *first_1)
        query_pair, kv_pair = (query_pair[0], query_last), (kv_pair[0], kv_last)
    if spots == 4:
        passed, middle = first_1
        far_1 = (far_1.astype(F32) + passed.astype(F32)).astype(BF)
        came_1 = [middle, swap(far_1, "ctx", 2), swap(near_1, "ctx", 1)]
        query_pair = (query_pair[0], after(query_pair[1], far_1))
    else:
        came_1 = first_1 + [swap(t, "ctx", k + 2) for k, t in enumerate(sent_1[1:])]

    def side_cuts(pair, offset):
        cuts = []
        for start in (0, heads_width):
            pieces_of, at = [], start
            while at < start + heads_width:
                w = min(PAIR - at % PAIR, start + heads_width - at)
                pieces_of.append((pair, 2 * (at - at % PAIR) + offset + at % PAIR, w))
                at += w
            cuts.append(pieces_of)
        return tuple(cuts)

    kept, sent = fold_sides(
        [query_pair, kv_pair, output_pair],
        [sides_of(0, heads_width), side_cuts(1, 0), side_cuts(1, PAIR), sides_of(2, heads_width)],
    )
    vector_came = other_side(vector)
    term, feed_spread, vector_came, *rest = together(other_side(sent), feed_spread, vector_came, *came_1[1:])
    came_1[1:] = rest
    vector = vector + vector_came
    early, vector = vector[:, : early.shape[1]], vector[:, early.shape[1] :]
    spare = -vector.shape[1] % kept.shape[1]
    vector = jnp.pad(vector, ((0, 0), (0, spare))).reshape(-1, kept.shape[1])
    rows = fold_spots(kept, term, vector)
    terms = [swap(t, "ctx", k + 1) for k, t in enumerate(rows[1:])]
    feed_owned = jnp.sum(feed_spread.reshape(spots, -1, feed_spread.shape[1]).astype(F32), axis=0)
    size = rows[0].shape[0]
    owned = rows[0] + sum(t[:size].astype(F32) for t in terms)
    vector = (vector + sum(unpacked_rows(t[size:], vector.shape[0]) for t in terms)).reshape(-1)
    first_grad = first_grad.reshape(seqs, local, width)
    input_grad = jnp.stack(
        [
            first_grad[s] + query_term[s] + kept + sum(t.astype(F32) for t in came)
            for s, (kept, came) in enumerate(((kept_0, came_0), (kept_1, came_1)))
        ]
    )

    early = early[0]
    shared = early[: 6 * width].reshape(6, width)

    def own_side(value, start, size):
        return jnp.where(is_upper_side, value[start + size : start + 2 * size], value[start : start + size])

    return (
        output.reshape(seqs, local, width),
        input_grad,
        owned[:, :heads_width],
        own_side(vector, 0, heads_width),
        owned[:, heads_width:own_width],
        owned[:, own_width : own_width + heads_width],
        own_side(vector, own_width, heads_width),
        owned[:, 3 * heads_width : 4 * heads_width].T,
        shared[5],
        shared[3],
        shared[4],
        feed_owned[:, :unit_width],
        own_side(early, 6 * width, unit_width),
        feed_owned[:, unit_width : 2 * unit_width].T,
        shared[2],
        shared[0],
        shared[1],
    )


def solution(mesh):
    rows = P("dp", ("ctx", "tp"), None)
    into = P(("dp", "ctx"), "tp")
    out_of = P("tp", ("dp", "ctx"))
    split, whole = P("tp"), P()
    return jax.shard_map(
        on_device,
        mesh=mesh,
        in_specs=(
            rows, P("dp"), rows, into, split, into, into, split, out_of, whole, whole, whole,
            into, split, out_of, whole, whole, whole,
        ),
        out_specs=(
            rows, rows, into, split, into, into, split, out_of, whole, whole, whole,
            into, split, out_of, whole, whole, whole,
        ),
        check_vma=False,
    )
```

```python
import functools
import math

import jax
import jax.numpy as jnp
from jax import lax
from jax.experimental import pallas as pl
from jax.experimental.pallas import tpu as pltpu
from jax.sharding import PartitionSpec as P

HD = 64
PAIR = 2 * HD
EPSILON = 1e-12
NEGATIVE = -1e30
LARGEST = 1e30
BF = jnp.bfloat16
F32 = jnp.float32
VMEM_LIMIT = 56 << 20
FEED_ROWS = 256

NN = (((1,), (0,)), ((), ()))
NT = (((1,), (1,)), ((), ()))
TN = (((0,), (0,)), ((), ()))


def dot(a, b, dims):
    return lax.dot_general(a, b, dims, preferred_element_type=F32)


def params():
    return pltpu.CompilerParams(vmem_limit_bytes=VMEM_LIMIT)


def cost(flops, moved, transcendentals=0):
    return pl.CostEstimate(flops=int(flops), bytes_accessed=int(moved), transcendentals=int(transcendentals))


def after(value, *others):
    if not others:
        return value
    return lax.optimization_barrier((value, *others))[0]


def swap(value, axis, bit, start=(), done=()):
    count = lax.axis_size(axis)
    return after(lax.ppermute(after(value, *start), axis, [(i, i ^ bit) for i in range(count)]), *done)


def bits_of(axis):
    count = lax.axis_size(axis)
    return [1 << k for k in range(count.bit_length() - 1)]


def halves(value, upper, dim):
    size = value.shape[dim] // 2
    at = upper.astype(jnp.int32) * size
    mine = lax.dynamic_slice_in_dim(value, at, size, dim)
    return mine, lax.dynamic_slice_in_dim(value, size - at, size, dim)


def ordered(mine, other, upper, dim):
    return jnp.concatenate([jnp.where(upper, other, mine), jnp.where(upper, mine, other)], axis=dim)


def call(kernel, name, outs, *arrays, prefetch=None, scratch=(), flops=0):
    spec = lambda shape: pl.BlockSpec(shape, lambda i, *c: (0,) * len(shape))
    arrays_moved = sum(a.size * a.dtype.itemsize for a in arrays) + sum(4 * math.prod(shape) for shape, _ in outs)
    return pl.pallas_call(
        kernel,
        grid_spec=pltpu.PrefetchScalarGridSpec(
            num_scalar_prefetch=0 if prefetch is None else 1,
            grid=(1,),
            in_specs=[spec(a.shape) for a in arrays],
            out_specs=[spec(shape) for shape, _ in outs],
            scratch_shapes=list(scratch),
        ),
        out_shape=[jax.ShapeDtypeStruct(shape, kind) for shape, kind in outs],
        compiler_params=params(),
        cost_estimate=cost(flops, arrays_moved),
        name=name,
    )(*(() if prefetch is None else (prefetch,)), *arrays)


def fits(rows):
    return rows % 16 == 0


def pack(groups):
    flat = [piece for group in groups for piece in group]
    widths = [sum(w.shape[0] if t else w.shape[1] for w, t in group) for group in groups]
    first, turned = flat[0]
    rows = first.shape[1] if turned else first.shape[0]

    def joined(values):
        values, out = list(values), []
        for group, width in zip(groups, widths):
            out += [values.pop(0) for _ in group]
            if -width % 128:
                out.append(jnp.zeros((rows, -width % 128), F32))
        return jnp.concatenate(out, axis=1).astype(BF)

    if not fits(rows):
        return joined(w.T if t else w for w, t in flat)

    def kernel(*refs):
        refs[-1][...] = joined(r[...].T if t else r[...] for r, (_, t) in zip(refs, flat))

    total = sum(w + -w % 128 for w in widths)
    return call(kernel, "pack", [((rows, total), BF)], *[w for w, _ in flat])[0]


def stack(parts, cuts=None):
    rows, width = parts[0].shape
    ranges = [(0, width)] if cuts is None else [(0, cuts), (cuts, width)]
    if not fits(rows):
        whole = jnp.concatenate(parts, axis=0)
        return [whole[:, start:stop] for start, stop in ranges]

    def kernel(*refs):
        for k, ref in enumerate(refs[: len(parts)]):
            for out, (start, stop) in zip(refs[len(parts) :], ranges):
                out[k * rows : k * rows + rows, :] = ref[:, start:stop]

    return call(kernel, "stack", [((rows * len(parts), stop - start), BF) for start, stop in ranges], *parts)


def over_dp(arrays, done=()):
    found = [arrays]
    for bit in bits_of("dp"):
        found = found + [[swap(a, "dp", bit, (), done) for a in one] for one in found]
    return found


def place(found, widths, joined):
    spots, spot = lax.axis_size("ctx"), lax.axis_index("ctx")
    line, side = lax.axis_index("dp"), lax.axis_index("tp") // 2
    lines = len(found)
    starts = [sum(widths[:k]) for k in range(len(widths))]
    block = found[0][0].shape[0]
    rows = block // spots
    cuts = list(zip(starts, widths))
    shapes = [(block * lines, 2 * sum(widths[m] for m in members)) for members in joined]
    if not fits(rows):
        order = ((jnp.arange(lines)[:, None] ^ line) * spots + (jnp.arange(spots)[None, :] ^ spot)).reshape(-1)
        own, oth = (
            jnp.stack([f[h] for f in found]).reshape(lines * spots, rows, -1)[order].reshape(lines * block, -1)
            for h in range(2)
        )
        low, high = jnp.where(side == 1, oth, own), jnp.where(side == 1, own, oth)
        full = [jnp.concatenate([low[:, t : t + w], high[:, t : t + w]], axis=1) for t, w in cuts]
        return [full[m[0]] if len(m) == 1 else interleaved(full[m[0]], full[m[1]]) for m in joined]

    def kernel(where, *refs):
        outs = refs[2 * lines :]
        upper = where[2] == 1
        for k in range(lines):
            own_ref, oth_ref = refs[2 * k], refs[2 * k + 1]
            for c in range(spots):
                came = pl.ds(pl.multiple_of((where[0] ^ c) * rows, rows), rows)
                to = pl.ds(pl.multiple_of(((where[1] ^ k) * spots + c) * rows, rows), rows)
                own, oth = own_ref[came, :], oth_ref[came, :]
                low, high = jnp.where(upper, oth, own), jnp.where(upper, own, oth)
                full = [jnp.concatenate([low[:, t : t + w], high[:, t : t + w]], axis=1) for t, w in cuts]
                for out, members in zip(outs, joined):
                    if len(members) == 1:
                        out[to, :] = full[members[0]]
                    else:
                        both = []
                        for p in range(0, full[members[0]].shape[1], PAIR):
                            both += [full[m][:, p : p + PAIR] for m in members]
                        out[to, :] = jnp.concatenate(both, axis=1)

    where = jnp.stack([spot, line, side]).astype(jnp.int32)
    flat = [a for one in found for a in one]
    return call(kernel, "place", [(shape, BF) for shape in shapes], *flat, prefetch=where)


def fold_sides(pairs, cuts, kind=F32):
    rows = pairs[0][0].shape[0]
    width = sum(w for low, _ in cuts for _, _, w in low)
    spare = -width % 128
    width += spare
    side = lax.axis_index("tp") // 2

    def both(totals):
        end = [jnp.zeros((totals[0].shape[0], spare), F32)] if spare else []
        low = jnp.concatenate([totals[p][:, t : t + w] for cut, _ in cuts for p, t, w in cut] + end, axis=1)
        high = jnp.concatenate([totals[p][:, t : t + w] for _, cut in cuts for p, t, w in cut] + end, axis=1)
        return low, high

    if not fits(rows):
        low, high = both([a.astype(F32) + b.astype(F32) for a, b in pairs])
        return jnp.where(side == 1, high, low).astype(kind), jnp.where(side == 1, low, high).astype(BF)

    block = rows // 2 if fits(rows // 2) else rows
    steps = rows // block

    def kernel(where, *refs):
        kept, sent = refs[2 * len(pairs) :]
        totals = [refs[2 * k][...].astype(F32) + refs[2 * k + 1][...].astype(F32) for k in range(len(pairs))]
        low, high = both(totals)
        upper = where[0] == 1
        kept[...] = jnp.where(upper, high, low).astype(kind)
        sent[...] = jnp.where(upper, low, high).astype(BF)

    spec = lambda w: pl.BlockSpec((block, w), lambda i, c: (i, 0))
    flat = [a for pair in pairs for a in pair]
    return pl.pallas_call(
        kernel,
        grid_spec=pltpu.PrefetchScalarGridSpec(
            num_scalar_prefetch=1,
            grid=(steps,),
            in_specs=[spec(a.shape[1]) for a in flat],
            out_specs=[spec(width), spec(width)],
        ),
        out_shape=[jax.ShapeDtypeStruct((rows, width), kind), jax.ShapeDtypeStruct((rows, width), BF)],
        compiler_params=params(),
        cost_estimate=cost(0, sum(a.size * a.dtype.itemsize for a in flat) + 6 * rows * width),
        name="fold_sides",
    )(side.astype(jnp.int32).reshape(1), *flat)


def fold_spots(kept, came, vector):
    spots, spot = lax.axis_size("ctx"), lax.axis_index("ctx")
    rows, width = kept.shape[0] // spots, kept.shape[1]
    count = vector.shape[0]
    below_rows = 3 * count + -3 * count % 16
    if not fits(rows):
        total = kept + came.astype(F32)
        cut = lambda k: lax.dynamic_slice_in_dim(total, (spot ^ k) * rows, rows, 0)
        terms = jnp.concatenate([*in_three(vector), jnp.zeros((below_rows - 3 * count, width), BF)], axis=0)
        return [cut(0)] + [jnp.concatenate([cut(k).astype(BF), terms], axis=0) for k in range(1, spots)]

    def kernel(where, kept_ref, came_ref, vector_ref, own, *outs):
        at = pl.ds(pl.multiple_of(where[0] * rows, rows), rows)
        own[...] = kept_ref[at, :] + came_ref[at, :].astype(F32)
        terms = jnp.concatenate(in_three(vector_ref[...]), axis=0)
        terms = jnp.concatenate([terms, jnp.zeros((below_rows - 3 * count, width), BF)], axis=0)
        for k, out in enumerate(outs):
            at = pl.ds(pl.multiple_of((where[0] ^ (k + 1)) * rows, rows), rows)
            out[:rows, :] = (kept_ref[at, :] + came_ref[at, :].astype(F32)).astype(BF)
            out[rows:, :] = terms

    outs = [((rows, width), F32)] + [((rows + below_rows, width), BF)] * (spots - 1)
    return call(kernel, "fold_spots", outs, kept, came, vector, prefetch=spot.astype(jnp.int32).reshape(1))


def add_low(kept, came):
    if not fits(kept.shape[0] // 2):
        return (kept.astype(F32) + came.astype(F32)).astype(BF)

    def kernel(kept_ref, came_ref, out):
        out[...] = (kept_ref[...].astype(F32) + came_ref[...].astype(F32)).astype(BF)

    rows, width = kept.shape
    spec = pl.BlockSpec((rows // 2, width), lambda i: (i, 0))
    return pl.pallas_call(
        kernel,
        grid=(2,),
        in_specs=[spec, spec],
        out_specs=spec,
        out_shape=jax.ShapeDtypeStruct(kept.shape, BF),
        compiler_params=params(),
        cost_estimate=cost(kept.size, 8 * kept.size),
        name="add_low",
    )(kept, came)


def own_rows(where, value, rows):
    mine = pl.ds(pl.multiple_of(where * rows, rows), rows)
    other = pl.ds(pl.multiple_of((1 - where) * rows, rows), rows)
    return value[mine, :], value[other, :]


def assemble(upper, pieces, held):
    local = pieces[0].shape[0]
    for k in range(len(pieces) // 2):
        mine, came = pieces[2 * k][...], pieces[2 * k + 1][...]
        held[2 * k * local : (2 * k + 1) * local, :] = jnp.where(upper, came, mine)
        held[(2 * k + 1) * local : (2 * k + 2) * local, :] = jnp.where(upper, mine, came)


def query_back_kernel(seqs, lines, where, *refs):
    dq_own, dq_came, own, came = (refs[k * seqs : k * seqs + seqs] for k in range(4))
    weight, mine_ref, other_ref, bias_ref = refs[4 * seqs : 4 * seqs + 4]
    weight_refs, total = refs[4 * seqs + 4 : -1], refs[-1]
    upper = where[0] == 1
    half = own[0].shape[0]
    bias = None
    for s in range(seqs):
        low = (dq_own[s][...] + dq_came[s][...].astype(F32)).astype(BF)
        rows = jnp.concatenate(
            [jnp.where(upper, came[s][...], own[s][...]), jnp.where(upper, own[s][...], came[s][...])], axis=0
        )
        part = dot(low, weight[...], (((0,), (1,)), ((), ())))
        to = slice(s * half, s * half + half)
        mine_ref[to, :] = jnp.where(upper, part[half:], part[:half])
        other_ref[to, :] = jnp.where(upper, part[:half], part[half:]).astype(BF)
        grad = dot(rows, low, (((0,), (1,)), ((), ())))
        total[...] = grad if s == 0 else total[...] + grad
        sums = jnp.sum(low.astype(F32), axis=1, keepdims=True)
        bias = sums if bias is None else bias + sums
    bias_ref[...] = bias
    if lines == 2:
        kept, sent = own_rows(where[1], total, total.shape[0] // 2)
        weight_refs[0][...] = kept
        weight_refs[1][...] = sent.astype(BF)
    else:
        weight_refs[0][...] = total[...]


def query_back(where, dq_own, dq_came, own, came, weight):
    seqs, lines = len(dq_own), lax.axis_size("dp")
    local, width = own[0].shape
    own_width = weight.shape[1]
    outs = [((seqs * local, width), F32), ((seqs * local, width), BF), ((own_width, 1), F32)]
    if lines == 2:
        outs += [((width // 2, own_width), F32), ((width // 2, own_width), BF)]
    else:
        outs += [((width, own_width), F32)]
    return call(
        functools.partial(query_back_kernel, seqs, lines),
        "query_back",
        outs,
        *dq_own,
        *dq_came,
        *own,
        *came,
        weight,
        prefetch=where,
        scratch=[pltpu.VMEM((width, own_width), F32)],
        flops=8 * seqs * local * width * own_width,
    )


def half_lanes(value):
    lane = lax.broadcasted_iota(jnp.int32, value.shape, 1)
    zero = jnp.zeros_like(value)
    return [jnp.where(lane < HD, value, zero), jnp.where(lane >= HD, value, zero)]


def half_rows(value):
    row = lax.broadcasted_iota(jnp.int32, value.shape, 0)
    zero = jnp.zeros_like(value)
    return [jnp.where(row < HD, value, zero), jnp.where(row >= HD, value, zero)]


def top_bits(value):
    spread = value * 65537.0
    return spread - (spread - value)


def in_three(value):
    first = top_bits(value)
    rest = value - first
    second = top_bits(rest)
    return first.astype(BF), second.astype(BF), (rest - second).astype(BF)


def packed_rows(values):
    terms = jnp.concatenate(in_three(values), axis=0)
    return jnp.concatenate([terms, jnp.zeros((16 - terms.shape[0], terms.shape[1]), BF)], axis=0)


def unpacked_rows(packed, count):
    packed = packed.astype(F32)
    return packed[:count] + packed[count : 2 * count] + packed[2 * count : 3 * count]


def below(shape, count):
    return lax.broadcasted_iota(jnp.int32, shape, 0) < count


def attend_kernel(slots, probe, old, counts, *refs):
    pieces = refs[: 2 * slots + 2]
    w_query, w_kv, b_query, b_kv = refs[2 * slots + 2 : 2 * slots + 6]
    queries, kv, o_own, packed, lse_ref, held, top, total, acc, heads = refs[2 * slots + 6 + old :]
    local = pieces[0].shape[0]
    rows = keys = 2 * local

    @pl.when(pl.program_id(0) == 0)
    def _():
        assemble(counts[slots + 1] == 1, pieces, held)

    scale = jnp.asarray(1.0 / math.sqrt(HD), BF)
    for start, to in ((0, 0), (slots * keys, rows)):
        query = (dot(held[start : start + rows, :], w_query[...], NN) + b_query[...]).astype(BF)
        queries[to : to + rows, :] = query * scale
    for h, query in enumerate(half_lanes(queries[...])):
        heads[h] = query

    @pl.loop(0, slots)
    def _(k):
        at = pl.ds(pl.multiple_of(k * keys, keys), keys)

        @pl.when(counts[k] > 0)
        def _():
            kv[at, :] = (dot(held[at, :], w_kv[...], NN) + b_kv[...]).astype(BF)

        @pl.when(counts[k] <= 0)
        def _():
            kv[at, :] = jnp.zeros((keys, 2 * PAIR), BF)

    def block(k):
        at = pl.ds(pl.multiple_of(k * keys, keys), keys)
        return kv[at, :PAIR], kv[at, PAIR:]

    first = pl.ds(pl.multiple_of(counts[slots] * keys, keys), probe)
    for h in range(2):
        top[h] = jnp.max(dot(kv[first, :PAIR], heads[h], NT), axis=0, keepdims=True)
    total[...] = jnp.zeros_like(total)
    acc[...] = jnp.zeros_like(acc)

    def quick(k, h, valid):
        key, value = block(k)
        expo = jnp.exp(dot(key, heads[h], NT) - top[h])
        if valid is not None:
            expo = jnp.where(below(expo.shape, valid), expo, 0.0)
        total[h] += jnp.sum(expo, axis=0, keepdims=True)
        acc[h] += dot(value, expo.astype(BF), TN)

    @pl.loop(0, slots)
    def _(k):
        valid = counts[k]

        @pl.when(valid >= keys)
        def _():
            quick(k, 0, None)
            quick(k, 1, None)

        @pl.when(jnp.logical_and(valid > 0, valid < keys))
        def _():
            pl.loop(0, 2)(lambda h: quick(k, h, valid))

    @pl.when(jnp.logical_not(jnp.max(total[...]) < LARGEST))
    def _():
        total[...] = jnp.zeros_like(total)
        acc[...] = jnp.zeros_like(acc)

        def careful(k, h, valid):
            key, value = block(k)
            scores = dot(key, heads[h], NT)
            scores = jnp.where(below(scores.shape, valid), scores, NEGATIVE)
            before = top[h]
            new = jnp.maximum(before, jnp.max(scores, axis=0, keepdims=True))
            expo = jnp.where(below(scores.shape, valid), jnp.exp(scores - new), 0.0)
            ratio = jnp.exp(before - new)
            total[h] = total[h] * ratio + jnp.sum(expo, axis=0, keepdims=True)
            acc[h] = acc[h] * ratio + dot(value, expo.astype(BF), TN)
            top[h] = new

        @pl.loop(0, slots)
        def _(k):
            valid = counts[k]

            @pl.when(valid > 0)
            def _():
                pl.loop(0, 2)(lambda h: careful(k, h, valid))

    lse = []
    for h in range(2):
        at = slice(h * HD, h * HD + HD)
        part = acc[h, at, :] / total[h]
        o_own[0, at, :] = part[:, :rows]
        packed[at, :] = part[:, rows:].astype(BF)
        lse.append(top[h] + jnp.log(total[h]))
        lse_ref[0, 0, h : h + 1, :] = lse[h][:, :rows]
    packed[PAIR:, :] = packed_rows(jnp.concatenate([l[:, rows:] for l in lse], axis=0))


def attend(counts, seqs, s, pieces, weights, before):
    w_query, w_kv, b_query, b_kv = weights
    slots = len(pieces) - 1
    local, model = pieces[0][0].shape
    rows, width = 2 * local, w_query.shape[1]
    pairs = width // PAIR
    keys = 2 * local
    total = width * 2 * rows * slots * keys
    anywhere = pl.BlockSpec(memory_space=pl.ANY)
    across = lambda p, c: (0, p)
    flat = [p for pair in pieces for p in pair]
    held = ((slots + 1) * keys, model)
    return pl.pallas_call(
        functools.partial(attend_kernel, slots, min(128, keys), len(before)),
        grid_spec=pltpu.PrefetchScalarGridSpec(
            num_scalar_prefetch=1,
            grid=(pairs,),
            in_specs=[pl.BlockSpec((local, model), lambda p, c: (0, 0), pipeline_mode=pl.Buffered(1)) for _ in flat]
            + [
                pl.BlockSpec((model, PAIR), across),
                pl.BlockSpec((model, 2 * PAIR), across),
                pl.BlockSpec((1, PAIR), across),
                pl.BlockSpec((1, 2 * PAIR), across),
            ]
            + [anywhere] * len(before),
            out_specs=[
                pl.BlockSpec((2 * rows, PAIR), across),
                pl.BlockSpec((slots * keys, 2 * PAIR), across),
                pl.BlockSpec((1, PAIR, rows), lambda p, c: (s, p, 0)),
                pl.BlockSpec((PAIR + 16, rows), lambda p, c: (p, 0)),
                pl.BlockSpec((1, 1, 2, rows), lambda p, c: (s, p, 0, 0)),
            ],
            scratch_shapes=[
                pltpu.VMEM(held, BF),
                pltpu.VMEM((2, 1, 2 * rows), F32),
                pltpu.VMEM((2, 1, 2 * rows), F32),
                pltpu.VMEM((2, PAIR, 2 * rows), F32),
                pltpu.VMEM((2, 2 * rows, PAIR), BF),
            ],
        ),
        out_shape=[
            jax.ShapeDtypeStruct((2 * rows, width), BF),
            jax.ShapeDtypeStruct((slots * keys, 2 * width), BF),
            jax.ShapeDtypeStruct((seqs, width, rows), F32),
            jax.ShapeDtypeStruct((pairs * (PAIR + 16), rows), BF),
            jax.ShapeDtypeStruct((seqs, pairs, 2, rows), F32),
        ],
        input_output_aliases={2 * slots + 7: 2, 2 * slots + 8: 4} if before else {},
        compiler_params=params(),
        cost_estimate=cost(16 * total, 2 * len(flat) * local * model + 8 * slots * keys * width, total // HD),
        name="attend",
    )(counts, *flat, *weights, *before)


def attend_back_kernel(slots, steps, split, first, counts, both, g_own, g_oth, kv, w_kv, *refs):
    pieces = refs[: 2 * slots]
    refs = refs[2 * slots :]
    if not first:
        before, bias_before = refs[:2]
        refs = refs[2:]
    dq_own, dq_oth, mine_ref, other_ref, bias_ref = refs[:5]
    weight_refs = refs[5:-8]
    acc, queries, grads, summed, facts, turned, part, d_weight = refs[-8:]
    rows = both.shape[0] // 2
    local = pieces[0].shape[0]
    keys = 2 * local
    step = pl.program_id(0)
    upper = counts[slots + 1] == 1

    @pl.when(step == 0)
    def _():
        part[...] = jnp.zeros_like(part)
        for k in range(slots):
            mine, came = pieces[2 * k][...], pieces[2 * k + 1][...]
            turned[:, 2 * k * local : (2 * k + 1) * local] = jnp.where(upper, came, mine).T
            turned[:, (2 * k + 1) * local : (2 * k + 2) * local] = jnp.where(upper, mine, came).T

    acc[...] = jnp.zeros_like(acc)
    d_weight[...] = jnp.zeros_like(d_weight) if first else before[...]
    bias_ref[...] = jnp.zeros_like(bias_ref) if first else bias_before[...]
    for block, g_ref in enumerate((g_own, g_oth)):
        stats = unpacked_rows(g_ref[PAIR:, :], 4)
        for h, (query, grad) in enumerate(
            zip(half_lanes(both[block * rows : block * rows + rows, :]), half_rows(g_ref[:PAIR, :]))
        ):
            queries[2 * block + h] = query
            grads[2 * block + h] = grad
            facts[2 * block + h, 0:1, :] = stats[h : h + 1]
            facts[2 * block + h, 1:2, :] = stats[2 + h : 3 + h]

    @pl.loop(0, slots)
    def _(k):
        valid = counts[k]
        rows_at = pl.ds(pl.multiple_of(k * keys, keys), keys)

        def one(at, valid):
            key, value = kv[rows_at, :PAIR], kv[rows_at, PAIR:]
            query, grad = queries[at], grads[at]
            prob = jnp.exp(dot(key, query, NT) - facts[at, 0:1, :])
            if valid is not None:
                prob = jnp.where(below(prob.shape, valid), prob, 0.0)
            change = dot(value, grad, NN) - facts[at, 1:2, :]
            score = (prob * change).astype(BF)
            summed[:, PAIR:] += dot(prob.astype(BF), grad, NT)
            summed[:, :PAIR] += dot(score, query, NN)
            acc[at] += dot(key, score, TN)

        summed[...] = jnp.zeros_like(summed)

        @pl.when(valid >= keys)
        def _():
            for at in range(4):
                one(at, None)

        @pl.when(jnp.logical_and(valid > 0, valid < keys))
        def _():
            pl.loop(0, 4)(lambda at: one(at, valid))

        @pl.when(valid > 0)
        def _():
            low = summed[...].astype(BF)
            part[rows_at, :] += dot(low, w_kv[...], NT)
            d_weight[...] += dot(turned[:, rows_at], low, NN)
            bias_ref[...] += jnp.sum(low.astype(F32), axis=0, keepdims=True)

    scale = 1.0 / math.sqrt(HD)
    for h in range(2):
        at = slice(h * HD, h * HD + HD)
        dq_own[at, :] = acc[h, at, :] * scale
        dq_oth[at, :] = (acc[2 + h, at, :] * scale).astype(BF)
    half = d_weight.shape[0] // 2
    if split:
        lower_line = counts[slots + 2] == 0
        low_half, high_half = d_weight[:half, :], d_weight[half:, :]
        weight_refs[0][...] = jnp.where(lower_line, low_half, high_half)
        weight_refs[1][...] = jnp.where(lower_line, high_half, low_half).astype(BF)
    else:
        weight_refs[0][...] = d_weight[...]

    @pl.when(step == steps - 1)
    def _():
        for k in range(slots):
            low = part[2 * k * local : (2 * k + 1) * local, :]
            high = part[(2 * k + 1) * local : (2 * k + 2) * local, :]
            to = slice(k * local, k * local + local)
            mine_ref[to, :] = jnp.where(upper, high, low).astype(BF)
            other_ref[to, :] = jnp.where(upper, low, high).astype(BF)


def attend_back(counts, both, g_own, g_oth, kv, w_kv, pieces, before, last):
    rows, width = both.shape[0] // 2, both.shape[1]
    pairs = width // PAIR
    slots = len(pieces)
    local, model = pieces[0][0].shape
    keys = 2 * local
    split = last and lax.axis_size("dp") == 2
    across = lambda p, c: (0, p)
    whole = lambda p, c: (0, 0)
    once = pl.Buffered(1)
    t_spec = pl.BlockSpec((PAIR, rows), lambda p, c: (p, 0))
    g_spec = pl.BlockSpec((PAIR + 16, rows), lambda p, c: (p, 0))
    flat = [p for pair in pieces for p in pair]
    extra = () if before is None else before
    if split:
        weight_outs = [((model // 2, 2 * width), F32), ((model // 2, 2 * width), BF)]
    else:
        weight_outs = [((model, 2 * width), F32)]
    total = width * 2 * rows * kv.shape[0]
    return pl.pallas_call(
        functools.partial(attend_back_kernel, slots, pairs, split, before is None),
        grid_spec=pltpu.PrefetchScalarGridSpec(
            num_scalar_prefetch=1,
            grid=(pairs,),
            in_specs=[
                pl.BlockSpec((2 * rows, PAIR), across),
                g_spec,
                g_spec,
                pl.BlockSpec((kv.shape[0], 2 * PAIR), across),
                pl.BlockSpec((model, 2 * PAIR), across),
            ]
            + [pl.BlockSpec((local, model), whole, pipeline_mode=once) for _ in flat]
            + [pl.BlockSpec((a.shape[0], 2 * PAIR), across) for a in extra],
            out_specs=[
                t_spec,
                t_spec,
                pl.BlockSpec((slots * local, model), whole, pipeline_mode=once),
                pl.BlockSpec((slots * local, model), whole, pipeline_mode=once),
                pl.BlockSpec((1, 2 * PAIR), across),
            ]
            + [pl.BlockSpec((shape[0], 2 * PAIR), across) for shape, _ in weight_outs],
            scratch_shapes=[
                pltpu.VMEM((4, PAIR, rows), F32),
                pltpu.VMEM((4, rows, PAIR), BF),
                pltpu.VMEM((4, PAIR, rows), BF),
                pltpu.VMEM((keys, 2 * PAIR), F32),
                pltpu.VMEM((4, 2, rows), F32),
                pltpu.VMEM((model, slots * keys), BF),
                pltpu.VMEM((slots * keys, model), F32),
                pltpu.VMEM((model, 2 * PAIR), F32),
            ],
        ),
        out_shape=[
            jax.ShapeDtypeStruct((width, rows), F32),
            jax.ShapeDtypeStruct((width, rows), BF),
            jax.ShapeDtypeStruct((slots * local, model), BF),
            jax.ShapeDtypeStruct((slots * local, model), BF),
            jax.ShapeDtypeStruct((1, 2 * width), F32),
        ]
        + [jax.ShapeDtypeStruct(shape, kind) for shape, kind in weight_outs],
        compiler_params=params(),
        cost_estimate=cost(40 * total, 8 * both.size + 4 * kv.size + 8 * len(flat) * local * model, total // HD),
        name="attend_back",
    )(counts, both, g_own, g_oth, kv, w_kv, *flat, *extra)


def merge_kernel(pairs, seqs, where, o_own, lse_own, *refs):
    packs = refs[:seqs]
    weight, full_ref, low_ref, mine_ref, other_ref, lse_ref, low_s, packed = refs[seqs:]
    rows = o_own.shape[2]
    for s in range(seqs):

        @pl.when(pl.program_id(0) == s)
        def _(s=s):
            packed[...] = packs[s][...]

    for p in range(pairs):
        base = p * (PAIR + 16)
        own = lse_own[0, p]
        came = unpacked_rows(packed[base + PAIR : base + PAIR + 16, :], 2)
        highest = jnp.maximum(own, came)
        share_own, share_came = jnp.exp(own - highest), jnp.exp(came - highest)
        both = share_own + share_came
        lse_ref[0, p] = highest + jnp.log(both)
        share_own, share_came = share_own / both, share_came / both
        for h in range(2):
            at = slice(p * PAIR + h * HD, p * PAIR + h * HD + HD)
            term = packed[base + h * HD : base + h * HD + HD, :].astype(F32)
            merged = o_own[0, at, :] * share_own[h : h + 1] + term * share_came[h : h + 1]
            full_ref[0, at, :] = merged
            low_s[at, :] = merged.astype(BF)
    low_ref[0] = low_s[...]
    half = rows // 2
    mine = pl.ds(pl.multiple_of(where[0] * half, half), half)
    other = pl.ds(pl.multiple_of((1 - where[0]) * half, half), half)
    dims = (((0,), (1,)), ((), ()))
    mine_ref[0] = dot(low_s[:, mine], weight[...], dims)
    other_ref[0] = dot(low_s[:, other], weight[...], dims).astype(BF)


def merge(where, o_own, lse_own, packs, weight):
    seqs, width, rows = o_own.shape
    pairs = width // PAIR
    model = weight.shape[0]
    one = lambda *shape: pl.BlockSpec((1, *shape), lambda s, w: (s,) + (0,) * len(shape))
    return pl.pallas_call(
        functools.partial(merge_kernel, pairs, seqs),
        grid_spec=pltpu.PrefetchScalarGridSpec(
            num_scalar_prefetch=1,
            grid=(seqs,),
            in_specs=[
                one(width, rows),
                one(pairs, 2, rows),
            ]
            + [pl.BlockSpec(p.shape, lambda s, w: (0, 0)) for p in packs]
            + [
                pl.BlockSpec(weight.shape, lambda s, w: (0, 0)),
            ],
            out_specs=[one(width, rows), one(width, rows), one(rows // 2, model), one(rows // 2, model), one(pairs, 2, rows)],
            scratch_shapes=[pltpu.VMEM((width, rows), BF), pltpu.VMEM(packs[0].shape, BF)],
        ),
        out_shape=[
            jax.ShapeDtypeStruct((seqs, width, rows), F32),
            jax.ShapeDtypeStruct((seqs, width, rows), BF),
            jax.ShapeDtypeStruct((seqs, rows // 2, model), F32),
            jax.ShapeDtypeStruct((seqs, rows // 2, model), BF),
            jax.ShapeDtypeStruct((seqs, pairs, 2, rows), F32),
        ],
        compiler_params=params(),
        cost_estimate=cost(2 * seqs * width * rows * model, 12 * o_own.size + 4 * seqs * rows * model),
        name="merge",
    )(where, o_own, lse_own, *packs, weight)


def turn_kernel(pairs, seqs, where, own_ref, came_ref, weight, full_ref, lse_ref, *refs):
    packs, packed = refs[:seqs], refs[-1]
    step = pl.program_id(0)
    upper = where[0] == 1
    own, came = own_ref[0], came_ref[0]
    rows = jnp.concatenate([jnp.where(upper, came, own), jnp.where(upper, own, came)], axis=0)
    grad = dot(weight[...], rows, (((0,), (1,)), ((), ()))).astype(BF)
    product = grad.astype(F32) * full_ref[0]
    for p in range(pairs):
        base = p * (PAIR + 16)
        packed[base : base + PAIR, :] = grad[p * PAIR : p * PAIR + PAIR]
        stats = [lse_ref[0, p]]
        for h in range(2):
            at = slice(p * PAIR + h * HD, p * PAIR + h * HD + HD)
            stats.append(jnp.sum(product[at], axis=0, keepdims=True))
        packed[base + PAIR : base + PAIR + 16, :] = packed_rows(jnp.concatenate(stats, axis=0))
    for s in range(seqs):

        @pl.when(step == s)
        def _(s=s):
            packs[s][...] = packed[...]


def output_kernel(seqs, lines, where, own_ref, came_ref, low_ref, *refs):
    weight_refs, d_weight = refs[:-1], refs[-1]
    step = pl.program_id(0)
    upper = where[0] == 1
    own, came = own_ref[0], came_ref[0]
    rows = jnp.concatenate([jnp.where(upper, came, own), jnp.where(upper, own, came)], axis=0)

    @pl.when(step == 0)
    def _():
        d_weight[...] = jnp.zeros_like(d_weight)

    d_weight[...] += dot(rows, low_ref[0], (((0,), (1,)), ((), ())))

    @pl.when(step == seqs - 1)
    def _():
        if lines == 2:
            kept, sent = own_rows(where[1], d_weight, d_weight.shape[0] // 2)
            weight_refs[0][...] = kept
            weight_refs[1][...] = sent.astype(BF)
        else:
            weight_refs[0][...] = d_weight[...]


def output_grad(where, own, came, low):
    seqs, width, rows = low.shape
    model = own.shape[2]
    lines = lax.axis_size("dp")
    one = lambda *shape: pl.BlockSpec((1, *shape), lambda s, w: (s,) + (0,) * len(shape))
    outs = [((model // 2, width), F32), ((model // 2, width), BF)] if lines == 2 else [((model, width), F32)]
    return pl.pallas_call(
        functools.partial(output_kernel, seqs, lines),
        grid_spec=pltpu.PrefetchScalarGridSpec(
            num_scalar_prefetch=1,
            grid=(seqs,),
            in_specs=[one(*own.shape[1:]), one(*own.shape[1:]), one(width, rows)],
            out_specs=[pl.BlockSpec(shape, lambda s, w: (0, 0)) for shape, _ in outs],
            scratch_shapes=[pltpu.VMEM((model, width), F32)],
        ),
        out_shape=[jax.ShapeDtypeStruct(shape, kind) for shape, kind in outs],
        compiler_params=params(),
        cost_estimate=cost(2 * seqs * rows * model * width, 4 * low.size + 4 * own.size),
        name="output_grad",
    )(where, own, came, low)


def turn(where, own, came, weight, full, lse):
    seqs, width, rows = full.shape
    pairs = width // PAIR
    one = lambda *shape: pl.BlockSpec((1, *shape), lambda s, w: (s,) + (0,) * len(shape))
    whole = lambda *shape: pl.BlockSpec(shape, lambda s, w: (0, 0))
    pack_shape = (pairs * (PAIR + 16), rows)
    return pl.pallas_call(
        functools.partial(turn_kernel, pairs, seqs),
        grid_spec=pltpu.PrefetchScalarGridSpec(
            num_scalar_prefetch=1,
            grid=(seqs,),
            in_specs=[
                one(*own.shape[1:]),
                one(*own.shape[1:]),
                whole(*weight.shape),
                one(width, rows),
                one(pairs, 2, rows),
            ],
            out_specs=[whole(*pack_shape)] * seqs,
            scratch_shapes=[pltpu.VMEM(pack_shape, BF)],
        ),
        out_shape=[jax.ShapeDtypeStruct(pack_shape, BF)] * seqs,
        compiler_params=params(),
        cost_estimate=cost(2 * seqs * rows * weight.size, 6 * full.size + 4 * own.size),
        name="turn",
    )(where, own, came, weight, full, lse)


def gelu_parts(u):
    density = jnp.exp(-0.5 * u * u)
    t = 1.0 / (1.0 + (0.3275911 / math.sqrt(2.0)) * jnp.abs(u))
    series = t * (
        0.254829592
        + t * (-0.284496736 + t * (1.421413741 + t * (-1.453152027 + t * 1.061405429)))
    )
    tail = 0.5 * series * density
    share = jnp.where(u < 0.0, tail, 1.0 - tail)
    return u * share, share + u * (density * (1.0 / math.sqrt(2.0 * math.pi)))


def feed_kernel(chunk, half, own_ref, came_ref, w_in, bias, w_out, active_ref, slope_ref, mine_ref, other_ref):
    step = pl.program_id(0)
    rows = jnp.where(step < half, own_ref[...], came_ref[...])
    part = None
    for start in range(0, w_in.shape[1], chunk):
        at = slice(start, start + chunk)
        inner = dot(rows, w_in[:, at], NN) + bias[:, at]
        active, slope = gelu_parts(inner)
        active = active.astype(BF)
        active_ref[:, at] = active
        slope_ref[:, at] = slope.astype(BF)
        term = dot(active, w_out[:, at], NT)
        part = term if part is None else part + term

    @pl.when(step < half)
    def _():
        mine_ref[...] = part

    @pl.when(step >= half)
    def _():
        other_ref[...] = part.astype(BF)


def row_specs(block, half, width):
    own = pl.BlockSpec((block, width), lambda i, *c: (jnp.minimum(i, half - 1), 0))
    came = pl.BlockSpec((block, width), lambda i, *c: (jnp.maximum(i - half, 0), 0))
    return own, came


def feed(own, came, w_in, bias, w_out):
    count, width = own.shape
    units = w_in.shape[1]
    block = min(FEED_ROWS, count)
    half = count // block
    whole = lambda i: (0, 0)
    by_row = lambda i: (i, 0)
    own_spec, came_spec = row_specs(block, half, width)
    return pl.pallas_call(
        functools.partial(feed_kernel, units // 3 if units % 384 == 0 else units, half),
        grid=(2 * half,),
        in_specs=[
            own_spec,
            came_spec,
            pl.BlockSpec((width, units), whole, pipeline_mode=pl.Buffered(1)),
            pl.BlockSpec((1, units), whole),
            pl.BlockSpec((width, units), whole, pipeline_mode=pl.Buffered(1)),
        ],
        out_specs=[pl.BlockSpec((block, units), by_row), pl.BlockSpec((block, units), by_row), own_spec, came_spec],
        out_shape=[
            jax.ShapeDtypeStruct((2 * count, units), BF),
            jax.ShapeDtypeStruct((2 * count, units), BF),
            jax.ShapeDtypeStruct((count, width), F32),
            jax.ShapeDtypeStruct((count, width), BF),
        ],
        compiler_params=params(),
        cost_estimate=cost(8 * count * width * units, 4 * width * units + 8 * count * units + 12 * count * width, 2 * count * units),
        name="feed",
    )(own, came, w_in, bias, w_out)


def feed_back_kernel(half, lines, where, low_own, low_came, own_ref, came_ref, active_ref, slope_ref, w_in, w_out, *refs):
    mine_ref, other_ref, d_bias_ref = refs[:3]
    weight_refs, (d_in, d_out) = refs[3:-2], refs[-2:]
    step = pl.program_id(0)
    units = w_in.shape[1]

    @pl.when(step == 0)
    def _():
        d_in[...] = jnp.zeros_like(d_in)
        d_out[...] = jnp.zeros_like(d_out)
        d_bias_ref[...] = jnp.zeros_like(d_bias_ref)

    low = jnp.where(step < half, low_own[...], low_came[...])
    rows = jnp.where(step < half, own_ref[...], came_ref[...])
    inner = (dot(low, w_out[...], NN) * slope_ref[...].astype(F32)).astype(BF)
    part = dot(inner, w_in[...], NT)
    d_out[...] += dot(low, active_ref[...], TN)
    d_in[...] += dot(rows, inner, TN)
    d_bias_ref[...] += jnp.sum(inner.astype(F32), axis=0, keepdims=True)

    @pl.when(step < half)
    def _():
        mine_ref[...] = part

    @pl.when(step >= half)
    def _():
        other_ref[...] = part.astype(BF)

    @pl.when(step == 2 * half - 1)
    def _():
        for total, cut in ((d_in, slice(0, units)), (d_out, slice(units, 2 * units))):
            if lines == 2:
                kept, sent = own_rows(where[1], total, total.shape[0] // 2)
                weight_refs[0][:, cut] = kept.astype(BF)
                weight_refs[1][:, cut] = sent.astype(BF)
            else:
                weight_refs[0][:, cut] = total[...].astype(BF)


def feed_back(where, low_own, low_came, own, came, active, slope, w_in, w_out):
    count, width = own.shape
    units = w_in.shape[1]
    block = min(FEED_ROWS, count)
    half = count // block
    whole = lambda i, *c: (0, 0)
    by_row = lambda i, *c: (i, 0)
    once = pl.Buffered(1)
    lines = lax.axis_size("dp")
    own_spec, came_spec = row_specs(block, half, width)
    d_shape = (width // 2 if lines == 2 else width, 2 * units)
    d_count = 2 if lines == 2 else 1
    return pl.pallas_call(
        functools.partial(feed_back_kernel, half, lines),
        grid_spec=pltpu.PrefetchScalarGridSpec(
            num_scalar_prefetch=1,
            grid=(2 * half,),
            in_specs=[
                own_spec,
                came_spec,
                own_spec,
                came_spec,
                pl.BlockSpec((block, units), by_row),
                pl.BlockSpec((block, units), by_row),
                pl.BlockSpec((width, units), whole, pipeline_mode=once),
                pl.BlockSpec((width, units), whole, pipeline_mode=once),
            ],
            out_specs=[own_spec, came_spec, pl.BlockSpec((1, units), whole)]
            + [pl.BlockSpec(d_shape, whole, pipeline_mode=once)] * d_count,
            scratch_shapes=[pltpu.VMEM((width, units), F32), pltpu.VMEM((width, units), F32)],
        ),
        out_shape=[
            jax.ShapeDtypeStruct((count, width), F32),
            jax.ShapeDtypeStruct((count, width), BF),
            jax.ShapeDtypeStruct((1, units), F32),
        ]
        + [jax.ShapeDtypeStruct(d_shape, BF)] * d_count,
        compiler_params=params(),
        cost_estimate=cost(16 * count * width * units, 8 * width * units + 8 * count * units + 16 * count * width),
        name="feed_back",
    )(where, low_own, low_came, own, came, active, slope, w_in, w_out)


def centre(values):
    middle = values - jnp.mean(values, axis=-1, keepdims=True)
    scale = lax.rsqrt(jnp.mean(middle * middle, axis=-1, keepdims=True) + EPSILON)
    return middle * scale, scale


def back_through(weighted, normal, scale):
    first = jnp.mean(weighted, axis=-1, keepdims=True)
    second = jnp.mean(weighted * normal, axis=-1, keepdims=True)
    return (weighted - first - normal * second) * scale


def first_kernel(x_ref, mine_ref, came_ref, vec_ref, normal_ref, scale_ref, low_ref):
    sums = x_ref[...].astype(F32) + (mine_ref[...] + came_ref[...].astype(F32)) + vec_ref[0:1, :]
    normal, scale = centre(sums)
    normal_ref[...] = normal
    scale_ref[...] = scale
    low_ref[...] = (normal * vec_ref[1:2, :] + vec_ref[2:3, :]).astype(BF)


def second_kernel(per_seq, counts, normal_ref, mine_ref, came_ref, cot_ref, vec_ref, out_ref, grad_ref, low_ref, sums_ref):
    step = pl.program_id(0)
    block = normal_ref.shape[0]
    valid = counts[step // per_seq] - (step % per_seq) * block
    keep = lax.broadcasted_iota(jnp.int32, normal_ref.shape, 0) < valid

    @pl.when(step == 0)
    def _():
        sums_ref[...] = jnp.zeros_like(sums_ref)

    first = normal_ref[...] * vec_ref[1:2, :] + vec_ref[2:3, :]
    sums = first + (mine_ref[...] + came_ref[...].astype(F32)) + vec_ref[3:4, :]
    normal, scale = centre(sums)
    out_ref[...] = jnp.where(keep, normal * vec_ref[4:5, :] + vec_ref[5:6, :], 0.0)
    out_grad = jnp.where(keep, cot_ref[...].astype(F32), 0.0)
    grad = back_through(out_grad * vec_ref[4:5, :], normal, scale)
    grad_ref[...] = grad
    low_ref[...] = grad.astype(BF)
    sums_ref[0:1, :] += jnp.sum(out_grad * normal, axis=0, keepdims=True)
    sums_ref[1:2, :] += jnp.sum(out_grad, axis=0, keepdims=True)
    sums_ref[2:3, :] += jnp.sum(grad, axis=0, keepdims=True)


def first_back_kernel(grad_ref, mine_ref, came_ref, normal_ref, scale_ref, vec_ref, out_ref, low_ref, sums_ref):
    @pl.when(pl.program_id(0) == 0)
    def _():
        sums_ref[...] = jnp.zeros_like(sums_ref)

    given = grad_ref[...] + (mine_ref[...] + came_ref[...].astype(F32))
    normal = normal_ref[...]
    grad = back_through(given * vec_ref[1:2, :], normal, scale_ref[...])
    out_ref[...] = grad
    low_ref[...] = grad.astype(BF)
    sums_ref[0:1, :] += jnp.sum(given * normal, axis=0, keepdims=True)
    sums_ref[1:2, :] += jnp.sum(given, axis=0, keepdims=True)
    sums_ref[2:3, :] += jnp.sum(grad, axis=0, keepdims=True)


def row_call(kernel, name, block, count, width, inputs, whole_inputs, outs, sums, counts=None):
    by_row = lambda i, *c: (i, 0)
    whole = lambda i, *c: (0, 0)
    in_specs = [pl.BlockSpec((block, a.shape[1]), by_row) for a in inputs]
    in_specs += [pl.BlockSpec(a.shape, whole) for a in whole_inputs]
    out_specs = [pl.BlockSpec((block, w), by_row) for w, _ in outs]
    out_shape = [jax.ShapeDtypeStruct((count, w), t) for w, t in outs]
    if sums:
        out_specs.append(pl.BlockSpec((8, width), whole))
        out_shape.append(jax.ShapeDtypeStruct((8, width), F32))
    prefetch = 0 if counts is None else 1
    moved = sum(a.size * a.dtype.itemsize for a in inputs) + sum(count * w * 4 for w, _ in outs)
    return pl.pallas_call(
        kernel,
        grid_spec=pltpu.PrefetchScalarGridSpec(
            num_scalar_prefetch=prefetch, grid=(count // block,), in_specs=in_specs, out_specs=out_specs
        ),
        out_shape=out_shape,
        compiler_params=params(),
        cost_estimate=cost(20 * count * width, moved),
        name=name,
    )(*(() if counts is None else (counts,)), *inputs, *whole_inputs)


def interleaved(key, value):
    width = key.shape[1]
    pieces = []
    for start in range(0, width, PAIR):
        pieces += [key[:, start : start + PAIR], value[:, start : start + PAIR]]
    return jnp.concatenate(pieces, axis=1)


def apart(both):
    keys, values = [], []
    for start in range(0, both.shape[1], 2 * PAIR):
        keys.append(both[:, start : start + PAIR])
        values.append(both[:, start + PAIR : start + 2 * PAIR])
    return jnp.concatenate(keys, axis=1), jnp.concatenate(values, axis=1)


def on_device(
    block_input,
    lengths,
    cotangent,
    query_weight,
    query_bias,
    key_weight,
    value_weight,
    value_bias,
    output_weight,
    output_bias,
    first_gain,
    first_shift,
    inner_weight,
    inner_bias,
    outer_weight,
    closing_offset_vector,
    second_gain,
    second_shift,
):
    seqs, local, width = block_input.shape
    chip = 2 * local
    spots = lax.axis_size("ctx")
    spot = lax.axis_index("ctx")
    part = lax.axis_index("tp")
    core, side = part % 2, part // 2
    is_upper_core, is_upper_side = core == 1, side == 1
    span = local * lax.axis_size("tp")
    heads_width = query_weight.shape[1]
    unit_width = inner_weight.shape[1]
    count = seqs * local

    def other_core(value, **ties):
        return swap(value, "tp", 1, **ties)

    def other_side(value, **ties):
        return swap(value, "tp", 2, **ties)

    def flat(value):
        return value.reshape(-1, value.shape[-1])

    starts = jnp.stack([(spot ^ k) * span + side * chip for k in range(spots)])
    key_counts = jnp.clip(lengths[:, None] - starts[None, :], 0, chip)
    facts = jnp.stack([spot, core, lax.axis_index("dp")]).astype(jnp.int32)
    counts = jnp.concatenate([key_counts.astype(jnp.int32), jnp.broadcast_to(facts, (seqs, 3))], axis=1)
    row_counts = jnp.clip(lengths - (spot * span + part * local), 0, local).astype(jnp.int32)
    where = jnp.stack([core, lax.axis_index("dp")]).astype(jnp.int32)

    def together(*values):
        return lax.optimization_barrier(values)

    def over_spots(value, done=()):
        return [swap(value, "ctx", k, (), done) for k in range(1, spots)]

    lines = lax.axis_size("dp")
    own_width = 2 * heads_width
    attention_shard = pack([[(query_weight, False), (key_weight, False), (value_weight, False)]])
    biases = jnp.concatenate([query_bias, value_bias, inner_bias])[None, :]
    x_rows = [block_input[s] for s in range(seqs)]

    def send_near(own):
        return [swap(own, "ctx", 2), swap(own, "ctx", 1)] if spots == 4 else over_spots(own)

    def send_last(own, far):
        return [
            lax.ppermute(own, "ctx", [(1, 2), (2, 1)]),
            lax.ppermute(far, "ctx", [(2, 3), (1, 0)]),
        ]

    def finish(nears, lasts):
        if spots != 4:
            return nears
        in_middle = jnp.logical_or(spot == 1, spot == 2)
        return [nears[1], nears[0], jnp.where(in_middle, lasts[0], lasts[1])]

    came, across, *near = together(other_core(block_input), other_side(block_input), *over_spots(attention_shard))
    first_out = after(x_rows[0], *near)
    (attention_near,) = stack([attention_shard, *near])
    diagonal = [(d * 4 + t, (1 - d) * 4 + (t ^ 2)) for d in range(2) for t in range(4)]
    over_both = [lax.ppermute(attention_near, ("dp", "tp"), diagonal)] if lines == 2 else []
    attention_other, attention_line, *nears = together(
        other_side(attention_near), swap(attention_near, "dp", 1), *over_both, *send_near(first_out)
    )
    if lines == 2:
        other_line, *nears = nears
    cores = [other_core(n) for n in nears]
    lasts = send_last(after(x_rows[0], *nears), nears[0]) if spots == 4 else []
    biases_came = other_side(after(biases, *nears))
    biases_came, *rest = together(biases_came, *lasts, *cores)
    lasts, cores = rest[: len(lasts)], rest[len(lasts) :]
    arrived = [finish(nears, lasts)]
    if spots == 4:
        cores = [cores[1], cores[0], other_core(arrived[0][2])]
    if lines == 2:
        attention_all = [[attention_near, attention_other], [attention_line, other_line]]
    else:
        attention_all = over_dp([attention_near, attention_other])
    query_full, kv_full = place(attention_all, [heads_width] * 3, [(0,), (1, 2)])

    query_b = ordered(biases[:, :heads_width], biases_came[:, :heads_width], is_upper_side, 1)
    cut = slice(heads_width, own_width)
    value_b = ordered(biases[:, cut], biases_came[:, cut], is_upper_side, 1)
    cut = slice(own_width, None)
    inner_b = ordered(biases[:, cut], biases_came[:, cut], is_upper_side, 1)
    kv_bias = interleaved(jnp.zeros_like(value_b), value_b)

    pieces = [[(x_rows[0], came[0])] + list(zip(arrived[0], cores))]
    across_core = other_core(across[0])
    late_weights = together(output_weight, inner_weight, outer_weight, *nears)
    feed_shard = pack([[(late_weights[0], True), (late_weights[1], False)], [(late_weights[2], True)]])
    feed_shard = after(feed_shard, arrived[0][-1])
    feed_near = over_spots(feed_shard)
    second_nears = send_near(after(x_rows[1], arrived[0][-1]))
    weights = (query_full, kv_full, query_b, kv_bias)
    q, made, own, packed, lse = attend(counts[0], seqs, 0, pieces[0] + [(across[0], across_core)], weights, ())
    queries, kv = [q], [made]
    packs = [packed]

    own, *feed_near = together(own, *feed_near)
    near_a, near_b = stack([feed_shard] + feed_near, feed_shard.shape[1] - unit_width - -unit_width % 128)
    sending_a, sending_b = other_side(near_a), swap(near_b, "dp", 1)
    nears = together(near_a, *second_nears)[1:]
    across_core = other_core(across[1])
    cores = [other_core(n) for n in nears]
    lasts = send_last(after(x_rows[1], own), nears[0]) if spots == 4 else []
    other_a, line_b, *rest = together(sending_a, sending_b, *lasts, *cores)
    packs[0] = other_side(after(packs[0], other_a))
    lasts, cores = rest[: len(lasts)], rest[len(lasts) :]
    arrived.append(finish(nears, lasts))
    if spots == 4:
        cores = [cores[1], cores[0], other_core(arrived[1][2])]
    pieces.append([(x_rows[1], came[1])] + list(zip(arrived[1], cores)))
    if lines == 2:
        last_b = [near_b, line_b]
        sent_a = [swap(after(a, line_b), "dp", 1) for a in (near_a, other_a)]
        sent_b = [other_side(after(b, other_a)) for b in last_b]
    q, made, own, packed, lse = attend(counts[1], seqs, 1, pieces[1] + [(across[1], across_core)], weights, (own, lse))
    queries.append(q)
    kv.append(made)
    buffers = (own, lse)
    packs.append(other_side(packed))
    if lines == 2:
        sent = together(*sent_a, *sent_b, own)
        sent_a, sent_b = list(sent[:2]), list(sent[2:4])
        all_a = [[near_a, other_a], sent_a]
        all_b = [[near_b, sent_b[0]], [line_b, sent_b[1]]]
    else:
        all_a, all_b = over_dp([near_a, other_a]), over_dp([near_b, other_side(near_b)])
    output_full, inner_full = place(all_a, [heads_width, unit_width], [(0,), (1,)])
    (outer_full,) = place(all_b, [unit_width], [(0,)])

    vectors = jnp.stack([output_bias, first_gain, first_shift, closing_offset_vector, second_gain, second_shift])
    vectors = jnp.concatenate([vectors, jnp.zeros((2, width), F32)])
    block = local

    attended, attended_low, mine, other, lse_all = merge(where, *buffers, packs, output_full)
    normal, spread, first_low = row_call(
        first_kernel,
        "first_norm",
        block,
        count,
        width,
        [flat(block_input), flat(mine), flat(other_core(other))],
        [vectors],
        [(width, F32), (1, F32), (width, BF)],
        False,
    )
    first_came = other_core(first_low)
    active, slope, mine, other = feed(first_low, first_came, inner_full, inner_b, outer_full)
    output, second_grad, outer_low, second_sums = row_call(
        functools.partial(second_kernel, local // block),
        "second_norm",
        block,
        count,
        width,
        [normal, mine, other_core(other), flat(cotangent)],
        [vectors],
        [(width, F32), (width, F32), (width, BF)],
        True,
        row_counts,
    )
    mine, other, d_inner_bias, *d_feed = feed_back(
        where, outer_low, other_core(outer_low), first_low, first_came, active, slope, inner_full, outer_full
    )
    first_grad, attn_low, first_sums = row_call(
        first_back_kernel,
        "first_norm_back",
        block,
        count,
        width,
        [second_grad, mine, other_core(other), normal, spread],
        [vectors],
        [(width, F32), (width, BF)],
        True,
    )
    attn_low = attn_low.reshape(seqs, local, width)
    attn_came = other_core(attn_low)
    g_own = turn(where, attn_low, attn_came, output_full, attended, lse_all)
    d_output = output_grad(where, after(attn_low, *g_own), attn_came, attended_low)
    g_oth = [other_side(g) for g in g_own]

    lines = lax.axis_size("dp")

    def over_lines(made, done=()):
        if lines == 2:
            return made[0], swap(made[1], "dp", 1, (), done)
        value, place_at = made[0].astype(F32), lax.axis_index("dp")
        for bit in reversed(bits_of("dp")):
            mine, sent = halves(value, (place_at & bit) != 0, 0)
            term = swap(sent.astype(BF), "dp", bit, (), done)
            value = mine + term.astype(F32)
        return mine, term

    def sides_of(pair, width_of_side):
        return [(pair, 0, width_of_side)], [(pair, width_of_side, width_of_side)]

    def back(s, g_in, before):
        return attend_back(
            counts[s], queries[s], g_own[s], g_in, kv[s], kv_full, pieces[s], before, s == seqs - 1
        )

    def by_spot(mine, came):
        total = (mine.astype(F32) + came.astype(F32)).reshape(spots, local, width)
        return total[0], [total[k].astype(BF) for k in range(1, spots)]

    shared = jnp.concatenate([second_sums[:3], first_sums[:3]])
    shared_came = other_core(shared)
    output_mine, output_came = over_lines(d_output)
    g_in, shared_came = together(g_oth[0], shared_came)
    early = jnp.concatenate([(shared + shared_came).reshape(1, -1), d_inner_bias], axis=1)
    early_near = swap(early, "ctx", 1)
    own, oth, mine, other, kv_bias_sum, *kv_grads = back(0, g_in, None)
    dq_own = [own]
    oth, other, g_oth[1], output_came, early_near = together(oth, other, g_oth[1], output_came, early_near)
    output_pair = (output_mine, output_came)
    dq_came_0 = other_side(oth)
    kept_0, sent_0 = by_spot(mine, other_core(other))
    early = early + early_near
    early_far = [swap(early, "ctx", bit) for bit in bits_of("ctx")[1:]]
    feed_pairs = [over_lines(d_feed, (kv_bias_sum,))]
    feed_kept, feed_sent = fold_sides(
        feed_pairs,
        [
            sides_of(0, unit_width),
            ([(0, 2 * unit_width, unit_width)], [(0, 3 * unit_width, unit_width)]),
        ],
        BF,
    )
    feed_term = other_side(feed_sent)
    came_0 = [swap(t, "ctx", k + 1) for k, t in enumerate(sent_0)]
    g_in, dq_came_0, early, *rest = together(g_oth[1], dq_came_0, early, *early_far, feed_sent, *sent_0)
    early = sum(rest[: len(early_far)], early)
    own, oth, mine, other, kv_bias_sum, *kv_grads = back(1, g_in, (kv_grads[0], kv_bias_sum))
    dq_own.append(own)

    oth, other, feed_term, *rest = together(oth, other, feed_term, *came_0, *kv_grads)
    came_0, kv_grads = rest[: spots - 1], rest[spots - 1 :]
    dq_came_1 = other_side(oth)
    kept_1, sent_1 = by_spot(mine, other_core(other))
    feed_all_rows = add_low(feed_kept, feed_term)
    feed_spread = lax.all_to_all(feed_all_rows, "ctx", split_axis=0, concat_axis=0, tiled=True)
    dq_came = [dq_came_0, after(dq_came_1, feed_all_rows, *sent_1)]
    kv_pair = over_lines(kv_grads)
    mine, other, query_bias_sum, *query_grads = query_back(
        where, dq_own, dq_came, x_rows, [came[s] for s in range(seqs)], query_full
    )
    query_term = (mine + other_core(other).astype(F32)).reshape(seqs, local, width)
    query_pair = over_lines(query_grads)
    value_bias_sum = apart(kv_bias_sum)[1]
    vector = jnp.concatenate([early, query_bias_sum.reshape(1, -1), value_bias_sum], axis=1)
    for bit in bits_of("dp"):
        vector = vector + swap(vector, "dp", bit)
    if spots == 4:
        near_1, far_1, last_1 = sent_1
        first_1 = [
            lax.ppermute(last_1, "ctx", [(3, 2), (0, 1)]),
            lax.ppermute(last_1, "ctx", [(1, 2), (2, 1)]),
        ]
    else:
        first_1 = [swap(sent_1[0], "ctx", 1)]
    if lines == 2:
        query_last, kv_last, vector, *first_1 = together(query_pair[1], kv_pair[1], vector, *first_1)
        query_pair, kv_pair = (query_pair[0], query_last), (kv_pair[0], kv_last)
    if spots == 4:
        passed, middle = first_1
        far_1 = (far_1.astype(F32) + passed.astype(F32)).astype(BF)
        came_1 = [middle, swap(far_1, "ctx", 2), swap(near_1, "ctx", 1)]
        query_pair = (query_pair[0], after(query_pair[1], far_1))
    else:
        came_1 = first_1 + [swap(t, "ctx", k + 2) for k, t in enumerate(sent_1[1:])]

    def side_cuts(pair, offset):
        cuts = []
        for start in (0, heads_width):
            pieces_of, at = [], start
            while at < start + heads_width:
                w = min(PAIR - at % PAIR, start + heads_width - at)
                pieces_of.append((pair, 2 * (at - at % PAIR) + offset + at % PAIR, w))
                at += w
            cuts.append(pieces_of)
        return tuple(cuts)

    kept, sent = fold_sides(
        [query_pair, kv_pair, output_pair],
        [sides_of(0, heads_width), side_cuts(1, 0), side_cuts(1, PAIR), sides_of(2, heads_width)],
    )
    vector_came = other_side(vector)
    term, feed_spread, vector_came, *rest = together(other_side(sent), feed_spread, vector_came, *came_1[1:])
    came_1[1:] = rest
    vector = vector + vector_came
    early, vector = vector[:, : early.shape[1]], vector[:, early.shape[1] :]
    spare = -vector.shape[1] % kept.shape[1]
    vector = jnp.pad(vector, ((0, 0), (0, spare))).reshape(-1, kept.shape[1])
    rows = fold_spots(kept, term, vector)
    terms = [swap(t, "ctx", k + 1) for k, t in enumerate(rows[1:])]
    feed_owned = jnp.sum(feed_spread.reshape(spots, -1, feed_spread.shape[1]).astype(F32), axis=0)
    size = rows[0].shape[0]
    owned = rows[0] + sum(t[:size].astype(F32) for t in terms)
    vector = (vector + sum(unpacked_rows(t[size:], vector.shape[0]) for t in terms)).reshape(-1)
    first_grad = first_grad.reshape(seqs, local, width)
    input_grad = jnp.stack(
        [
            first_grad[s] + query_term[s] + kept + sum(t.astype(F32) for t in came)
            for s, (kept, came) in enumerate(((kept_0, came_0), (kept_1, came_1)))
        ]
    )

    early = early[0]
    shared = early[: 6 * width].reshape(6, width)

    def own_side(value, start, size):
        return jnp.where(is_upper_side, value[start + size : start + 2 * size], value[start : start + size])

    return (
        output.reshape(seqs, local, width),
        input_grad,
        owned[:, :heads_width],
        own_side(vector, 0, heads_width),
        owned[:, heads_width:own_width],
        owned[:, own_width : own_width + heads_width],
        own_side(vector, own_width, heads_width),
        owned[:, 3 * heads_width : 4 * heads_width].T,
        shared[5],
        shared[3],
        shared[4],
        feed_owned[:, :unit_width],
        own_side(early, 6 * width, unit_width),
        feed_owned[:, unit_width : 2 * unit_width].T,
        shared[2],
        shared[0],
        shared[1],
    )


def solution(mesh):
    rows = P("dp", ("ctx", "tp"), None)
    into = P(("dp", "ctx"), "tp")
    out_of = P("tp", ("dp", "ctx"))
    split, whole = P("tp"), P()
    return jax.shard_map(
        on_device,
        mesh=mesh,
        in_specs=(
            rows, P("dp"), rows, into, split, into, into, split, out_of, whole, whole, whole,
            into, split, out_of, whole, whole, whole,
        ),
        out_specs=(
            rows, rows, into, split, into, into, split, out_of, whole, whole, whole,
            into, split, out_of, whole, whole, whole,
        ),
        check_vma=False,
    )
```

```python
import functools
import math

import jax
import jax.numpy as jnp
from jax import lax
from jax.experimental import pallas as pl
from jax.experimental.pallas import tpu as pltpu
from jax.sharding import PartitionSpec as P

HD = 64
PAIR = 2 * HD
EPSILON = 1e-12
NEGATIVE = -1e30
LARGEST = 1e30
BF = jnp.bfloat16
F32 = jnp.float32
VMEM_LIMIT = 56 << 20
FEED_ROWS = 256

NN = (((1,), (0,)), ((), ()))
NT = (((1,), (1,)), ((), ()))
TN = (((0,), (0,)), ((), ()))


def dot(a, b, dims):
    return lax.dot_general(a, b, dims, preferred_element_type=F32)


def params():
    return pltpu.CompilerParams(vmem_limit_bytes=VMEM_LIMIT)


def cost(flops, moved, transcendentals=0):
    return pl.CostEstimate(flops=int(flops), bytes_accessed=int(moved), transcendentals=int(transcendentals))


def after(value, *others):
    if not others:
        return value
    return lax.optimization_barrier((value, *others))[0]


def swap(value, axis, bit, start=(), done=()):
    count = lax.axis_size(axis)
    return after(lax.ppermute(after(value, *start), axis, [(i, i ^ bit) for i in range(count)]), *done)


def bits_of(axis):
    count = lax.axis_size(axis)
    return [1 << k for k in range(count.bit_length() - 1)]


def halves(value, upper, dim):
    size = value.shape[dim] // 2
    at = upper.astype(jnp.int32) * size
    mine = lax.dynamic_slice_in_dim(value, at, size, dim)
    return mine, lax.dynamic_slice_in_dim(value, size - at, size, dim)


def ordered(mine, other, upper, dim):
    return jnp.concatenate([jnp.where(upper, other, mine), jnp.where(upper, mine, other)], axis=dim)


def call(kernel, name, outs, *arrays, prefetch=None, scratch=(), flops=0):
    spec = lambda shape: pl.BlockSpec(shape, lambda i, *c: (0,) * len(shape))
    arrays_moved = sum(a.size * a.dtype.itemsize for a in arrays) + sum(4 * math.prod(shape) for shape, _ in outs)
    return pl.pallas_call(
        kernel,
        grid_spec=pltpu.PrefetchScalarGridSpec(
            num_scalar_prefetch=0 if prefetch is None else 1,
            grid=(1,),
            in_specs=[spec(a.shape) for a in arrays],
            out_specs=[spec(shape) for shape, _ in outs],
            scratch_shapes=list(scratch),
        ),
        out_shape=[jax.ShapeDtypeStruct(shape, kind) for shape, kind in outs],
        compiler_params=params(),
        cost_estimate=cost(flops, arrays_moved),
        name=name,
    )(*(() if prefetch is None else (prefetch,)), *arrays)


def fits(rows):
    return rows % 16 == 0


def pack(groups):
    flat = [piece for group in groups for piece in group]
    widths = [sum(w.shape[0] if t else w.shape[1] for w, t in group) for group in groups]
    first, turned = flat[0]
    rows = first.shape[1] if turned else first.shape[0]

    def joined(values):
        values, out = list(values), []
        for group, width in zip(groups, widths):
            out += [values.pop(0) for _ in group]
            if -width % 128:
                out.append(jnp.zeros((rows, -width % 128), F32))
        return jnp.concatenate(out, axis=1).astype(BF)

    if not fits(rows):
        return joined(w.T if t else w for w, t in flat)

    def kernel(*refs):
        refs[-1][...] = joined(r[...].T if t else r[...] for r, (_, t) in zip(refs, flat))

    total = sum(w + -w % 128 for w in widths)
    return call(kernel, "pack", [((rows, total), BF)], *[w for w, _ in flat])[0]


def stack(parts, cuts=None):
    rows, width = parts[0].shape
    ranges = [(0, width)] if cuts is None else [(0, cuts), (cuts, width)]
    if not fits(rows):
        whole = jnp.concatenate(parts, axis=0)
        return [whole[:, start:stop] for start, stop in ranges]

    def kernel(*refs):
        for k, ref in enumerate(refs[: len(parts)]):
            for out, (start, stop) in zip(refs[len(parts) :], ranges):
                out[k * rows : k * rows + rows, :] = ref[:, start:stop]

    return call(kernel, "stack", [((rows * len(parts), stop - start), BF) for start, stop in ranges], *parts)


def over_dp(arrays, done=()):
    found = [arrays]
    for bit in bits_of("dp"):
        found = found + [[swap(a, "dp", bit, (), done) for a in one] for one in found]
    return found


def place(found, widths, joined):
    spots, spot = lax.axis_size("ctx"), lax.axis_index("ctx")
    line, side = lax.axis_index("dp"), lax.axis_index("tp") // 2
    lines = len(found)
    starts = [sum(widths[:k]) for k in range(len(widths))]
    block = found[0][0].shape[0]
    rows = block // spots
    cuts = list(zip(starts, widths))
    shapes = [(block * lines, 2 * sum(widths[m] for m in members)) for members in joined]
    if not fits(rows):
        order = ((jnp.arange(lines)[:, None] ^ line) * spots + (jnp.arange(spots)[None, :] ^ spot)).reshape(-1)
        own, oth = (
            jnp.stack([f[h] for f in found]).reshape(lines * spots, rows, -1)[order].reshape(lines * block, -1)
            for h in range(2)
        )
        low, high = jnp.where(side == 1, oth, own), jnp.where(side == 1, own, oth)
        full = [jnp.concatenate([low[:, t : t + w], high[:, t : t + w]], axis=1) for t, w in cuts]
        return [full[m[0]] if len(m) == 1 else interleaved(full[m[0]], full[m[1]]) for m in joined]

    def kernel(where, *refs):
        outs = refs[2 * lines :]
        upper = where[2] == 1
        for k in range(lines):
            own_ref, oth_ref = refs[2 * k], refs[2 * k + 1]
            for c in range(spots):
                came = pl.ds(pl.multiple_of((where[0] ^ c) * rows, rows), rows)
                to = pl.ds(pl.multiple_of(((where[1] ^ k) * spots + c) * rows, rows), rows)
                own, oth = own_ref[came, :], oth_ref[came, :]
                low, high = jnp.where(upper, oth, own), jnp.where(upper, own, oth)
                full = [jnp.concatenate([low[:, t : t + w], high[:, t : t + w]], axis=1) for t, w in cuts]
                for out, members in zip(outs, joined):
                    if len(members) == 1:
                        out[to, :] = full[members[0]]
                    else:
                        both = []
                        for p in range(0, full[members[0]].shape[1], PAIR):
                            both += [full[m][:, p : p + PAIR] for m in members]
                        out[to, :] = jnp.concatenate(both, axis=1)

    where = jnp.stack([spot, line, side]).astype(jnp.int32)
    flat = [a for one in found for a in one]
    return call(kernel, "place", [(shape, BF) for shape in shapes], *flat, prefetch=where)


def fold_sides(pairs, cuts, kind=F32):
    rows = pairs[0][0].shape[0]
    width = sum(w for low, _ in cuts for _, _, w in low)
    spare = -width % 128
    width += spare
    side = lax.axis_index("tp") // 2

    def both(totals):
        end = [jnp.zeros((totals[0].shape[0], spare), F32)] if spare else []
        low = jnp.concatenate([totals[p][:, t : t + w] for cut, _ in cuts for p, t, w in cut] + end, axis=1)
        high = jnp.concatenate([totals[p][:, t : t + w] for _, cut in cuts for p, t, w in cut] + end, axis=1)
        return low, high

    if not fits(rows):
        low, high = both([a.astype(F32) + b.astype(F32) for a, b in pairs])
        return jnp.where(side == 1, high, low).astype(kind), jnp.where(side == 1, low, high).astype(BF)

    block = rows // 2 if fits(rows // 2) else rows
    steps = rows // block

    def kernel(where, *refs):
        kept, sent = refs[2 * len(pairs) :]
        totals = [refs[2 * k][...].astype(F32) + refs[2 * k + 1][...].astype(F32) for k in range(len(pairs))]
        low, high = both(totals)
        upper = where[0] == 1
        kept[...] = jnp.where(upper, high, low).astype(kind)
        sent[...] = jnp.where(upper, low, high).astype(BF)

    spec = lambda w: pl.BlockSpec((block, w), lambda i, c: (i, 0))
    flat = [a for pair in pairs for a in pair]
    return pl.pallas_call(
        kernel,
        grid_spec=pltpu.PrefetchScalarGridSpec(
            num_scalar_prefetch=1,
            grid=(steps,),
            in_specs=[spec(a.shape[1]) for a in flat],
            out_specs=[spec(width), spec(width)],
        ),
        out_shape=[jax.ShapeDtypeStruct((rows, width), kind), jax.ShapeDtypeStruct((rows, width), BF)],
        compiler_params=params(),
        cost_estimate=cost(0, sum(a.size * a.dtype.itemsize for a in flat) + 6 * rows * width),
        name="fold_sides",
    )(side.astype(jnp.int32).reshape(1), *flat)


def fold_spots(kept, came, vector):
    spots, spot = lax.axis_size("ctx"), lax.axis_index("ctx")
    rows, width = kept.shape[0] // spots, kept.shape[1]
    count = vector.shape[0]
    below_rows = 3 * count + -3 * count % 16
    if not fits(rows):
        total = kept.astype(F32) + came.astype(F32)
        cut = lambda k: lax.dynamic_slice_in_dim(total, (spot ^ k) * rows, rows, 0)
        terms = jnp.concatenate([*in_three(vector), jnp.zeros((below_rows - 3 * count, width), BF)], axis=0)
        return [cut(0)] + [jnp.concatenate([cut(k).astype(BF), terms], axis=0) for k in range(1, spots)]

    def kernel(where, kept_ref, came_ref, vector_ref, own, *outs):
        at = pl.ds(pl.multiple_of(where[0] * rows, rows), rows)
        own[...] = kept_ref[at, :].astype(F32) + came_ref[at, :].astype(F32)
        terms = jnp.concatenate(in_three(vector_ref[...]), axis=0)
        terms = jnp.concatenate([terms, jnp.zeros((below_rows - 3 * count, width), BF)], axis=0)
        for k, out in enumerate(outs):
            at = pl.ds(pl.multiple_of((where[0] ^ (k + 1)) * rows, rows), rows)
            out[:rows, :] = (kept_ref[at, :].astype(F32) + came_ref[at, :].astype(F32)).astype(BF)
            out[rows:, :] = terms

    outs = [((rows, width), F32)] + [((rows + below_rows, width), BF)] * (spots - 1)
    return call(kernel, "fold_spots", outs, kept, came, vector, prefetch=spot.astype(jnp.int32).reshape(1))


def add_low(kept, came):
    if not fits(kept.shape[0] // 2):
        return (kept.astype(F32) + came.astype(F32)).astype(BF)

    def kernel(kept_ref, came_ref, out):
        out[...] = (kept_ref[...].astype(F32) + came_ref[...].astype(F32)).astype(BF)

    rows, width = kept.shape
    spec = pl.BlockSpec((rows // 2, width), lambda i: (i, 0))
    return pl.pallas_call(
        kernel,
        grid=(2,),
        in_specs=[spec, spec],
        out_specs=spec,
        out_shape=jax.ShapeDtypeStruct(kept.shape, BF),
        compiler_params=params(),
        cost_estimate=cost(kept.size, 8 * kept.size),
        name="add_low",
    )(kept, came)


def own_rows(where, value, rows):
    mine = pl.ds(pl.multiple_of(where * rows, rows), rows)
    other = pl.ds(pl.multiple_of((1 - where) * rows, rows), rows)
    return value[mine, :], value[other, :]


def assemble(upper, pieces, held):
    local = pieces[0].shape[0]
    for k in range(len(pieces) // 2):
        mine, came = pieces[2 * k][...], pieces[2 * k + 1][...]
        held[2 * k * local : (2 * k + 1) * local, :] = jnp.where(upper, came, mine)
        held[(2 * k + 1) * local : (2 * k + 2) * local, :] = jnp.where(upper, mine, came)


def query_back_kernel(seqs, lines, where, *refs):
    dq_own, dq_came, own, came = (refs[k * seqs : k * seqs + seqs] for k in range(4))
    weight, mine_ref, other_ref, bias_ref = refs[4 * seqs : 4 * seqs + 4]
    weight_refs, total = refs[4 * seqs + 4 : -1], refs[-1]
    upper = where[0] == 1
    half = own[0].shape[0]
    bias = None
    for s in range(seqs):
        low = (dq_own[s][...] + dq_came[s][...].astype(F32)).astype(BF)
        rows = jnp.concatenate(
            [jnp.where(upper, came[s][...], own[s][...]), jnp.where(upper, own[s][...], came[s][...])], axis=0
        )
        part = dot(low, weight[...], (((0,), (1,)), ((), ())))
        to = slice(s * half, s * half + half)
        mine_ref[to, :] = jnp.where(upper, part[half:], part[:half]).astype(BF)
        other_ref[to, :] = jnp.where(upper, part[:half], part[half:]).astype(BF)
        grad = dot(rows, low, (((0,), (1,)), ((), ())))
        total[...] = grad if s == 0 else total[...] + grad
        sums = jnp.sum(low.astype(F32), axis=1, keepdims=True)
        bias = sums if bias is None else bias + sums
    bias_ref[...] = bias
    if lines == 2:
        kept, sent = own_rows(where[1], total, total.shape[0] // 2)
        weight_refs[0][...] = kept
        weight_refs[1][...] = sent.astype(BF)
    else:
        weight_refs[0][...] = total[...]


def query_back(where, dq_own, dq_came, own, came, weight):
    seqs, lines = len(dq_own), lax.axis_size("dp")
    local, width = own[0].shape
    own_width = weight.shape[1]
    outs = [((seqs * local, width), BF), ((seqs * local, width), BF), ((own_width, 1), F32)]
    if lines == 2:
        outs += [((width // 2, own_width), F32), ((width // 2, own_width), BF)]
    else:
        outs += [((width, own_width), F32)]
    return call(
        functools.partial(query_back_kernel, seqs, lines),
        "query_back",
        outs,
        *dq_own,
        *dq_came,
        *own,
        *came,
        weight,
        prefetch=where,
        scratch=[pltpu.VMEM((width, own_width), F32)],
        flops=8 * seqs * local * width * own_width,
    )


def half_lanes(value):
    lane = lax.broadcasted_iota(jnp.int32, value.shape, 1)
    zero = jnp.zeros_like(value)
    return [jnp.where(lane < HD, value, zero), jnp.where(lane >= HD, value, zero)]


def half_rows(value):
    row = lax.broadcasted_iota(jnp.int32, value.shape, 0)
    zero = jnp.zeros_like(value)
    return [jnp.where(row < HD, value, zero), jnp.where(row >= HD, value, zero)]


def top_bits(value):
    spread = value * 65537.0
    return spread - (spread - value)


def in_three(value):
    first = top_bits(value)
    rest = value - first
    second = top_bits(rest)
    return first.astype(BF), second.astype(BF), (rest - second).astype(BF)


def packed_rows(values):
    terms = jnp.concatenate(in_three(values), axis=0)
    return jnp.concatenate([terms, jnp.zeros((16 - terms.shape[0], terms.shape[1]), BF)], axis=0)


def unpacked_rows(packed, count):
    packed = packed.astype(F32)
    return packed[:count] + packed[count : 2 * count] + packed[2 * count : 3 * count]


def below(shape, count):
    return lax.broadcasted_iota(jnp.int32, shape, 0) < count


def attend_kernel(slots, probe, old, counts, *refs):
    pieces = refs[: 2 * slots + 2]
    w_query, w_kv, b_query, b_kv = refs[2 * slots + 2 : 2 * slots + 6]
    queries, kv, o_own, packed, lse_ref, held, top, total, acc, heads = refs[2 * slots + 6 + old :]
    local = pieces[0].shape[0]
    rows = keys = 2 * local

    @pl.when(pl.program_id(0) == 0)
    def _():
        assemble(counts[slots + 1] == 1, pieces, held)

    scale = jnp.asarray(1.0 / math.sqrt(HD), BF)
    for start, to in ((0, 0), (slots * keys, rows)):
        query = (dot(held[start : start + rows, :], w_query[...], NN) + b_query[...]).astype(BF)
        queries[to : to + rows, :] = query * scale
    for h, query in enumerate(half_lanes(queries[...])):
        heads[h] = query

    @pl.loop(0, slots)
    def _(k):
        at = pl.ds(pl.multiple_of(k * keys, keys), keys)

        @pl.when(counts[k] > 0)
        def _():
            kv[at, :] = (dot(held[at, :], w_kv[...], NN) + b_kv[...]).astype(BF)

        @pl.when(counts[k] <= 0)
        def _():
            kv[at, :] = jnp.zeros((keys, 2 * PAIR), BF)

    def block(k):
        at = pl.ds(pl.multiple_of(k * keys, keys), keys)
        return kv[at, :PAIR], kv[at, PAIR:]

    first = pl.ds(pl.multiple_of(counts[slots] * keys, keys), probe)
    for h in range(2):
        top[h] = jnp.max(dot(kv[first, :PAIR], heads[h], NT), axis=0, keepdims=True)
    total[...] = jnp.zeros_like(total)
    acc[...] = jnp.zeros_like(acc)

    def quick(k, h, valid):
        key, value = block(k)
        expo = jnp.exp(dot(key, heads[h], NT) - top[h])
        if valid is not None:
            expo = jnp.where(below(expo.shape, valid), expo, 0.0)
        total[h] += jnp.sum(expo, axis=0, keepdims=True)
        acc[h] += dot(value, expo.astype(BF), TN)

    @pl.loop(0, slots)
    def _(k):
        valid = counts[k]

        @pl.when(valid >= keys)
        def _():
            quick(k, 0, None)
            quick(k, 1, None)

        @pl.when(jnp.logical_and(valid > 0, valid < keys))
        def _():
            pl.loop(0, 2)(lambda h: quick(k, h, valid))

    @pl.when(jnp.logical_not(jnp.max(total[...]) < LARGEST))
    def _():
        total[...] = jnp.zeros_like(total)
        acc[...] = jnp.zeros_like(acc)

        def careful(k, h, valid):
            key, value = block(k)
            scores = dot(key, heads[h], NT)
            scores = jnp.where(below(scores.shape, valid), scores, NEGATIVE)
            before = top[h]
            new = jnp.maximum(before, jnp.max(scores, axis=0, keepdims=True))
            expo = jnp.where(below(scores.shape, valid), jnp.exp(scores - new), 0.0)
            ratio = jnp.exp(before - new)
            total[h] = total[h] * ratio + jnp.sum(expo, axis=0, keepdims=True)
            acc[h] = acc[h] * ratio + dot(value, expo.astype(BF), TN)
            top[h] = new

        @pl.loop(0, slots)
        def _(k):
            valid = counts[k]

            @pl.when(valid > 0)
            def _():
                pl.loop(0, 2)(lambda h: careful(k, h, valid))

    lse = []
    for h in range(2):
        at = slice(h * HD, h * HD + HD)
        part = acc[h, at, :] / total[h]
        o_own[0, at, :] = part[:, :rows]
        packed[at, :] = part[:, rows:].astype(BF)
        lse.append(top[h] + jnp.log(total[h]))
        lse_ref[0, 0, h : h + 1, :] = lse[h][:, :rows]
    packed[PAIR:, :] = packed_rows(jnp.concatenate([l[:, rows:] for l in lse], axis=0))


def attend(counts, seqs, s, pieces, weights, before):
    w_query, w_kv, b_query, b_kv = weights
    slots = len(pieces) - 1
    local, model = pieces[0][0].shape
    rows, width = 2 * local, w_query.shape[1]
    pairs = width // PAIR
    keys = 2 * local
    total = width * 2 * rows * slots * keys
    anywhere = pl.BlockSpec(memory_space=pl.ANY)
    across = lambda p, c: (0, p)
    flat = [p for pair in pieces for p in pair]
    held = ((slots + 1) * keys, model)
    return pl.pallas_call(
        functools.partial(attend_kernel, slots, min(128, keys), len(before)),
        grid_spec=pltpu.PrefetchScalarGridSpec(
            num_scalar_prefetch=1,
            grid=(pairs,),
            in_specs=[pl.BlockSpec((local, model), lambda p, c: (0, 0), pipeline_mode=pl.Buffered(1)) for _ in flat]
            + [
                pl.BlockSpec((model, PAIR), across),
                pl.BlockSpec((model, 2 * PAIR), across),
                pl.BlockSpec((1, PAIR), across),
                pl.BlockSpec((1, 2 * PAIR), across),
            ]
            + [anywhere] * len(before),
            out_specs=[
                pl.BlockSpec((2 * rows, PAIR), across),
                pl.BlockSpec((slots * keys, 2 * PAIR), across),
                pl.BlockSpec((1, PAIR, rows), lambda p, c: (s, p, 0)),
                pl.BlockSpec((PAIR + 16, rows), lambda p, c: (p, 0)),
                pl.BlockSpec((1, 1, 2, rows), lambda p, c: (s, p, 0, 0)),
            ],
            scratch_shapes=[
                pltpu.VMEM(held, BF),
                pltpu.VMEM((2, 1, 2 * rows), F32),
                pltpu.VMEM((2, 1, 2 * rows), F32),
                pltpu.VMEM((2, PAIR, 2 * rows), F32),
                pltpu.VMEM((2, 2 * rows, PAIR), BF),
            ],
        ),
        out_shape=[
            jax.ShapeDtypeStruct((2 * rows, width), BF),
            jax.ShapeDtypeStruct((slots * keys, 2 * width), BF),
            jax.ShapeDtypeStruct((seqs, width, rows), F32),
            jax.ShapeDtypeStruct((pairs * (PAIR + 16), rows), BF),
            jax.ShapeDtypeStruct((seqs, pairs, 2, rows), F32),
        ],
        input_output_aliases={2 * slots + 7: 2, 2 * slots + 8: 4} if before else {},
        compiler_params=params(),
        cost_estimate=cost(16 * total, 2 * len(flat) * local * model + 8 * slots * keys * width, total // HD),
        name="attend",
    )(counts, *flat, *weights, *before)


def attend_back_kernel(slots, steps, split, first, counts, both, g_own, g_oth, kv, w_kv, *refs):
    pieces = refs[: 2 * slots]
    refs = refs[2 * slots :]
    if not first:
        before, bias_before = refs[:2]
        refs = refs[2:]
    dq_own, dq_oth, mine_ref, other_ref, bias_ref = refs[:5]
    weight_refs = refs[5:-8]
    acc, queries, grads, summed, facts, turned, part, d_weight = refs[-8:]
    rows = both.shape[0] // 2
    local = pieces[0].shape[0]
    keys = 2 * local
    step = pl.program_id(0)
    upper = counts[slots + 1] == 1

    @pl.when(step == 0)
    def _():
        part[...] = jnp.zeros_like(part)
        for k in range(slots):
            mine, came = pieces[2 * k][...], pieces[2 * k + 1][...]
            turned[:, 2 * k * local : (2 * k + 1) * local] = jnp.where(upper, came, mine).T
            turned[:, (2 * k + 1) * local : (2 * k + 2) * local] = jnp.where(upper, mine, came).T

    acc[...] = jnp.zeros_like(acc)
    d_weight[...] = jnp.zeros_like(d_weight) if first else before[...]
    bias_ref[...] = jnp.zeros_like(bias_ref) if first else bias_before[...]
    for block, g_ref in enumerate((g_own, g_oth)):
        stats = unpacked_rows(g_ref[PAIR:, :], 4)
        for h, (query, grad) in enumerate(
            zip(half_lanes(both[block * rows : block * rows + rows, :]), half_rows(g_ref[:PAIR, :]))
        ):
            queries[2 * block + h] = query
            grads[2 * block + h] = grad
            facts[2 * block + h, 0:1, :] = stats[h : h + 1]
            facts[2 * block + h, 1:2, :] = stats[2 + h : 3 + h]

    @pl.loop(0, slots)
    def _(k):
        valid = counts[k]
        rows_at = pl.ds(pl.multiple_of(k * keys, keys), keys)

        def one(at, valid):
            key, value = kv[rows_at, :PAIR], kv[rows_at, PAIR:]
            query, grad = queries[at], grads[at]
            prob = jnp.exp(dot(key, query, NT) - facts[at, 0:1, :])
            if valid is not None:
                prob = jnp.where(below(prob.shape, valid), prob, 0.0)
            change = dot(value, grad, NN) - facts[at, 1:2, :]
            score = (prob * change).astype(BF)
            summed[:, PAIR:] += dot(prob.astype(BF), grad, NT)
            summed[:, :PAIR] += dot(score, query, NN)
            acc[at] += dot(key, score, TN)

        summed[...] = jnp.zeros_like(summed)

        @pl.when(valid >= keys)
        def _():
            for at in range(4):
                one(at, None)

        @pl.when(jnp.logical_and(valid > 0, valid < keys))
        def _():
            pl.loop(0, 4)(lambda at: one(at, valid))

        @pl.when(valid > 0)
        def _():
            low = summed[...].astype(BF)
            part[rows_at, :] += dot(low, w_kv[...], NT)
            d_weight[...] += dot(turned[:, rows_at], low, NN)
            bias_ref[...] += jnp.sum(low.astype(F32), axis=0, keepdims=True)

    scale = 1.0 / math.sqrt(HD)
    for h in range(2):
        at = slice(h * HD, h * HD + HD)
        dq_own[at, :] = acc[h, at, :] * scale
        dq_oth[at, :] = (acc[2 + h, at, :] * scale).astype(BF)
    half = d_weight.shape[0] // 2
    if split:
        lower_line = counts[slots + 2] == 0
        low_half, high_half = d_weight[:half, :], d_weight[half:, :]
        weight_refs[0][...] = jnp.where(lower_line, low_half, high_half)
        weight_refs[1][...] = jnp.where(lower_line, high_half, low_half).astype(BF)
    else:
        weight_refs[0][...] = d_weight[...]

    @pl.when(step == steps - 1)
    def _():
        for k in range(slots):
            low = part[2 * k * local : (2 * k + 1) * local, :]
            high = part[(2 * k + 1) * local : (2 * k + 2) * local, :]
            to = slice(k * local, k * local + local)
            mine_ref[to, :] = jnp.where(upper, high, low).astype(BF)
            other_ref[to, :] = jnp.where(upper, low, high).astype(BF)


def attend_back(counts, both, g_own, g_oth, kv, w_kv, pieces, before, last):
    rows, width = both.shape[0] // 2, both.shape[1]
    pairs = width // PAIR
    slots = len(pieces)
    local, model = pieces[0][0].shape
    keys = 2 * local
    split = last and lax.axis_size("dp") == 2
    across = lambda p, c: (0, p)
    whole = lambda p, c: (0, 0)
    once = pl.Buffered(1)
    t_spec = pl.BlockSpec((PAIR, rows), lambda p, c: (p, 0))
    g_spec = pl.BlockSpec((PAIR + 16, rows), lambda p, c: (p, 0))
    flat = [p for pair in pieces for p in pair]
    extra = () if before is None else before
    if split:
        weight_outs = [((model // 2, 2 * width), F32), ((model // 2, 2 * width), BF)]
    else:
        weight_outs = [((model, 2 * width), F32)]
    total = width * 2 * rows * kv.shape[0]
    return pl.pallas_call(
        functools.partial(attend_back_kernel, slots, pairs, split, before is None),
        grid_spec=pltpu.PrefetchScalarGridSpec(
            num_scalar_prefetch=1,
            grid=(pairs,),
            in_specs=[
                pl.BlockSpec((2 * rows, PAIR), across),
                g_spec,
                g_spec,
                pl.BlockSpec((kv.shape[0], 2 * PAIR), across),
                pl.BlockSpec((model, 2 * PAIR), across),
            ]
            + [pl.BlockSpec((local, model), whole, pipeline_mode=once) for _ in flat]
            + [pl.BlockSpec((a.shape[0], 2 * PAIR), across) for a in extra],
            out_specs=[
                t_spec,
                t_spec,
                pl.BlockSpec((slots * local, model), whole, pipeline_mode=once),
                pl.BlockSpec((slots * local, model), whole, pipeline_mode=once),
                pl.BlockSpec((1, 2 * PAIR), across),
            ]
            + [pl.BlockSpec((shape[0], 2 * PAIR), across) for shape, _ in weight_outs],
            scratch_shapes=[
                pltpu.VMEM((4, PAIR, rows), F32),
                pltpu.VMEM((4, rows, PAIR), BF),
                pltpu.VMEM((4, PAIR, rows), BF),
                pltpu.VMEM((keys, 2 * PAIR), F32),
                pltpu.VMEM((4, 2, rows), F32),
                pltpu.VMEM((model, slots * keys), BF),
                pltpu.VMEM((slots * keys, model), F32),
                pltpu.VMEM((model, 2 * PAIR), F32),
            ],
        ),
        out_shape=[
            jax.ShapeDtypeStruct((width, rows), F32),
            jax.ShapeDtypeStruct((width, rows), BF),
            jax.ShapeDtypeStruct((slots * local, model), BF),
            jax.ShapeDtypeStruct((slots * local, model), BF),
            jax.ShapeDtypeStruct((1, 2 * width), F32),
        ]
        + [jax.ShapeDtypeStruct(shape, kind) for shape, kind in weight_outs],
        compiler_params=params(),
        cost_estimate=cost(40 * total, 8 * both.size + 4 * kv.size + 8 * len(flat) * local * model, total // HD),
        name="attend_back",
    )(counts, both, g_own, g_oth, kv, w_kv, *flat, *extra)


def merge_kernel(pairs, seqs, where, o_own, lse_own, *refs):
    packs = refs[:seqs]
    weight, full_ref, low_ref, mine_ref, other_ref, lse_ref, low_s, packed = refs[seqs:]
    rows = o_own.shape[2]
    for s in range(seqs):

        @pl.when(pl.program_id(0) == s)
        def _(s=s):
            packed[...] = packs[s][...]

    for p in range(pairs):
        base = p * (PAIR + 16)
        own = lse_own[0, p]
        came = unpacked_rows(packed[base + PAIR : base + PAIR + 16, :], 2)
        highest = jnp.maximum(own, came)
        share_own, share_came = jnp.exp(own - highest), jnp.exp(came - highest)
        both = share_own + share_came
        lse_ref[0, p] = highest + jnp.log(both)
        share_own, share_came = share_own / both, share_came / both
        for h in range(2):
            at = slice(p * PAIR + h * HD, p * PAIR + h * HD + HD)
            term = packed[base + h * HD : base + h * HD + HD, :].astype(F32)
            merged = o_own[0, at, :] * share_own[h : h + 1] + term * share_came[h : h + 1]
            full_ref[0, at, :] = merged
            low_s[at, :] = merged.astype(BF)
    low_ref[0] = low_s[...]
    half = rows // 2
    mine = pl.ds(pl.multiple_of(where[0] * half, half), half)
    other = pl.ds(pl.multiple_of((1 - where[0]) * half, half), half)
    dims = (((0,), (1,)), ((), ()))
    mine_ref[0] = dot(low_s[:, mine], weight[...], dims)
    other_ref[0] = dot(low_s[:, other], weight[...], dims).astype(BF)


def merge(where, o_own, lse_own, packs, weight):
    seqs, width, rows = o_own.shape
    pairs = width // PAIR
    model = weight.shape[0]
    one = lambda *shape: pl.BlockSpec((1, *shape), lambda s, w: (s,) + (0,) * len(shape))
    return pl.pallas_call(
        functools.partial(merge_kernel, pairs, seqs),
        grid_spec=pltpu.PrefetchScalarGridSpec(
            num_scalar_prefetch=1,
            grid=(seqs,),
            in_specs=[
                one(width, rows),
                one(pairs, 2, rows),
            ]
            + [pl.BlockSpec(p.shape, lambda s, w: (0, 0)) for p in packs]
            + [
                pl.BlockSpec(weight.shape, lambda s, w: (0, 0)),
            ],
            out_specs=[one(width, rows), one(width, rows), one(rows // 2, model), one(rows // 2, model), one(pairs, 2, rows)],
            scratch_shapes=[pltpu.VMEM((width, rows), BF), pltpu.VMEM(packs[0].shape, BF)],
        ),
        out_shape=[
            jax.ShapeDtypeStruct((seqs, width, rows), F32),
            jax.ShapeDtypeStruct((seqs, width, rows), BF),
            jax.ShapeDtypeStruct((seqs, rows // 2, model), F32),
            jax.ShapeDtypeStruct((seqs, rows // 2, model), BF),
            jax.ShapeDtypeStruct((seqs, pairs, 2, rows), F32),
        ],
        compiler_params=params(),
        cost_estimate=cost(2 * seqs * width * rows * model, 12 * o_own.size + 4 * seqs * rows * model),
        name="merge",
    )(where, o_own, lse_own, *packs, weight)


def turn_kernel(pairs, seqs, where, own_ref, came_ref, weight, full_ref, lse_ref, *refs):
    packs, packed = refs[:seqs], refs[-1]
    step = pl.program_id(0)
    upper = where[0] == 1
    own, came = own_ref[0], came_ref[0]
    rows = jnp.concatenate([jnp.where(upper, came, own), jnp.where(upper, own, came)], axis=0)
    grad = dot(weight[...], rows, (((0,), (1,)), ((), ()))).astype(BF)
    product = grad.astype(F32) * full_ref[0]
    for p in range(pairs):
        base = p * (PAIR + 16)
        packed[base : base + PAIR, :] = grad[p * PAIR : p * PAIR + PAIR]
        stats = [lse_ref[0, p]]
        for h in range(2):
            at = slice(p * PAIR + h * HD, p * PAIR + h * HD + HD)
            stats.append(jnp.sum(product[at], axis=0, keepdims=True))
        packed[base + PAIR : base + PAIR + 16, :] = packed_rows(jnp.concatenate(stats, axis=0))
    for s in range(seqs):

        @pl.when(step == s)
        def _(s=s):
            packs[s][...] = packed[...]


def output_kernel(seqs, lines, where, own_ref, came_ref, low_ref, *refs):
    weight_refs, d_weight = refs[:-1], refs[-1]
    step = pl.program_id(0)
    upper = where[0] == 1
    own, came = own_ref[0], came_ref[0]
    rows = jnp.concatenate([jnp.where(upper, came, own), jnp.where(upper, own, came)], axis=0)

    @pl.when(step == 0)
    def _():
        d_weight[...] = jnp.zeros_like(d_weight)

    d_weight[...] += dot(rows, low_ref[0], (((0,), (1,)), ((), ())))

    @pl.when(step == seqs - 1)
    def _():
        if lines == 2:
            kept, sent = own_rows(where[1], d_weight, d_weight.shape[0] // 2)
            weight_refs[0][...] = kept
            weight_refs[1][...] = sent.astype(BF)
        else:
            weight_refs[0][...] = d_weight[...]


def output_grad(where, own, came, low):
    seqs, width, rows = low.shape
    model = own.shape[2]
    lines = lax.axis_size("dp")
    one = lambda *shape: pl.BlockSpec((1, *shape), lambda s, w: (s,) + (0,) * len(shape))
    outs = [((model // 2, width), F32), ((model // 2, width), BF)] if lines == 2 else [((model, width), F32)]
    return pl.pallas_call(
        functools.partial(output_kernel, seqs, lines),
        grid_spec=pltpu.PrefetchScalarGridSpec(
            num_scalar_prefetch=1,
            grid=(seqs,),
            in_specs=[one(*own.shape[1:]), one(*own.shape[1:]), one(width, rows)],
            out_specs=[pl.BlockSpec(shape, lambda s, w: (0, 0)) for shape, _ in outs],
            scratch_shapes=[pltpu.VMEM((model, width), F32)],
        ),
        out_shape=[jax.ShapeDtypeStruct(shape, kind) for shape, kind in outs],
        compiler_params=params(),
        cost_estimate=cost(2 * seqs * rows * model * width, 4 * low.size + 4 * own.size),
        name="output_grad",
    )(where, own, came, low)


def turn(where, own, came, weight, full, lse):
    seqs, width, rows = full.shape
    pairs = width // PAIR
    one = lambda *shape: pl.BlockSpec((1, *shape), lambda s, w: (s,) + (0,) * len(shape))
    whole = lambda *shape: pl.BlockSpec(shape, lambda s, w: (0, 0))
    pack_shape = (pairs * (PAIR + 16), rows)
    return pl.pallas_call(
        functools.partial(turn_kernel, pairs, seqs),
        grid_spec=pltpu.PrefetchScalarGridSpec(
            num_scalar_prefetch=1,
            grid=(seqs,),
            in_specs=[
                one(*own.shape[1:]),
                one(*own.shape[1:]),
                whole(*weight.shape),
                one(width, rows),
                one(pairs, 2, rows),
            ],
            out_specs=[whole(*pack_shape)] * seqs,
            scratch_shapes=[pltpu.VMEM(pack_shape, BF)],
        ),
        out_shape=[jax.ShapeDtypeStruct(pack_shape, BF)] * seqs,
        compiler_params=params(),
        cost_estimate=cost(2 * seqs * rows * weight.size, 6 * full.size + 4 * own.size),
        name="turn",
    )(where, own, came, weight, full, lse)


def gelu_parts(u):
    density = jnp.exp(-0.5 * u * u)
    t = 1.0 / (1.0 + (0.3275911 / math.sqrt(2.0)) * jnp.abs(u))
    series = t * (
        0.254829592
        + t * (-0.284496736 + t * (1.421413741 + t * (-1.453152027 + t * 1.061405429)))
    )
    tail = 0.5 * series * density
    share = jnp.where(u < 0.0, tail, 1.0 - tail)
    return u * share, share + u * (density * (1.0 / math.sqrt(2.0 * math.pi)))


def feed_kernel(chunk, half, own_ref, came_ref, w_in, bias, w_out, active_ref, slope_ref, mine_ref, other_ref):
    step = pl.program_id(0)
    rows = jnp.where(step < half, own_ref[...], came_ref[...])
    part = None
    for start in range(0, w_in.shape[1], chunk):
        at = slice(start, start + chunk)
        inner = dot(rows, w_in[:, at], NN) + bias[:, at]
        active, slope = gelu_parts(inner)
        active = active.astype(BF)
        active_ref[:, at] = active
        slope_ref[:, at] = slope.astype(BF)
        term = dot(active, w_out[:, at], NT)
        part = term if part is None else part + term

    @pl.when(step < half)
    def _():
        mine_ref[...] = part

    @pl.when(step >= half)
    def _():
        other_ref[...] = part.astype(BF)


def row_specs(block, half, width):
    own = pl.BlockSpec((block, width), lambda i, *c: (jnp.minimum(i, half - 1), 0))
    came = pl.BlockSpec((block, width), lambda i, *c: (jnp.maximum(i - half, 0), 0))
    return own, came


def feed(own, came, w_in, bias, w_out):
    count, width = own.shape
    units = w_in.shape[1]
    block = min(FEED_ROWS, count)
    half = count // block
    whole = lambda i: (0, 0)
    by_row = lambda i: (i, 0)
    own_spec, came_spec = row_specs(block, half, width)
    return pl.pallas_call(
        functools.partial(feed_kernel, units // 3 if units % 384 == 0 else units, half),
        grid=(2 * half,),
        in_specs=[
            own_spec,
            came_spec,
            pl.BlockSpec((width, units), whole, pipeline_mode=pl.Buffered(1)),
            pl.BlockSpec((1, units), whole),
            pl.BlockSpec((width, units), whole, pipeline_mode=pl.Buffered(1)),
        ],
        out_specs=[pl.BlockSpec((block, units), by_row), pl.BlockSpec((block, units), by_row), own_spec, came_spec],
        out_shape=[
            jax.ShapeDtypeStruct((2 * count, units), BF),
            jax.ShapeDtypeStruct((2 * count, units), BF),
            jax.ShapeDtypeStruct((count, width), F32),
            jax.ShapeDtypeStruct((count, width), BF),
        ],
        compiler_params=params(),
        cost_estimate=cost(8 * count * width * units, 4 * width * units + 8 * count * units + 12 * count * width, 2 * count * units),
        name="feed",
    )(own, came, w_in, bias, w_out)


def feed_back_kernel(half, lines, where, low_own, low_came, own_ref, came_ref, active_ref, slope_ref, w_in, w_out, *refs):
    mine_ref, other_ref, d_bias_ref = refs[:3]
    weight_refs, (d_in, d_out) = refs[3:-2], refs[-2:]
    step = pl.program_id(0)
    units = w_in.shape[1]

    @pl.when(step == 0)
    def _():
        d_in[...] = jnp.zeros_like(d_in)
        d_out[...] = jnp.zeros_like(d_out)
        d_bias_ref[...] = jnp.zeros_like(d_bias_ref)

    low = jnp.where(step < half, low_own[...], low_came[...])
    rows = jnp.where(step < half, own_ref[...], came_ref[...])
    inner = (dot(low, w_out[...], NN) * slope_ref[...].astype(F32)).astype(BF)
    part = dot(inner, w_in[...], NT)
    d_out[...] += dot(low, active_ref[...], TN)
    d_in[...] += dot(rows, inner, TN)
    d_bias_ref[...] += jnp.sum(inner.astype(F32), axis=0, keepdims=True)

    @pl.when(step < half)
    def _():
        mine_ref[...] = part

    @pl.when(step >= half)
    def _():
        other_ref[...] = part.astype(BF)

    @pl.when(step == 2 * half - 1)
    def _():
        for total, cut in ((d_in, slice(0, units)), (d_out, slice(units, 2 * units))):
            if lines == 2:
                kept, sent = own_rows(where[1], total, total.shape[0] // 2)
                weight_refs[0][:, cut] = kept.astype(BF)
                weight_refs[1][:, cut] = sent.astype(BF)
            else:
                weight_refs[0][:, cut] = total[...].astype(BF)


def feed_back(where, low_own, low_came, own, came, active, slope, w_in, w_out):
    count, width = own.shape
    units = w_in.shape[1]
    block = min(FEED_ROWS, count)
    half = count // block
    whole = lambda i, *c: (0, 0)
    by_row = lambda i, *c: (i, 0)
    once = pl.Buffered(1)
    lines = lax.axis_size("dp")
    own_spec, came_spec = row_specs(block, half, width)
    d_shape = (width // 2 if lines == 2 else width, 2 * units)
    d_count = 2 if lines == 2 else 1
    return pl.pallas_call(
        functools.partial(feed_back_kernel, half, lines),
        grid_spec=pltpu.PrefetchScalarGridSpec(
            num_scalar_prefetch=1,
            grid=(2 * half,),
            in_specs=[
                own_spec,
                came_spec,
                own_spec,
                came_spec,
                pl.BlockSpec((block, units), by_row),
                pl.BlockSpec((block, units), by_row),
                pl.BlockSpec((width, units), whole, pipeline_mode=once),
                pl.BlockSpec((width, units), whole, pipeline_mode=once),
            ],
            out_specs=[own_spec, came_spec, pl.BlockSpec((1, units), whole)]
            + [pl.BlockSpec(d_shape, whole, pipeline_mode=once)] * d_count,
            scratch_shapes=[pltpu.VMEM((width, units), F32), pltpu.VMEM((width, units), F32)],
        ),
        out_shape=[
            jax.ShapeDtypeStruct((count, width), F32),
            jax.ShapeDtypeStruct((count, width), BF),
            jax.ShapeDtypeStruct((1, units), F32),
        ]
        + [jax.ShapeDtypeStruct(d_shape, BF)] * d_count,
        compiler_params=params(),
        cost_estimate=cost(16 * count * width * units, 8 * width * units + 8 * count * units + 16 * count * width),
        name="feed_back",
    )(where, low_own, low_came, own, came, active, slope, w_in, w_out)


def centre(values):
    middle = values - jnp.mean(values, axis=-1, keepdims=True)
    scale = lax.rsqrt(jnp.mean(middle * middle, axis=-1, keepdims=True) + EPSILON)
    return middle * scale, scale


def back_through(weighted, normal, scale):
    first = jnp.mean(weighted, axis=-1, keepdims=True)
    second = jnp.mean(weighted * normal, axis=-1, keepdims=True)
    return (weighted - first - normal * second) * scale


def first_kernel(x_ref, mine_ref, came_ref, vec_ref, normal_ref, scale_ref, low_ref):
    sums = x_ref[...].astype(F32) + (mine_ref[...] + came_ref[...].astype(F32)) + vec_ref[0:1, :]
    normal, scale = centre(sums)
    normal_ref[...] = normal
    scale_ref[...] = scale
    low_ref[...] = (normal * vec_ref[1:2, :] + vec_ref[2:3, :]).astype(BF)


def second_kernel(per_seq, counts, normal_ref, mine_ref, came_ref, cot_ref, vec_ref, out_ref, grad_ref, low_ref, sums_ref):
    step = pl.program_id(0)
    block = normal_ref.shape[0]
    valid = counts[step // per_seq] - (step % per_seq) * block
    keep = lax.broadcasted_iota(jnp.int32, normal_ref.shape, 0) < valid

    @pl.when(step == 0)
    def _():
        sums_ref[...] = jnp.zeros_like(sums_ref)

    first = normal_ref[...] * vec_ref[1:2, :] + vec_ref[2:3, :]
    sums = first + (mine_ref[...] + came_ref[...].astype(F32)) + vec_ref[3:4, :]
    normal, scale = centre(sums)
    out_ref[...] = jnp.where(keep, normal * vec_ref[4:5, :] + vec_ref[5:6, :], 0.0)
    out_grad = jnp.where(keep, cot_ref[...].astype(F32), 0.0)
    grad = back_through(out_grad * vec_ref[4:5, :], normal, scale)
    grad_ref[...] = grad
    low_ref[...] = grad.astype(BF)
    sums_ref[0:1, :] += jnp.sum(out_grad * normal, axis=0, keepdims=True)
    sums_ref[1:2, :] += jnp.sum(out_grad, axis=0, keepdims=True)
    sums_ref[2:3, :] += jnp.sum(grad, axis=0, keepdims=True)


def first_back_kernel(grad_ref, mine_ref, came_ref, normal_ref, scale_ref, vec_ref, out_ref, low_ref, sums_ref):
    @pl.when(pl.program_id(0) == 0)
    def _():
        sums_ref[...] = jnp.zeros_like(sums_ref)

    given = grad_ref[...] + (mine_ref[...] + came_ref[...].astype(F32))
    normal = normal_ref[...]
    grad = back_through(given * vec_ref[1:2, :], normal, scale_ref[...])
    out_ref[...] = grad
    low_ref[...] = grad.astype(BF)
    sums_ref[0:1, :] += jnp.sum(given * normal, axis=0, keepdims=True)
    sums_ref[1:2, :] += jnp.sum(given, axis=0, keepdims=True)
    sums_ref[2:3, :] += jnp.sum(grad, axis=0, keepdims=True)


def row_call(kernel, name, block, count, width, inputs, whole_inputs, outs, sums, counts=None):
    by_row = lambda i, *c: (i, 0)
    whole = lambda i, *c: (0, 0)
    in_specs = [pl.BlockSpec((block, a.shape[1]), by_row) for a in inputs]
    in_specs += [pl.BlockSpec(a.shape, whole) for a in whole_inputs]
    out_specs = [pl.BlockSpec((block, w), by_row) for w, _ in outs]
    out_shape = [jax.ShapeDtypeStruct((count, w), t) for w, t in outs]
    if sums:
        out_specs.append(pl.BlockSpec((8, width), whole))
        out_shape.append(jax.ShapeDtypeStruct((8, width), F32))
    prefetch = 0 if counts is None else 1
    moved = sum(a.size * a.dtype.itemsize for a in inputs) + sum(count * w * 4 for w, _ in outs)
    return pl.pallas_call(
        kernel,
        grid_spec=pltpu.PrefetchScalarGridSpec(
            num_scalar_prefetch=prefetch, grid=(count // block,), in_specs=in_specs, out_specs=out_specs
        ),
        out_shape=out_shape,
        compiler_params=params(),
        cost_estimate=cost(20 * count * width, moved),
        name=name,
    )(*(() if counts is None else (counts,)), *inputs, *whole_inputs)


def interleaved(key, value):
    width = key.shape[1]
    pieces = []
    for start in range(0, width, PAIR):
        pieces += [key[:, start : start + PAIR], value[:, start : start + PAIR]]
    return jnp.concatenate(pieces, axis=1)


def apart(both):
    keys, values = [], []
    for start in range(0, both.shape[1], 2 * PAIR):
        keys.append(both[:, start : start + PAIR])
        values.append(both[:, start + PAIR : start + 2 * PAIR])
    return jnp.concatenate(keys, axis=1), jnp.concatenate(values, axis=1)


def on_device(
    block_input,
    lengths,
    cotangent,
    query_weight,
    query_bias,
    key_weight,
    value_weight,
    value_bias,
    output_weight,
    output_bias,
    first_gain,
    first_shift,
    inner_weight,
    inner_bias,
    outer_weight,
    closing_offset_vector,
    second_gain,
    second_shift,
):
    seqs, local, width = block_input.shape
    chip = 2 * local
    spots = lax.axis_size("ctx")
    spot = lax.axis_index("ctx")
    part = lax.axis_index("tp")
    core, side = part % 2, part // 2
    is_upper_core, is_upper_side = core == 1, side == 1
    span = local * lax.axis_size("tp")
    heads_width = query_weight.shape[1]
    unit_width = inner_weight.shape[1]
    count = seqs * local

    def other_core(value, **ties):
        return swap(value, "tp", 1, **ties)

    def other_side(value, **ties):
        return swap(value, "tp", 2, **ties)

    def flat(value):
        return value.reshape(-1, value.shape[-1])

    starts = jnp.stack([(spot ^ k) * span + side * chip for k in range(spots)])
    key_counts = jnp.clip(lengths[:, None] - starts[None, :], 0, chip)
    facts = jnp.stack([spot, core, lax.axis_index("dp")]).astype(jnp.int32)
    counts = jnp.concatenate([key_counts.astype(jnp.int32), jnp.broadcast_to(facts, (seqs, 3))], axis=1)
    row_counts = jnp.clip(lengths - (spot * span + part * local), 0, local).astype(jnp.int32)
    where = jnp.stack([core, lax.axis_index("dp")]).astype(jnp.int32)

    def together(*values):
        return lax.optimization_barrier(values)

    def over_spots(value, done=()):
        return [swap(value, "ctx", k, (), done) for k in range(1, spots)]

    lines = lax.axis_size("dp")
    own_width = 2 * heads_width
    attention_shard = pack([[(query_weight, False), (key_weight, False), (value_weight, False)]])
    biases = jnp.concatenate([query_bias, value_bias, inner_bias])[None, :]
    x_rows = [block_input[s] for s in range(seqs)]

    def send_near(own):
        return [swap(own, "ctx", 2), swap(own, "ctx", 1)] if spots == 4 else over_spots(own)

    def send_last(own, far):
        return [
            lax.ppermute(own, "ctx", [(1, 2), (2, 1)]),
            lax.ppermute(far, "ctx", [(2, 3), (1, 0)]),
        ]

    def finish(nears, lasts):
        if spots != 4:
            return nears
        in_middle = jnp.logical_or(spot == 1, spot == 2)
        return [nears[1], nears[0], jnp.where(in_middle, lasts[0], lasts[1])]

    came, across, *near = together(other_core(block_input), other_side(block_input), *over_spots(attention_shard))
    first_out = after(x_rows[0], *near)
    (attention_near,) = stack([attention_shard, *near])
    diagonal = [(d * 4 + t, (1 - d) * 4 + (t ^ 2)) for d in range(2) for t in range(4)]
    over_both = [lax.ppermute(attention_near, ("dp", "tp"), diagonal)] if lines == 2 else []
    attention_other, attention_line, *nears = together(
        other_side(attention_near), swap(attention_near, "dp", 1), *over_both, *send_near(first_out)
    )
    if lines == 2:
        other_line, *nears = nears
    cores = [other_core(n) for n in nears]
    lasts = send_last(after(x_rows[0], *nears), nears[0]) if spots == 4 else []
    biases_came = other_side(after(biases, *nears))
    biases_came, *rest = together(biases_came, *lasts, *cores)
    lasts, cores = rest[: len(lasts)], rest[len(lasts) :]
    arrived = [finish(nears, lasts)]
    if spots == 4:
        cores = [cores[1], cores[0], other_core(arrived[0][2])]
    if lines == 2:
        attention_all = [[attention_near, attention_other], [attention_line, other_line]]
    else:
        attention_all = over_dp([attention_near, attention_other])
    query_full, kv_full = place(attention_all, [heads_width] * 3, [(0,), (1, 2)])

    query_b = ordered(biases[:, :heads_width], biases_came[:, :heads_width], is_upper_side, 1)
    cut = slice(heads_width, own_width)
    value_b = ordered(biases[:, cut], biases_came[:, cut], is_upper_side, 1)
    cut = slice(own_width, None)
    inner_b = ordered(biases[:, cut], biases_came[:, cut], is_upper_side, 1)
    kv_bias = interleaved(jnp.zeros_like(value_b), value_b)

    pieces = [[(x_rows[0], came[0])] + list(zip(arrived[0], cores))]
    across_core = other_core(across[0])
    late_weights = together(output_weight, inner_weight, outer_weight, *nears)
    feed_shard = pack([[(late_weights[0], True), (late_weights[1], False)], [(late_weights[2], True)]])
    feed_shard = after(feed_shard, arrived[0][-1])
    feed_near = over_spots(feed_shard)
    second_nears = send_near(after(x_rows[1], arrived[0][-1]))
    weights = (query_full, kv_full, query_b, kv_bias)
    q, made, own, packed, lse = attend(counts[0], seqs, 0, pieces[0] + [(across[0], across_core)], weights, ())
    queries, kv = [q], [made]
    packs = [packed]

    own, *feed_near = together(own, *feed_near)
    near_a, near_b = stack([feed_shard] + feed_near, feed_shard.shape[1] - unit_width - -unit_width % 128)
    sending_a, sending_b = other_side(near_a), swap(near_b, "dp", 1)
    nears = together(near_a, *second_nears)[1:]
    across_core = other_core(across[1])
    cores = [other_core(n) for n in nears]
    lasts = send_last(after(x_rows[1], own), nears[0]) if spots == 4 else []
    other_a, line_b, *rest = together(sending_a, sending_b, *lasts, *cores)
    packs[0] = other_side(after(packs[0], other_a))
    lasts, cores = rest[: len(lasts)], rest[len(lasts) :]
    arrived.append(finish(nears, lasts))
    if spots == 4:
        cores = [cores[1], cores[0], other_core(arrived[1][2])]
    pieces.append([(x_rows[1], came[1])] + list(zip(arrived[1], cores)))
    if lines == 2:
        last_b = [near_b, line_b]
        sent_a = [swap(after(a, line_b), "dp", 1) for a in (near_a, other_a)]
        sent_b = [other_side(after(b, other_a)) for b in last_b]
    q, made, own, packed, lse = attend(counts[1], seqs, 1, pieces[1] + [(across[1], across_core)], weights, (own, lse))
    queries.append(q)
    kv.append(made)
    buffers = (own, lse)
    packs.append(other_side(packed))
    if lines == 2:
        sent = together(*sent_a, *sent_b, own)
        sent_a, sent_b = list(sent[:2]), list(sent[2:4])
        all_a = [[near_a, other_a], sent_a]
        all_b = [[near_b, sent_b[0]], [line_b, sent_b[1]]]
    else:
        all_a, all_b = over_dp([near_a, other_a]), over_dp([near_b, other_side(near_b)])
    output_full, inner_full = place(all_a, [heads_width, unit_width], [(0,), (1,)])
    (outer_full,) = place(all_b, [unit_width], [(0,)])

    vectors = jnp.stack([output_bias, first_gain, first_shift, closing_offset_vector, second_gain, second_shift])
    vectors = jnp.concatenate([vectors, jnp.zeros((2, width), F32)])
    block = local

    attended, attended_low, mine, other, lse_all = merge(where, *buffers, packs, output_full)
    normal, spread, first_low = row_call(
        first_kernel,
        "first_norm",
        block,
        count,
        width,
        [flat(block_input), flat(mine), flat(other_core(other))],
        [vectors],
        [(width, F32), (1, F32), (width, BF)],
        False,
    )
    first_came = other_core(first_low)
    active, slope, mine, other = feed(first_low, first_came, inner_full, inner_b, outer_full)
    output, second_grad, outer_low, second_sums = row_call(
        functools.partial(second_kernel, local // block),
        "second_norm",
        block,
        count,
        width,
        [normal, mine, other_core(other), flat(cotangent)],
        [vectors],
        [(width, F32), (width, F32), (width, BF)],
        True,
        row_counts,
    )
    mine, other, d_inner_bias, *d_feed = feed_back(
        where, outer_low, other_core(outer_low), first_low, first_came, active, slope, inner_full, outer_full
    )
    first_grad, attn_low, first_sums = row_call(
        first_back_kernel,
        "first_norm_back",
        block,
        count,
        width,
        [second_grad, mine, other_core(other), normal, spread],
        [vectors],
        [(width, F32), (width, BF)],
        True,
    )
    attn_low = attn_low.reshape(seqs, local, width)
    attn_came = other_core(attn_low)
    g_own = turn(where, attn_low, attn_came, output_full, attended, lse_all)
    d_output = output_grad(where, after(attn_low, *g_own), attn_came, attended_low)
    g_oth = [other_side(g) for g in g_own]

    lines = lax.axis_size("dp")

    def over_lines(made, done=()):
        if lines == 2:
            return made[0], swap(made[1], "dp", 1, (), done)
        value, place_at = made[0].astype(F32), lax.axis_index("dp")
        for bit in reversed(bits_of("dp")):
            mine, sent = halves(value, (place_at & bit) != 0, 0)
            term = swap(sent.astype(BF), "dp", bit, (), done)
            value = mine + term.astype(F32)
        return mine, term

    def sides_of(pair, width_of_side):
        return [(pair, 0, width_of_side)], [(pair, width_of_side, width_of_side)]

    def back(s, g_in, before):
        return attend_back(
            counts[s], queries[s], g_own[s], g_in, kv[s], kv_full, pieces[s], before, s == seqs - 1
        )

    def by_spot(mine, came):
        total = (mine.astype(F32) + came.astype(F32)).reshape(spots, local, width)
        return total[0], [total[k].astype(BF) for k in range(1, spots)]

    shared = jnp.concatenate([second_sums[:3], first_sums[:3]])
    shared_came = other_core(shared)
    output_mine, output_came = over_lines(d_output)
    g_in, shared_came = together(g_oth[0], shared_came)
    early = jnp.concatenate([(shared + shared_came).reshape(1, -1), d_inner_bias], axis=1)
    early_near = swap(early, "ctx", 1)
    own, oth, mine, other, kv_bias_sum, *kv_grads = back(0, g_in, None)
    dq_own = [own]
    oth, other, g_oth[1], output_came, early_near = together(oth, other, g_oth[1], output_came, early_near)
    output_pair = (output_mine, output_came)
    dq_came_0 = other_side(oth)
    kept_0, sent_0 = by_spot(mine, other_core(other))
    early = early + early_near
    early_far = [swap(early, "ctx", bit) for bit in bits_of("ctx")[1:]]
    feed_pairs = [over_lines(d_feed, (kv_bias_sum,))]
    feed_kept, feed_sent = fold_sides(
        feed_pairs,
        [
            sides_of(0, unit_width),
            ([(0, 2 * unit_width, unit_width)], [(0, 3 * unit_width, unit_width)]),
        ],
        BF,
    )
    feed_term = other_side(feed_sent)
    came_0 = [swap(t, "ctx", k + 1) for k, t in enumerate(sent_0)]
    g_in, dq_came_0, early, *rest = together(g_oth[1], dq_came_0, early, *early_far, feed_sent, *sent_0)
    early = sum(rest[: len(early_far)], early)
    own, oth, mine, other, kv_bias_sum, *kv_grads = back(1, g_in, (kv_grads[0], kv_bias_sum))
    dq_own.append(own)

    oth, other, feed_term, *rest = together(oth, other, feed_term, *came_0, *kv_grads)
    came_0, kv_grads = rest[: spots - 1], rest[spots - 1 :]
    dq_came_1 = other_side(oth)
    kept_1, sent_1 = by_spot(mine, other_core(other))
    feed_all_rows = add_low(feed_kept, feed_term)
    feed_spread = lax.all_to_all(feed_all_rows, "ctx", split_axis=0, concat_axis=0, tiled=True)
    dq_came = [dq_came_0, after(dq_came_1, feed_all_rows, *sent_1)]
    kv_pair = over_lines(kv_grads)
    mine, other, query_bias_sum, *query_grads = query_back(
        where, dq_own, dq_came, x_rows, [came[s] for s in range(seqs)], query_full
    )
    query_term = (mine.astype(F32) + other_core(other).astype(F32)).reshape(seqs, local, width)
    query_pair = over_lines(query_grads)
    value_bias_sum = apart(kv_bias_sum)[1]
    vector = jnp.concatenate([early, query_bias_sum.reshape(1, -1), value_bias_sum], axis=1)
    for bit in bits_of("dp"):
        vector = vector + swap(vector, "dp", bit)
    if spots == 4:
        near_1, far_1, last_1 = sent_1
        first_1 = [
            lax.ppermute(last_1, "ctx", [(3, 2), (0, 1)]),
            lax.ppermute(last_1, "ctx", [(1, 2), (2, 1)]),
        ]
    else:
        first_1 = [swap(sent_1[0], "ctx", 1)]
    if lines == 2:
        query_last, kv_last, vector, *first_1 = together(query_pair[1], kv_pair[1], vector, *first_1)
        query_pair, kv_pair = (query_pair[0], query_last), (kv_pair[0], kv_last)
    if spots == 4:
        passed, middle = first_1
        far_1 = (far_1.astype(F32) + passed.astype(F32)).astype(BF)
        came_1 = [middle, swap(far_1, "ctx", 2), swap(near_1, "ctx", 1)]
        query_pair = (query_pair[0], after(query_pair[1], far_1))
    else:
        came_1 = first_1 + [swap(t, "ctx", k + 2) for k, t in enumerate(sent_1[1:])]

    def side_cuts(pair, offset):
        cuts = []
        for start in (0, heads_width):
            pieces_of, at = [], start
            while at < start + heads_width:
                w = min(PAIR - at % PAIR, start + heads_width - at)
                pieces_of.append((pair, 2 * (at - at % PAIR) + offset + at % PAIR, w))
                at += w
            cuts.append(pieces_of)
        return tuple(cuts)

    kept, sent = fold_sides(
        [query_pair, kv_pair, output_pair],
        [sides_of(0, heads_width), side_cuts(1, 0), side_cuts(1, PAIR), sides_of(2, heads_width)],
        BF,
    )
    vector_came = other_side(vector)
    term, feed_spread, vector_came, *rest = together(other_side(sent), feed_spread, vector_came, *came_1[1:])
    came_1[1:] = rest
    vector = vector + vector_came
    early, vector = vector[:, : early.shape[1]], vector[:, early.shape[1] :]
    spare = -vector.shape[1] % kept.shape[1]
    vector = jnp.pad(vector, ((0, 0), (0, spare))).reshape(-1, kept.shape[1])
    rows = fold_spots(kept, term, vector)
    terms = [swap(t, "ctx", k + 1) for k, t in enumerate(rows[1:])]
    feed_owned = jnp.sum(feed_spread.reshape(spots, -1, feed_spread.shape[1]).astype(F32), axis=0)
    size = rows[0].shape[0]
    owned = rows[0] + sum(t[:size].astype(F32) for t in terms)
    vector = (vector + sum(unpacked_rows(t[size:], vector.shape[0]) for t in terms)).reshape(-1)
    first_grad = first_grad.reshape(seqs, local, width)
    input_grad = jnp.stack(
        [
            first_grad[s] + query_term[s] + kept + sum(t.astype(F32) for t in came)
            for s, (kept, came) in enumerate(((kept_0, came_0), (kept_1, came_1)))
        ]
    )

    early = early[0]
    shared = early[: 6 * width].reshape(6, width)

    def own_side(value, start, size):
        return jnp.where(is_upper_side, value[start + size : start + 2 * size], value[start : start + size])

    return (
        output.reshape(seqs, local, width),
        input_grad,
        owned[:, :heads_width],
        own_side(vector, 0, heads_width),
        owned[:, heads_width:own_width],
        owned[:, own_width : own_width + heads_width],
        own_side(vector, own_width, heads_width),
        owned[:, 3 * heads_width : 4 * heads_width].T,
        shared[5],
        shared[3],
        shared[4],
        feed_owned[:, :unit_width],
        own_side(early, 6 * width, unit_width),
        feed_owned[:, unit_width : 2 * unit_width].T,
        shared[2],
        shared[0],
        shared[1],
    )


def solution(mesh):
    rows = P("dp", ("ctx", "tp"), None)
    into = P(("dp", "ctx"), "tp")
    out_of = P("tp", ("dp", "ctx"))
    split, whole = P("tp"), P()
    return jax.shard_map(
        on_device,
        mesh=mesh,
        in_specs=(
            rows, P("dp"), rows, into, split, into, into, split, out_of, whole, whole, whole,
            into, split, out_of, whole, whole, whole,
        ),
        out_specs=(
            rows, rows, into, split, into, into, split, out_of, whole, whole, whole,
            into, split, out_of, whole, whole, whole,
        ),
        check_vma=False,
    )
```
